32 devices in a mesh: fsdp: 16 (over z, y, core), tp: 2 (over x).
Axes of the slice: x: 2, y: 2, z: 4, core: 2. Of those that a mesh axis runs over, the one named last changes fastest.
Arguments:
- inputs: bfloat16 [4096, 2048], P(('fsdp', 'tp')), may hold values from -6 to 6
- teacher: bfloat16 [4096, 2048], P('fsdp'), may hold values from -6 to 6
- valid_mask: int32 [4096], P('fsdp'), may hold values from 0 to 1
- prefix: int32 [16], P('fsdp'), may hold values from 0 to 256
- routes: int32 [4096, 6], P('fsdp'), may hold values from 0 to 15, all different within a row; in each aligned block of 256 rows (0 to 255, 256 to 511, ...) at most 128 rows name the same one
- norm_gain: bfloat16 [2048], P('fsdp'), may hold values from 0.5 to 1.5
- query_weight: bfloat16 [2048, 3072], P('fsdp', 'tp'), may hold values from -0.125 to 0.125
- latent_weight: bfloat16 [2048, 576], P('fsdp'), may hold values from -0.125 to 0.125
- latent_gain: bfloat16 [512], P('fsdp'), may hold values from 0.5 to 1.5
- expand_weight: bfloat16 [512, 4096], P('fsdp', 'tp'), may hold values from -0.25 to 0.25
- output_weight: bfloat16 [2048, 2048], P('tp', 'fsdp'), may hold values from -0.75 to 0.75
- moe_gain: bfloat16 [2048], P('fsdp'), may hold values from 0.5 to 1.5
- router_weight: bfloat16 [2048, 16], P('fsdp'), may hold values from -0.0625 to 0.0625
- shared_gate: bfloat16 [2048, 2816], P('fsdp', 'tp'), may hold values from -0.125 to 0.125
- shared_up: bfloat16 [2048, 2816], P('fsdp', 'tp'), may hold values from -0.125 to 0.125
- shared_down: bfloat16 [2816, 2048], P('tp', 'fsdp'), may hold values from -0.109375 to 0.109375
- expert_gate: bfloat16 [16, 2048, 1408], P('fsdp', None, 'tp'), may hold values from -0.125 to 0.125
- expert_up: bfloat16 [16, 2048, 1408], P('fsdp', None, 'tp'), may hold values from -0.125 to 0.125
- expert_down: bfloat16 [16, 1408, 2048], P('fsdp', 'tp'), may hold values from -1.5 to 1.5
Outputs:
- loss_value: float32 [], replicated
- activations: float32 [4096, 2048], P(('fsdp', 'tp'))
- input_grad: float32 [4096, 2048], P(('fsdp', 'tp'))
- norm_gain_grad: float32 [2048], P('fsdp')
- query_weight_grad: float32 [2048, 3072], P('fsdp', 'tp')
- latent_weight_grad: float32 [2048, 576], P('fsdp')
- latent_gain_grad: float32 [512], P('fsdp')
- expand_weight_grad: float32 [512, 4096], P('fsdp', 'tp')
- output_weight_grad: float32 [2048, 2048], P('tp', 'fsdp')
- moe_gain_grad: float32 [2048], P('fsdp')
- router_weight_grad: float32 [2048, 16], P('fsdp')
- shared_gate_grad: float32 [2048, 2816], P('fsdp', 'tp')
- shared_up_grad: float32 [2048, 2816], P('fsdp', 'tp')
- shared_down_grad: float32 [2816, 2048], P('tp', 'fsdp')
- expert_gate_grad: float32 [16, 2048, 1408], P('fsdp', None, 'tp')
- expert_up_grad: float32 [16, 2048, 1408], P('fsdp', None, 'tp')
- expert_down_grad: float32 [16, 1408, 2048], P('fsdp', 'tp')
The draws below stay inside these ranges and needn't reach their ends.
Inputs may be any that keep to these rules, and one draw needn't show every extreme that they name: `routes`: in each aligned block of 256 rows (the tokens of one sequence) no expert is named more than 128 times; a token names 6 different experts.
All inputs are finite; a program needn't handle non-finite values.
Results may differ from the reference program's by a relative error of at most 0.018.
Values may be sent and summed in bfloat16 or wider, within the bound.
A program may use at most 320 MiB of HBM per device.

```python
import math
import jax
import jax.numpy as jnp
import numpy as np
from jax import lax

D = 2048
HEADS = 16
NOPE = 128
ROPE = 64
RANK = 512
VDIM = 128
FF = 1408
SHARED_FF = 2816
TOPK = 6
GROUP = 256
SEQS = 16
TOKENS = 4096
EXPERTS = 16
CAP = 128


def draw_valid_mask(key, part):
    places = jnp.arange(TOKENS, dtype=jnp.int32)
    levels = jax.random.randint(key, (TOKENS,), 0, 900, dtype=jnp.int32)
    return (levels < 300 + 600 * places // TOKENS).astype(jnp.int32)


def with_ends(values, own_key, low, top_value):
    shape = values.shape
    index_at = [jax.random.randint(jax.random.fold_in(own_key, axis), (), 0, shape[axis]) for axis in range(len(shape))]
    values = values.at[tuple(index_at)].set(low)
    longest = shape.index(max(shape))
    index_at[longest] = (index_at[longest] + 1) % shape[longest]
    return values.at[tuple(index_at)].set(top_value)


def steps_of(stream_key, shape, split, low, top_value):
    factor_of, own = 1.0, jax.random.fold_in(stream_key, 6)
    for dim, parts in split:
        draws = jnp.exp(jax.random.uniform(jax.random.fold_in(own, dim), (parts,), jnp.float32, low / len(split), top_value / len(split)))
        factor_of = factor_of * jnp.repeat(draws, shape[dim] // parts).reshape([-1 if axis == dim else 1 for axis in range(len(shape))])
    return factor_of


def deal_out(key, own, number, rows, number_of, top, reach, skew):
    sequence = jax.random.permutation(key, number_of)
    heavy_load, ordinary = portions_of(number_of, rows * top, reach, skew, True), portions_of(number_of, rows * top, reach, skew, False)
    places = jnp.arange(number_of)

    def named(sizes, offset_by):
        used = int((sizes > 0).sum())
        fixed = max(1, used // 4)
        moved = fixed + (places - fixed + offset_by * (used - fixed)) % max(1, number_of - fixed)
        return jnp.zeros((number_of,), jnp.int32).at[sequence[jnp.where(places < fixed, places, moved)]].set(jnp.asarray(sizes, jnp.int32))

    sizes = jnp.where(number % 4 == 0, named(heavy_load, number // 4), named(ordinary, number - number // 4 - 1))
    mixed = jax.random.permutation(jax.random.fold_in(own, 3), number_of)
    giver, taker = mixed[0:number_of // 2 * 2:2], mixed[1:number_of // 2 * 2:2]
    slack = jnp.minimum(sizes[giver] - 1, reach - sizes[taker]) // 2
    slack = jnp.where((giver == sequence[0]) | (taker == sequence[0]) | (sizes[taker] == 0), 0, jnp.maximum(slack, 0))
    moved = jax.random.randint(jax.random.fold_in(own, 4), (number_of // 2,), 0, 1 << 20) % (slack + 1)
    sizes = sizes.at[giver].add(-moved).at[taker].add(moved)
    members = jnp.searchsorted(jnp.cumsum(sizes), jnp.arange(rows * top), side="right").astype(jnp.int32)
    grid = members.reshape(top, rows).T
    grid = grid[jax.random.permutation(jax.random.fold_in(own, 1), rows)]
    offset_by = jax.random.randint(jax.random.fold_in(own, 2), (rows, 1), 0, top)
    return jnp.take_along_axis(grid, (jnp.arange(top)[None, :] + offset_by) % top, axis=1)


def portions_of(count, total, reach, skew, full):
    portions = [(1 << 20) // math.isqrt(rank ** skew) + 1 for rank in range(1, count + 1)]
    largest = reach if full else min(reach, max(-(-total // count), total * portions[0] // sum(portions)))
    least = 1 if total - largest >= count - 1 else 0
    counts, spare = [largest] + [least] * (count - 1), total - largest - least * (count - 1)
    while spare > 0:
        free = [i for i in range(1, count) if counts[i] < largest] or [i for i in range(1, count) if counts[i] < reach]
        mass, left = sum([portions[i] for i in free]), spare
        for i in free:
            more = min(reach - counts[i], max(1, left * portions[i] // mass), spare)
            counts[i] = counts[i] + more
            spare = spare - more
    return np.array(counts)


def centred(key, dims, scale, bound, shards=(), held_as=jnp.bfloat16):
    values = scale * jax.random.normal(key, dims, jnp.float32)
    if shards:
        values = values * steps_of(key, dims, shards, -0.22, 0.18)
    return jnp.clip(values, -bound, bound).astype(held_as)


def setup_inputs(seed: int = 0) -> dict:
    key_list = jax.random.split(jax.random.key(seed), 20)
    inputs = centred(key_list[0], (TOKENS, D), 1.0, 6.0, ((0, 32),))
    teacher = centred(key_list[1], (TOKENS, D), 1.0, 6.0, ((0, 16),))
    valid_mask = draw_valid_mask(jax.random.fold_in(key_list[19], 71), 0)
    prefix = with_ends(jax.random.randint(key_list[3], (SEQS,), 0, GROUP + 1), jax.random.fold_in(key_list[3], 1), 0, GROUP).astype(jnp.int32)
    routes_keys = jax.random.split(jax.random.fold_in(key_list[4], 1), TOKENS // GROUP)
    routes_turns = jax.random.permutation(jax.random.fold_in(key_list[4], 3), TOKENS // GROUP)
    routes = jax.vmap(lambda own, number: deal_out(jax.random.fold_in(key_list[4], 2), own, number, GROUP, EXPERTS, TOPK, CAP, 1))(routes_keys, routes_turns).reshape((TOKENS, TOPK))
    norm_gain = jnp.clip(1.0 + 0.1 * jax.random.normal(key_list[5], (D,), jnp.float32), 0.5, 1.5).astype(jnp.bfloat16)
    query_weight = centred(key_list[6], (D, HEADS * (NOPE + ROPE)), D ** -0.5, 0.125, ((0, 16), (1, 2)))
    latent_weight = centred(key_list[7], (D, RANK + ROPE), D ** -0.5, 0.125, ((0, 16),))
    latent_gain = jnp.clip(1.0 + 0.1 * jax.random.normal(key_list[8], (RANK,), jnp.float32), 0.5, 1.5).astype(jnp.bfloat16)
    expand_weight = centred(key_list[9], (RANK, HEADS * (NOPE + VDIM)), RANK ** -0.5, 0.25, ((0, 16), (1, 2)))
    output_weight = centred(key_list[10], (HEADS * VDIM, D), (HEADS * VDIM // 32) ** -0.5, 0.75, ((0, 2), (1, 16)))
    moe_gain = jnp.clip(1.0 + 0.1 * jax.random.normal(key_list[11], (D,), jnp.float32), 0.5, 1.5).astype(jnp.bfloat16)
    router_weight = centred(key_list[12], (D, EXPERTS), (4 * D) ** -0.5, 0.0625, ((0, 16),))
    shared_gate = centred(key_list[13], (D, SHARED_FF), D ** -0.5, 0.125, ((0, 16), (1, 2)))
    shared_up = centred(key_list[14], (D, SHARED_FF), D ** -0.5, 0.125, ((0, 16), (1, 2)))
    shared_down = centred(key_list[15], (SHARED_FF, D), SHARED_FF ** -0.5, 0.109375, ((0, 2), (1, 16)))
    expert_gate = centred(key_list[16], (EXPERTS, D, FF), D ** -0.5, 0.125, ((0, 16), (2, 2)))
    expert_up = centred(key_list[17], (EXPERTS, D, FF), D ** -0.5, 0.125, ((0, 16), (2, 2)))
    expert_down = centred(key_list[18], (EXPERTS, FF, D), (max(1, 4750 // (EXPERTS * EXPERTS))) ** -0.5, 1.5, ((0, 16), (1, 2)))
    return dict(inputs=inputs, teacher=teacher, valid_mask=valid_mask, prefix=prefix, routes=routes, norm_gain=norm_gain, query_weight=query_weight, latent_weight=latent_weight, latent_gain=latent_gain, expand_weight=expand_weight, output_weight=output_weight, moe_gain=moe_gain, router_weight=router_weight, shared_gate=shared_gate, shared_up=shared_up, shared_down=shared_down, expert_gate=expert_gate, expert_up=expert_up, expert_down=expert_down)


EPSILON = 1e-06
HIGHEST = lax.Precision.HIGHEST
MASKED = -1e+30

@jax.custom_vjp
def low(v):
    return lax.optimization_barrier(v.astype(jnp.bfloat16)).astype(jnp.float32)

@jax.custom_vjp
def low_back(v):
    return v

def low_keep(v):
    return (low(v), None)

def low_pass(kept, grad):
    return (grad,)

def back_keep(v):
    return (v, None)

def back_low(kept, grad):
    return (low(grad),)
low.defvjp(low_keep, low_pass)
low_back.defvjp(back_keep, back_low)

def matmul(left, right):
    return jnp.dot(left, right, precision=HIGHEST, preferred_element_type=jnp.float32)

def rms_scale(values):
    return values * lax.rsqrt(lax.optimization_barrier(jnp.mean(values * values, axis=-1, keepdims=True)) + EPSILON)

def softmax_rows(scores):
    row_max = lax.optimization_barrier(jnp.max(scores, axis=-1, keepdims=True))
    shifted = jnp.exp(scores - row_max)
    return shifted / lax.optimization_barrier(jnp.sum(shifted, axis=-1, keepdims=True))

def silu(values):
    return values * jax.nn.sigmoid(values)

def rope_tables(length, dim_size):
    places = jnp.arange(length).astype(jnp.float32)
    exponent = jnp.arange(dim_size // 2).astype(jnp.float32) * (2.0 / dim_size)
    angles = places[:, None] * jnp.exp(exponent * -math.log(10000.0))[None, :]
    return (jnp.cos(angles), jnp.sin(angles))

def rotate(values, cosine, sine_part):
    half_width = values.shape[-1] // 2
    lower_half = values[..., :half_width]
    upper_half = values[..., half_width:]
    return jnp.concatenate([lower_half * cosine - upper_half * sine_part, upper_half * cosine + lower_half * sine_part], axis=-1)

def expert_ffn(expert_rows, gate_matrix, up_matrix, down_matrix):
    gate_act = low_back(matmul(expert_rows, gate_matrix))
    up_act = low_back(matmul(expert_rows, up_matrix))
    expert_hidden = low(silu(gate_act) * up_act)
    return matmul(expert_hidden, down_matrix)

def take_rows(table, index):
    return jnp.take(table, index, axis=0)

def reference(inputs, teacher, valid_mask, prefix, routes, norm_gain, query_weight, latent_weight, latent_gain, expand_weight, output_weight, moe_gain, router_weight, shared_gate, shared_up, shared_down, expert_gate, expert_up, expert_down):
    flat_routes = routes.reshape(SEQS, GROUP * TOPK)
    onehot = (flat_routes[:, :, None] == jnp.arange(EXPERTS, dtype=jnp.int32)[None, None, :]).astype(jnp.int32)
    earlier = jnp.cumsum(onehot, axis=1) - onehot
    slot_index = (flat_routes * CAP + lax.optimization_barrier(jnp.sum(earlier * onehot, axis=2))).astype(jnp.int32)
    token_of = (jnp.arange(GROUP * TOPK, dtype=jnp.int32) // TOPK).astype(jnp.int32)

    def owners_of(slots_one):
        return jnp.zeros((EXPERTS * CAP,), jnp.int32).at[slots_one].set(token_of)

    def live_of(slots_one):
        return jnp.zeros((EXPERTS * CAP,), jnp.float32).at[slots_one].set(1.0)
    slot_owner = jax.vmap(owners_of)(slot_index)
    slot_live = jax.vmap(live_of)(slot_index)
    cosine, sine_part = rope_tables(GROUP, ROPE)
    position = jnp.arange(GROUP, dtype=jnp.int32)
    visible = (position[None, None, :] <= position[None, :, None]) | (position[None, None, :] < prefix[:, None, None])
    score_scale = 1.0 / math.sqrt(NOPE + ROPE)
    expert_step = jax.checkpoint(expert_ffn)

    def model(hidden, gain_in, query_mat, latent_mat, gain_latent, expand_mat, output_mat, gain_moe, router_mat, gate_shared, up_shared, down_shared, gate_expert, up_expert, down_expert):
        normed = low(rms_scale(hidden) * gain_in)
        query_lin = low_back(matmul(normed, query_mat)).reshape(SEQS, GROUP, HEADS, NOPE + ROPE)
        queries = low(jnp.concatenate([query_lin[..., :NOPE], rotate(query_lin[..., NOPE:], cosine[None, :, None, :], sine_part[None, :, None, :])], axis=-1))
        latent_lin = low_back(matmul(normed, latent_mat))
        latent = low(rms_scale(latent_lin[:, :RANK]) * gain_latent)
        key_rope = low(rotate(latent_lin[:, RANK:].reshape(SEQS, GROUP, ROPE), cosine[None], sine_part[None]))
        keys_values = low_back(low(matmul(latent, expand_mat))).reshape(SEQS, GROUP, HEADS, NOPE + VDIM)
        raw_scores = jnp.einsum('sihd,sjhd->shij', queries[..., :NOPE], keys_values[..., :NOPE], precision=HIGHEST, preferred_element_type=jnp.float32)
        raw_scores = raw_scores + jnp.einsum('sihd,sjd->shij', queries[..., NOPE:], key_rope, precision=HIGHEST, preferred_element_type=jnp.float32)
        scores = low_back(raw_scores * score_scale)
        scores = jnp.where(visible[:, None, :, :], scores, MASKED)
        attn_probs = softmax_rows(scores)
        heads_out = jnp.einsum('shij,sjhd->sihd', low(attn_probs), keys_values[..., NOPE:], precision=HIGHEST, preferred_element_type=jnp.float32)
        heads_out = low_back(low(heads_out)).reshape(TOKENS, HEADS * VDIM)
        attended = low_back(matmul(heads_out, output_mat))
        middle = hidden + attended
        moe_in = low(rms_scale(middle) * gain_moe)
        router_probs = softmax_rows(matmul(moe_in, router_mat))
        gate_values = jnp.take_along_axis(router_probs, routes, axis=1)
        gate_sh = low_back(matmul(moe_in, gate_shared))
        up_sh = low_back(matmul(moe_in, up_shared))
        shared_hidden = low(silu(gate_sh) * up_sh)
        shared_out = matmul(shared_hidden, down_shared)
        moe_seq = moe_in.reshape(SEQS, GROUP, D)
        expert_rows = jax.vmap(take_rows)(moe_seq, slot_owner) * slot_live[:, :, None]
        by_expert = expert_rows.reshape(SEQS, EXPERTS, CAP, D).transpose(1, 0, 2, 3).reshape(EXPERTS, SEQS * CAP, D)

        def one_expert(packed):
            return expert_step(packed[0], packed[1], packed[2], packed[3])
        expert_out = lax.map(one_expert, (by_expert, gate_expert, up_expert, down_expert))
        back_rows = expert_out.reshape(EXPERTS, SEQS, CAP, D).transpose(1, 0, 2, 3).reshape(SEQS, EXPERTS * CAP, D)
        picked = jax.vmap(take_rows)(back_rows, slot_index).reshape(TOKENS, TOPK, D)
        picked = low_back(picked)
        routed = lax.optimization_barrier(jnp.sum(gate_values[:, :, None] * picked, axis=1))
        moe_out = low_back(shared_out + routed)
        return middle + moe_out
    activations, pullback = jax.vjp(model, inputs.astype(jnp.float32), norm_gain.astype(jnp.float32), query_weight.astype(jnp.float32), latent_weight.astype(jnp.float32), latent_gain.astype(jnp.float32), expand_weight.astype(jnp.float32), output_weight.astype(jnp.float32), moe_gain.astype(jnp.float32), router_weight.astype(jnp.float32), shared_gate.astype(jnp.float32), shared_up.astype(jnp.float32), shared_down.astype(jnp.float32), expert_gate.astype(jnp.float32), expert_up.astype(jnp.float32), expert_down.astype(jnp.float32))
    mask_float = valid_mask.astype(jnp.float32)
    valid_total = jnp.maximum(jnp.sum(mask_float), 1.0)
    offset = activations - teacher.astype(jnp.float32)
    loss_value = jnp.sum(mask_float[:, None] * offset * offset) / (D * valid_total)
    grad_out = TOKENS / valid_total * mask_float[:, None] * offset
    gradients = pullback(grad_out)
    return (loss_value, activations, gradients[0], gradients[1], gradients[2], gradients[3], gradients[4], gradients[5], gradients[6], gradients[7], gradients[8], gradients[9], gradients[10], gradients[11], gradients[12], gradients[13], gradients[14])
```

```python
import math

import jax
import jax.numpy as jnp
from jax import lax
from jax.sharding import PartitionSpec as P

HEADS = 16
NOPE = 128
ROPE = 64
RANK = 512
VDIM = 128


EPSILON = 1e-06
HIGHEST = lax.Precision.HIGHEST
MASKED = -1e30


def rope_tables(length, dim_size):
    places = jnp.arange(length).astype(jnp.float32)
    exponent = jnp.arange(dim_size // 2).astype(jnp.float32) * (2.0 / dim_size)
    angles = places[:, None] * jnp.exp(exponent * -math.log(10000.0))[None, :]
    return (jnp.cos(angles), jnp.sin(angles))


def rotate(values, cosine, sine_part):
    half_width = values.shape[-1] // 2
    lower_half = values[..., :half_width]
    upper_half = values[..., half_width:]
    return jnp.concatenate(
        [
            lower_half * cosine - upper_half * sine_part,
            upper_half * cosine + lower_half * sine_part,
        ],
        axis=-1,
    )


def unrotate(gradient, cosine, sine_part):
    half_width = gradient.shape[-1] // 2
    lower_half = gradient[..., :half_width]
    upper_half = gradient[..., half_width:]
    return jnp.concatenate(
        [
            lower_half * cosine + upper_half * sine_part,
            upper_half * cosine - lower_half * sine_part,
        ],
        axis=-1,
    )


def silu_parts(gate_act):
    sigmoid_val = jax.nn.sigmoid(gate_act)
    return (gate_act * sigmoid_val, sigmoid_val * (1.0 + gate_act * (1.0 - sigmoid_val)))


def norm_back(grad_scaled, unit_rows, inverse):
    return inverse * (
        grad_scaled - unit_rows * jnp.mean(grad_scaled * unit_rows, axis=-1, keepdims=True)
    )


def swap_tp(value):
    return lax.ppermute(value, "tp", [(0, 1), (1, 0)])


def half_rows(value, which, rows):
    return lax.dynamic_slice_in_dim(value, which * rows, rows, 0)


def tp_scatter(partial, which, rows):
    other = half_rows(partial, 1 - which, rows).astype(jnp.bfloat16)
    return half_rows(partial, which, rows) + swap_tp(other).astype(jnp.float32)


def tp_sum(partial):
    low_partial = partial.astype(jnp.bfloat16)
    return low_partial.astype(jnp.float32) + swap_tp(low_partial).astype(jnp.float32)


def tp_gather(own, which):
    other = swap_tp(own)
    first = jnp.where(which == 0, own, other)
    second = jnp.where(which == 0, other, own)
    return jnp.concatenate([first, second], axis=0)


def gather_tokens(own):
    return lax.all_gather(own, ("fsdp", "tp"), axis=0, tiled=True)


def reduce_tokens(partial):
    return lax.psum_scatter(partial, ("fsdp", "tp"), scatter_dimension=0, tiled=True).astype(
        jnp.float32
    )


def scatter_grad(partial, dim):
    return lax.psum_scatter(
        partial.astype(jnp.bfloat16), "fsdp", scatter_dimension=dim, tiled=True
    ).astype(jnp.float32)


def to_blocks(weight, dim, parts):
    width = -(-(weight.shape[dim] // 128) // parts) * 128
    pads = [(0, 0), (0, 0)]
    pads[dim] = (0, parts * width - weight.shape[dim])
    return lax.all_to_all(jnp.pad(weight, pads), "fsdp", split_axis=dim, concat_axis=1 - dim, tiled=True)


def from_blocks(grad, dim, size):
    moved = lax.all_to_all(
        grad.astype(jnp.bfloat16), "fsdp", split_axis=1 - dim, concat_axis=dim, tiled=True
    )
    return lax.slice_in_dim(moved, 0, size, axis=dim).astype(jnp.float32)


def token_shards(
    inputs,
    teacher,
    valid_mask,
    prefix,
    routes,
    norm_gain,
    query_weight,
    latent_weight,
    latent_gain,
    expand_weight,
    output_weight,
    moe_gain,
    router_weight,
    shared_gate,
    shared_up,
    shared_down,
    expert_gate,
    expert_up,
    expert_down,
):
    f32 = jnp.float32
    bf16 = jnp.bfloat16
    tp_size = lax.axis_size("tp")
    fsdp_size = lax.axis_size("fsdp")
    own_tp = lax.axis_index("tp")
    own_expert = lax.axis_index("fsdp")
    local_heads = HEADS // tp_size
    own_rows = inputs.shape[0]
    width = inputs.shape[1]
    seq_len = own_rows * tp_size

    def gather(weight, dim):
        return lax.all_gather(weight, "fsdp", axis=dim, tiled=True)

    norm_gains = gather(norm_gain, 0)
    query_full = gather(query_weight, 0)
    latent_full = gather(latent_weight, 0)
    latent_gains = gather(latent_gain, 0)
    expand_full = gather(expand_weight, 0)
    output_full = gather(output_weight, 1)
    moe_gains = gather(moe_gain, 0)
    router_full = gather(router_weight, 0)
    routes_all = gather(routes, 0)
    valid_all = gather(valid_mask, 0)
    gate_block = to_blocks(shared_gate, 1, fsdp_size)
    up_block = to_blocks(shared_up, 1, fsdp_size)
    down_block = to_blocks(shared_down, 0, fsdp_size)

    hidden = tp_gather(inputs, own_tp).astype(f32)
    cosine, sine_part = rope_tables(seq_len, ROPE)
    inverse_in = lax.rsqrt(jnp.mean(hidden * hidden, axis=-1, keepdims=True) + EPSILON)
    normal_in = hidden * inverse_in
    norm_scale = norm_gains.astype(f32)
    normed = (normal_in * norm_scale).astype(bf16)
    query_lin = jnp.dot(normed, query_full, preferred_element_type=f32).reshape(
        seq_len, local_heads, NOPE + ROPE
    )
    queries = jnp.concatenate(
        [
            query_lin[..., :NOPE],
            rotate(query_lin[..., NOPE:], cosine[:, None, :], sine_part[:, None, :]),
        ],
        axis=-1,
    ).astype(bf16)
    latent_lin = jnp.dot(normed, latent_full, preferred_element_type=f32)
    latent_raw = latent_lin[:, :RANK]
    inverse_lat = lax.rsqrt(jnp.mean(latent_raw * latent_raw, axis=-1, keepdims=True) + EPSILON)
    latent_unit = latent_raw * inverse_lat
    latent_scale = latent_gains.astype(f32)
    latent = (latent_unit * latent_scale).astype(bf16)
    key_rope = rotate(latent_lin[:, RANK:], cosine, sine_part).astype(bf16)
    keys_values = (
        jnp.dot(latent, expand_full, preferred_element_type=f32)
        .astype(bf16)
        .reshape(seq_len, local_heads, NOPE + VDIM)
    )
    key_nope = keys_values[..., :NOPE]
    values = keys_values[..., NOPE:]
    query_nope = queries[..., :NOPE]
    query_rope = queries[..., NOPE:]
    score_scale = 1.0 / math.sqrt(NOPE + ROPE)
    position = jnp.arange(seq_len, dtype=jnp.int32)
    visible = (position[None, :] <= position[:, None]) | (position[None, :] < prefix[0])
    raw_scores = jnp.einsum("ihd,jhd->hij", query_nope, key_nope, preferred_element_type=f32)
    raw_scores = raw_scores + jnp.einsum(
        "ihd,jd->hij", query_rope, key_rope, preferred_element_type=f32
    )
    scores = jnp.where(visible[None], raw_scores * score_scale, MASKED)
    row_max = jnp.max(scores, axis=-1, keepdims=True)
    shifted = jnp.exp(scores - row_max)
    attn_probs = shifted / jnp.sum(shifted, axis=-1, keepdims=True)
    probs_low = attn_probs.astype(bf16)
    heads_out = (
        jnp.einsum("hij,jhd->ihd", probs_low, values, preferred_element_type=f32)
        .astype(bf16)
        .reshape(seq_len, local_heads * VDIM)
    )
    attended = tp_scatter(
        jnp.dot(heads_out, output_full, preferred_element_type=f32), own_tp, own_rows
    )

    middle = inputs.astype(f32) + attended
    inverse_mid = lax.rsqrt(jnp.mean(middle * middle, axis=-1, keepdims=True) + EPSILON)
    normal_mid = middle * inverse_mid
    moe_scale = moe_gains.astype(f32)
    moe_in = (normal_mid * moe_scale).astype(bf16)

    def route(rows):
        logits = jnp.dot(rows, router_full, preferred_element_type=f32)
        logit_exp = jnp.exp(logits - jnp.max(logits, axis=-1, keepdims=True))
        return logit_exp / jnp.sum(logit_exp, axis=-1, keepdims=True)

    router_probs = route(moe_in)
    experts = router_full.shape[1]
    top_count = routes.shape[1]
    capacity = top_count * seq_len * 4 // (3 * experts)
    slots = fsdp_size * capacity

    tokens = gather_tokens(moe_in)
    tokens_seq = tokens.reshape(fsdp_size, seq_len, width)
    named = jnp.any(routes_all == own_expert, axis=1).reshape(fsdp_size, seq_len)
    ahead = jnp.dot(
        named.astype(bf16),
        (position[:, None] < position[None, :]).astype(bf16),
        preferred_element_type=f32,
    ).astype(jnp.int32)
    place = jnp.where(named, ahead, -1)
    dispatch = (
        place[:, None, :] == jnp.arange(capacity, dtype=jnp.int32)[None, :, None]
    ).astype(bf16)
    own_probs = jnp.sum(
        jnp.where(jnp.arange(experts, dtype=jnp.int32) == own_expert, route(tokens), 0.0), axis=1
    ).reshape(fsdp_size, 1, seq_len)
    gate_slot = jnp.sum(dispatch.astype(f32) * own_probs, axis=2).reshape(slots, 1)
    gate_matrix, up_matrix, down_matrix = expert_gate[0], expert_up[0], expert_down[0]

    def pick(rows_seq):
        return (
            jnp.einsum("sct,std->scd", dispatch, rows_seq, preferred_element_type=f32)
            .astype(bf16)
            .reshape(slots, width)
        )

    def put_back(slot_rows):
        return jnp.einsum(
            "sct,scd->std",
            dispatch,
            slot_rows.astype(bf16).reshape(fsdp_size, capacity, width),
            preferred_element_type=f32,
        ).reshape(fsdp_size * seq_len, width)

    received = pick(tokens_seq)
    gate_act = jnp.dot(received, gate_matrix, preferred_element_type=f32)
    up_act = jnp.dot(received, up_matrix, preferred_element_type=f32)
    silu_gate, silu_slope = silu_parts(gate_act)
    expert_hidden = silu_gate * up_act
    gated_hidden = (gate_slot * expert_hidden).astype(bf16)
    expert_out = jnp.dot(gated_hidden, down_matrix, preferred_element_type=f32)
    gate_sh = jnp.dot(tokens, gate_block, preferred_element_type=f32)
    up_sh = jnp.dot(tokens, up_block, preferred_element_type=f32)
    silu_sh, slope_sh = silu_parts(gate_sh)
    shared_hidden = (silu_sh * up_sh).astype(bf16)
    moe_part = put_back(expert_out) + jnp.dot(
        shared_hidden, down_block, preferred_element_type=f32
    )
    activations = middle + reduce_tokens(moe_part.astype(bf16))

    own_mask = half_rows(valid_mask, own_tp, own_rows).astype(f32)
    offset = activations - half_rows(teacher, own_tp, own_rows).astype(f32)
    valid_total = jnp.maximum(jnp.sum(valid_all.astype(f32)), 1.0)
    square_sum = lax.psum(jnp.sum(own_mask[:, None] * offset * offset), ("fsdp", "tp"))
    loss_value = square_sum / (width * valid_total)
    grad_out = seq_len * fsdp_size / valid_total * own_mask[:, None] * offset
    grad_moe = grad_out.astype(bf16)

    grads = gather_tokens(grad_moe)
    grad_slots = pick(grads.reshape(fsdp_size, seq_len, width))
    grad_raw = jnp.einsum("cd,fd->cf", grad_slots, down_matrix, preferred_element_type=f32)
    grad_gate_slot = jnp.sum(grad_raw * expert_hidden, axis=1)
    grad_hidden = gate_slot * grad_raw
    grad_gate_act = (grad_hidden * up_act * silu_slope).astype(bf16)
    grad_up_act = (grad_hidden * silu_gate).astype(bf16)
    expert_down_grad = jnp.einsum(
        "cf,cd->fd", gated_hidden, grad_slots, preferred_element_type=f32
    )
    expert_gate_grad = jnp.einsum(
        "cd,cf->df", received, grad_gate_act, preferred_element_type=f32
    )
    expert_up_grad = jnp.einsum("cd,cf->df", received, grad_up_act, preferred_element_type=f32)
    grad_expert_in = jnp.einsum(
        "cf,df->cd", grad_gate_act, gate_matrix, preferred_element_type=f32
    ) + jnp.einsum("cf,df->cd", grad_up_act, up_matrix, preferred_element_type=f32)
    grad_sh_hidden = jnp.einsum("td,fd->tf", grads, down_block, preferred_element_type=f32)
    grad_gate_sh = (grad_sh_hidden * up_sh * slope_sh).astype(bf16)
    grad_up_sh = (grad_sh_hidden * silu_sh).astype(bf16)
    down_shared_grad = jnp.einsum("tf,td->fd", shared_hidden, grads, preferred_element_type=f32)
    gate_shared_grad = jnp.einsum("td,tf->df", tokens, grad_gate_sh, preferred_element_type=f32)
    up_shared_grad = jnp.einsum("td,tf->df", tokens, grad_up_sh, preferred_element_type=f32)
    grad_part = (
        put_back(grad_expert_in)
        + jnp.einsum("tf,df->td", grad_gate_sh, gate_block, preferred_element_type=f32)
        + jnp.einsum("tf,df->td", grad_up_sh, up_block, preferred_element_type=f32)
    )
    grad_probs_col = jnp.sum(
        dispatch.astype(f32) * grad_gate_slot.reshape(fsdp_size, capacity, 1), axis=1
    ).reshape(fsdp_size * seq_len, 1)
    grad_probs_part = jnp.where(
        jnp.arange(128, dtype=jnp.int32)[None, :] == own_expert, grad_probs_col, 0.0
    )
    grad_moe_in = reduce_tokens(grad_part.astype(bf16))
    grad_router_probs = reduce_tokens(grad_probs_part.astype(bf16))[:, :experts]

    grad_logits = router_probs * (
        grad_router_probs - jnp.sum(router_probs * grad_router_probs, axis=-1, keepdims=True)
    )
    router_grad = jnp.einsum(
        "td,te->de", moe_in.astype(f32), grad_logits, precision=HIGHEST, preferred_element_type=f32
    )
    grad_moe_in = grad_moe_in + jnp.einsum(
        "te,de->td",
        grad_logits,
        router_full.astype(f32),
        precision=HIGHEST,
        preferred_element_type=f32,
    )
    moe_gain_grad = jnp.sum(grad_moe_in * normal_mid, axis=0)
    grad_middle = grad_out + norm_back(grad_moe_in * moe_scale, normal_mid, inverse_mid)
    grad_attended = tp_gather(grad_middle.astype(bf16), own_tp)

    output_grad = jnp.einsum("tf,td->fd", heads_out, grad_attended, preferred_element_type=f32)
    grad_heads = (
        jnp.einsum("td,fd->tf", grad_attended, output_full, preferred_element_type=f32)
        .astype(bf16)
        .reshape(seq_len, local_heads, VDIM)
    )
    grad_probs = jnp.einsum("ihd,jhd->hij", grad_heads, values, preferred_element_type=f32)
    grad_values = jnp.einsum("hij,ihd->jhd", probs_low, grad_heads, preferred_element_type=f32)
    grad_scores = (
        attn_probs * (grad_probs - jnp.sum(attn_probs * grad_probs, axis=-1, keepdims=True))
    ).astype(bf16)
    grad_q_nope = (
        jnp.einsum("hij,jhd->ihd", grad_scores, key_nope, preferred_element_type=f32) * score_scale
    )
    grad_q_rope = (
        jnp.einsum("hij,jd->ihd", grad_scores, key_rope, preferred_element_type=f32) * score_scale
    )
    grad_keys = (
        jnp.einsum("hij,ihd->jhd", grad_scores, query_nope, preferred_element_type=f32)
        * score_scale
    )
    grad_key_rope = (
        jnp.einsum("hij,ihd->jd", grad_scores, query_rope, preferred_element_type=f32) * score_scale
    )
    grad_query = (
        jnp.concatenate(
            [grad_q_nope, unrotate(grad_q_rope, cosine[:, None, :], sine_part[:, None, :])], axis=-1
        )
        .astype(bf16)
        .reshape(seq_len, local_heads * (NOPE + ROPE))
    )
    query_grad = jnp.einsum("td,tq->dq", normed, grad_query, preferred_element_type=f32)
    grad_normed = jnp.einsum("tq,dq->td", grad_query, query_full, preferred_element_type=f32)
    grad_kv = (
        jnp.concatenate([grad_keys, grad_values], axis=-1)
        .astype(bf16)
        .reshape(seq_len, local_heads * (NOPE + VDIM))
    )
    expand_grad = jnp.einsum("tr,tq->rq", latent, grad_kv, preferred_element_type=f32)
    grad_latent = jnp.einsum("tq,rq->tr", grad_kv, expand_full, preferred_element_type=f32)
    grad_both = tp_sum(jnp.concatenate([grad_latent, grad_key_rope], axis=1))
    grad_latent, grad_key_rope = grad_both[:, :RANK], grad_both[:, RANK:]
    latent_gain_grad = jnp.sum(grad_latent * latent_unit, axis=0)
    grad_latent_raw = norm_back(grad_latent * latent_scale, latent_unit, inverse_lat)
    grad_latent_lin = jnp.concatenate(
        [grad_latent_raw, unrotate(grad_key_rope, cosine, sine_part)], axis=-1
    ).astype(bf16)
    latent_grad = jnp.einsum("td,tr->dr", normed, grad_latent_lin, preferred_element_type=f32)
    grad_normed = tp_scatter(grad_normed, own_tp, own_rows) + jnp.einsum(
        "tr,dr->td",
        half_rows(grad_latent_lin, own_tp, own_rows),
        latent_full,
        preferred_element_type=f32,
    )
    own_normal = half_rows(normal_in, own_tp, own_rows)
    own_inverse = half_rows(inverse_in, own_tp, own_rows)
    norm_gain_grad = jnp.sum(grad_normed * own_normal, axis=0)
    input_grad = grad_middle + norm_back(grad_normed * norm_scale, own_normal, own_inverse)

    small = jnp.concatenate([router_grad, norm_gain_grad[:, None], moe_gain_grad[:, None]], axis=1)
    small = small + swap_tp(small)
    small_out = lax.psum_scatter(small, "fsdp", scatter_dimension=0, tiled=True)
    lgain_out = lax.psum_scatter(latent_gain_grad, "fsdp", scatter_dimension=0, tiled=True)
    return (
        loss_value,
        activations,
        input_grad,
        small_out[:, experts],
        scatter_grad(query_grad, 0),
        scatter_grad(latent_grad, 0),
        lgain_out,
        scatter_grad(expand_grad, 0),
        scatter_grad(output_grad, 1),
        small_out[:, experts + 1],
        small_out[:, :experts],
        from_blocks(gate_shared_grad, 1, shared_gate.shape[1]),
        from_blocks(up_shared_grad, 1, shared_up.shape[1]),
        from_blocks(down_shared_grad, 0, shared_down.shape[0]),
        expert_gate_grad[None],
        expert_up_grad[None],
        expert_down_grad[None],
    )


def slot_shards(
    inputs,
    teacher,
    valid_mask,
    prefix,
    routes,
    norm_gain,
    query_weight,
    latent_weight,
    latent_gain,
    expand_weight,
    output_weight,
    moe_gain,
    router_weight,
    shared_gate,
    shared_up,
    shared_down,
    expert_gate,
    expert_up,
    expert_down,
):
    f32 = jnp.float32
    bf16 = jnp.bfloat16
    tp_size = lax.axis_size("tp")
    fsdp_size = lax.axis_size("fsdp")
    local_heads = HEADS // tp_size
    (
        norm_gains,
        query_full,
        latent_full,
        latent_gains,
        expand_full,
        output_full,
        moe_gains,
        router_full,
        gate_full,
        up_full,
        down_full,
    ) = (
        lax.all_gather(norm_gain, "fsdp", axis=0, tiled=True),
        lax.all_gather(query_weight, "fsdp", axis=0, tiled=True),
        lax.all_gather(latent_weight, "fsdp", axis=0, tiled=True),
        lax.all_gather(latent_gain, "fsdp", axis=0, tiled=True),
        lax.all_gather(expand_weight, "fsdp", axis=0, tiled=True),
        lax.all_gather(output_weight, "fsdp", axis=1, tiled=True),
        lax.all_gather(moe_gain, "fsdp", axis=0, tiled=True),
        lax.all_gather(router_weight, "fsdp", axis=0, tiled=True),
        lax.all_gather(shared_gate, "fsdp", axis=0, tiled=True),
        lax.all_gather(shared_up, "fsdp", axis=0, tiled=True),
        lax.all_gather(shared_down, "fsdp", axis=1, tiled=True),
    )
    gathered = lax.all_gather(inputs, "tp", axis=0, tiled=True)
    seq_len = gathered.shape[0]
    width = gathered.shape[1]
    hidden = gathered.astype(f32)
    cosine, sine_part = rope_tables(seq_len, ROPE)
    inverse_in = lax.rsqrt(jnp.mean(hidden * hidden, axis=-1, keepdims=True) + EPSILON)
    normal_in = hidden * inverse_in
    norm_scale = norm_gains.astype(f32)
    normed = (normal_in * norm_scale).astype(bf16)
    query_lin = jnp.dot(normed, query_full, preferred_element_type=f32).reshape(
        seq_len, local_heads, NOPE + ROPE
    )
    queries = jnp.concatenate(
        [
            query_lin[..., :NOPE],
            rotate(query_lin[..., NOPE:], cosine[:, None, :], sine_part[:, None, :]),
        ],
        axis=-1,
    ).astype(bf16)
    latent_lin = jnp.dot(normed, latent_full, preferred_element_type=f32)
    latent_raw = latent_lin[:, :RANK]
    inverse_lat = lax.rsqrt(jnp.mean(latent_raw * latent_raw, axis=-1, keepdims=True) + EPSILON)
    latent_unit = latent_raw * inverse_lat
    latent_scale = latent_gains.astype(f32)
    latent = (latent_unit * latent_scale).astype(bf16)
    key_rope = rotate(latent_lin[:, RANK:], cosine, sine_part).astype(bf16)
    keys_values = (
        jnp.dot(latent, expand_full, preferred_element_type=f32)
        .astype(bf16)
        .reshape(seq_len, local_heads, NOPE + VDIM)
    )
    key_nope = keys_values[..., :NOPE]
    values = keys_values[..., NOPE:]
    query_nope = queries[..., :NOPE]
    query_rope = queries[..., NOPE:]
    score_scale = 1.0 / math.sqrt(NOPE + ROPE)
    position = jnp.arange(seq_len, dtype=jnp.int32)
    visible = (position[None, :] <= position[:, None]) | (position[None, :] < prefix[0])

    def scores_of():
        raw_scores = jnp.einsum("ihd,jhd->hij", query_nope, key_nope, preferred_element_type=f32)
        raw_scores = raw_scores + jnp.einsum(
            "ihd,jd->hij", query_rope, key_rope, preferred_element_type=f32
        )
        return jnp.where(visible[None], raw_scores * score_scale, MASKED)

    scores = scores_of()
    row_max = jnp.max(scores, axis=-1, keepdims=True)
    shifted = jnp.exp(scores - row_max)
    row_total = jnp.sum(shifted, axis=-1, keepdims=True)
    log_total = row_max + jnp.log(row_total)
    probs_low = (shifted / row_total).astype(bf16)
    heads_out = (
        jnp.einsum("hij,jhd->ihd", probs_low, values, preferred_element_type=f32)
        .astype(bf16)
        .reshape(seq_len, local_heads * VDIM)
    )
    attended = lax.psum(jnp.dot(heads_out, output_full, preferred_element_type=f32), "tp")
    middle = hidden + attended
    inverse_mid = lax.rsqrt(jnp.mean(middle * middle, axis=-1, keepdims=True) + EPSILON)
    normal_mid = middle * inverse_mid
    moe_scale = moe_gains.astype(f32)
    moe_in = (normal_mid * moe_scale).astype(bf16)
    logits = jnp.dot(moe_in, router_full, preferred_element_type=f32)
    logit_max = jnp.max(logits, axis=-1, keepdims=True)
    logit_exp = jnp.exp(logits - logit_max)
    router_probs = logit_exp / jnp.sum(logit_exp, axis=-1, keepdims=True)
    experts = router_full.shape[1]
    top_count = routes.shape[1]
    choose = routes[:, :, None] == jnp.arange(experts, dtype=jnp.int32)[None, None, :]
    gate_values = jnp.sum(jnp.where(choose, router_probs[:, None, :], 0.0), axis=-1)
    capacity = top_count * seq_len * 4 // (3 * experts)
    flat_routes = routes.reshape(seq_len * top_count)
    onehot = (flat_routes[:, None] == jnp.arange(experts, dtype=jnp.int32)[None, :]).astype(
        jnp.int32
    )
    earlier = jnp.cumsum(onehot, axis=0) - onehot
    slot_index = flat_routes * capacity + jnp.sum(earlier * onehot, axis=1)
    placed = jnp.arange(experts * capacity, dtype=jnp.int32)[:, None] == slot_index[None, :]
    dispatch = jnp.sum(
        placed.reshape(experts * capacity, seq_len, top_count).astype(f32), axis=2
    ).astype(bf16)
    gate_slot = jnp.sum(jnp.where(placed, gate_values.reshape(1, seq_len * top_count), 0.0), axis=1)

    def send_slots(slot_rows):
        return lax.all_to_all(slot_rows, "fsdp", split_axis=0, concat_axis=1, tiled=True)

    def return_slots(partials):
        return (
            lax.all_to_all(
                partials.astype(jnp.bfloat16), "fsdp", split_axis=1, concat_axis=0, tiled=True
            )
            .astype(partials.dtype)
            .reshape(experts * capacity, width)
        )

    expert_in = (
        jnp.dot(dispatch, moe_in, preferred_element_type=f32)
        .astype(bf16)
        .reshape(experts, capacity, width)
    )
    received = send_slots(expert_in)
    gate_act = jnp.einsum("ecd,edf->ecf", received, expert_gate, preferred_element_type=f32)
    up_act = jnp.einsum("ecd,edf->ecf", received, expert_up, preferred_element_type=f32)
    silu_gate, silu_slope = silu_parts(gate_act)
    expert_hidden = (silu_gate * up_act).astype(bf16)
    expert_out = jnp.einsum("ecf,efd->ecd", expert_hidden, expert_down, preferred_element_type=f32)
    returned = return_slots(expert_out)
    picked = jnp.take(returned, slot_index, axis=0).reshape(seq_len, top_count, width)
    routed = jnp.sum(gate_values[:, :, None] * picked, axis=1)
    gate_sh = jnp.dot(moe_in, gate_full, preferred_element_type=f32)
    up_sh = jnp.dot(moe_in, up_full, preferred_element_type=f32)
    silu_sh, slope_sh = silu_parts(gate_sh)
    shared_hidden = (silu_sh * up_sh).astype(bf16)
    moe_part = routed + jnp.dot(shared_hidden, down_full, preferred_element_type=f32)
    moe_out = lax.psum(moe_part.astype(jnp.bfloat16), "tp").astype(jnp.float32)
    activations = middle + moe_out
    mask_float = valid_mask.astype(f32)
    offset = activations - teacher.astype(f32)
    square_sum, valid_sum = lax.psum(
        (jnp.sum(mask_float[:, None] * offset * offset), jnp.sum(mask_float)), "fsdp"
    )
    valid_total = jnp.maximum(valid_sum, 1.0)
    loss_value = square_sum / (width * valid_total)
    grad_out = seq_len * fsdp_size / valid_total * mask_float[:, None] * offset
    grad_moe = grad_out.astype(bf16)
    down_shared_grad = jnp.einsum("tf,td->fd", shared_hidden, grad_moe, preferred_element_type=f32)
    grad_sh_hidden = jnp.einsum("td,fd->tf", grad_moe, down_full, preferred_element_type=f32)
    grad_gate_sh = (grad_sh_hidden * up_sh * slope_sh).astype(bf16)
    grad_up_sh = (grad_sh_hidden * silu_sh).astype(bf16)
    gate_shared_grad = jnp.einsum("td,tf->df", moe_in, grad_gate_sh, preferred_element_type=f32)
    up_shared_grad = jnp.einsum("td,tf->df", moe_in, grad_up_sh, preferred_element_type=f32)
    grad_moe_in = jnp.einsum("tf,df->td", grad_gate_sh, gate_full, preferred_element_type=f32)
    grad_moe_in = grad_moe_in + jnp.einsum(
        "tf,df->td", grad_up_sh, up_full, preferred_element_type=f32
    )
    grad_gates = jnp.sum(picked * grad_moe.astype(f32)[:, None, :], axis=-1)
    grad_slots = (
        (jnp.dot(dispatch, grad_moe, preferred_element_type=f32) * gate_slot[:, None])
        .astype(bf16)
        .reshape(experts, capacity, width)
    )
    grad_received = send_slots(grad_slots)
    expert_down_grad = jnp.einsum(
        "ecf,ecd->efd", expert_hidden, grad_received, preferred_element_type=f32
    )
    grad_expert_hidden = jnp.einsum(
        "ecd,efd->ecf", grad_received, expert_down, preferred_element_type=f32
    )
    grad_gate_act = (grad_expert_hidden * up_act * silu_slope).astype(bf16)
    grad_up_act = (grad_expert_hidden * silu_gate).astype(bf16)
    expert_gate_grad = jnp.einsum(
        "ecd,ecf->edf", received, grad_gate_act, preferred_element_type=f32
    )
    expert_up_grad = jnp.einsum("ecd,ecf->edf", received, grad_up_act, preferred_element_type=f32)
    grad_expert_in = jnp.einsum(
        "ecf,edf->ecd", grad_gate_act, expert_gate, preferred_element_type=f32
    )
    grad_expert_in = grad_expert_in + jnp.einsum(
        "ecf,edf->ecd", grad_up_act, expert_up, preferred_element_type=f32
    )
    grad_returned = return_slots(grad_expert_in)
    grad_moe_in = grad_moe_in + jnp.sum(
        jnp.take(grad_returned, slot_index, axis=0).reshape(seq_len, top_count, width), axis=1
    )
    grad_moe_in, grad_gates = (
        lax.psum(grad_moe_in.astype(jnp.bfloat16), "tp").astype(jnp.float32),
        lax.psum(grad_gates.astype(jnp.bfloat16), "tp").astype(jnp.float32),
    )
    grad_router_probs = jnp.sum(jnp.where(choose, grad_gates[:, :, None], 0.0), axis=1)
    grad_logits = router_probs * (
        grad_router_probs - jnp.sum(router_probs * grad_router_probs, axis=-1, keepdims=True)
    )
    router_grad = jnp.einsum(
        "td,te->de", moe_in.astype(f32), grad_logits, precision=HIGHEST, preferred_element_type=f32
    )
    grad_moe_in = grad_moe_in + jnp.einsum(
        "te,de->td",
        grad_logits,
        router_full.astype(f32),
        precision=HIGHEST,
        preferred_element_type=f32,
    )
    moe_gain_grad = jnp.sum(grad_moe_in * normal_mid, axis=0)
    grad_middle = grad_out + norm_back(grad_moe_in * moe_scale, normal_mid, inverse_mid)
    grad_attended = grad_middle.astype(bf16)
    output_grad = jnp.einsum("tf,td->fd", heads_out, grad_attended, preferred_element_type=f32)
    grad_heads = (
        jnp.einsum("td,fd->tf", grad_attended, output_full, preferred_element_type=f32)
        .astype(bf16)
        .reshape(seq_len, local_heads, VDIM)
    )
    attn_probs = jnp.exp(scores_of() - log_total)
    probs_again = attn_probs.astype(bf16)
    grad_probs = jnp.einsum("ihd,jhd->hij", grad_heads, values, preferred_element_type=f32)
    grad_values = jnp.einsum("hij,ihd->jhd", probs_again, grad_heads, preferred_element_type=f32)
    grad_scores = (
        attn_probs * (grad_probs - jnp.sum(attn_probs * grad_probs, axis=-1, keepdims=True))
    ).astype(bf16)
    grad_q_nope = (
        jnp.einsum("hij,jhd->ihd", grad_scores, key_nope, preferred_element_type=f32) * score_scale
    )
    grad_q_rope = (
        jnp.einsum("hij,jd->ihd", grad_scores, key_rope, preferred_element_type=f32) * score_scale
    )
    grad_keys = (
        jnp.einsum("hij,ihd->jhd", grad_scores, query_nope, preferred_element_type=f32)
        * score_scale
    )
    grad_key_rope = (
        jnp.einsum("hij,ihd->jd", grad_scores, query_rope, preferred_element_type=f32) * score_scale
    )
    grad_query = (
        jnp.concatenate(
            [grad_q_nope, unrotate(grad_q_rope, cosine[:, None, :], sine_part[:, None, :])], axis=-1
        )
        .astype(bf16)
        .reshape(seq_len, local_heads * (NOPE + ROPE))
    )
    query_grad = jnp.einsum("td,tq->dq", normed, grad_query, preferred_element_type=f32)
    grad_normed = jnp.einsum("tq,dq->td", grad_query, query_full, preferred_element_type=f32)
    grad_kv = (
        jnp.concatenate([grad_keys, grad_values], axis=-1)
        .astype(bf16)
        .reshape(seq_len, local_heads * (NOPE + VDIM))
    )
    expand_grad = jnp.einsum("tr,tq->rq", latent, grad_kv, preferred_element_type=f32)
    grad_latent = jnp.einsum("tq,rq->tr", grad_kv, expand_full, preferred_element_type=f32)
    grad_normed, grad_latent, grad_key_rope = (
        lax.psum(grad_normed.astype(jnp.bfloat16), "tp").astype(jnp.float32),
        lax.psum(grad_latent.astype(jnp.bfloat16), "tp").astype(jnp.float32),
        lax.psum(grad_key_rope.astype(jnp.bfloat16), "tp").astype(jnp.float32),
    )
    latent_gain_grad = jnp.sum(grad_latent * latent_unit, axis=0)
    grad_latent_raw = norm_back(grad_latent * latent_scale, latent_unit, inverse_lat)
    grad_latent_lin = jnp.concatenate(
        [grad_latent_raw, unrotate(grad_key_rope, cosine, sine_part)], axis=-1
    ).astype(bf16)
    latent_grad = jnp.einsum("td,tr->dr", normed, grad_latent_lin, preferred_element_type=f32)
    grad_normed = grad_normed + jnp.einsum(
        "tr,dr->td", grad_latent_lin, latent_full, preferred_element_type=f32
    )
    norm_gain_grad = jnp.sum(grad_normed * normal_in, axis=0)
    input_grad = grad_middle + norm_back(grad_normed * norm_scale, normal_in, inverse_in)
    (
        norm_out,
        query_out,
        latent_out,
        lgain_out,
        expand_out,
        output_out,
        mgain_out,
        router_out,
        gate_out,
        up_out,
        down_out,
    ) = (
        lax.psum_scatter(norm_gain_grad, "fsdp", scatter_dimension=0, tiled=True),
        lax.psum_scatter(query_grad, "fsdp", scatter_dimension=0, tiled=True),
        lax.psum_scatter(latent_grad, "fsdp", scatter_dimension=0, tiled=True),
        lax.psum_scatter(latent_gain_grad, "fsdp", scatter_dimension=0, tiled=True),
        lax.psum_scatter(expand_grad, "fsdp", scatter_dimension=0, tiled=True),
        lax.psum_scatter(output_grad, "fsdp", scatter_dimension=1, tiled=True),
        lax.psum_scatter(moe_gain_grad, "fsdp", scatter_dimension=0, tiled=True),
        lax.psum_scatter(router_grad, "fsdp", scatter_dimension=0, tiled=True),
        lax.psum_scatter(gate_shared_grad, "fsdp", scatter_dimension=0, tiled=True),
        lax.psum_scatter(up_shared_grad, "fsdp", scatter_dimension=0, tiled=True),
        lax.psum_scatter(down_shared_grad, "fsdp", scatter_dimension=1, tiled=True),
    )
    own_start = lax.axis_index("tp") * inputs.shape[0]
    own_activations = lax.dynamic_slice_in_dim(activations, own_start, inputs.shape[0], 0)
    own_input_grad = lax.dynamic_slice_in_dim(input_grad, own_start, inputs.shape[0], 0)
    return (
        loss_value,
        own_activations,
        own_input_grad,
        norm_out,
        query_out,
        latent_out,
        lgain_out,
        expand_out,
        output_out,
        mgain_out,
        router_out,
        gate_out,
        up_out,
        down_out,
        expert_gate_grad,
        expert_up_grad,
        expert_down_grad,
    )


def shards(*arrays):
    fsdp_size = lax.axis_size("fsdp")
    seq_len = arrays[4].shape[0]
    experts = arrays[12].shape[1]
    capacity = arrays[4].shape[1] * seq_len * 4 // (3 * experts)
    if fsdp_size * seq_len <= 2 * experts * capacity and fsdp_size == experts:
        return token_shards(*arrays)
    return slot_shards(*arrays)


def solution(mesh):
    return jax.shard_map(
        shards,
        mesh=mesh,
        in_specs=(
            P(("fsdp", "tp"), None),
            P("fsdp", None),
            P("fsdp"),
            P("fsdp"),
            P("fsdp", None),
            P("fsdp"),
            P("fsdp", "tp"),
            P("fsdp", None),
            P("fsdp"),
            P("fsdp", "tp"),
            P("tp", "fsdp"),
            P("fsdp"),
            P("fsdp", None),
            P("fsdp", "tp"),
            P("fsdp", "tp"),
            P("tp", "fsdp"),
            P("fsdp", None, "tp"),
            P("fsdp", None, "tp"),
            P("fsdp", "tp", None),
        ),
        out_specs=(
            P(),
            P(("fsdp", "tp"), None),
            P(("fsdp", "tp"), None),
            P("fsdp"),
            P("fsdp", "tp"),
            P("fsdp", None),
            P("fsdp"),
            P("fsdp", "tp"),
            P("tp", "fsdp"),
            P("fsdp"),
            P("fsdp", None),
            P("fsdp", "tp"),
            P("fsdp", "tp"),
            P("tp", "fsdp"),
            P("fsdp", None, "tp"),
            P("fsdp", None, "tp"),
            P("fsdp", "tp", None),
        ),
        check_vma=False,
    )
```

```python
import functools
import math

import jax
import jax.numpy as jnp
from jax import lax
from jax.experimental import pallas as pl
from jax.experimental.pallas import tpu as pltpu
from jax.sharding import PartitionSpec as P

HEADS = 16
NOPE = 128
ROPE = 64
RANK = 512
VDIM = 128


EPSILON = 1e-06
HIGHEST = lax.Precision.HIGHEST
MASKED = -1e30


def rope_tables(length, dim_size):
    places = jnp.arange(length).astype(jnp.float32)
    exponent = jnp.arange(dim_size // 2).astype(jnp.float32) * (2.0 / dim_size)
    angles = places[:, None] * jnp.exp(exponent * -math.log(10000.0))[None, :]
    return (jnp.cos(angles), jnp.sin(angles))


def rotate(values, cosine, sine_part):
    half_width = values.shape[-1] // 2
    lower_half = values[..., :half_width]
    upper_half = values[..., half_width:]
    return jnp.concatenate(
        [
            lower_half * cosine - upper_half * sine_part,
            upper_half * cosine + lower_half * sine_part,
        ],
        axis=-1,
    )


def unrotate(gradient, cosine, sine_part):
    half_width = gradient.shape[-1] // 2
    lower_half = gradient[..., :half_width]
    upper_half = gradient[..., half_width:]
    return jnp.concatenate(
        [
            lower_half * cosine + upper_half * sine_part,
            upper_half * cosine - lower_half * sine_part,
        ],
        axis=-1,
    )


def silu_parts(gate_act):
    sigmoid_val = jax.nn.sigmoid(gate_act)
    return (gate_act * sigmoid_val, sigmoid_val * (1.0 + gate_act * (1.0 - sigmoid_val)))


def norm_back(grad_scaled, unit_rows, inverse):
    return inverse * (
        grad_scaled - unit_rows * jnp.mean(grad_scaled * unit_rows, axis=-1, keepdims=True)
    )


def swap_tp(value):
    return lax.ppermute(value, "tp", [(0, 1), (1, 0)])


def half_rows(value, which, rows):
    return lax.dynamic_slice_in_dim(value, which * rows, rows, 0)


def tp_scatter(partial, which, rows):
    other = half_rows(partial, 1 - which, rows).astype(jnp.bfloat16)
    return half_rows(partial, which, rows) + swap_tp(other).astype(jnp.float32)


def tp_sum(partial):
    low_partial = partial.astype(jnp.bfloat16)
    return low_partial.astype(jnp.float32) + swap_tp(low_partial).astype(jnp.float32)


def tp_gather(own, which):
    other = swap_tp(own)
    first = jnp.where(which == 0, own, other)
    second = jnp.where(which == 0, other, own)
    return jnp.concatenate([first, second], axis=0)


MESH = pl.DeviceIdType.MESH
CROSS = ("x", "y", "up", "down")


class Grid:
    def __init__(self, fsdp_size, dims):
        index = lax.axis_index("fsdp")
        self.core = lax.rem(index, 2)
        self.y = lax.rem(lax.div(index, 2), 2)
        self.z = lax.div(index, 4)
        self.x = lax.axis_index("tp")
        self.depth = fsdp_size // 4
        self.dims = dims
        self.chips = self.depth * 2 * (2 if "x" in dims else 1)

    def device(self, x, y, z, core):
        return {"fsdp": z * 4 + y * 2 + core, "tp": x}

    def chip(self, x, y, z):
        return (z * 2 + y) * 2 + x if "x" in self.dims else z * 2 + y

    def partner(self):
        return self.device(self.x, self.y, self.z, 1 - self.core)

    def neighbour(self, cross):
        if cross == "x":
            return (1 - self.x, self.y, self.z), None
        if cross == "y":
            return (self.x, 1 - self.y, self.z), None
        if cross == "up":
            return (self.x, self.y, self.z + 1), self.z + 1 < self.depth
        return (self.x, self.y, self.z - 1), self.z >= 1

    def at(self, offset):
        dx, dy, dz = offset
        x = 1 - self.x if dx else self.x
        y = 1 - self.y if dy else self.y
        z = self.z + dz
        if dz == 0:
            return (x, y, z), None
        return (x, y, z), (z < self.depth if dz > 0 else z >= 0)


def offsets_of(depth, dims):
    xs = (0, 1) if "x" in dims else (0,)
    found = [(dx, dy, dz) for dx in xs for dy in (0, 1) for dz in range(1 - depth, depth)]
    return sorted(found, key=lambda o: (abs(o[0]) + abs(o[1]) + abs(o[2]), abs(o[2])))


def arrival(order, offset):
    by_dim = dict(x=offset[0], y=offset[1], z=offset[2])
    last = None
    for dim in order:
        if by_dim[dim]:
            last = dim
    return last


def children(order, offset):
    last = arrival(order, offset)
    after = order if last is None else order[order.index(last) + 1 :]
    found = []
    if last == "z":
        found.append("down" if offset[2] > 0 else "up")
    for dim in after:
        found.extend(("up", "down") if dim == "z" else (dim,))
    return found


def parent(order, offset):
    last = arrival(order, offset)
    if last == "z":
        return ("up", "down") if offset[2] > 0 else ("down", "up")
    return last, last


def both(first, second):
    if first is None:
        return second
    if second is None:
        return first
    return jnp.logical_and(first, second)


def under(condition, body):
    if condition is None:
        body()
    else:
        pl.when(condition)(body)


def greet_plane(grid, fsdp_size):
    barrier = pltpu.get_barrier_semaphore()
    me = lax.axis_index("fsdp")

    def send(step, carry):
        there = lax.rem(me + step, fsdp_size)
        pl.semaphore_signal(barrier, inc=1, device_id={"fsdp": there, "tp": grid.x}, device_id_type=MESH)
        return carry

    lax.fori_loop(1, fsdp_size, send, 0)
    pl.semaphore_wait(barrier, fsdp_size - 1)


def greet(grid):
    barrier = pltpu.get_barrier_semaphore()
    pl.semaphore_signal(barrier, inc=1, device_id=grid.partner(), device_id_type=MESH)
    count = 1
    for cross in CROSS:
        if cross in ("x", "y") and cross not in grid.dims:
            continue
        chip, exists = grid.neighbour(cross)

        def send(chip=chip):
            pl.semaphore_signal(
                barrier, inc=1, device_id=grid.device(*chip, grid.core), device_id_type=MESH
            )

        under(exists, send)
        count = count + (1 if exists is None else jnp.where(exists, 1, 0))
    pl.semaphore_wait(barrier, count)


class Exchange:
    def __init__(self, fsdp_size, tp, blocks, sources, targets, cut, to_owner, send_sem, recv_sem, own_sem):
        self.size, self.tp, self.blocks = fsdp_size, tp, blocks
        self.sources, self.targets, self.cut, self.to_owner = sources, targets, cut, to_owner
        self.send_sem, self.recv_sem, self.own_sem = send_sem, recv_sem, own_sem
        self.me = lax.axis_index("fsdp")
        self.block = lax.div(self.me * blocks + fsdp_size - 1, fsdp_size)
        self.owns = jnp.logical_and(
            self.block < blocks, lax.div(self.block * fsdp_size, blocks) == self.me
        )

    def owner(self, block):
        return block * self.size // self.blocks

    def remote(self, array, block, other, there, send, recv):
        source, target = self.cut[array](self.sources[array], self.targets[array], block, other)
        return pltpu.make_async_remote_copy(
            src_ref=source,
            dst_ref=target,
            send_sem=self.send_sem.at[array, send],
            recv_sem=self.recv_sem.at[array, recv],
            device_id={"fsdp": there, "tp": self.tp},
            device_id_type=MESH,
        )

    def local(self, array, block):
        source, target = self.cut[array](self.sources[array], self.targets[array], block, self.me)
        return pltpu.make_async_copy(source, target, self.own_sem.at[array])

    def each(self, act_send, act_recv, act_local):
        arrays = range(len(self.sources))
        for block in range(self.blocks):
            owner = self.owner(block)
            for array in arrays:
                if self.to_owner:
                    if act_send:
                        copy = self.remote(array, block, self.me, owner, block, self.me)
                        pl.when(self.me != owner)(getattr(copy, act_send))
                    if act_local:
                        pl.when(self.me == owner)(getattr(self.local(array, block), act_local))
                elif act_recv:
                    copy = self.remote(array, block, self.me, owner, 0, block)
                    pl.when(self.me != owner)(getattr(copy, act_recv))

        def owning():
            for other in range(self.size):
                for array in arrays:
                    if self.to_owner:
                        if act_recv:
                            copy = self.remote(array, self.block, other, other, 0, other)
                            pl.when(self.me != other)(getattr(copy, act_recv))
                    elif act_send:
                        copy = self.remote(array, self.block, other, other, other, self.block)
                        pl.when(self.me != other)(getattr(copy, act_send))
            for array in arrays:
                if act_local and not self.to_owner:
                    getattr(self.local(array, self.block), act_local)()

        pl.when(self.owns)(owning)

    def start(self):
        self.each("start", None, "start")

    def finish(self):
        self.each(None, "wait_recv", None)
        self.each("wait_send", None, "wait")


def gather_kernel(fsdp_size, dims, pieces, places, count, blocks, cut, *refs):
    moved = len(cut)
    shards, sources = refs[:count], refs[count : count + moved]
    refs = refs[count + moved :]
    outs, targets = refs[:count], refs[count : count + moved]
    send_sem, recv_sem, pair_send, pair_recv, own_sem = refs[count + moved : count + moved + 5]
    grid = Grid(fsdp_size, dims)
    if moved:
        exchange = Exchange(
            fsdp_size, grid.x, blocks, sources, targets, cut, True, *refs[count + moved + 5 :]
        )
    me = (grid.x, grid.y, grid.z)
    offsets = offsets_of(grid.depth, dims)

    def target(piece, chip, core):
        array, first, rows, _ = pieces[piece]
        return places[array](outs[array], chip, core, first, rows)

    def source(piece, offset, chip):
        array, first, rows, _ = pieces[piece]
        if offset == (0, 0, 0):
            return shards[array].at[pl.ds(first, rows)]
        return target(piece, chip, grid.core)

    def hop(piece, offset, chip, cross):
        there, exists = grid.neighbour(cross)
        index = grid.chip(*chip)
        copy = pltpu.make_async_remote_copy(
            src_ref=source(piece, offset, chip),
            dst_ref=target(piece, chip, grid.core),
            send_sem=send_sem.at[piece, index, CROSS.index(cross)],
            recv_sem=recv_sem.at[piece, index],
            device_id=grid.device(*there, grid.core),
            device_id_type=MESH,
        )
        return copy, exists

    def pair(piece, offset, chip, core):
        index = grid.chip(*chip)
        return pltpu.make_async_remote_copy(
            src_ref=source(piece, offset, chip),
            dst_ref=target(piece, chip, core),
            send_sem=pair_send.at[piece, index],
            recv_sem=pair_recv.at[piece, index],
            device_id=grid.partner(),
            device_id_type=MESH,
        )

    own_copies = [
        pltpu.make_async_copy(
            source(piece, (0, 0, 0), me), target(piece, me, grid.core), own_sem.at[piece]
        )
        for piece in range(len(pieces))
    ]
    if moved:
        greet_plane(grid, fsdp_size)
    else:
        greet(grid)
    for offset in offsets:
        chip, valid = grid.at(offset)

        def step(offset=offset, chip=chip):
            for piece in range(len(pieces)):
                order = pieces[piece][3]
                if offset != (0, 0, 0):
                    back = parent(order, offset)[0]
                    hop(piece, offset, chip, back)[0].wait_recv()
                for cross in children(order, offset):
                    copy, exists = hop(piece, offset, chip, cross)
                    under(exists, copy.start)
                pair(piece, offset, chip, grid.core).start()

        under(valid, step)
        if moved and offset == (0, 0, 0):
            exchange.start()
    for copy in own_copies:
        copy.start()
    for offset in offsets:
        chip, valid = grid.at(offset)

        def finish(offset=offset, chip=chip):
            for piece in range(len(pieces)):
                for cross in children(pieces[piece][3], offset):
                    copy, exists = hop(piece, offset, chip, cross)
                    under(exists, copy.wait_send)
                pair(piece, offset, chip, grid.core).wait_send()
                pair(piece, offset, chip, 1 - grid.core).wait_recv()

        under(valid, finish)
    for copy in own_copies:
        copy.wait()
    if moved:
        exchange.finish()


def exchange_sems(fsdp_size, arrays):
    dma = pltpu.SemaphoreType.DMA
    return [dma((arrays, fsdp_size)), dma((arrays, fsdp_size)), dma((arrays,))] if arrays else []


def gather_call(
    fsdp_size, dims, pieces, places, shards, out_shapes, collective_id, blocks=0, cut=(), sources=(), targets=()
):
    count = len(shards)
    chips = fsdp_size // 2 * (2 if "x" in dims else 1)
    dma = pltpu.SemaphoreType.DMA
    sent = sum(s.size * s.dtype.itemsize for s in shards)
    return pl.pallas_call(
        functools.partial(gather_kernel, fsdp_size, dims, pieces, places, count, blocks, cut),
        out_shape=tuple(out_shapes) + tuple(targets),
        in_specs=[pl.BlockSpec(memory_space=pltpu.VMEM)] * count
        + [pl.BlockSpec(memory_space=pl.ANY)] * len(sources),
        out_specs=tuple([pl.BlockSpec(memory_space=pl.ANY)] * (count + len(targets))),
        scratch_shapes=[
            dma((len(pieces), chips, 4)),
            dma((len(pieces), chips)),
            dma((len(pieces), chips)),
            dma((len(pieces), chips)),
            dma((len(pieces),)),
            *exchange_sems(fsdp_size, len(sources)),
        ],
        compiler_params=pltpu.CompilerParams(collective_id=collective_id, has_side_effects=True),
        cost_estimate=pl.CostEstimate(flops=0, bytes_accessed=8 * sent * chips, transcendentals=0),
    )(*shards, *sources)


def reduce_kernel(fsdp_size, dims, pieces, places, count, blocks, cut, *refs):
    moved = len(cut)
    partials, sources = refs[:count], refs[count : count + moved]
    refs = refs[count + moved :]
    outs, targets = refs[:count], refs[count : count + moved]
    refs = refs[count + moved :]
    held, other, landed = (refs[i * count : (1 + i) * count] for i in range(3))
    send_sem, recv_sem, load_sem, pair_send, pair_recv = refs[3 * count : 3 * count + 5]
    grid = Grid(fsdp_size, dims)
    if moved:
        exchange = Exchange(
            fsdp_size, grid.x, blocks, sources, targets, cut, False, *refs[3 * count + 5 :]
        )
    offsets = offsets_of(grid.depth, dims)[::-1]
    empty = grid.chips * 4

    def load(array, chip):
        index = grid.chip(*chip)
        return pltpu.make_async_copy(
            places[array](partials[array], chip, grid.core), held[array].at[index],
            load_sem.at[array, index],
        )

    def pair(array, chip):
        index = grid.chip(*chip)
        return pltpu.make_async_remote_copy(
            src_ref=places[array](partials[array], chip, 1 - grid.core),
            dst_ref=other[array].at[index],
            send_sem=pair_send.at[array, index],
            recv_sem=pair_recv.at[array, index],
            device_id=grid.partner(),
            device_id_type=MESH,
        )

    def hop(piece, chip, cross, seen_as):
        array, first, rows, _ = pieces[piece]
        there, _ = grid.neighbour(cross)
        index = grid.chip(*chip)
        slot = index * 4 + CROSS.index(seen_as)
        return pltpu.make_async_remote_copy(
            src_ref=held[array].at[index, pl.ds(first, rows)],
            dst_ref=landed[array].at[slot, pl.ds(first, rows)],
            send_sem=send_sem.at[piece, index],
            recv_sem=recv_sem.at[piece, slot],
            device_id=grid.device(*there, grid.core),
            device_id_type=MESH,
        )

    for array in range(count):
        landed[array][empty] = jnp.zeros(landed[array].shape[1:], landed[array].dtype)
    if moved:
        greet_plane(grid, fsdp_size)
    else:
        greet(grid)
    for offset in offsets:
        chip, valid = grid.at(offset)

        def begin(chip=chip):
            for array in range(count):
                load(array, chip).start()
                pair(array, chip).start()

        under(valid, begin)
    if moved:
        exchange.start()
    for offset in offsets:
        chip, valid = grid.at(offset)

        def step(offset=offset, chip=chip):
            index = grid.chip(*chip)
            ready = set()
            for piece, (array, first, rows, order) in enumerate(pieces):
                if array not in ready:
                    ready.add(array)
                    load(array, chip).wait()
                    pair(array, chip).wait_recv()
                slots = []
                for cross in children(order, offset):
                    copy = hop(piece, chip, cross, cross)
                    _, exists = grid.neighbour(cross)
                    under(exists, copy.wait_recv)
                    slot = index * 4 + CROSS.index(cross)
                    slots.append(slot if exists is None else jnp.where(exists, slot, empty))
                tile = 16 if rows % 16 == 0 else rows

                def add(i, carry, array=array, first=first, slots=slots, tile=tile):
                    span = pl.ds(pl.multiple_of(first + i * tile, tile), tile)
                    total = held[array][index, span].astype(jnp.float32)
                    total += other[array][index, span].astype(jnp.float32)
                    for slot in slots:
                        total += landed[array][slot, span].astype(jnp.float32)
                    if offset == (0, 0, 0):
                        outs[array][span] = total
                    else:
                        held[array][index, span] = total.astype(held[array].dtype)
                    return carry

                lax.fori_loop(0, rows // tile, add, 0)
                if offset != (0, 0, 0):
                    hop(piece, chip, *parent(order, offset)).start()

        under(valid, step)
    for offset in offsets:
        chip, valid = grid.at(offset)

        def finish(offset=offset, chip=chip):
            for array in range(count):
                pair(array, chip).wait_send()
            if offset != (0, 0, 0):
                for piece in range(len(pieces)):
                    hop(piece, chip, *parent(pieces[piece][3], offset)).wait_send()

        under(valid, finish)
    if moved:
        exchange.finish()


def reduce_call(
    fsdp_size, dims, pieces, places, partials, shapes, collective_id, blocks=0, cut=(), sources=(), targets=()
):
    count = len(partials)
    chips = fsdp_size // 2 * (2 if "x" in dims else 1)
    dma = pltpu.SemaphoreType.DMA
    held = [pltpu.VMEM((chips, *s), p.dtype) for s, p in zip(shapes, partials)]
    landed = [pltpu.VMEM((chips * 4 + 1, *s), p.dtype) for s, p in zip(shapes, partials)]
    moved = sum(p.size * p.dtype.itemsize for p in partials)
    return pl.pallas_call(
        functools.partial(reduce_kernel, fsdp_size, dims, pieces, places, count, blocks, cut),
        out_shape=tuple(jax.ShapeDtypeStruct(s, jnp.float32) for s in shapes) + tuple(targets),
        in_specs=[pl.BlockSpec(memory_space=pl.ANY)] * (count + len(sources)),
        out_specs=tuple(
            [pl.BlockSpec(memory_space=pltpu.VMEM)] * count
            + [pl.BlockSpec(memory_space=pl.ANY)] * len(targets)
        ),
        scratch_shapes=[
            *held,
            *held,
            *landed,
            dma((len(pieces), chips)),
            dma((len(pieces), chips * 4)),
            dma((count, chips)),
            dma((count, chips)),
            dma((count, chips)),
            *exchange_sems(fsdp_size, len(sources)),
        ],
        compiler_params=pltpu.CompilerParams(
            collective_id=collective_id, has_side_effects=True, vmem_limit_bytes=67043328
        ),
        cost_estimate=pl.CostEstimate(flops=0, bytes_accessed=16 * moved, transcendentals=0),
    )(*partials, *sources)


def token_pieces(rows):
    unit = rows // 4
    return [
        (0, 0, unit, "xyz"),
        (0, unit, unit, "zyx"),
        (0, 2 * unit, unit, "zxy"),
        (0, 3 * unit, unit, "zyx"),
    ]


def token_row(chip, core, rows):
    x, y, z = chip
    return ((z * 4 + y * 2 + core) * 2 + x) * rows


def gather_tokens(owns, collective_id):
    fsdp_size, rows = lax.axis_size("fsdp"), owns[0].shape[0]
    places, shapes, pieces = [], [], token_pieces(rows)
    for array, own in enumerate(owns):

        def place(ref, chip, core, first, count, own_rows=own.shape[0]):
            start = pl.multiple_of(token_row(chip, core, own_rows) + first, 8)
            return ref.at[pl.ds(start, count)]

        places.append(place)
        shapes.append(jax.ShapeDtypeStruct((fsdp_size * 2 * own.shape[0], own.shape[1]), own.dtype))
        if array:
            pieces.append((array, 0, own.shape[0], "zyx"))
    return gather_call(fsdp_size, "xyz", pieces, places, owns, shapes, collective_id)


def reduce_tokens(partials, collective_id):
    fsdp_size = lax.axis_size("fsdp")
    rows = partials[0].shape[0] // (2 * fsdp_size)

    def place(ref, chip, core):
        return ref.at[pl.ds(pl.multiple_of(token_row(chip, core, rows), 16), rows)]

    pieces = token_pieces(rows)
    pieces += [(array, 0, rows, "zyx") for array in range(1, len(partials))]
    shapes = [(rows, p.shape[1]) for p in partials]
    return reduce_call(
        fsdp_size, "xyz", pieces, [place] * len(partials), partials, shapes, collective_id
    )


BLOCK = 128


def plane_row(chip, core):
    return chip[2] * 4 + chip[1] * 2 + core


def row_place(rows):
    def place(ref, chip, core, first=0, count=rows):
        return ref.at[pl.ds(pl.multiple_of(plane_row(chip, core) * rows + first, 8), count)]

    return place


def column_place(columns, rows):
    def place(ref, chip, core, first=0, count=rows):
        start = pl.multiple_of(plane_row(chip, core) * columns, 128)
        return ref.at[pl.ds(first, count), pl.ds(start, columns)]

    return place


def weight_pieces(query, latent, expand, output, small):
    return [
        (4, 0, small, "zy"),
        (0, 0, query // 2, "zy"),
        (1, 0, latent, "zy"),
        (0, query // 2, query // 2, "zy"),
        (2, 0, expand, "yz"),
        (3, 0, output // 2, "zy"),
        (3, output // 2, output // 2, "zy"),
    ]


def block_span(block):
    return pl.ds(pl.multiple_of(block * BLOCK, BLOCK), BLOCK)


def cut_columns(rows):
    def to_owner(source, target, block, other):
        there = pl.ds(pl.multiple_of(other * rows, rows), rows)
        return source.at[:, block_span(block)], target.at[there]

    def from_owner(source, target, block, other):
        there = pl.ds(pl.multiple_of(other * rows, rows), rows)
        return source.at[there], target.at[:, block_span(block)]

    return to_owner, from_owner


def cut_rows(columns):
    def to_owner(source, target, block, other):
        there = pl.ds(pl.multiple_of(other * columns, columns), columns)
        return source.at[block_span(block)], target.at[:, there]

    def from_owner(source, target, block, other):
        there = pl.ds(pl.multiple_of(other * columns, columns), columns)
        return source.at[:, there], target.at[block_span(block)]

    return to_owner, from_owner


def gather_weights(query, latent, expand, output, small, gate, up, down, collective_id):
    size = lax.axis_size("fsdp")
    shards = [query, latent, expand, output, small]
    places = [row_place(query.shape[0]), row_place(latent.shape[0]), row_place(expand.shape[0])]
    places += [column_place(output.shape[1], output.shape[0]), row_place(small.shape[0])]
    shapes = [
        jax.ShapeDtypeStruct((s.shape[0] * size, s.shape[1]), s.dtype) for s in shards
    ]
    shapes[3] = jax.ShapeDtypeStruct((output.shape[0], output.shape[1] * size), output.dtype)
    columns, rows = cut_columns(gate.shape[0]), cut_rows(down.shape[1])
    tall = jax.ShapeDtypeStruct((gate.shape[0] * size, BLOCK), gate.dtype)
    flat = jax.ShapeDtypeStruct((BLOCK, down.shape[1] * size), down.dtype)
    return gather_call(
        size,
        "zy",
        weight_pieces(*[s.shape[0] for s in shards]),
        places,
        shards,
        shapes,
        collective_id,
        gate.shape[1] // BLOCK,
        (columns[0], columns[0], rows[0]),
        [gate, up, down],
        [tall, tall, flat],
    )


def reduce_weights(query, latent, expand, output, small, gate, up, down, blocks, collective_id):
    size = lax.axis_size("fsdp")
    partials = [query, latent, expand, output, small]
    shapes = [(p.shape[0] // size, p.shape[1]) for p in partials]
    shapes[3] = (output.shape[0], output.shape[1] // size)
    places = [row_place(shapes[i][0]) for i in range(5)]
    places[3] = column_place(shapes[3][1], shapes[3][0])
    columns, rows = cut_columns(gate.shape[0] // size), cut_rows(down.shape[1] // size)
    wide = jax.ShapeDtypeStruct((gate.shape[0] // size, blocks * BLOCK), gate.dtype)
    long = jax.ShapeDtypeStruct((blocks * BLOCK, down.shape[1] // size), down.dtype)
    return reduce_call(
        size,
        "zy",
        weight_pieces(*[s[0] for s in shapes]),
        places,
        partials,
        shapes,
        collective_id,
        blocks,
        (columns[1], columns[1], rows[1]),
        [gate, up, down],
        [wide, wide, long],
    )


def token_shards(
    inputs,
    teacher,
    valid_mask,
    prefix,
    routes,
    norm_gain,
    query_weight,
    latent_weight,
    latent_gain,
    expand_weight,
    output_weight,
    moe_gain,
    router_weight,
    shared_gate,
    shared_up,
    shared_down,
    expert_gate,
    expert_up,
    expert_down,
):
    f32 = jnp.float32
    bf16 = jnp.bfloat16
    tp_size = lax.axis_size("tp")
    fsdp_size = lax.axis_size("fsdp")
    own_tp = lax.axis_index("tp")
    own_expert = lax.axis_index("fsdp")
    local_heads = HEADS // tp_size
    own_rows = inputs.shape[0]
    width = inputs.shape[1]
    seq_len = own_rows * tp_size

    expert_count = router_weight.shape[1]
    route_rows = routes.shape[1] * seq_len // BLOCK
    valid_rows = seq_len // BLOCK
    parts = [
        routes.T.reshape(route_rows, BLOCK).astype(f32),
        valid_mask.reshape(valid_rows, BLOCK).astype(f32),
        norm_gain.reshape(1, BLOCK).astype(f32),
        moe_gain.reshape(1, BLOCK).astype(f32),
        jnp.pad(latent_gain, (0, BLOCK - latent_gain.shape[0])).reshape(1, BLOCK).astype(f32),
        router_weight.T.astype(f32),
    ]
    small = jnp.concatenate(parts, axis=0)
    small_rows = -(-small.shape[0] // 8) * 8
    small = jnp.pad(small, ((0, small_rows - small.shape[0]), (0, 0)))
    blocks = shared_gate.shape[1] // BLOCK
    (
        query_full,
        latent_full,
        expand_full,
        output_full,
        small_all,
        gate_block,
        up_block,
        down_block,
    ) = gather_weights(
        query_weight,
        latent_weight,
        expand_weight,
        output_weight,
        small,
        shared_gate,
        shared_up,
        shared_down,
        1,
    )
    small_all = small_all.reshape(fsdp_size, small_rows, BLOCK)
    routes_all = small_all[:, :route_rows].reshape(fsdp_size, routes.shape[1], seq_len)
    gain_row = route_rows + valid_rows
    valid_all = small_all[:, route_rows:gain_row]
    norm_gains = small_all[:, gain_row].reshape(width)
    moe_gains = small_all[:, gain_row + 1].reshape(width)
    latent_gains = small_all[:, gain_row + 2, : latent_gain.shape[0]].reshape(RANK)
    router_rows = small_all[:, gain_row + 3 : gain_row + 3 + expert_count]
    router_full = jnp.transpose(router_rows, (1, 0, 2)).reshape(expert_count, width).astype(bf16)
    own_block = (own_expert * blocks + fsdp_size - 1) // fsdp_size
    holds_block = (own_block < blocks) & (own_block * fsdp_size // blocks == own_expert)
    gate_block = jnp.where(holds_block, gate_block, 0)
    up_block = jnp.where(holds_block, up_block, 0)
    down_block = jnp.where(holds_block, down_block, 0)

    hidden = tp_gather(inputs, own_tp).astype(f32)
    cosine, sine_part = rope_tables(seq_len, ROPE)
    inverse_in = lax.rsqrt(jnp.mean(hidden * hidden, axis=-1, keepdims=True) + EPSILON)
    normal_in = hidden * inverse_in
    norm_scale = norm_gains.astype(f32)
    normed = (normal_in * norm_scale).astype(bf16)
    query_lin = jnp.dot(normed, query_full, preferred_element_type=f32).reshape(
        seq_len, local_heads, NOPE + ROPE
    )
    queries = jnp.concatenate(
        [
            query_lin[..., :NOPE],
            rotate(query_lin[..., NOPE:], cosine[:, None, :], sine_part[:, None, :]),
        ],
        axis=-1,
    ).astype(bf16)
    latent_lin = jnp.dot(normed, latent_full, preferred_element_type=f32)
    latent_raw = latent_lin[:, :RANK]
    inverse_lat = lax.rsqrt(jnp.mean(latent_raw * latent_raw, axis=-1, keepdims=True) + EPSILON)
    latent_unit = latent_raw * inverse_lat
    latent_scale = latent_gains.astype(f32)
    latent = (latent_unit * latent_scale).astype(bf16)
    key_rope = rotate(latent_lin[:, RANK:], cosine, sine_part).astype(bf16)
    keys_values = (
        jnp.dot(latent, expand_full, preferred_element_type=f32)
        .astype(bf16)
        .reshape(seq_len, local_heads, NOPE + VDIM)
    )
    key_nope = keys_values[..., :NOPE]
    values = keys_values[..., NOPE:]
    query_nope = queries[..., :NOPE]
    query_rope = queries[..., NOPE:]
    score_scale = 1.0 / math.sqrt(NOPE + ROPE)
    position = jnp.arange(seq_len, dtype=jnp.int32)
    visible = (position[None, :] <= position[:, None]) | (position[None, :] < prefix[0])
    raw_scores = jnp.einsum("ihd,jhd->hij", query_nope, key_nope, preferred_element_type=f32)
    raw_scores = raw_scores + jnp.einsum(
        "ihd,jd->hij", query_rope, key_rope, preferred_element_type=f32
    )
    scores = jnp.where(visible[None], raw_scores * score_scale, MASKED)
    row_max = jnp.max(scores, axis=-1, keepdims=True)
    shifted = jnp.exp(scores - row_max)
    attn_probs = shifted / jnp.sum(shifted, axis=-1, keepdims=True)
    probs_low = attn_probs.astype(bf16)
    heads_out = (
        jnp.einsum("hij,jhd->ihd", probs_low, values, preferred_element_type=f32)
        .astype(bf16)
        .reshape(seq_len, local_heads * VDIM)
    )
    attended = tp_scatter(
        jnp.dot(heads_out, output_full, preferred_element_type=f32), own_tp, own_rows
    )

    middle = inputs.astype(f32) + attended
    inverse_mid = lax.rsqrt(jnp.mean(middle * middle, axis=-1, keepdims=True) + EPSILON)
    normal_mid = middle * inverse_mid
    moe_scale = moe_gains.astype(f32)
    moe_in = (normal_mid * moe_scale).astype(bf16)

    def route(logits):
        logit_exp = jnp.exp(logits - jnp.max(logits, axis=-1, keepdims=True))
        return logit_exp / jnp.sum(logit_exp, axis=-1, keepdims=True)

    router_probs = route(jnp.einsum("td,ed->te", moe_in, router_full, preferred_element_type=f32))
    experts = expert_count
    top_count = routes.shape[1]
    capacity = top_count * seq_len * 4 // (3 * experts)
    slots = fsdp_size * capacity

    tokens = gather_tokens([moe_in], 2)[0]
    tokens_seq = tokens.reshape(fsdp_size, seq_len, width)
    named = jnp.any(routes_all == own_expert.astype(f32), axis=1)
    ahead = jnp.dot(
        named.astype(bf16),
        (position[:, None] < position[None, :]).astype(bf16),
        preferred_element_type=f32,
    ).astype(jnp.int32)
    place = jnp.where(named, ahead, -1)
    dispatch = (
        place[:, None, :] == jnp.arange(capacity, dtype=jnp.int32)[None, :, None]
    ).astype(bf16)
    wide_block = jnp.concatenate(
        [gate_block, up_block, jnp.pad(router_full, ((0, BLOCK - experts), (0, 0))).T], axis=1
    )
    wide_out = jnp.dot(tokens, wide_block, preferred_element_type=f32)
    gate_sh = wide_out[:, :BLOCK]
    up_sh = wide_out[:, BLOCK : 2 * BLOCK]
    token_probs = route(wide_out[:, 2 * BLOCK : 2 * BLOCK + experts])
    own_probs = jnp.sum(
        jnp.where(jnp.arange(experts, dtype=jnp.int32) == own_expert, token_probs, 0.0), axis=1
    ).reshape(fsdp_size, 1, seq_len)
    gate_slot = jnp.sum(dispatch.astype(f32) * own_probs, axis=2).reshape(slots, 1)
    gate_matrix, up_matrix, down_matrix = expert_gate[0], expert_up[0], expert_down[0]

    def pick(rows_seq):
        return (
            jnp.einsum("sct,std->scd", dispatch, rows_seq, preferred_element_type=f32)
            .astype(bf16)
            .reshape(slots, width)
        )

    def put_back(slot_rows):
        return jnp.einsum(
            "sct,scd->std",
            dispatch,
            slot_rows.astype(bf16).reshape(fsdp_size, capacity, width),
            preferred_element_type=f32,
        ).reshape(fsdp_size * seq_len, width)

    received = pick(tokens_seq)
    gate_act = jnp.dot(received, gate_matrix, preferred_element_type=f32)
    up_act = jnp.dot(received, up_matrix, preferred_element_type=f32)
    silu_gate, silu_slope = silu_parts(gate_act)
    expert_hidden = silu_gate * up_act
    gated_hidden = (gate_slot * expert_hidden).astype(bf16)
    expert_out = jnp.dot(gated_hidden, down_matrix, preferred_element_type=f32)
    silu_sh, slope_sh = silu_parts(gate_sh)
    shared_hidden = (silu_sh * up_sh).astype(bf16)
    moe_part = put_back(expert_out) + jnp.dot(
        shared_hidden, down_block, preferred_element_type=f32
    )
    activations = middle + reduce_tokens([moe_part.astype(bf16)], 3)[0]

    own_mask = half_rows(valid_mask, own_tp, own_rows).astype(f32)
    offset = activations - half_rows(teacher, own_tp, own_rows).astype(f32)
    valid_total = jnp.maximum(jnp.sum(valid_all), 1.0)
    square_part = jnp.sum(own_mask[:, None] * offset * offset)
    grad_out = seq_len * fsdp_size / valid_total * own_mask[:, None] * offset
    grad_moe = grad_out.astype(bf16)

    grads, square_parts = gather_tokens([grad_moe, jnp.full((8, BLOCK), square_part)], 4)
    loss_value = jnp.sum(square_parts[::8, 0]) / (width * valid_total)
    grad_slots = pick(grads.reshape(fsdp_size, seq_len, width))
    grad_raw = jnp.einsum("cd,fd->cf", grad_slots, down_matrix, preferred_element_type=f32)
    grad_gate_slot = jnp.sum(grad_raw * expert_hidden, axis=1)
    grad_hidden = gate_slot * grad_raw
    grad_gate_act = (grad_hidden * up_act * silu_slope).astype(bf16)
    grad_up_act = (grad_hidden * silu_gate).astype(bf16)
    expert_down_grad = jnp.einsum(
        "cf,cd->fd", gated_hidden, grad_slots, preferred_element_type=f32
    )
    expert_gate_grad = jnp.einsum(
        "cd,cf->df", received, grad_gate_act, preferred_element_type=f32
    )
    expert_up_grad = jnp.einsum("cd,cf->df", received, grad_up_act, preferred_element_type=f32)
    grad_expert_in = jnp.einsum(
        "cf,df->cd", grad_gate_act, gate_matrix, preferred_element_type=f32
    ) + jnp.einsum("cf,df->cd", grad_up_act, up_matrix, preferred_element_type=f32)
    grad_sh_hidden = jnp.einsum("td,fd->tf", grads, down_block, preferred_element_type=f32)
    grad_gate_sh = (grad_sh_hidden * up_sh * slope_sh).astype(bf16)
    grad_up_sh = (grad_sh_hidden * silu_sh).astype(bf16)
    down_shared_grad = jnp.einsum("tf,td->fd", shared_hidden, grads, preferred_element_type=f32)
    grad_sh_pair = jnp.concatenate([grad_gate_sh, grad_up_sh], axis=1)
    pair_grad = jnp.einsum("td,tf->df", tokens, grad_sh_pair, preferred_element_type=f32)
    gate_shared_grad = pair_grad[:, :BLOCK].astype(bf16)
    up_shared_grad = pair_grad[:, BLOCK:].astype(bf16)
    grad_part = put_back(grad_expert_in) + jnp.einsum(
        "tf,df->td",
        grad_sh_pair,
        jnp.concatenate([gate_block, up_block], axis=1),
        preferred_element_type=f32,
    )
    grad_probs_col = jnp.sum(
        dispatch.astype(f32) * grad_gate_slot.reshape(fsdp_size, capacity, 1), axis=1
    ).reshape(fsdp_size * seq_len, 1)
    grad_probs_part = jnp.where(
        jnp.arange(128, dtype=jnp.int32)[None, :] == own_expert, grad_probs_col, 0.0
    )
    grad_moe_in, grad_router_probs = reduce_tokens(
        [grad_part.astype(bf16), grad_probs_part.astype(bf16)], 5
    )
    grad_router_probs = grad_router_probs[:, :experts]

    grad_logits = router_probs * (
        grad_router_probs - jnp.sum(router_probs * grad_router_probs, axis=-1, keepdims=True)
    )
    router_grad = jnp.einsum(
        "td,te->ed", moe_in.astype(f32), grad_logits, precision=HIGHEST, preferred_element_type=f32
    )
    grad_moe_in = grad_moe_in + jnp.einsum(
        "te,ed->td",
        grad_logits,
        router_full.astype(f32),
        precision=HIGHEST,
        preferred_element_type=f32,
    )
    moe_gain_grad = jnp.sum(grad_moe_in * normal_mid, axis=0)
    grad_middle = grad_out + norm_back(grad_moe_in * moe_scale, normal_mid, inverse_mid)
    grad_attended = tp_gather(grad_middle.astype(bf16), own_tp)

    output_grad = jnp.einsum("tf,td->fd", heads_out, grad_attended, preferred_element_type=f32)
    grad_heads = (
        jnp.einsum("td,fd->tf", grad_attended, output_full, preferred_element_type=f32)
        .astype(bf16)
        .reshape(seq_len, local_heads, VDIM)
    )
    grad_probs = jnp.einsum("ihd,jhd->hij", grad_heads, values, preferred_element_type=f32)
    grad_values = jnp.einsum("hij,ihd->jhd", probs_low, grad_heads, preferred_element_type=f32)
    grad_scores = (
        attn_probs * (grad_probs - jnp.sum(attn_probs * grad_probs, axis=-1, keepdims=True))
    ).astype(bf16)
    grad_q_nope = (
        jnp.einsum("hij,jhd->ihd", grad_scores, key_nope, preferred_element_type=f32) * score_scale
    )
    grad_q_rope = (
        jnp.einsum("hij,jd->ihd", grad_scores, key_rope, preferred_element_type=f32) * score_scale
    )
    grad_keys = (
        jnp.einsum("hij,ihd->jhd", grad_scores, query_nope, preferred_element_type=f32)
        * score_scale
    )
    grad_key_rope = (
        jnp.einsum("hij,ihd->jd", grad_scores, query_rope, preferred_element_type=f32) * score_scale
    )
    grad_query = (
        jnp.concatenate(
            [grad_q_nope, unrotate(grad_q_rope, cosine[:, None, :], sine_part[:, None, :])], axis=-1
        )
        .astype(bf16)
        .reshape(seq_len, local_heads * (NOPE + ROPE))
    )
    query_grad = jnp.einsum("td,tq->dq", normed, grad_query, preferred_element_type=f32)
    grad_normed = jnp.einsum("tq,dq->td", grad_query, query_full, preferred_element_type=f32)
    grad_kv = (
        jnp.concatenate([grad_keys, grad_values], axis=-1)
        .astype(bf16)
        .reshape(seq_len, local_heads * (NOPE + VDIM))
    )
    expand_grad = jnp.einsum("tr,tq->rq", latent, grad_kv, preferred_element_type=f32)
    grad_latent = jnp.einsum("tq,rq->tr", grad_kv, expand_full, preferred_element_type=f32)
    grad_both = tp_sum(jnp.concatenate([grad_latent, grad_key_rope], axis=1))
    grad_latent, grad_key_rope = grad_both[:, :RANK], grad_both[:, RANK:]
    latent_gain_grad = jnp.sum(grad_latent * latent_unit, axis=0)
    grad_latent_raw = norm_back(grad_latent * latent_scale, latent_unit, inverse_lat)
    grad_latent_lin = jnp.concatenate(
        [grad_latent_raw, unrotate(grad_key_rope, cosine, sine_part)], axis=-1
    ).astype(bf16)
    latent_grad = jnp.einsum("td,tr->dr", normed, grad_latent_lin, preferred_element_type=f32)
    grad_normed = tp_scatter(grad_normed, own_tp, own_rows) + jnp.einsum(
        "tr,dr->td",
        half_rows(grad_latent_lin, own_tp, own_rows),
        latent_full,
        preferred_element_type=f32,
    )
    own_normal = half_rows(normal_in, own_tp, own_rows)
    own_inverse = half_rows(inverse_in, own_tp, own_rows)
    norm_gain_grad = jnp.sum(grad_normed * own_normal, axis=0)
    input_grad = grad_middle + norm_back(grad_normed * norm_scale, own_normal, own_inverse)

    small = jnp.concatenate(
        [
            jnp.transpose(router_grad.reshape(experts, fsdp_size, BLOCK), (1, 0, 2)),
            norm_gain_grad.reshape(fsdp_size, 1, BLOCK),
            moe_gain_grad.reshape(fsdp_size, 1, BLOCK),
            jnp.pad(
                0.5 * latent_gain_grad.reshape(fsdp_size, 1, RANK // fsdp_size),
                ((0, 0), (0, 0), (0, BLOCK - RANK // fsdp_size)),
            ),
        ],
        axis=1,
    )
    small = jnp.pad(small, ((0, 0), (0, -(experts + 3) % 8), (0, 0))).reshape(-1, BLOCK)
    small = small + swap_tp(small)
    query_out, latent_out, expand_out, output_out, small_out, gate_out, up_out, down_out = (
        reduce_weights(
            query_grad.astype(bf16),
            latent_grad.astype(bf16),
            expand_grad.astype(bf16),
            output_grad.astype(bf16),
            small,
            gate_shared_grad,
            up_shared_grad,
            down_shared_grad.astype(bf16),
            blocks,
            6,
        )
    )
    return (
        loss_value,
        activations,
        input_grad,
        small_out[experts],
        query_out,
        latent_out,
        small_out[experts + 2, : RANK // fsdp_size],
        expand_out,
        output_out,
        small_out[experts + 1],
        small_out[:experts].T,
        gate_out.astype(f32),
        up_out.astype(f32),
        down_out.astype(f32),
        expert_gate_grad[None],
        expert_up_grad[None],
        expert_down_grad[None],
    )


def slot_shards(
    inputs,
    teacher,
    valid_mask,
    prefix,
    routes,
    norm_gain,
    query_weight,
    latent_weight,
    latent_gain,
    expand_weight,
    output_weight,
    moe_gain,
    router_weight,
    shared_gate,
    shared_up,
    shared_down,
    expert_gate,
    expert_up,
    expert_down,
):
    f32 = jnp.float32
    bf16 = jnp.bfloat16
    tp_size = lax.axis_size("tp")
    fsdp_size = lax.axis_size("fsdp")
    local_heads = HEADS // tp_size
    (
        norm_gains,
        query_full,
        latent_full,
        latent_gains,
        expand_full,
        output_full,
        moe_gains,
        router_full,
        gate_full,
        up_full,
        down_full,
    ) = (
        lax.all_gather(norm_gain, "fsdp", axis=0, tiled=True),
        lax.all_gather(query_weight, "fsdp", axis=0, tiled=True),
        lax.all_gather(latent_weight, "fsdp", axis=0, tiled=True),
        lax.all_gather(latent_gain, "fsdp", axis=0, tiled=True),
        lax.all_gather(expand_weight, "fsdp", axis=0, tiled=True),
        lax.all_gather(output_weight, "fsdp", axis=1, tiled=True),
        lax.all_gather(moe_gain, "fsdp", axis=0, tiled=True),
        lax.all_gather(router_weight, "fsdp", axis=0, tiled=True),
        lax.all_gather(shared_gate, "fsdp", axis=0, tiled=True),
        lax.all_gather(shared_up, "fsdp", axis=0, tiled=True),
        lax.all_gather(shared_down, "fsdp", axis=1, tiled=True),
    )
    gathered = lax.all_gather(inputs, "tp", axis=0, tiled=True)
    seq_len = gathered.shape[0]
    width = gathered.shape[1]
    hidden = gathered.astype(f32)
    cosine, sine_part = rope_tables(seq_len, ROPE)
    inverse_in = lax.rsqrt(jnp.mean(hidden * hidden, axis=-1, keepdims=True) + EPSILON)
    normal_in = hidden * inverse_in
    norm_scale = norm_gains.astype(f32)
    normed = (normal_in * norm_scale).astype(bf16)
    query_lin = jnp.dot(normed, query_full, preferred_element_type=f32).reshape(
        seq_len, local_heads, NOPE + ROPE
    )
    queries = jnp.concatenate(
        [
            query_lin[..., :NOPE],
            rotate(query_lin[..., NOPE:], cosine[:, None, :], sine_part[:, None, :]),
        ],
        axis=-1,
    ).astype(bf16)
    latent_lin = jnp.dot(normed, latent_full, preferred_element_type=f32)
    latent_raw = latent_lin[:, :RANK]
    inverse_lat = lax.rsqrt(jnp.mean(latent_raw * latent_raw, axis=-1, keepdims=True) + EPSILON)
    latent_unit = latent_raw * inverse_lat
    latent_scale = latent_gains.astype(f32)
    latent = (latent_unit * latent_scale).astype(bf16)
    key_rope = rotate(latent_lin[:, RANK:], cosine, sine_part).astype(bf16)
    keys_values = (
        jnp.dot(latent, expand_full, preferred_element_type=f32)
        .astype(bf16)
        .reshape(seq_len, local_heads, NOPE + VDIM)
    )
    key_nope = keys_values[..., :NOPE]
    values = keys_values[..., NOPE:]
    query_nope = queries[..., :NOPE]
    query_rope = queries[..., NOPE:]
    score_scale = 1.0 / math.sqrt(NOPE + ROPE)
    position = jnp.arange(seq_len, dtype=jnp.int32)
    visible = (position[None, :] <= position[:, None]) | (position[None, :] < prefix[0])

    def scores_of():
        raw_scores = jnp.einsum("ihd,jhd->hij", query_nope, key_nope, preferred_element_type=f32)
        raw_scores = raw_scores + jnp.einsum(
            "ihd,jd->hij", query_rope, key_rope, preferred_element_type=f32
        )
        return jnp.where(visible[None], raw_scores * score_scale, MASKED)

    scores = scores_of()
    row_max = jnp.max(scores, axis=-1, keepdims=True)
    shifted = jnp.exp(scores - row_max)
    row_total = jnp.sum(shifted, axis=-1, keepdims=True)
    log_total = row_max + jnp.log(row_total)
    probs_low = (shifted / row_total).astype(bf16)
    heads_out = (
        jnp.einsum("hij,jhd->ihd", probs_low, values, preferred_element_type=f32)
        .astype(bf16)
        .reshape(seq_len, local_heads * VDIM)
    )
    attended = lax.psum(jnp.dot(heads_out, output_full, preferred_element_type=f32), "tp")
    middle = hidden + attended
    inverse_mid = lax.rsqrt(jnp.mean(middle * middle, axis=-1, keepdims=True) + EPSILON)
    normal_mid = middle * inverse_mid
    moe_scale = moe_gains.astype(f32)
    moe_in = (normal_mid * moe_scale).astype(bf16)
    logits = jnp.dot(moe_in, router_full, preferred_element_type=f32)
    logit_max = jnp.max(logits, axis=-1, keepdims=True)
    logit_exp = jnp.exp(logits - logit_max)
    router_probs = logit_exp / jnp.sum(logit_exp, axis=-1, keepdims=True)
    experts = router_full.shape[1]
    top_count = routes.shape[1]
    choose = routes[:, :, None] == jnp.arange(experts, dtype=jnp.int32)[None, None, :]
    gate_values = jnp.sum(jnp.where(choose, router_probs[:, None, :], 0.0), axis=-1)
    capacity = top_count * seq_len * 4 // (3 * experts)
    flat_routes = routes.reshape(seq_len * top_count)
    onehot = (flat_routes[:, None] == jnp.arange(experts, dtype=jnp.int32)[None, :]).astype(
        jnp.int32
    )
    earlier = jnp.cumsum(onehot, axis=0) - onehot
    slot_index = flat_routes * capacity + jnp.sum(earlier * onehot, axis=1)
    placed = jnp.arange(experts * capacity, dtype=jnp.int32)[:, None] == slot_index[None, :]
    dispatch = jnp.sum(
        placed.reshape(experts * capacity, seq_len, top_count).astype(f32), axis=2
    ).astype(bf16)
    gate_slot = jnp.sum(jnp.where(placed, gate_values.reshape(1, seq_len * top_count), 0.0), axis=1)

    def send_slots(slot_rows):
        return lax.all_to_all(slot_rows, "fsdp", split_axis=0, concat_axis=1, tiled=True)

    def return_slots(partials):
        return (
            lax.all_to_all(
                partials.astype(jnp.bfloat16), "fsdp", split_axis=1, concat_axis=0, tiled=True
            )
            .astype(partials.dtype)
            .reshape(experts * capacity, width)
        )

    expert_in = (
        jnp.dot(dispatch, moe_in, preferred_element_type=f32)
        .astype(bf16)
        .reshape(experts, capacity, width)
    )
    received = send_slots(expert_in)
    gate_act = jnp.einsum("ecd,edf->ecf", received, expert_gate, preferred_element_type=f32)
    up_act = jnp.einsum("ecd,edf->ecf", received, expert_up, preferred_element_type=f32)
    silu_gate, silu_slope = silu_parts(gate_act)
    expert_hidden = (silu_gate * up_act).astype(bf16)
    expert_out = jnp.einsum("ecf,efd->ecd", expert_hidden, expert_down, preferred_element_type=f32)
    returned = return_slots(expert_out)
    picked = jnp.take(returned, slot_index, axis=0).reshape(seq_len, top_count, width)
    routed = jnp.sum(gate_values[:, :, None] * picked, axis=1)
    gate_sh = jnp.dot(moe_in, gate_full, preferred_element_type=f32)
    up_sh = jnp.dot(moe_in, up_full, preferred_element_type=f32)
    silu_sh, slope_sh = silu_parts(gate_sh)
    shared_hidden = (silu_sh * up_sh).astype(bf16)
    moe_part = routed + jnp.dot(shared_hidden, down_full, preferred_element_type=f32)
    moe_out = lax.psum(moe_part.astype(jnp.bfloat16), "tp").astype(jnp.float32)
    activations = middle + moe_out
    mask_float = valid_mask.astype(f32)
    offset = activations - teacher.astype(f32)
    square_sum, valid_sum = lax.psum(
        (jnp.sum(mask_float[:, None] * offset * offset), jnp.sum(mask_float)), "fsdp"
    )
    valid_total = jnp.maximum(valid_sum, 1.0)
    loss_value = square_sum / (width * valid_total)
    grad_out = seq_len * fsdp_size / valid_total * mask_float[:, None] * offset
    grad_moe = grad_out.astype(bf16)
    down_shared_grad = jnp.einsum("tf,td->fd", shared_hidden, grad_moe, preferred_element_type=f32)
    grad_sh_hidden = jnp.einsum("td,fd->tf", grad_moe, down_full, preferred_element_type=f32)
    grad_gate_sh = (grad_sh_hidden * up_sh * slope_sh).astype(bf16)
    grad_up_sh = (grad_sh_hidden * silu_sh).astype(bf16)
    gate_shared_grad = jnp.einsum("td,tf->df", moe_in, grad_gate_sh, preferred_element_type=f32)
    up_shared_grad = jnp.einsum("td,tf->df", moe_in, grad_up_sh, preferred_element_type=f32)
    grad_moe_in = jnp.einsum("tf,df->td", grad_gate_sh, gate_full, preferred_element_type=f32)
    grad_moe_in = grad_moe_in + jnp.einsum(
        "tf,df->td", grad_up_sh, up_full, preferred_element_type=f32
    )
    grad_gates = jnp.sum(picked * grad_moe.astype(f32)[:, None, :], axis=-1)
    grad_slots = (
        (jnp.dot(dispatch, grad_moe, preferred_element_type=f32) * gate_slot[:, None])
        .astype(bf16)
        .reshape(experts, capacity, width)
    )
    grad_received = send_slots(grad_slots)
    expert_down_grad = jnp.einsum(
        "ecf,ecd->efd", expert_hidden, grad_received, preferred_element_type=f32
    )
    grad_expert_hidden = jnp.einsum(
        "ecd,efd->ecf", grad_received, expert_down, preferred_element_type=f32
    )
    grad_gate_act = (grad_expert_hidden * up_act * silu_slope).astype(bf16)
    grad_up_act = (grad_expert_hidden * silu_gate).astype(bf16)
    expert_gate_grad = jnp.einsum(
        "ecd,ecf->edf", received, grad_gate_act, preferred_element_type=f32
    )
    expert_up_grad = jnp.einsum("ecd,ecf->edf", received, grad_up_act, preferred_element_type=f32)
    grad_expert_in = jnp.einsum(
        "ecf,edf->ecd", grad_gate_act, expert_gate, preferred_element_type=f32
    )
    grad_expert_in = grad_expert_in + jnp.einsum(
        "ecf,edf->ecd", grad_up_act, expert_up, preferred_element_type=f32
    )
    grad_returned = return_slots(grad_expert_in)
    grad_moe_in = grad_moe_in + jnp.sum(
        jnp.take(grad_returned, slot_index, axis=0).reshape(seq_len, top_count, width), axis=1
    )
    grad_moe_in, grad_gates = (
        lax.psum(grad_moe_in.astype(jnp.bfloat16), "tp").astype(jnp.float32),
        lax.psum(grad_gates.astype(jnp.bfloat16), "tp").astype(jnp.float32),
    )
    grad_router_probs = jnp.sum(jnp.where(choose, grad_gates[:, :, None], 0.0), axis=1)
    grad_logits = router_probs * (
        grad_router_probs - jnp.sum(router_probs * grad_router_probs, axis=-1, keepdims=True)
    )
    router_grad = jnp.einsum(
        "td,te->de", moe_in.astype(f32), grad_logits, precision=HIGHEST, preferred_element_type=f32
    )
    grad_moe_in = grad_moe_in + jnp.einsum(
        "te,de->td",
        grad_logits,
        router_full.astype(f32),
        precision=HIGHEST,
        preferred_element_type=f32,
    )
    moe_gain_grad = jnp.sum(grad_moe_in * normal_mid, axis=0)
    grad_middle = grad_out + norm_back(grad_moe_in * moe_scale, normal_mid, inverse_mid)
    grad_attended = grad_middle.astype(bf16)
    output_grad = jnp.einsum("tf,td->fd", heads_out, grad_attended, preferred_element_type=f32)
    grad_heads = (
        jnp.einsum("td,fd->tf", grad_attended, output_full, preferred_element_type=f32)
        .astype(bf16)
        .reshape(seq_len, local_heads, VDIM)
    )
    attn_probs = jnp.exp(scores_of() - log_total)
    probs_again = attn_probs.astype(bf16)
    grad_probs = jnp.einsum("ihd,jhd->hij", grad_heads, values, preferred_element_type=f32)
    grad_values = jnp.einsum("hij,ihd->jhd", probs_again, grad_heads, preferred_element_type=f32)
    grad_scores = (
        attn_probs * (grad_probs - jnp.sum(attn_probs * grad_probs, axis=-1, keepdims=True))
    ).astype(bf16)
    grad_q_nope = (
        jnp.einsum("hij,jhd->ihd", grad_scores, key_nope, preferred_element_type=f32) * score_scale
    )
    grad_q_rope = (
        jnp.einsum("hij,jd->ihd", grad_scores, key_rope, preferred_element_type=f32) * score_scale
    )
    grad_keys = (
        jnp.einsum("hij,ihd->jhd", grad_scores, query_nope, preferred_element_type=f32)
        * score_scale
    )
    grad_key_rope = (
        jnp.einsum("hij,ihd->jd", grad_scores, query_rope, preferred_element_type=f32) * score_scale
    )
    grad_query = (
        jnp.concatenate(
            [grad_q_nope, unrotate(grad_q_rope, cosine[:, None, :], sine_part[:, None, :])], axis=-1
        )
        .astype(bf16)
        .reshape(seq_len, local_heads * (NOPE + ROPE))
    )
    query_grad = jnp.einsum("td,tq->dq", normed, grad_query, preferred_element_type=f32)
    grad_normed = jnp.einsum("tq,dq->td", grad_query, query_full, preferred_element_type=f32)
    grad_kv = (
        jnp.concatenate([grad_keys, grad_values], axis=-1)
        .astype(bf16)
        .reshape(seq_len, local_heads * (NOPE + VDIM))
    )
    expand_grad = jnp.einsum("tr,tq->rq", latent, grad_kv, preferred_element_type=f32)
    grad_latent = jnp.einsum("tq,rq->tr", grad_kv, expand_full, preferred_element_type=f32)
    grad_normed, grad_latent, grad_key_rope = (
        lax.psum(grad_normed.astype(jnp.bfloat16), "tp").astype(jnp.float32),
        lax.psum(grad_latent.astype(jnp.bfloat16), "tp").astype(jnp.float32),
        lax.psum(grad_key_rope.astype(jnp.bfloat16), "tp").astype(jnp.float32),
    )
    latent_gain_grad = jnp.sum(grad_latent * latent_unit, axis=0)
    grad_latent_raw = norm_back(grad_latent * latent_scale, latent_unit, inverse_lat)
    grad_latent_lin = jnp.concatenate(
        [grad_latent_raw, unrotate(grad_key_rope, cosine, sine_part)], axis=-1
    ).astype(bf16)
    latent_grad = jnp.einsum("td,tr->dr", normed, grad_latent_lin, preferred_element_type=f32)
    grad_normed = grad_normed + jnp.einsum(
        "tr,dr->td", grad_latent_lin, latent_full, preferred_element_type=f32
    )
    norm_gain_grad = jnp.sum(grad_normed * normal_in, axis=0)
    input_grad = grad_middle + norm_back(grad_normed * norm_scale, normal_in, inverse_in)
    (
        norm_out,
        query_out,
        latent_out,
        lgain_out,
        expand_out,
        output_out,
        mgain_out,
        router_out,
        gate_out,
        up_out,
        down_out,
    ) = (
        lax.psum_scatter(norm_gain_grad, "fsdp", scatter_dimension=0, tiled=True),
        lax.psum_scatter(query_grad, "fsdp", scatter_dimension=0, tiled=True),
        lax.psum_scatter(latent_grad, "fsdp", scatter_dimension=0, tiled=True),
        lax.psum_scatter(latent_gain_grad, "fsdp", scatter_dimension=0, tiled=True),
        lax.psum_scatter(expand_grad, "fsdp", scatter_dimension=0, tiled=True),
        lax.psum_scatter(output_grad, "fsdp", scatter_dimension=1, tiled=True),
        lax.psum_scatter(moe_gain_grad, "fsdp", scatter_dimension=0, tiled=True),
        lax.psum_scatter(router_grad, "fsdp", scatter_dimension=0, tiled=True),
        lax.psum_scatter(gate_shared_grad, "fsdp", scatter_dimension=0, tiled=True),
        lax.psum_scatter(up_shared_grad, "fsdp", scatter_dimension=0, tiled=True),
        lax.psum_scatter(down_shared_grad, "fsdp", scatter_dimension=1, tiled=True),
    )
    own_start = lax.axis_index("tp") * inputs.shape[0]
    own_activations = lax.dynamic_slice_in_dim(activations, own_start, inputs.shape[0], 0)
    own_input_grad = lax.dynamic_slice_in_dim(input_grad, own_start, inputs.shape[0], 0)
    return (
        loss_value,
        own_activations,
        own_input_grad,
        norm_out,
        query_out,
        latent_out,
        lgain_out,
        expand_out,
        output_out,
        mgain_out,
        router_out,
        gate_out,
        up_out,
        down_out,
        expert_gate_grad,
        expert_up_grad,
        expert_down_grad,
    )


def shards(*arrays):
    fsdp_size = lax.axis_size("fsdp")
    seq_len = arrays[4].shape[0]
    experts = arrays[12].shape[1]
    capacity = arrays[4].shape[1] * seq_len * 4 // (3 * experts)
    fits = fsdp_size * seq_len <= 2 * experts * capacity and fsdp_size == experts
    aligned = arrays[5].shape[0] == BLOCK and arrays[13].shape[1] % BLOCK == 0
    if fits and aligned and fsdp_size % 4 == 0:
        return token_shards(*arrays)
    return slot_shards(*arrays)


def solution(mesh):
    return jax.shard_map(
        shards,
        mesh=mesh,
        in_specs=(
            P(("fsdp", "tp"), None),
            P("fsdp", None),
            P("fsdp"),
            P("fsdp"),
            P("fsdp", None),
            P("fsdp"),
            P("fsdp", "tp"),
            P("fsdp", None),
            P("fsdp"),
            P("fsdp", "tp"),
            P("tp", "fsdp"),
            P("fsdp"),
            P("fsdp", None),
            P("fsdp", "tp"),
            P("fsdp", "tp"),
            P("tp", "fsdp"),
            P("fsdp", None, "tp"),
            P("fsdp", None, "tp"),
            P("fsdp", "tp", None),
        ),
        out_specs=(
            P(),
            P(("fsdp", "tp"), None),
            P(("fsdp", "tp"), None),
            P("fsdp"),
            P("fsdp", "tp"),
            P("fsdp", None),
            P("fsdp"),
            P("fsdp", "tp"),
            P("tp", "fsdp"),
            P("fsdp"),
            P("fsdp", None),
            P("fsdp", "tp"),
            P("fsdp", "tp"),
            P("tp", "fsdp"),
            P("fsdp", None, "tp"),
            P("fsdp", None, "tp"),
            P("fsdp", "tp", None),
        ),
        check_vma=False,
    )
```

```python
import functools
import math

import jax
import jax.numpy as jnp
from jax import lax
from jax.experimental import pallas as pl
from jax.experimental.pallas import tpu as pltpu
from jax.sharding import PartitionSpec as P

HEADS = 16
NOPE = 128
ROPE = 64
RANK = 512
VDIM = 128


EPSILON = 1e-06
HIGHEST = lax.Precision.HIGHEST
MASKED = -1e30


def rope_tables(length, dim_size):
    places = jnp.arange(length).astype(jnp.float32)
    exponent = jnp.arange(dim_size // 2).astype(jnp.float32) * (2.0 / dim_size)
    angles = places[:, None] * jnp.exp(exponent * -math.log(10000.0))[None, :]
    return (jnp.cos(angles), jnp.sin(angles))


def rotate(values, cosine, sine_part):
    half_width = values.shape[-1] // 2
    lower_half = values[..., :half_width]
    upper_half = values[..., half_width:]
    return jnp.concatenate(
        [
            lower_half * cosine - upper_half * sine_part,
            upper_half * cosine + lower_half * sine_part,
        ],
        axis=-1,
    )


def unrotate(gradient, cosine, sine_part):
    half_width = gradient.shape[-1] // 2
    lower_half = gradient[..., :half_width]
    upper_half = gradient[..., half_width:]
    return jnp.concatenate(
        [
            lower_half * cosine + upper_half * sine_part,
            upper_half * cosine - lower_half * sine_part,
        ],
        axis=-1,
    )


def silu_parts(gate_act):
    sigmoid_val = jax.nn.sigmoid(gate_act)
    return (gate_act * sigmoid_val, sigmoid_val * (1.0 + gate_act * (1.0 - sigmoid_val)))


def norm_back(grad_scaled, unit_rows, inverse):
    return inverse * (
        grad_scaled - unit_rows * jnp.mean(grad_scaled * unit_rows, axis=-1, keepdims=True)
    )


def swap_tp(value):
    return lax.ppermute(value, "tp", [(0, 1), (1, 0)])


def half_rows(value, which, rows):
    return lax.dynamic_slice_in_dim(value, which * rows, rows, 0)


def tp_scatter(partial, which, rows):
    other = half_rows(partial, 1 - which, rows).astype(jnp.bfloat16)
    return half_rows(partial, which, rows) + swap_tp(other).astype(jnp.float32)


def tp_sum(partial):
    low_partial = partial.astype(jnp.bfloat16)
    return low_partial.astype(jnp.float32) + swap_tp(low_partial).astype(jnp.float32)


def tp_gather(own, which):
    other = swap_tp(own)
    first = jnp.where(which == 0, own, other)
    second = jnp.where(which == 0, other, own)
    return jnp.concatenate([first, second], axis=0)


MESH = pl.DeviceIdType.MESH
CROSS = ("x", "y", "up", "down")


class Grid:
    def __init__(self, fsdp_size, dims):
        index = lax.axis_index("fsdp")
        self.core = lax.rem(index, 2)
        self.y = lax.rem(lax.div(index, 2), 2)
        self.z = lax.div(index, 4)
        self.x = lax.axis_index("tp")
        self.depth = fsdp_size // 4
        self.dims = dims
        self.chips = self.depth * 2 * (2 if "x" in dims else 1)

    def device(self, x, y, z, core):
        return {"fsdp": z * 4 + y * 2 + core, "tp": x}

    def chip(self, x, y, z):
        return (z * 2 + y) * 2 + x if "x" in self.dims else z * 2 + y

    def partner(self):
        return self.device(self.x, self.y, self.z, 1 - self.core)

    def neighbour(self, cross):
        if cross == "x":
            return (1 - self.x, self.y, self.z), None
        if cross == "y":
            return (self.x, 1 - self.y, self.z), None
        if cross == "up":
            return (self.x, self.y, self.z + 1), self.z + 1 < self.depth
        return (self.x, self.y, self.z - 1), self.z >= 1

    def at(self, offset):
        dx, dy, dz = offset
        x = 1 - self.x if dx else self.x
        y = 1 - self.y if dy else self.y
        z = self.z + dz
        if dz == 0:
            return (x, y, z), None
        return (x, y, z), (z < self.depth if dz > 0 else z >= 0)


def offsets_of(depth, dims):
    xs = (0, 1) if "x" in dims else (0,)
    found = [(dx, dy, dz) for dx in xs for dy in (0, 1) for dz in range(1 - depth, depth)]
    return sorted(found, key=lambda o: (abs(o[0]) + abs(o[1]) + abs(o[2]), abs(o[2])))


def arrival(order, offset):
    by_dim = dict(x=offset[0], y=offset[1], z=offset[2])
    last = None
    for dim in order:
        if by_dim[dim]:
            last = dim
    return last


def children(order, offset):
    last = arrival(order, offset)
    after = order if last is None else order[order.index(last) + 1 :]
    found = []
    if last == "z":
        found.append("down" if offset[2] > 0 else "up")
    for dim in after:
        found.extend(("up", "down") if dim == "z" else (dim,))
    return found


def parent(order, offset):
    last = arrival(order, offset)
    if last == "z":
        return ("up", "down") if offset[2] > 0 else ("down", "up")
    return last, last


def both(first, second):
    if first is None:
        return second
    if second is None:
        return first
    return jnp.logical_and(first, second)


def under(condition, body):
    if condition is None:
        body()
    else:
        pl.when(condition)(body)


def greet_plane(grid, fsdp_size):
    barrier = pltpu.get_barrier_semaphore()
    me = lax.axis_index("fsdp")

    def send(step, carry):
        there = lax.rem(me + step, fsdp_size)
        pl.semaphore_signal(barrier, inc=1, device_id={"fsdp": there, "tp": grid.x}, device_id_type=MESH)
        return carry

    lax.fori_loop(1, fsdp_size, send, 0)
    pl.semaphore_wait(barrier, fsdp_size - 1)


def greet(grid):
    barrier = pltpu.get_barrier_semaphore()
    pl.semaphore_signal(barrier, inc=1, device_id=grid.partner(), device_id_type=MESH)
    count = 1
    for cross in CROSS:
        if cross in ("x", "y") and cross not in grid.dims:
            continue
        chip, exists = grid.neighbour(cross)

        def send(chip=chip):
            pl.semaphore_signal(
                barrier, inc=1, device_id=grid.device(*chip, grid.core), device_id_type=MESH
            )

        under(exists, send)
        count = count + (1 if exists is None else jnp.where(exists, 1, 0))
    pl.semaphore_wait(barrier, count)


class Exchange:
    def __init__(self, fsdp_size, tp, blocks, sources, targets, cut, to_owner, send_sem, recv_sem, own_sem):
        self.size, self.tp, self.blocks = fsdp_size, tp, blocks
        self.sources, self.targets, self.cut, self.to_owner = sources, targets, cut, to_owner
        self.send_sem, self.recv_sem, self.own_sem = send_sem, recv_sem, own_sem
        self.me = lax.axis_index("fsdp")
        self.block = lax.div(self.me * blocks + fsdp_size - 1, fsdp_size)
        self.owns = jnp.logical_and(
            self.block < blocks, lax.div(self.block * fsdp_size, blocks) == self.me
        )

    def owner(self, block):
        return block * self.size // self.blocks

    def remote(self, array, block, other, there, send, recv):
        source, target = self.cut[array](self.sources[array], self.targets[array], block, other)
        return pltpu.make_async_remote_copy(
            src_ref=source,
            dst_ref=target,
            send_sem=self.send_sem.at[array, send],
            recv_sem=self.recv_sem.at[array, recv],
            device_id={"fsdp": there, "tp": self.tp},
            device_id_type=MESH,
        )

    def local(self, array, block):
        source, target = self.cut[array](self.sources[array], self.targets[array], block, self.me)
        return pltpu.make_async_copy(source, target, self.own_sem.at[array])

    def each(self, act_send, act_recv, act_local):
        arrays = range(len(self.sources))
        for block in range(self.blocks):
            owner = self.owner(block)
            for array in arrays:
                if self.to_owner:
                    if act_send:
                        copy = self.remote(array, block, self.me, owner, block, self.me)
                        pl.when(self.me != owner)(getattr(copy, act_send))
                    if act_local:
                        pl.when(self.me == owner)(getattr(self.local(array, block), act_local))
                elif act_recv:
                    copy = self.remote(array, block, self.me, owner, 0, block)
                    pl.when(self.me != owner)(getattr(copy, act_recv))

        def owning():
            for other in range(self.size):
                for array in arrays:
                    if self.to_owner:
                        if act_recv:
                            copy = self.remote(array, self.block, other, other, 0, other)
                            pl.when(self.me != other)(getattr(copy, act_recv))
                    elif act_send:
                        copy = self.remote(array, self.block, other, other, other, self.block)
                        pl.when(self.me != other)(getattr(copy, act_send))
            for array in arrays:
                if act_local and not self.to_owner:
                    getattr(self.local(array, self.block), act_local)()

        pl.when(self.owns)(owning)

    def start(self):
        self.each("start", None, "start")

    def finish(self):
        self.each(None, "wait_recv", None)
        self.each("wait_send", None, "wait")


def gather_kernel(fsdp_size, dims, pieces, places, count, blocks, cut, *refs):
    moved = len(cut)
    shards, sources = refs[:count], refs[count : count + moved]
    refs = refs[count + moved :]
    outs, targets = refs[:count], refs[count : count + moved]
    send_sem, recv_sem, pair_send, pair_recv, own_sem = refs[count + moved : count + moved + 5]
    grid = Grid(fsdp_size, dims)
    if moved:
        exchange = Exchange(
            fsdp_size, grid.x, blocks, sources, targets, cut, True, *refs[count + moved + 5 :]
        )
    me = (grid.x, grid.y, grid.z)
    offsets = offsets_of(grid.depth, dims)

    def target(piece, chip, core):
        array, first, rows, _ = pieces[piece]
        return places[array](outs[array], chip, core, first, rows)

    def source(piece, offset, chip):
        array, first, rows, _ = pieces[piece]
        if offset == (0, 0, 0):
            return shards[array].at[pl.ds(first, rows)]
        return target(piece, chip, grid.core)

    def hop(piece, offset, chip, cross):
        there, exists = grid.neighbour(cross)
        index = grid.chip(*chip)
        copy = pltpu.make_async_remote_copy(
            src_ref=source(piece, offset, chip),
            dst_ref=target(piece, chip, grid.core),
            send_sem=send_sem.at[piece, index, CROSS.index(cross)],
            recv_sem=recv_sem.at[piece, index],
            device_id=grid.device(*there, grid.core),
            device_id_type=MESH,
        )
        return copy, exists

    def pair(piece, offset, chip, core):
        index = grid.chip(*chip)
        return pltpu.make_async_remote_copy(
            src_ref=source(piece, offset, chip),
            dst_ref=target(piece, chip, core),
            send_sem=pair_send.at[piece, index],
            recv_sem=pair_recv.at[piece, index],
            device_id=grid.partner(),
            device_id_type=MESH,
        )

    own_copies = [
        pltpu.make_async_copy(
            source(piece, (0, 0, 0), me), target(piece, me, grid.core), own_sem.at[piece]
        )
        for piece in range(len(pieces))
    ]
    if moved:
        greet_plane(grid, fsdp_size)
    else:
        greet(grid)
    for offset in offsets:
        chip, valid = grid.at(offset)

        def step(offset=offset, chip=chip):
            for piece in range(len(pieces)):
                order = pieces[piece][3]
                if offset != (0, 0, 0):
                    back = parent(order, offset)[0]
                    hop(piece, offset, chip, back)[0].wait_recv()
                for cross in children(order, offset):
                    copy, exists = hop(piece, offset, chip, cross)
                    under(exists, copy.start)
                pair(piece, offset, chip, grid.core).start()

        under(valid, step)
        if moved and offset == (0, 0, 0):
            exchange.start()
    for copy in own_copies:
        copy.start()
    for offset in offsets:
        chip, valid = grid.at(offset)

        def finish(offset=offset, chip=chip):
            for piece in range(len(pieces)):
                for cross in children(pieces[piece][3], offset):
                    copy, exists = hop(piece, offset, chip, cross)
                    under(exists, copy.wait_send)
                pair(piece, offset, chip, grid.core).wait_send()
                pair(piece, offset, chip, 1 - grid.core).wait_recv()

        under(valid, finish)
    for copy in own_copies:
        copy.wait()
    if moved:
        exchange.finish()


def exchange_sems(fsdp_size, arrays):
    dma = pltpu.SemaphoreType.DMA
    return [dma((arrays, fsdp_size)), dma((arrays, fsdp_size)), dma((arrays,))] if arrays else []


def gather_call(
    fsdp_size, dims, pieces, places, shards, out_shapes, collective_id, blocks=0, cut=(), sources=(), targets=()
):
    count = len(shards)
    chips = fsdp_size // 2 * (2 if "x" in dims else 1)
    dma = pltpu.SemaphoreType.DMA
    sent = sum(s.size * s.dtype.itemsize for s in shards)
    return pl.pallas_call(
        functools.partial(gather_kernel, fsdp_size, dims, pieces, places, count, blocks, cut),
        out_shape=tuple(out_shapes) + tuple(targets),
        in_specs=[pl.BlockSpec(memory_space=pltpu.VMEM)] * count
        + [pl.BlockSpec(memory_space=pl.ANY)] * len(sources),
        out_specs=tuple([pl.BlockSpec(memory_space=pl.ANY)] * (count + len(targets))),
        scratch_shapes=[
            dma((len(pieces), chips, 4)),
            dma((len(pieces), chips)),
            dma((len(pieces), chips)),
            dma((len(pieces), chips)),
            dma((len(pieces),)),
            *exchange_sems(fsdp_size, len(sources)),
        ],
        compiler_params=pltpu.CompilerParams(collective_id=collective_id, has_side_effects=True),
        cost_estimate=pl.CostEstimate(flops=0, bytes_accessed=8 * sent * chips, transcendentals=0),
    )(*shards, *sources)


def reduce_kernel(fsdp_size, dims, pieces, places, count, blocks, cut, *refs):
    moved = len(cut)
    partials, sources = refs[:count], refs[count : count + moved]
    refs = refs[count + moved :]
    outs, targets = refs[:count], refs[count : count + moved]
    refs = refs[count + moved :]
    held, other, landed = (refs[i * count : (1 + i) * count] for i in range(3))
    send_sem, recv_sem, load_sem, pair_send, pair_recv = refs[3 * count : 3 * count + 5]
    grid = Grid(fsdp_size, dims)
    if moved:
        exchange = Exchange(
            fsdp_size, grid.x, blocks, sources, targets, cut, False, *refs[3 * count + 5 :]
        )
    offsets = offsets_of(grid.depth, dims)[::-1]
    empty = grid.chips * 4

    def load(array, chip):
        index = grid.chip(*chip)
        return pltpu.make_async_copy(
            places[array](partials[array], chip, grid.core), held[array].at[index],
            load_sem.at[array, index],
        )

    def pair(array, chip):
        index = grid.chip(*chip)
        return pltpu.make_async_remote_copy(
            src_ref=places[array](partials[array], chip, 1 - grid.core),
            dst_ref=other[array].at[index],
            send_sem=pair_send.at[array, index],
            recv_sem=pair_recv.at[array, index],
            device_id=grid.partner(),
            device_id_type=MESH,
        )

    def hop(piece, chip, cross, seen_as):
        array, first, rows, _ = pieces[piece]
        there, _ = grid.neighbour(cross)
        index = grid.chip(*chip)
        slot = index * 4 + CROSS.index(seen_as)
        return pltpu.make_async_remote_copy(
            src_ref=held[array].at[index, pl.ds(first, rows)],
            dst_ref=landed[array].at[slot, pl.ds(first, rows)],
            send_sem=send_sem.at[piece, index],
            recv_sem=recv_sem.at[piece, slot],
            device_id=grid.device(*there, grid.core),
            device_id_type=MESH,
        )

    for array in range(count):
        landed[array][empty] = jnp.zeros(landed[array].shape[1:], landed[array].dtype)
    if moved:
        greet_plane(grid, fsdp_size)
    else:
        greet(grid)
    for offset in offsets:
        chip, valid = grid.at(offset)

        def begin(chip=chip):
            for array in range(count):
                load(array, chip).start()
                pair(array, chip).start()

        under(valid, begin)
    if moved:
        exchange.start()
    for offset in offsets:
        chip, valid = grid.at(offset)

        def step(offset=offset, chip=chip):
            index = grid.chip(*chip)
            ready = set()
            for piece, (array, first, rows, order) in enumerate(pieces):
                if array not in ready:
                    ready.add(array)
                    load(array, chip).wait()
                    pair(array, chip).wait_recv()
                slots = []
                for cross in children(order, offset):
                    copy = hop(piece, chip, cross, cross)
                    _, exists = grid.neighbour(cross)
                    under(exists, copy.wait_recv)
                    slot = index * 4 + CROSS.index(cross)
                    slots.append(slot if exists is None else jnp.where(exists, slot, empty))
                tile = 16 if rows % 16 == 0 else rows

                def add(i, carry, array=array, first=first, slots=slots, tile=tile):
                    span = pl.ds(pl.multiple_of(first + i * tile, tile), tile)
                    total = held[array][index, span].astype(jnp.float32)
                    total += other[array][index, span].astype(jnp.float32)
                    for slot in slots:
                        total += landed[array][slot, span].astype(jnp.float32)
                    if offset == (0, 0, 0):
                        outs[array][span] = total
                    else:
                        held[array][index, span] = total.astype(held[array].dtype)
                    return carry

                lax.fori_loop(0, rows // tile, add, 0)
                if offset != (0, 0, 0):
                    hop(piece, chip, *parent(order, offset)).start()

        under(valid, step)
    for offset in offsets:
        chip, valid = grid.at(offset)

        def finish(offset=offset, chip=chip):
            for array in range(count):
                pair(array, chip).wait_send()
            if offset != (0, 0, 0):
                for piece in range(len(pieces)):
                    hop(piece, chip, *parent(pieces[piece][3], offset)).wait_send()

        under(valid, finish)
    if moved:
        exchange.finish()


def reduce_call(
    fsdp_size, dims, pieces, places, partials, shapes, collective_id, blocks=0, cut=(), sources=(), targets=()
):
    count = len(partials)
    chips = fsdp_size // 2 * (2 if "x" in dims else 1)
    dma = pltpu.SemaphoreType.DMA
    held = [pltpu.VMEM((chips, *s), p.dtype) for s, p in zip(shapes, partials)]
    landed = [pltpu.VMEM((chips * 4 + 1, *s), p.dtype) for s, p in zip(shapes, partials)]
    moved = sum(p.size * p.dtype.itemsize for p in partials)
    return pl.pallas_call(
        functools.partial(reduce_kernel, fsdp_size, dims, pieces, places, count, blocks, cut),
        out_shape=tuple(jax.ShapeDtypeStruct(s, jnp.float32) for s in shapes) + tuple(targets),
        in_specs=[pl.BlockSpec(memory_space=pl.ANY)] * (count + len(sources)),
        out_specs=tuple(
            [pl.BlockSpec(memory_space=pltpu.VMEM)] * count
            + [pl.BlockSpec(memory_space=pl.ANY)] * len(targets)
        ),
        scratch_shapes=[
            *held,
            *held,
            *landed,
            dma((len(pieces), chips)),
            dma((len(pieces), chips * 4)),
            dma((count, chips)),
            dma((count, chips)),
            dma((count, chips)),
            *exchange_sems(fsdp_size, len(sources)),
        ],
        compiler_params=pltpu.CompilerParams(
            collective_id=collective_id, has_side_effects=True, vmem_limit_bytes=67043328
        ),
        cost_estimate=pl.CostEstimate(flops=0, bytes_accessed=16 * moved, transcendentals=0),
    )(*partials, *sources)


def token_pieces(rows):
    unit = rows // 4
    return [
        (0, 0, unit, "xyz"),
        (0, unit, unit, "zyx"),
        (0, 2 * unit, unit, "zxy"),
        (0, 3 * unit, unit, "zyx"),
    ]


def token_row(chip, core, rows):
    x, y, z = chip
    return ((z * 4 + y * 2 + core) * 2 + x) * rows


def gather_tokens(owns, collective_id):
    fsdp_size, rows = lax.axis_size("fsdp"), owns[0].shape[0]
    places, shapes, pieces = [], [], token_pieces(rows)
    for array, own in enumerate(owns):

        def place(ref, chip, core, first, count, own_rows=own.shape[0]):
            start = pl.multiple_of(token_row(chip, core, own_rows) + first, 8)
            return ref.at[pl.ds(start, count)]

        places.append(place)
        shapes.append(jax.ShapeDtypeStruct((fsdp_size * 2 * own.shape[0], own.shape[1]), own.dtype))
        if array:
            pieces.append((array, 0, own.shape[0], "zyx"))
    return gather_call(fsdp_size, "xyz", pieces, places, owns, shapes, collective_id)


def reduce_tokens(partials, collective_id):
    fsdp_size = lax.axis_size("fsdp")
    rows = partials[0].shape[0] // (2 * fsdp_size)

    def place(ref, chip, core):
        return ref.at[pl.ds(pl.multiple_of(token_row(chip, core, rows), 16), rows)]

    pieces = token_pieces(rows)
    pieces += [(array, 0, rows, "zyx") for array in range(1, len(partials))]
    shapes = [(rows, p.shape[1]) for p in partials]
    return reduce_call(
        fsdp_size, "xyz", pieces, [place] * len(partials), partials, shapes, collective_id
    )


BLOCK = 128


def plane_row(chip, core):
    return chip[2] * 4 + chip[1] * 2 + core


def row_place(rows):
    def place(ref, chip, core, first=0, count=rows):
        return ref.at[pl.ds(pl.multiple_of(plane_row(chip, core) * rows + first, 8), count)]

    return place


def column_place(columns, rows):
    def place(ref, chip, core, first=0, count=rows):
        start = pl.multiple_of(plane_row(chip, core) * columns, 128)
        return ref.at[pl.ds(first, count), pl.ds(start, columns)]

    return place


def weight_pieces(query, latent, expand, output, small):
    return [
        (4, 0, small, "zy"),
        (0, 0, query // 2, "zy"),
        (1, 0, latent, "zy"),
        (0, query // 2, query // 2, "zy"),
        (2, 0, expand, "yz"),
        (3, 0, output // 2, "zy"),
        (3, output // 2, output // 2, "zy"),
    ]


def block_span(block):
    return pl.ds(pl.multiple_of(block * BLOCK, BLOCK), BLOCK)


def cut_columns(rows):
    def to_owner(source, target, block, other):
        there = pl.ds(pl.multiple_of(other * rows, rows), rows)
        return source.at[:, block_span(block)], target.at[there]

    def from_owner(source, target, block, other):
        there = pl.ds(pl.multiple_of(other * rows, rows), rows)
        return source.at[there], target.at[:, block_span(block)]

    return to_owner, from_owner


def cut_rows(columns):
    def to_owner(source, target, block, other):
        there = pl.ds(pl.multiple_of(other * columns, columns), columns)
        return source.at[block_span(block)], target.at[:, there]

    def from_owner(source, target, block, other):
        there = pl.ds(pl.multiple_of(other * columns, columns), columns)
        return source.at[:, there], target.at[block_span(block)]

    return to_owner, from_owner


def gather_weights(query, latent, expand, output, small, gate, up, down, collective_id):
    size = lax.axis_size("fsdp")
    shards = [query, latent, expand, output, small]
    places = [row_place(query.shape[0]), row_place(latent.shape[0]), row_place(expand.shape[0])]
    places += [column_place(output.shape[1], output.shape[0]), row_place(small.shape[0])]
    shapes = [
        jax.ShapeDtypeStruct((s.shape[0] * size, s.shape[1]), s.dtype) for s in shards
    ]
    shapes[3] = jax.ShapeDtypeStruct((output.shape[0], output.shape[1] * size), output.dtype)
    columns, rows = cut_columns(gate.shape[0]), cut_rows(down.shape[1])
    tall = jax.ShapeDtypeStruct((gate.shape[0] * size, BLOCK), gate.dtype)
    flat = jax.ShapeDtypeStruct((BLOCK, down.shape[1] * size), down.dtype)
    return gather_call(
        size,
        "zy",
        weight_pieces(*[s.shape[0] for s in shards]),
        places,
        shards,
        shapes,
        collective_id,
        gate.shape[1] // BLOCK,
        (columns[0], columns[0], rows[0]),
        [gate, up, down],
        [tall, tall, flat],
    )


def reduce_weights(query, latent, expand, output, small, gate, up, down, blocks, collective_id):
    size = lax.axis_size("fsdp")
    partials = [query, latent, expand, output, small]
    shapes = [(p.shape[0] // size, p.shape[1]) for p in partials]
    shapes[3] = (output.shape[0], output.shape[1] // size)
    places = [row_place(shapes[i][0]) for i in range(5)]
    places[3] = column_place(shapes[3][1], shapes[3][0])
    columns, rows = cut_columns(gate.shape[0] // size), cut_rows(down.shape[1] // size)
    wide = jax.ShapeDtypeStruct((gate.shape[0] // size, blocks * BLOCK), gate.dtype)
    long = jax.ShapeDtypeStruct((blocks * BLOCK, down.shape[1] // size), down.dtype)
    return reduce_call(
        size,
        "zy",
        weight_pieces(*[s[0] for s in shapes]),
        places,
        partials,
        shapes,
        collective_id,
        blocks,
        (columns[1], columns[1], rows[1]),
        [gate, up, down],
        [wide, wide, long],
    )


def meet(first, second):
    if first is False or second is False:
        return False
    return both(first, second)


class Spread:
    ORDERS = ("xyz", "zyx", "zxy", "zyx")

    def __init__(self, fsdp_size, own, room, sems):
        self.grid = Grid(fsdp_size, "xyz")
        self.own, self.room = own, room
        self.rows = own.shape[0]
        self.part = self.rows // len(self.ORDERS)
        self.send_sem, self.recv_sem, self.pair_send, self.pair_recv = sems
        self.units = fsdp_size // 2

    def unit(self, step):
        grid = self.grid
        rank, flip = lax.div(step, 2), lax.rem(step, 2)
        inner = jnp.logical_or(grid.z == 1, grid.z == 2)
        rank = jnp.where(jnp.logical_and(inner, rank >= 2), 5 - rank, rank)
        high, low = lax.div(grid.z, 2), lax.rem(grid.z, 2)
        far, near = lax.div(rank, 2), lax.rem(rank, 2)
        z = 2 * (high + far - 2 * high * far) + (low + near - 2 * low * near)
        return grid.y + flip - 2 * grid.y * flip, z

    def span(self, x, y, z, core, piece):
        start = token_row((x, y, z), core, self.rows) + piece * self.part
        return self.room.at[pl.ds(pl.multiple_of(start, self.part), self.part)]

    def copies(self, step, flip_x, piece, own=False):
        grid, order = self.grid, self.ORDERS[piece]
        y, z = self.unit(step)
        x = 1 - grid.x if flip_x else grid.x
        index = grid.chip(x, y, z)
        here = self.span(x, y, z, grid.core, piece)
        source = self.own.at[pl.ds(piece * self.part, self.part)] if own else here
        depth = z - grid.z
        zero = dict(x=None if not flip_x else False, y=y == grid.y, z=depth == 0)
        wanted, rest = {}, None
        for dim in reversed(order):
            if dim == "z":
                wanted["up"] = meet(rest, (depth <= 0) & (grid.z + 1 < grid.depth))
                wanted["down"] = meet(rest, (depth >= 0) & (grid.z >= 1))
            else:
                wanted[dim] = meet(rest, zero[dim])
            rest = meet(rest, zero[dim])
        found = []
        for cross in CROSS:
            there, _ = grid.neighbour(cross)
            if wanted[cross] is False:
                continue
            copy = pltpu.make_async_remote_copy(
                src_ref=source,
                dst_ref=here,
                send_sem=self.send_sem.at[piece, index, CROSS.index(cross)],
                recv_sem=self.recv_sem.at[piece, index],
                device_id=grid.device(*there, grid.core),
                device_id_type=MESH,
            )
            found.append((wanted[cross], copy))
        return found

    def pair(self, step, flip_x, piece, own=False):
        grid = self.grid
        y, z = self.unit(step)
        x = 1 - grid.x if flip_x else grid.x
        here = self.span(x, y, z, grid.core, piece)
        index = grid.chip(x, y, z)
        return pltpu.make_async_remote_copy(
            src_ref=self.own.at[pl.ds(piece * self.part, self.part)] if own else here,
            dst_ref=here,
            send_sem=self.pair_send.at[piece, index],
            recv_sem=self.pair_recv.at[piece, index],
            device_id=grid.partner(),
            device_id_type=MESH,
        )

    def landing(self, step, flip_x, piece):
        grid = self.grid
        y, z = self.unit(step)
        x = 1 - grid.x if flip_x else grid.x
        here = self.span(x, y, z, grid.core, piece)
        index = grid.chip(x, y, z)
        return pltpu.make_async_remote_copy(
            src_ref=here,
            dst_ref=here,
            send_sem=self.pair_send.at[piece, index],
            recv_sem=self.recv_sem.at[piece, index],
            device_id=grid.partner(),
            device_id_type=MESH,
        )

    def relay(self, step, flip_x, piece, own=False):
        if not own:
            self.landing(step, flip_x, piece).wait_recv()
        for wanted, copy in self.copies(step, flip_x, piece, own):
            under(wanted, copy.start)
        self.pair(step, flip_x, piece, own).start()

    def begin(self):
        greet(self.grid)
        pieces = range(len(self.ORDERS))
        for piece in pieces:
            self.relay(0, False, piece, own=True)
        start = token_row((self.grid.x, self.grid.y, self.grid.z), self.grid.core, self.rows)
        self.room[pl.ds(pl.multiple_of(start, self.rows), self.rows)] = self.own[...]
        for piece in pieces:
            self.relay(0, True, piece)

    def message(self, number):
        return number // len(self.ORDERS) == 1, number % len(self.ORDERS)

    def tick(self, step, number):
        pl.when(step < self.units)(lambda: self.relay(step, *self.message(number)))

    def arrived(self, step):
        for number in range(2 * len(self.ORDERS)):
            self.pair(step, *self.message(number)).wait_recv()

    def drain(self):
        def finish(step, carry):
            for number in range(2 * len(self.ORDERS)):
                for wanted, copy in self.copies(step, *self.message(number)):
                    under(wanted, copy.wait_send)
                self.pair(step, *self.message(number)).wait_send()
            return carry

        lax.fori_loop(0, self.units, finish, 0)


def spread_sems(fsdp_size):
    dma = pltpu.SemaphoreType.DMA
    return [dma((4, fsdp_size, 4)), dma((4, fsdp_size)), dma((4, fsdp_size)), dma((4, fsdp_size))]


class Stage:
    def __init__(self, buffers, results, sems):
        self.buffers, self.results, self.sems = buffers, results, sems

    def copy(self, number, step, unit):
        buffer = self.buffers[number]
        rows = buffer.shape[1]
        slot = lax.rem(step, 2)
        there = self.results[number].at[pl.ds(pl.multiple_of(unit * rows, rows), rows)]
        return pltpu.make_async_copy(buffer.at[slot], there, self.sems.at[number, slot])

    def reuse(self, step):
        def wait():
            for number in range(len(self.buffers)):
                self.copy(number, step, 0).wait()

        pl.when(step >= 2)(wait)

    def put(self, number, step, unit):
        self.copy(number, step, unit).start()

    def finish(self, steps):
        for step in (steps - 2, steps - 1):
            for number in range(len(self.buffers)):
                self.copy(number, step, 0).wait()


def dot(left, right):
    return jnp.dot(left, right, preferred_element_type=jnp.float32)


def dot_nt(left, right):
    return lax.dot_general(
        left, right, (((1,), (1,)), ((), ())), preferred_element_type=jnp.float32
    )


def dispatch_of(place_ref, sequence, capacity, seq_len):
    row = place_ref[pl.ds(sequence, 1), :]
    slot = lax.broadcasted_iota(jnp.int32, (capacity, seq_len), 0)
    return jnp.where(slot == row, 1.0, 0.0)


def forward_kernel(
    fsdp_size,
    experts,
    capacity,
    own,
    place_ref,
    gate_ref,
    up_ref,
    down_ref,
    wide_ref,
    block_ref,
    tokens_out,
    received_out,
    gate_out,
    up_out,
    hidden_out,
    weight_out,
    shared_out,
    sh_out,
    part_out,
    room,
    picks,
    packs,
    chances,
    tall,
    received,
    gate_act,
    up_act,
    hidden,
    weight,
    shared,
    sh_act,
    part,
    stage_sem,
    room_sem,
    *sems,
):
    f32, bf16 = jnp.float32, jnp.bfloat16
    seq_len = place_ref.shape[1]
    spread = Spread(fsdp_size, own, room, sems)
    expert = lax.axis_index("fsdp")
    stage = Stage(
        [received, gate_act, up_act, hidden, weight, shared, sh_act, part],
        [received_out, gate_out, up_out, hidden_out, weight_out, shared_out, sh_out, part_out],
        stage_sem,
    )
    lanes = lax.broadcasted_iota(jnp.int32, (2 * seq_len, BLOCK), 1)

    def tokens_copy(unit):
        span = pl.ds(pl.multiple_of(unit * 2 * seq_len, 2 * seq_len), 2 * seq_len)
        return pltpu.make_async_copy(room.at[span], tokens_out.at[span], room_sem.at[unit])

    for one in (0, 1):
        tall[one, capacity:] = block_ref[...]
    spread.begin()

    def body(step, carry):
        slot = lax.rem(step, 2)
        y, z = spread.unit(step)
        unit = z * 2 + y
        later = step + 1
        spread.arrived(step)
        tokens_copy(unit).start()
        stage.reuse(step)
        rows = [
            pl.ds(pl.multiple_of((2 * unit + one) * seq_len, seq_len), seq_len) for one in (0, 1)
        ]
        slots = [pl.ds(one * capacity, capacity) for one in (0, 1)]
        own_rows = [pl.ds(one * seq_len, seq_len) for one in (0, 1)]
        spread.tick(later, 0)
        for one in (0, 1):
            pick = dispatch_of(place_ref, 2 * unit + one, capacity, seq_len)
            picks[one] = pick.astype(bf16)
            packs[one, :, :capacity] = jnp.transpose(pick).astype(bf16)
            received[slot, slots[one]] = dot(picks[one], room[rows[one]]).astype(bf16)
        stage.put(0, step, unit)
        spread.tick(later, 1)
        both_rows = pl.ds(pl.multiple_of(unit * 2 * seq_len, 2 * seq_len), 2 * seq_len)
        wide = dot(room[both_rows], wide_ref[...])
        shared[slot] = wide[:, : 2 * BLOCK]
        gate_sh, up_sh = wide[:, :BLOCK], wide[:, BLOCK : 2 * BLOCK]
        act = (silu_parts(gate_sh)[0] * up_sh).astype(bf16)
        sh_act[slot] = act
        for one in (0, 1):
            packs[one, :, capacity:] = act[one * seq_len : (one + 1) * seq_len]
        logits = jnp.where(lanes < experts, wide[:, 2 * BLOCK :], MASKED)
        logit_exp = jnp.exp(logits - jnp.max(logits, axis=1, keepdims=True))
        chance = jnp.sum(jnp.where(lanes == expert, logit_exp, 0.0), axis=1, keepdims=True)
        chance = chance / jnp.sum(logit_exp, axis=1, keepdims=True)
        coarse = chance.astype(bf16).astype(f32)
        chances[...] = jnp.where(
            lanes == 0, coarse, jnp.where(lanes == 1, chance - coarse, 0.0)
        ).astype(bf16)
        stage.put(5, step, unit)
        stage.put(6, step, unit)
        spread.tick(later, 2)
        gate_act[slot] = dot(received[slot], gate_ref[...])
        stage.put(1, step, unit)
        spread.tick(later, 3)
        up_act[slot] = dot(received[slot], up_ref[...])
        stage.put(2, step, unit)
        spread.tick(later, 4)
        for one in (0, 1):
            halves = dot(picks[one], chances[own_rows[one]])
            scale = halves[:, 0:1] + halves[:, 1:2]
            weight[slot, slots[one]] = jnp.broadcast_to(scale, (capacity, BLOCK))
            act = silu_parts(gate_act[slot, slots[one]])[0] * up_act[slot, slots[one]]
            hidden[slot, slots[one]] = (scale * act).astype(bf16)
        stage.put(3, step, unit)
        stage.put(4, step, unit)
        spread.tick(later, 5)
        result = dot(hidden[slot], down_ref[...]).astype(bf16)
        for one in (0, 1):
            tall[one, :capacity] = result[one * capacity : (one + 1) * capacity]
        spread.tick(later, 6)
        part[slot, own_rows[0]] = dot(packs[0], tall[0]).astype(bf16)
        spread.tick(later, 7)
        part[slot, own_rows[1]] = dot(packs[1], tall[1]).astype(bf16)
        stage.put(7, step, unit)
        return carry

    lax.fori_loop(0, spread.units, body, 0)
    stage.finish(spread.units)
    for unit in range(spread.units):
        tokens_copy(unit).wait()
    spread.drain()


def experts_forward(own, place, gate, up, down, wide, block, capacity, experts, collective_id):
    fsdp_size = lax.axis_size("fsdp")
    f32, bf16 = jnp.float32, jnp.bfloat16
    seq_len, width, hidden = place.shape[1], own.shape[1], gate.shape[1]
    tokens, slots = fsdp_size * seq_len, fsdp_size * capacity
    shape = jax.ShapeDtypeStruct
    outs = [
        shape((tokens, width), bf16),
        shape((slots, width), bf16),
        shape((slots, hidden), f32),
        shape((slots, hidden), f32),
        shape((slots, hidden), bf16),
        shape((slots, BLOCK), f32),
        shape((tokens, 2 * BLOCK), f32),
        shape((tokens, BLOCK), bf16),
        shape((tokens, width), bf16),
    ]
    stages = [pltpu.VMEM((2, 2 * o.shape[0] // fsdp_size, o.shape[1]), o.dtype) for o in outs[1:]]
    dma = pltpu.SemaphoreType.DMA
    return pl.pallas_call(
        functools.partial(forward_kernel, fsdp_size, experts, capacity),
        out_shape=tuple(outs),
        in_specs=[pl.BlockSpec(memory_space=pltpu.VMEM)] * 7,
        out_specs=tuple([pl.BlockSpec(memory_space=pl.ANY)] * len(outs)),
        scratch_shapes=[
            pltpu.VMEM((tokens, width), bf16),
            pltpu.VMEM((2, capacity, seq_len), bf16),
            pltpu.VMEM((2, seq_len, capacity + BLOCK), bf16),
            pltpu.VMEM((2 * seq_len, BLOCK), bf16),
            pltpu.VMEM((2, capacity + BLOCK, width), bf16),
            *stages,
            dma((len(stages), 2)),
            dma((fsdp_size // 2,)),
            *spread_sems(fsdp_size),
        ],
        compiler_params=pltpu.CompilerParams(
            collective_id=collective_id, has_side_effects=True, vmem_limit_bytes=67043328
        ),
        cost_estimate=pl.CostEstimate(
            flops=6 * slots * width * hidden, bytes_accessed=100_000_000, transcendentals=0
        ),
    )(own, place, gate, up, down, wide, block)


def backward_kernel(
    fsdp_size,
    capacity,
    own,
    place_ref,
    gate_ref,
    up_ref,
    down_ref,
    pair_ref,
    block_ref,
    gate_in,
    up_in,
    weight_in,
    shared_in,
    grads_out,
    slots_out,
    gate_out,
    up_out,
    pair_out,
    chance_out,
    part_out,
    room,
    picks,
    packs,
    tall,
    gate_act,
    up_act,
    weight,
    shared,
    picked,
    gate_grad,
    up_grad,
    pair_grad,
    chance_grad,
    part,
    load_sem,
    stage_sem,
    room_sem,
    *sems,
):
    f32, bf16 = jnp.float32, jnp.bfloat16
    seq_len = place_ref.shape[1]
    spread = Spread(fsdp_size, own, room, sems)
    expert = lax.axis_index("fsdp")
    stage = Stage(
        [picked, gate_grad, up_grad, pair_grad, chance_grad, part],
        [slots_out, gate_out, up_out, pair_out, chance_out, part_out],
        stage_sem,
    )
    saved = [gate_in, up_in, weight_in, shared_in]
    loads = [gate_act, up_act, weight, shared]

    def load(number, step):
        y, z = spread.unit(step)
        slot, rows = lax.rem(step, 2), loads[number].shape[1]
        span = pl.ds(pl.multiple_of((z * 2 + y) * rows, rows), rows)
        return pltpu.make_async_copy(
            saved[number].at[span], loads[number].at[slot], load_sem.at[number, slot]
        )

    def grads_copy(unit):
        span = pl.ds(pl.multiple_of(unit * 2 * seq_len, 2 * seq_len), 2 * seq_len)
        return pltpu.make_async_copy(room.at[span], grads_out.at[span], room_sem.at[unit])

    for number in range(len(saved)):
        load(number, 0).start()
    for one in (0, 1):
        tall[one, capacity:] = pair_ref[...]
    spread.begin()
    expert_lane = lax.broadcasted_iota(jnp.int32, (capacity, BLOCK), 1) == expert

    def body(step, carry):
        slot = lax.rem(step, 2)
        y, z = spread.unit(step)
        unit = z * 2 + y
        later = step + 1
        spread.arrived(step)
        grads_copy(unit).start()
        stage.reuse(step)
        rows = [
            pl.ds(pl.multiple_of((2 * unit + one) * seq_len, seq_len), seq_len) for one in (0, 1)
        ]
        both_rows = pl.ds(pl.multiple_of(unit * 2 * seq_len, 2 * seq_len), 2 * seq_len)
        slots = [pl.ds(one * capacity, capacity) for one in (0, 1)]
        own_rows = [pl.ds(one * seq_len, seq_len) for one in (0, 1)]
        for number in range(len(saved)):
            load(number, step).wait()

        def ahead():
            for number in range(len(saved)):
                load(number, later).start()

        pl.when(later < spread.units)(ahead)
        spread.tick(later, 0)
        for one in (0, 1):
            pick = dispatch_of(place_ref, 2 * unit + one, capacity, seq_len)
            picks[one] = pick.astype(bf16)
            packs[one, :, :capacity] = jnp.transpose(pick).astype(bf16)
            picked[slot, slots[one]] = dot(picks[one], room[rows[one]]).astype(bf16)
        stage.put(0, step, unit)
        spread.tick(later, 1)
        raw = dot_nt(picked[slot], down_ref[...])
        scale = weight[slot, :, 0:1]
        silu_gate, slope = silu_parts(gate_act[slot])
        up_value = up_act[slot]
        gate_sum = jnp.sum(raw * (silu_gate * up_value), axis=1, keepdims=True)
        scaled = scale * raw
        gate_grad[slot] = (scaled * up_value * slope).astype(bf16)
        up_grad[slot] = (scaled * silu_gate).astype(bf16)
        stage.put(1, step, unit)
        stage.put(2, step, unit)
        spread.tick(later, 2)
        for one in (0, 1):
            column = gate_sum[one * capacity : (one + 1) * capacity]
            column = jnp.where(expert_lane, column, 0.0).astype(bf16)
            chance_grad[slot, own_rows[one]] = dot(packs[one, :, :capacity], column).astype(bf16)
        stage.put(4, step, unit)
        grad_sh = dot_nt(room[both_rows], block_ref[...])
        silu_sh, slope_sh = silu_parts(shared[slot, :, :BLOCK])
        gate_sh = (grad_sh * shared[slot, :, BLOCK:] * slope_sh).astype(bf16)
        up_sh = (grad_sh * silu_sh).astype(bf16)
        pair_grad[slot, :, :BLOCK] = gate_sh
        pair_grad[slot, :, BLOCK:] = up_sh
        for one in (0, 1):
            own_seq = slice(one * seq_len, (one + 1) * seq_len)
            packs[one, :, capacity : capacity + BLOCK] = gate_sh[own_seq]
            packs[one, :, capacity + BLOCK :] = up_sh[own_seq]
        stage.put(3, step, unit)
        spread.tick(later, 3)
        back = dot_nt(gate_grad[slot], gate_ref[...])
        spread.tick(later, 4)
        back = (back + dot_nt(up_grad[slot], up_ref[...])).astype(bf16)
        for one in (0, 1):
            tall[one, :capacity] = back[one * capacity : (one + 1) * capacity]
        spread.tick(later, 5)
        part[slot, own_rows[0]] = dot(packs[0], tall[0]).astype(bf16)
        spread.tick(later, 6)
        part[slot, own_rows[1]] = dot(packs[1], tall[1]).astype(bf16)
        stage.put(5, step, unit)
        spread.tick(later, 7)
        return carry

    lax.fori_loop(0, spread.units, body, 0)
    stage.finish(spread.units)
    for unit in range(spread.units):
        grads_copy(unit).wait()
    spread.drain()


def experts_backward(
    own, place, gate, up, down, pair, block, gate_act, up_act, weight, shared, capacity, collective_id
):
    fsdp_size = lax.axis_size("fsdp")
    bf16 = jnp.bfloat16
    seq_len, width, hidden = place.shape[1], own.shape[1], gate.shape[1]
    tokens, slots = fsdp_size * seq_len, fsdp_size * capacity
    shape = jax.ShapeDtypeStruct
    outs = [
        shape((tokens, width), bf16),
        shape((slots, width), bf16),
        shape((slots, hidden), bf16),
        shape((slots, hidden), bf16),
        shape((tokens, 2 * BLOCK), bf16),
        shape((tokens, BLOCK), bf16),
        shape((tokens, width), bf16),
    ]

    def slots_of(arrays):
        return [pltpu.VMEM((2, 2 * a.shape[0] // fsdp_size, a.shape[1]), a.dtype) for a in arrays]

    saved = [gate_act, up_act, weight, shared]
    dma = pltpu.SemaphoreType.DMA
    return pl.pallas_call(
        functools.partial(backward_kernel, fsdp_size, capacity),
        out_shape=tuple(outs),
        in_specs=[pl.BlockSpec(memory_space=pltpu.VMEM)] * 7
        + [pl.BlockSpec(memory_space=pl.ANY)] * 4,
        out_specs=tuple([pl.BlockSpec(memory_space=pl.ANY)] * len(outs)),
        scratch_shapes=[
            pltpu.VMEM((tokens, width), bf16),
            pltpu.VMEM((2, capacity, seq_len), bf16),
            pltpu.VMEM((2, seq_len, capacity + 2 * BLOCK), bf16),
            pltpu.VMEM((2, capacity + 2 * BLOCK, width), bf16),
            *slots_of(saved),
            *slots_of(outs[1:]),
            dma((4, 2)),
            dma((len(outs) - 1, 2)),
            dma((fsdp_size // 2,)),
            *spread_sems(fsdp_size),
        ],
        compiler_params=pltpu.CompilerParams(
            collective_id=collective_id, has_side_effects=True, vmem_limit_bytes=67043328
        ),
        cost_estimate=pl.CostEstimate(
            flops=6 * slots * width * hidden, bytes_accessed=100_000_000, transcendentals=0
        ),
    )(own, place, gate, up, down, pair, block, *saved)


def token_shards(
    inputs,
    teacher,
    valid_mask,
    prefix,
    routes,
    norm_gain,
    query_weight,
    latent_weight,
    latent_gain,
    expand_weight,
    output_weight,
    moe_gain,
    router_weight,
    shared_gate,
    shared_up,
    shared_down,
    expert_gate,
    expert_up,
    expert_down,
):
    f32 = jnp.float32
    bf16 = jnp.bfloat16
    tp_size = lax.axis_size("tp")
    fsdp_size = lax.axis_size("fsdp")
    own_tp = lax.axis_index("tp")
    own_expert = lax.axis_index("fsdp")
    local_heads = HEADS // tp_size
    own_rows = inputs.shape[0]
    width = inputs.shape[1]
    seq_len = own_rows * tp_size

    expert_count = router_weight.shape[1]
    route_rows = routes.shape[1] * seq_len // BLOCK
    valid_rows = seq_len // BLOCK
    parts = [
        routes.T.reshape(route_rows, BLOCK).astype(f32),
        valid_mask.reshape(valid_rows, BLOCK).astype(f32),
        norm_gain.reshape(1, BLOCK).astype(f32),
        moe_gain.reshape(1, BLOCK).astype(f32),
        jnp.pad(latent_gain, (0, BLOCK - latent_gain.shape[0])).reshape(1, BLOCK).astype(f32),
        router_weight.T.astype(f32),
    ]
    small = jnp.concatenate(parts, axis=0)
    small_rows = -(-small.shape[0] // 8) * 8
    small = jnp.pad(small, ((0, small_rows - small.shape[0]), (0, 0)))
    blocks = shared_gate.shape[1] // BLOCK
    (
        query_full,
        latent_full,
        expand_full,
        output_full,
        small_all,
        gate_block,
        up_block,
        down_block,
    ) = gather_weights(
        query_weight,
        latent_weight,
        expand_weight,
        output_weight,
        small,
        shared_gate,
        shared_up,
        shared_down,
        1,
    )
    small_all = small_all.reshape(fsdp_size, small_rows, BLOCK)
    routes_all = small_all[:, :route_rows].reshape(fsdp_size, routes.shape[1], seq_len)
    gain_row = route_rows + valid_rows
    valid_all = small_all[:, route_rows:gain_row]
    norm_gains = small_all[:, gain_row].reshape(width)
    moe_gains = small_all[:, gain_row + 1].reshape(width)
    latent_gains = small_all[:, gain_row + 2, : latent_gain.shape[0]].reshape(RANK)
    router_rows = small_all[:, gain_row + 3 : gain_row + 3 + expert_count]
    router_full = jnp.transpose(router_rows, (1, 0, 2)).reshape(expert_count, width).astype(bf16)
    own_block = (own_expert * blocks + fsdp_size - 1) // fsdp_size
    holds_block = (own_block < blocks) & (own_block * fsdp_size // blocks == own_expert)
    gate_block = jnp.where(holds_block, gate_block, 0)
    up_block = jnp.where(holds_block, up_block, 0)
    down_block = jnp.where(holds_block, down_block, 0)

    hidden = tp_gather(inputs, own_tp).astype(f32)
    cosine, sine_part = rope_tables(seq_len, ROPE)
    inverse_in = lax.rsqrt(jnp.mean(hidden * hidden, axis=-1, keepdims=True) + EPSILON)
    normal_in = hidden * inverse_in
    norm_scale = norm_gains.astype(f32)
    normed = (normal_in * norm_scale).astype(bf16)
    query_lin = jnp.dot(normed, query_full, preferred_element_type=f32).reshape(
        seq_len, local_heads, NOPE + ROPE
    )
    queries = jnp.concatenate(
        [
            query_lin[..., :NOPE],
            rotate(query_lin[..., NOPE:], cosine[:, None, :], sine_part[:, None, :]),
        ],
        axis=-1,
    ).astype(bf16)
    latent_lin = jnp.dot(normed, latent_full, preferred_element_type=f32)
    latent_raw = latent_lin[:, :RANK]
    inverse_lat = lax.rsqrt(jnp.mean(latent_raw * latent_raw, axis=-1, keepdims=True) + EPSILON)
    latent_unit = latent_raw * inverse_lat
    latent_scale = latent_gains.astype(f32)
    latent = (latent_unit * latent_scale).astype(bf16)
    key_rope = rotate(latent_lin[:, RANK:], cosine, sine_part).astype(bf16)
    keys_values = (
        jnp.dot(latent, expand_full, preferred_element_type=f32)
        .astype(bf16)
        .reshape(seq_len, local_heads, NOPE + VDIM)
    )
    key_nope = keys_values[..., :NOPE]
    values = keys_values[..., NOPE:]
    query_nope = queries[..., :NOPE]
    query_rope = queries[..., NOPE:]
    score_scale = 1.0 / math.sqrt(NOPE + ROPE)
    position = jnp.arange(seq_len, dtype=jnp.int32)
    visible = (position[None, :] <= position[:, None]) | (position[None, :] < prefix[0])
    raw_scores = jnp.einsum("ihd,jhd->hij", query_nope, key_nope, preferred_element_type=f32)
    raw_scores = raw_scores + jnp.einsum(
        "ihd,jd->hij", query_rope, key_rope, preferred_element_type=f32
    )
    scores = jnp.where(visible[None], raw_scores * score_scale, MASKED)
    row_max = jnp.max(scores, axis=-1, keepdims=True)
    shifted = jnp.exp(scores - row_max)
    attn_probs = shifted / jnp.sum(shifted, axis=-1, keepdims=True)
    probs_low = attn_probs.astype(bf16)
    heads_out = (
        jnp.einsum("hij,jhd->ihd", probs_low, values, preferred_element_type=f32)
        .astype(bf16)
        .reshape(seq_len, local_heads * VDIM)
    )
    attended = tp_scatter(
        jnp.dot(heads_out, output_full, preferred_element_type=f32), own_tp, own_rows
    )

    middle = inputs.astype(f32) + attended
    inverse_mid = lax.rsqrt(jnp.mean(middle * middle, axis=-1, keepdims=True) + EPSILON)
    normal_mid = middle * inverse_mid
    moe_scale = moe_gains.astype(f32)
    moe_in = (normal_mid * moe_scale).astype(bf16)

    def route(logits):
        logit_exp = jnp.exp(logits - jnp.max(logits, axis=-1, keepdims=True))
        return logit_exp / jnp.sum(logit_exp, axis=-1, keepdims=True)

    router_probs = route(jnp.einsum("td,ed->te", moe_in, router_full, preferred_element_type=f32))
    experts = expert_count
    top_count = routes.shape[1]
    capacity = top_count * seq_len * 4 // (3 * experts)

    named = jnp.any(routes_all == own_expert.astype(f32), axis=1)
    ahead = jnp.dot(
        named.astype(bf16),
        (position[:, None] < position[None, :]).astype(bf16),
        preferred_element_type=f32,
    ).astype(jnp.int32)
    place = jnp.where(named, ahead, -1)
    wide_block = jnp.concatenate(
        [gate_block, up_block, jnp.pad(router_full, ((0, BLOCK - experts), (0, 0))).T], axis=1
    )
    (
        tokens,
        received,
        gate_act,
        up_act,
        gated_hidden,
        gate_weight,
        shared_acts,
        shared_hidden,
        moe_part,
    ) = experts_forward(
        moe_in,
        place,
        expert_gate[0],
        expert_up[0],
        expert_down[0],
        wide_block,
        down_block,
        capacity,
        experts,
        2,
    )
    activations = middle + reduce_tokens([moe_part], 3)[0]

    own_mask = half_rows(valid_mask, own_tp, own_rows).astype(f32)
    offset = activations - half_rows(teacher, own_tp, own_rows).astype(f32)
    valid_total = jnp.maximum(jnp.sum(valid_all), 1.0)
    square_part = jnp.sum(own_mask[:, None] * offset * offset)
    grad_out = seq_len * fsdp_size / valid_total * own_mask[:, None] * offset
    grad_moe = grad_out.astype(bf16)

    (
        grads,
        grad_slots,
        grad_gate_act,
        grad_up_act,
        grad_sh_pair,
        grad_probs_part,
        grad_part,
    ) = experts_backward(
        grad_moe,
        place,
        expert_gate[0],
        expert_up[0],
        expert_down[0],
        jnp.concatenate([gate_block.T, up_block.T], axis=0),
        down_block,
        gate_act,
        up_act,
        gate_weight,
        shared_acts,
        capacity,
        4,
    )
    grad_moe_in, grad_router_probs = reduce_tokens([grad_part, grad_probs_part], 5)
    expert_down_grad = jnp.einsum(
        "cf,cd->fd", gated_hidden, grad_slots, preferred_element_type=f32
    )
    expert_gate_grad = jnp.einsum(
        "cd,cf->df", received, grad_gate_act, preferred_element_type=f32
    )
    expert_up_grad = jnp.einsum("cd,cf->df", received, grad_up_act, preferred_element_type=f32)
    down_shared_grad = jnp.einsum("tf,td->fd", shared_hidden, grads, preferred_element_type=f32)
    pair_grad = jnp.einsum("td,tf->df", tokens, grad_sh_pair, preferred_element_type=f32)
    gate_shared_grad = pair_grad[:, :BLOCK].astype(bf16)
    up_shared_grad = pair_grad[:, BLOCK:].astype(bf16)
    grad_router_probs = grad_router_probs[:, :experts]

    grad_logits = router_probs * (
        grad_router_probs - jnp.sum(router_probs * grad_router_probs, axis=-1, keepdims=True)
    )
    router_grad = jnp.einsum(
        "td,te->ed", moe_in.astype(f32), grad_logits, precision=HIGHEST, preferred_element_type=f32
    )
    grad_moe_in = grad_moe_in + jnp.einsum(
        "te,ed->td",
        grad_logits,
        router_full.astype(f32),
        precision=HIGHEST,
        preferred_element_type=f32,
    )
    moe_gain_grad = jnp.sum(grad_moe_in * normal_mid, axis=0)
    grad_middle = grad_out + norm_back(grad_moe_in * moe_scale, normal_mid, inverse_mid)
    grad_attended = tp_gather(grad_middle.astype(bf16), own_tp)

    output_grad = jnp.einsum("tf,td->fd", heads_out, grad_attended, preferred_element_type=f32)
    grad_heads = (
        jnp.einsum("td,fd->tf", grad_attended, output_full, preferred_element_type=f32)
        .astype(bf16)
        .reshape(seq_len, local_heads, VDIM)
    )
    grad_probs = jnp.einsum("ihd,jhd->hij", grad_heads, values, preferred_element_type=f32)
    grad_values = jnp.einsum("hij,ihd->jhd", probs_low, grad_heads, preferred_element_type=f32)
    grad_scores = (
        attn_probs * (grad_probs - jnp.sum(attn_probs * grad_probs, axis=-1, keepdims=True))
    ).astype(bf16)
    grad_q_nope = (
        jnp.einsum("hij,jhd->ihd", grad_scores, key_nope, preferred_element_type=f32) * score_scale
    )
    grad_q_rope = (
        jnp.einsum("hij,jd->ihd", grad_scores, key_rope, preferred_element_type=f32) * score_scale
    )
    grad_keys = (
        jnp.einsum("hij,ihd->jhd", grad_scores, query_nope, preferred_element_type=f32)
        * score_scale
    )
    grad_key_rope = (
        jnp.einsum("hij,ihd->jd", grad_scores, query_rope, preferred_element_type=f32) * score_scale
    )
    grad_query = (
        jnp.concatenate(
            [grad_q_nope, unrotate(grad_q_rope, cosine[:, None, :], sine_part[:, None, :])], axis=-1
        )
        .astype(bf16)
        .reshape(seq_len, local_heads * (NOPE + ROPE))
    )
    query_grad = jnp.einsum("td,tq->dq", normed, grad_query, preferred_element_type=f32)
    grad_normed = jnp.einsum("tq,dq->td", grad_query, query_full, preferred_element_type=f32)
    grad_kv = (
        jnp.concatenate([grad_keys, grad_values], axis=-1)
        .astype(bf16)
        .reshape(seq_len, local_heads * (NOPE + VDIM))
    )
    expand_grad = jnp.einsum("tr,tq->rq", latent, grad_kv, preferred_element_type=f32)
    grad_latent = jnp.einsum("tq,rq->tr", grad_kv, expand_full, preferred_element_type=f32)
    grad_both = tp_sum(jnp.concatenate([grad_latent, grad_key_rope], axis=1))
    grad_latent, grad_key_rope = grad_both[:, :RANK], grad_both[:, RANK:]
    latent_gain_grad = jnp.sum(grad_latent * latent_unit, axis=0)
    grad_latent_raw = norm_back(grad_latent * latent_scale, latent_unit, inverse_lat)
    grad_latent_lin = jnp.concatenate(
        [grad_latent_raw, unrotate(grad_key_rope, cosine, sine_part)], axis=-1
    ).astype(bf16)
    latent_grad = jnp.einsum("td,tr->dr", normed, grad_latent_lin, preferred_element_type=f32)
    grad_normed = tp_scatter(grad_normed, own_tp, own_rows) + jnp.einsum(
        "tr,dr->td",
        half_rows(grad_latent_lin, own_tp, own_rows),
        latent_full,
        preferred_element_type=f32,
    )
    own_normal = half_rows(normal_in, own_tp, own_rows)
    own_inverse = half_rows(inverse_in, own_tp, own_rows)
    norm_gain_grad = jnp.sum(grad_normed * own_normal, axis=0)
    input_grad = grad_middle + norm_back(grad_normed * norm_scale, own_normal, own_inverse)

    small = jnp.concatenate(
        [
            jnp.transpose(router_grad.reshape(experts, fsdp_size, BLOCK), (1, 0, 2)),
            norm_gain_grad.reshape(fsdp_size, 1, BLOCK),
            moe_gain_grad.reshape(fsdp_size, 1, BLOCK),
            jnp.pad(
                0.5 * latent_gain_grad.reshape(fsdp_size, 1, RANK // fsdp_size),
                ((0, 0), (0, 0), (0, BLOCK - RANK // fsdp_size)),
            ),
            jnp.full((fsdp_size, 1, BLOCK), square_part),
        ],
        axis=1,
    )
    small = jnp.pad(small, ((0, 0), (0, -(experts + 4) % 8), (0, 0))).reshape(-1, BLOCK)
    small = small + swap_tp(small)
    query_out, latent_out, expand_out, output_out, small_out, gate_out, up_out, down_out = (
        reduce_weights(
            query_grad.astype(bf16),
            latent_grad.astype(bf16),
            expand_grad.astype(bf16),
            output_grad.astype(bf16),
            small,
            gate_shared_grad,
            up_shared_grad,
            down_shared_grad.astype(bf16),
            blocks,
            6,
        )
    )
    return (
        small_out[experts + 3, 0] / (width * valid_total),
        activations,
        input_grad,
        small_out[experts],
        query_out,
        latent_out,
        small_out[experts + 2, : RANK // fsdp_size],
        expand_out,
        output_out,
        small_out[experts + 1],
        small_out[:experts].T,
        gate_out.astype(f32),
        up_out.astype(f32),
        down_out.astype(f32),
        expert_gate_grad[None],
        expert_up_grad[None],
        expert_down_grad[None],
    )


def slot_shards(
    inputs,
    teacher,
    valid_mask,
    prefix,
    routes,
    norm_gain,
    query_weight,
    latent_weight,
    latent_gain,
    expand_weight,
    output_weight,
    moe_gain,
    router_weight,
    shared_gate,
    shared_up,
    shared_down,
    expert_gate,
    expert_up,
    expert_down,
):
    f32 = jnp.float32
    bf16 = jnp.bfloat16
    tp_size = lax.axis_size("tp")
    fsdp_size = lax.axis_size("fsdp")
    local_heads = HEADS // tp_size
    (
        norm_gains,
        query_full,
        latent_full,
        latent_gains,
        expand_full,
        output_full,
        moe_gains,
        router_full,
        gate_full,
        up_full,
        down_full,
    ) = (
        lax.all_gather(norm_gain, "fsdp", axis=0, tiled=True),
        lax.all_gather(query_weight, "fsdp", axis=0, tiled=True),
        lax.all_gather(latent_weight, "fsdp", axis=0, tiled=True),
        lax.all_gather(latent_gain, "fsdp", axis=0, tiled=True),
        lax.all_gather(expand_weight, "fsdp", axis=0, tiled=True),
        lax.all_gather(output_weight, "fsdp", axis=1, tiled=True),
        lax.all_gather(moe_gain, "fsdp", axis=0, tiled=True),
        lax.all_gather(router_weight, "fsdp", axis=0, tiled=True),
        lax.all_gather(shared_gate, "fsdp", axis=0, tiled=True),
        lax.all_gather(shared_up, "fsdp", axis=0, tiled=True),
        lax.all_gather(shared_down, "fsdp", axis=1, tiled=True),
    )
    gathered = lax.all_gather(inputs, "tp", axis=0, tiled=True)
    seq_len = gathered.shape[0]
    width = gathered.shape[1]
    hidden = gathered.astype(f32)
    cosine, sine_part = rope_tables(seq_len, ROPE)
    inverse_in = lax.rsqrt(jnp.mean(hidden * hidden, axis=-1, keepdims=True) + EPSILON)
    normal_in = hidden * inverse_in
    norm_scale = norm_gains.astype(f32)
    normed = (normal_in * norm_scale).astype(bf16)
    query_lin = jnp.dot(normed, query_full, preferred_element_type=f32).reshape(
        seq_len, local_heads, NOPE + ROPE
    )
    queries = jnp.concatenate(
        [
            query_lin[..., :NOPE],
            rotate(query_lin[..., NOPE:], cosine[:, None, :], sine_part[:, None, :]),
        ],
        axis=-1,
    ).astype(bf16)
    latent_lin = jnp.dot(normed, latent_full, preferred_element_type=f32)
    latent_raw = latent_lin[:, :RANK]
    inverse_lat = lax.rsqrt(jnp.mean(latent_raw * latent_raw, axis=-1, keepdims=True) + EPSILON)
    latent_unit = latent_raw * inverse_lat
    latent_scale = latent_gains.astype(f32)
    latent = (latent_unit * latent_scale).astype(bf16)
    key_rope = rotate(latent_lin[:, RANK:], cosine, sine_part).astype(bf16)
    keys_values = (
        jnp.dot(latent, expand_full, preferred_element_type=f32)
        .astype(bf16)
        .reshape(seq_len, local_heads, NOPE + VDIM)
    )
    key_nope = keys_values[..., :NOPE]
    values = keys_values[..., NOPE:]
    query_nope = queries[..., :NOPE]
    query_rope = queries[..., NOPE:]
    score_scale = 1.0 / math.sqrt(NOPE + ROPE)
    position = jnp.arange(seq_len, dtype=jnp.int32)
    visible = (position[None, :] <= position[:, None]) | (position[None, :] < prefix[0])

    def scores_of():
        raw_scores = jnp.einsum("ihd,jhd->hij", query_nope, key_nope, preferred_element_type=f32)
        raw_scores = raw_scores + jnp.einsum(
            "ihd,jd->hij", query_rope, key_rope, preferred_element_type=f32
        )
        return jnp.where(visible[None], raw_scores * score_scale, MASKED)

    scores = scores_of()
    row_max = jnp.max(scores, axis=-1, keepdims=True)
    shifted = jnp.exp(scores - row_max)
    row_total = jnp.sum(shifted, axis=-1, keepdims=True)
    log_total = row_max + jnp.log(row_total)
    probs_low = (shifted / row_total).astype(bf16)
    heads_out = (
        jnp.einsum("hij,jhd->ihd", probs_low, values, preferred_element_type=f32)
        .astype(bf16)
        .reshape(seq_len, local_heads * VDIM)
    )
    attended = lax.psum(jnp.dot(heads_out, output_full, preferred_element_type=f32), "tp")
    middle = hidden + attended
    inverse_mid = lax.rsqrt(jnp.mean(middle * middle, axis=-1, keepdims=True) + EPSILON)
    normal_mid = middle * inverse_mid
    moe_scale = moe_gains.astype(f32)
    moe_in = (normal_mid * moe_scale).astype(bf16)
    logits = jnp.dot(moe_in, router_full, preferred_element_type=f32)
    logit_max = jnp.max(logits, axis=-1, keepdims=True)
    logit_exp = jnp.exp(logits - logit_max)
    router_probs = logit_exp / jnp.sum(logit_exp, axis=-1, keepdims=True)
    experts = router_full.shape[1]
    top_count = routes.shape[1]
    choose = routes[:, :, None] == jnp.arange(experts, dtype=jnp.int32)[None, None, :]
    gate_values = jnp.sum(jnp.where(choose, router_probs[:, None, :], 0.0), axis=-1)
    capacity = top_count * seq_len * 4 // (3 * experts)
    flat_routes = routes.reshape(seq_len * top_count)
    onehot = (flat_routes[:, None] == jnp.arange(experts, dtype=jnp.int32)[None, :]).astype(
        jnp.int32
    )
    earlier = jnp.cumsum(onehot, axis=0) - onehot
    slot_index = flat_routes * capacity + jnp.sum(earlier * onehot, axis=1)
    placed = jnp.arange(experts * capacity, dtype=jnp.int32)[:, None] == slot_index[None, :]
    dispatch = jnp.sum(
        placed.reshape(experts * capacity, seq_len, top_count).astype(f32), axis=2
    ).astype(bf16)
    gate_slot = jnp.sum(jnp.where(placed, gate_values.reshape(1, seq_len * top_count), 0.0), axis=1)

    def send_slots(slot_rows):
        return lax.all_to_all(slot_rows, "fsdp", split_axis=0, concat_axis=1, tiled=True)

    def return_slots(partials):
        return (
            lax.all_to_all(
                partials.astype(jnp.bfloat16), "fsdp", split_axis=1, concat_axis=0, tiled=True
            )
            .astype(partials.dtype)
            .reshape(experts * capacity, width)
        )

    expert_in = (
        jnp.dot(dispatch, moe_in, preferred_element_type=f32)
        .astype(bf16)
        .reshape(experts, capacity, width)
    )
    received = send_slots(expert_in)
    gate_act = jnp.einsum("ecd,edf->ecf", received, expert_gate, preferred_element_type=f32)
    up_act = jnp.einsum("ecd,edf->ecf", received, expert_up, preferred_element_type=f32)
    silu_gate, silu_slope = silu_parts(gate_act)
    expert_hidden = (silu_gate * up_act).astype(bf16)
    expert_out = jnp.einsum("ecf,efd->ecd", expert_hidden, expert_down, preferred_element_type=f32)
    returned = return_slots(expert_out)
    picked = jnp.take(returned, slot_index, axis=0).reshape(seq_len, top_count, width)
    routed = jnp.sum(gate_values[:, :, None] * picked, axis=1)
    gate_sh = jnp.dot(moe_in, gate_full, preferred_element_type=f32)
    up_sh = jnp.dot(moe_in, up_full, preferred_element_type=f32)
    silu_sh, slope_sh = silu_parts(gate_sh)
    shared_hidden = (silu_sh * up_sh).astype(bf16)
    moe_part = routed + jnp.dot(shared_hidden, down_full, preferred_element_type=f32)
    moe_out = lax.psum(moe_part.astype(jnp.bfloat16), "tp").astype(jnp.float32)
    activations = middle + moe_out
    mask_float = valid_mask.astype(f32)
    offset = activations - teacher.astype(f32)
    square_sum, valid_sum = lax.psum(
        (jnp.sum(mask_float[:, None] * offset * offset), jnp.sum(mask_float)), "fsdp"
    )
    valid_total = jnp.maximum(valid_sum, 1.0)
    loss_value = square_sum / (width * valid_total)
    grad_out = seq_len * fsdp_size / valid_total * mask_float[:, None] * offset
    grad_moe = grad_out.astype(bf16)
    down_shared_grad = jnp.einsum("tf,td->fd", shared_hidden, grad_moe, preferred_element_type=f32)
    grad_sh_hidden = jnp.einsum("td,fd->tf", grad_moe, down_full, preferred_element_type=f32)
    grad_gate_sh = (grad_sh_hidden * up_sh * slope_sh).astype(bf16)
    grad_up_sh = (grad_sh_hidden * silu_sh).astype(bf16)
    gate_shared_grad = jnp.einsum("td,tf->df", moe_in, grad_gate_sh, preferred_element_type=f32)
    up_shared_grad = jnp.einsum("td,tf->df", moe_in, grad_up_sh, preferred_element_type=f32)
    grad_moe_in = jnp.einsum("tf,df->td", grad_gate_sh, gate_full, preferred_element_type=f32)
    grad_moe_in = grad_moe_in + jnp.einsum(
        "tf,df->td", grad_up_sh, up_full, preferred_element_type=f32
    )
    grad_gates = jnp.sum(picked * grad_moe.astype(f32)[:, None, :], axis=-1)
    grad_slots = (
        (jnp.dot(dispatch, grad_moe, preferred_element_type=f32) * gate_slot[:, None])
        .astype(bf16)
        .reshape(experts, capacity, width)
    )
    grad_received = send_slots(grad_slots)
    expert_down_grad = jnp.einsum(
        "ecf,ecd->efd", expert_hidden, grad_received, preferred_element_type=f32
    )
    grad_expert_hidden = jnp.einsum(
        "ecd,efd->ecf", grad_received, expert_down, preferred_element_type=f32
    )
    grad_gate_act = (grad_expert_hidden * up_act * silu_slope).astype(bf16)
    grad_up_act = (grad_expert_hidden * silu_gate).astype(bf16)
    expert_gate_grad = jnp.einsum(
        "ecd,ecf->edf", received, grad_gate_act, preferred_element_type=f32
    )
    expert_up_grad = jnp.einsum("ecd,ecf->edf", received, grad_up_act, preferred_element_type=f32)
    grad_expert_in = jnp.einsum(
        "ecf,edf->ecd", grad_gate_act, expert_gate, preferred_element_type=f32
    )
    grad_expert_in = grad_expert_in + jnp.einsum(
        "ecf,edf->ecd", grad_up_act, expert_up, preferred_element_type=f32
    )
    grad_returned = return_slots(grad_expert_in)
    grad_moe_in = grad_moe_in + jnp.sum(
        jnp.take(grad_returned, slot_index, axis=0).reshape(seq_len, top_count, width), axis=1
    )
    grad_moe_in, grad_gates = (
        lax.psum(grad_moe_in.astype(jnp.bfloat16), "tp").astype(jnp.float32),
        lax.psum(grad_gates.astype(jnp.bfloat16), "tp").astype(jnp.float32),
    )
    grad_router_probs = jnp.sum(jnp.where(choose, grad_gates[:, :, None], 0.0), axis=1)
    grad_logits = router_probs * (
        grad_router_probs - jnp.sum(router_probs * grad_router_probs, axis=-1, keepdims=True)
    )
    router_grad = jnp.einsum(
        "td,te->de", moe_in.astype(f32), grad_logits, precision=HIGHEST, preferred_element_type=f32
    )
    grad_moe_in = grad_moe_in + jnp.einsum(
        "te,de->td",
        grad_logits,
        router_full.astype(f32),
        precision=HIGHEST,
        preferred_element_type=f32,
    )
    moe_gain_grad = jnp.sum(grad_moe_in * normal_mid, axis=0)
    grad_middle = grad_out + norm_back(grad_moe_in * moe_scale, normal_mid, inverse_mid)
    grad_attended = grad_middle.astype(bf16)
    output_grad = jnp.einsum("tf,td->fd", heads_out, grad_attended, preferred_element_type=f32)
    grad_heads = (
        jnp.einsum("td,fd->tf", grad_attended, output_full, preferred_element_type=f32)
        .astype(bf16)
        .reshape(seq_len, local_heads, VDIM)
    )
    attn_probs = jnp.exp(scores_of() - log_total)
    probs_again = attn_probs.astype(bf16)
    grad_probs = jnp.einsum("ihd,jhd->hij", grad_heads, values, preferred_element_type=f32)
    grad_values = jnp.einsum("hij,ihd->jhd", probs_again, grad_heads, preferred_element_type=f32)
    grad_scores = (
        attn_probs * (grad_probs - jnp.sum(attn_probs * grad_probs, axis=-1, keepdims=True))
    ).astype(bf16)
    grad_q_nope = (
        jnp.einsum("hij,jhd->ihd", grad_scores, key_nope, preferred_element_type=f32) * score_scale
    )
    grad_q_rope = (
        jnp.einsum("hij,jd->ihd", grad_scores, key_rope, preferred_element_type=f32) * score_scale
    )
    grad_keys = (
        jnp.einsum("hij,ihd->jhd", grad_scores, query_nope, preferred_element_type=f32)
        * score_scale
    )
    grad_key_rope = (
        jnp.einsum("hij,ihd->jd", grad_scores, query_rope, preferred_element_type=f32) * score_scale
    )
    grad_query = (
        jnp.concatenate(
            [grad_q_nope, unrotate(grad_q_rope, cosine[:, None, :], sine_part[:, None, :])], axis=-1
        )
        .astype(bf16)
        .reshape(seq_len, local_heads * (NOPE + ROPE))
    )
    query_grad = jnp.einsum("td,tq->dq", normed, grad_query, preferred_element_type=f32)
    grad_normed = jnp.einsum("tq,dq->td", grad_query, query_full, preferred_element_type=f32)
    grad_kv = (
        jnp.concatenate([grad_keys, grad_values], axis=-1)
        .astype(bf16)
        .reshape(seq_len, local_heads * (NOPE + VDIM))
    )
    expand_grad = jnp.einsum("tr,tq->rq", latent, grad_kv, preferred_element_type=f32)
    grad_latent = jnp.einsum("tq,rq->tr", grad_kv, expand_full, preferred_element_type=f32)
    grad_normed, grad_latent, grad_key_rope = (
        lax.psum(grad_normed.astype(jnp.bfloat16), "tp").astype(jnp.float32),
        lax.psum(grad_latent.astype(jnp.bfloat16), "tp").astype(jnp.float32),
        lax.psum(grad_key_rope.astype(jnp.bfloat16), "tp").astype(jnp.float32),
    )
    latent_gain_grad = jnp.sum(grad_latent * latent_unit, axis=0)
    grad_latent_raw = norm_back(grad_latent * latent_scale, latent_unit, inverse_lat)
    grad_latent_lin = jnp.concatenate(
        [grad_latent_raw, unrotate(grad_key_rope, cosine, sine_part)], axis=-1
    ).astype(bf16)
    latent_grad = jnp.einsum("td,tr->dr", normed, grad_latent_lin, preferred_element_type=f32)
    grad_normed = grad_normed + jnp.einsum(
        "tr,dr->td", grad_latent_lin, latent_full, preferred_element_type=f32
    )
    norm_gain_grad = jnp.sum(grad_normed * normal_in, axis=0)
    input_grad = grad_middle + norm_back(grad_normed * norm_scale, normal_in, inverse_in)
    (
        norm_out,
        query_out,
        latent_out,
        lgain_out,
        expand_out,
        output_out,
        mgain_out,
        router_out,
        gate_out,
        up_out,
        down_out,
    ) = (
        lax.psum_scatter(norm_gain_grad, "fsdp", scatter_dimension=0, tiled=True),
        lax.psum_scatter(query_grad, "fsdp", scatter_dimension=0, tiled=True),
        lax.psum_scatter(latent_grad, "fsdp", scatter_dimension=0, tiled=True),
        lax.psum_scatter(latent_gain_grad, "fsdp", scatter_dimension=0, tiled=True),
        lax.psum_scatter(expand_grad, "fsdp", scatter_dimension=0, tiled=True),
        lax.psum_scatter(output_grad, "fsdp", scatter_dimension=1, tiled=True),
        lax.psum_scatter(moe_gain_grad, "fsdp", scatter_dimension=0, tiled=True),
        lax.psum_scatter(router_grad, "fsdp", scatter_dimension=0, tiled=True),
        lax.psum_scatter(gate_shared_grad, "fsdp", scatter_dimension=0, tiled=True),
        lax.psum_scatter(up_shared_grad, "fsdp", scatter_dimension=0, tiled=True),
        lax.psum_scatter(down_shared_grad, "fsdp", scatter_dimension=1, tiled=True),
    )
    own_start = lax.axis_index("tp") * inputs.shape[0]
    own_activations = lax.dynamic_slice_in_dim(activations, own_start, inputs.shape[0], 0)
    own_input_grad = lax.dynamic_slice_in_dim(input_grad, own_start, inputs.shape[0], 0)
    return (
        loss_value,
        own_activations,
        own_input_grad,
        norm_out,
        query_out,
        latent_out,
        lgain_out,
        expand_out,
        output_out,
        mgain_out,
        router_out,
        gate_out,
        up_out,
        down_out,
        expert_gate_grad,
        expert_up_grad,
        expert_down_grad,
    )


def shards(*arrays):
    fsdp_size = lax.axis_size("fsdp")
    seq_len = arrays[4].shape[0]
    experts = arrays[12].shape[1]
    capacity = arrays[4].shape[1] * seq_len * 4 // (3 * experts)
    fits = fsdp_size * seq_len <= 2 * experts * capacity and fsdp_size == experts
    aligned = arrays[5].shape[0] == BLOCK and arrays[13].shape[1] % BLOCK == 0
    if fits and aligned and fsdp_size % 4 == 0:
        return token_shards(*arrays)
    return slot_shards(*arrays)


def solution(mesh):
    return jax.shard_map(
        shards,
        mesh=mesh,
        in_specs=(
            P(("fsdp", "tp"), None),
            P("fsdp", None),
            P("fsdp"),
            P("fsdp"),
            P("fsdp", None),
            P("fsdp"),
            P("fsdp", "tp"),
            P("fsdp", None),
            P("fsdp"),
            P("fsdp", "tp"),
            P("tp", "fsdp"),
            P("fsdp"),
            P("fsdp", None),
            P("fsdp", "tp"),
            P("fsdp", "tp"),
            P("tp", "fsdp"),
            P("fsdp", None, "tp"),
            P("fsdp", None, "tp"),
            P("fsdp", "tp", None),
        ),
        out_specs=(
            P(),
            P(("fsdp", "tp"), None),
            P(("fsdp", "tp"), None),
            P("fsdp"),
            P("fsdp", "tp"),
            P("fsdp", None),
            P("fsdp"),
            P("fsdp", "tp"),
            P("tp", "fsdp"),
            P("fsdp"),
            P("fsdp", None),
            P("fsdp", "tp"),
            P("fsdp", "tp"),
            P("tp", "fsdp"),
            P("fsdp", None, "tp"),
            P("fsdp", None, "tp"),
            P("fsdp", "tp", None),
        ),
        check_vma=False,
    )
```

```python
import functools
import math

import jax
import jax.numpy as jnp
from jax import lax
from jax.experimental import pallas as pl
from jax.experimental.pallas import tpu as pltpu
from jax.sharding import PartitionSpec as P

HEADS = 16
NOPE = 128
ROPE = 64
RANK = 512
VDIM = 128


EPSILON = 1e-06
HIGHEST = lax.Precision.HIGHEST
MASKED = -1e30


def rope_tables(length, dim_size):
    places = jnp.arange(length).astype(jnp.float32)
    exponent = jnp.arange(dim_size // 2).astype(jnp.float32) * (2.0 / dim_size)
    angles = places[:, None] * jnp.exp(exponent * -math.log(10000.0))[None, :]
    return (jnp.cos(angles), jnp.sin(angles))


def rotate(values, cosine, sine_part):
    half_width = values.shape[-1] // 2
    lower_half = values[..., :half_width]
    upper_half = values[..., half_width:]
    return jnp.concatenate(
        [
            lower_half * cosine - upper_half * sine_part,
            upper_half * cosine + lower_half * sine_part,
        ],
        axis=-1,
    )


def unrotate(gradient, cosine, sine_part):
    half_width = gradient.shape[-1] // 2
    lower_half = gradient[..., :half_width]
    upper_half = gradient[..., half_width:]
    return jnp.concatenate(
        [
            lower_half * cosine + upper_half * sine_part,
            upper_half * cosine - lower_half * sine_part,
        ],
        axis=-1,
    )


def silu_parts(gate_act):
    sigmoid_val = jax.nn.sigmoid(gate_act)
    return (gate_act * sigmoid_val, sigmoid_val * (1.0 + gate_act * (1.0 - sigmoid_val)))


def norm_back(grad_scaled, unit_rows, inverse):
    return inverse * (
        grad_scaled - unit_rows * jnp.mean(grad_scaled * unit_rows, axis=-1, keepdims=True)
    )


def swap_tp(value):
    return lax.ppermute(value, "tp", [(0, 1), (1, 0)])


def half_rows(value, which, rows):
    return lax.dynamic_slice_in_dim(value, which * rows, rows, 0)


def tp_scatter(partial, which, rows):
    other = half_rows(partial, 1 - which, rows).astype(jnp.bfloat16)
    return half_rows(partial, which, rows) + swap_tp(other).astype(jnp.float32)


def tp_sum(partial):
    low_partial = partial.astype(jnp.bfloat16)
    return low_partial.astype(jnp.float32) + swap_tp(low_partial).astype(jnp.float32)


def tp_gather(own, which):
    other = swap_tp(own)
    first = jnp.where(which == 0, own, other)
    second = jnp.where(which == 0, other, own)
    return jnp.concatenate([first, second], axis=0)


MESH = pl.DeviceIdType.MESH
CROSS = ("x", "y", "up", "down")
BLOCK = 128


def both(first, second):
    if first is None:
        return second
    if second is None:
        return first
    return jnp.logical_and(first, second)


def under(condition, body):
    if condition is None:
        body()
    else:
        pl.when(condition)(body)


class Grid:
    def __init__(self, fsdp_size, dims, tie=-1):
        self.tie = tie
        index = lax.axis_index("fsdp")
        self.core = lax.rem(index, 2)
        self.y = lax.rem(lax.div(index, 2), 2)
        self.z = lax.div(index, 4)
        self.x = lax.axis_index("tp")
        self.depth = fsdp_size // 4
        self.dims = dims
        self.crosses = CROSS if "x" in dims else CROSS[1:]
        self.chips = self.depth * 2 * (2 if "x" in dims else 1)

    def device(self, x, y, z, core):
        return {"fsdp": z * 4 + y * 2 + core, "tp": x}

    def chip(self, x, y, z):
        return (z * 2 + y) * 2 + x if "x" in self.dims else z * 2 + y

    def here(self):
        return self.x, self.y, self.z

    def partner(self):
        return self.device(self.x, self.y, self.z, 1 - self.core)

    def neighbour(self, cross):
        if cross == "x":
            return (1 - self.x, self.y, self.z), None
        if cross == "y":
            return (self.x, 1 - self.y, self.z), None
        if cross == "up":
            return (self.x, self.y, self.z + 1), self.z + 1 < self.depth
        return (self.x, self.y, self.z - 1), self.z >= 1

    def level(self, rank):
        inner = jnp.logical_or(self.z == 1, self.z == 2)
        rank = jnp.where(jnp.logical_and(inner, rank >= 2), 5 - rank, rank)
        high, low = lax.div(self.z, 2), lax.rem(self.z, 2)
        far, near = lax.div(rank, 2), lax.rem(rank, 2)
        return 2 * (high + far - 2 * high * far) + (low + near - 2 * low * near)

    def entry(self, number):
        steps = (0, 1) if "x" in self.dims else (0,)
        found = [(r, dy, dx) for r in range(self.depth) for dy in (0, 1) for dx in steps]
        codes = [4 * e[0] + 2 * e[1] + e[2] for e in sorted(found, key=lambda e: (sum(e), self.tie * e[0]))]
        code = jnp.int32(0) + (codes[number] if isinstance(number, int) else 0)
        if not isinstance(number, int):
            for at, value in enumerate(codes):
                code = jnp.where(number == at, value, code)
        dx, dy = lax.rem(code, 2), lax.rem(lax.div(code, 2), 2)
        x, y = self.x + dx - 2 * self.x * dx, self.y + dy - 2 * self.y * dy
        return x, y, self.level(lax.div(code, 4))

    def children(self, order, chip):
        zero = dict(x=chip[0] == self.x, y=chip[1] == self.y, z=chip[2] == self.z)
        found, rest = [], None
        for dim in reversed(order):
            if dim == "z":
                found.append(("up", both(rest, (chip[2] <= self.z) & (self.z + 1 < self.depth))))
                found.append(("down", both(rest, (chip[2] >= self.z) & (self.z >= 1))))
            else:
                found.append((dim, both(rest, zero[dim])))
            rest = both(rest, zero[dim])
        return found

    def parent(self, order, chip):
        zero = dict(x=chip[0] == self.x, y=chip[1] == self.y, z=chip[2] == self.z)
        rest, turned = None, {}
        for dim in reversed(order):
            turned[dim] = both(rest, jnp.logical_not(zero[dim]))
            rest = both(rest, zero[dim])
        x = jnp.where(turned["x"], 1 - self.x, self.x) if "x" in order else self.x
        y = jnp.where(turned["y"], 1 - self.y, self.y)
        above = chip[2] > self.z
        z = jnp.where(turned["z"], jnp.where(above, self.z + 1, self.z - 1), self.z)
        side = jnp.where(above, self.crosses.index("down"), self.crosses.index("up"))
        side = jnp.where(turned["y"], self.crosses.index("y"), side)
        if "x" in order:
            side = jnp.where(turned["x"], self.crosses.index("x"), side)
        return (x, y, z), side

    def greet(self):
        barrier = pltpu.get_barrier_semaphore()
        pl.semaphore_signal(barrier, inc=1, device_id=self.partner(), device_id_type=MESH)
        count = 1
        for cross in self.crosses:
            chip, exists = self.neighbour(cross)

            def send(chip=chip):
                there = self.device(*chip, self.core)
                pl.semaphore_signal(barrier, inc=1, device_id=there, device_id_type=MESH)

            under(exists, send)
            count = count + (1 if exists is None else jnp.where(exists, 1, 0))
        pl.semaphore_wait(barrier, count)

    def greet_plane(self):
        barrier = pltpu.get_barrier_semaphore()
        size = self.depth * 4
        me = lax.axis_index("fsdp")

        def send(step, carry):
            there = {"fsdp": lax.rem(me + step, size), "tp": self.x}
            pl.semaphore_signal(barrier, inc=1, device_id=there, device_id_type=MESH)
            return carry

        lax.fori_loop(1, size, send, 0)
        pl.semaphore_wait(barrier, size - 1)


class Exchange:
    def __init__(self, fsdp_size, tp, blocks, sources, targets, cut, to_owner, send_sem, recv_sem, own_sem):
        self.size, self.tp, self.blocks = fsdp_size, tp, blocks
        self.sources, self.targets, self.cut, self.to_owner = sources, targets, cut, to_owner
        self.send_sem, self.recv_sem, self.own_sem = send_sem, recv_sem, own_sem
        self.me = lax.axis_index("fsdp")
        self.block = lax.div(self.me * blocks + fsdp_size - 1, fsdp_size)
        self.owns = jnp.logical_and(
            self.block < blocks, lax.div(self.block * fsdp_size, blocks) == self.me
        )

    def remote(self, array, block, other, there, send, recv):
        source, target = self.cut[array](self.sources[array], self.targets[array], block, other)
        return pltpu.make_async_remote_copy(
            src_ref=source,
            dst_ref=target,
            send_sem=self.send_sem.at[array, send],
            recv_sem=self.recv_sem.at[array, recv],
            device_id={"fsdp": there, "tp": self.tp},
            device_id_type=MESH,
        )

    def local(self, array, block):
        source, target = self.cut[array](self.sources[array], self.targets[array], block, self.me)
        return pltpu.make_async_copy(source, target, self.own_sem.at[array])

    def by_block(self, act, act_local, low, high):
        def one(number, carry):
            block = lax.rem(number + lax.div(self.me * self.blocks, self.size), self.blocks)
            owner = lax.div(block * self.size, self.blocks)
            for array in range(len(self.sources)):
                if self.to_owner:
                    copy = self.remote(array, block, self.me, owner, block, self.me)
                else:
                    copy = self.remote(array, block, self.me, owner, 0, block)
                pl.when(self.me != owner)(getattr(copy, act))
                if act_local:
                    pl.when(self.me == owner)(getattr(self.local(array, block), act_local))
            return carry

        lax.fori_loop(low, high, one, 0)

    def by_device(self, act, act_local, low, high):
        def one(number, carry):
            other = lax.rem(self.me + number, self.size)
            for array in range(len(self.sources)):
                if self.to_owner:
                    copy = self.remote(array, self.block, other, other, 0, other)
                else:
                    copy = self.remote(array, self.block, other, other, other, self.block)
                pl.when(self.me != other)(getattr(copy, act))
                if act_local:
                    pl.when(self.me == other)(getattr(self.local(array, self.block), act_local))
            return carry

        def every():
            lax.fori_loop(low, high, one, 0)

        pl.when(self.owns)(every)

    def start(self, step, steps):
        total = self.blocks if self.to_owner else self.size
        low, high = lax.div(step * total, steps), lax.div((step + 1) * total, steps)
        (self.by_block if self.to_owner else self.by_device)("start", "start", low, high)

    def finish(self):
        if self.to_owner:
            self.by_device("wait_recv", None, 0, self.size)
            self.by_block("wait_send", "wait", 0, self.blocks)
        else:
            self.by_block("wait_recv", None, 0, self.blocks)
            self.by_device("wait_send", "wait", 0, self.size)


def exchange_sems(fsdp_size, arrays):
    dma = pltpu.SemaphoreType.DMA
    return [dma((arrays, fsdp_size)), dma((arrays, fsdp_size)), dma((arrays,))] if arrays else []


def gather_kernel(fsdp_size, pieces, places, count, blocks, cut, *refs):
    moved = len(cut)
    shards, sources = refs[:count], refs[count : count + moved]
    refs = refs[count + moved :]
    outs, targets = refs[:count], refs[count : count + moved]
    send_sem, recv_sem, pair_send, pair_recv, own_sem = refs[count + moved : count + moved + 5]
    grid = Grid(fsdp_size, "zy")
    exchange = Exchange(
        fsdp_size, grid.x, blocks, sources, targets, cut, True, *refs[count + moved + 5 :]
    )

    def target(piece, chip, core):
        array, first, rows, _ = pieces[piece]
        return places[array](outs[array], chip, core, first, rows)

    def source(piece, chip, own):
        array, first, rows, _ = pieces[piece]
        return shards[array].at[pl.ds(first, rows)] if own else target(piece, chip, grid.core)

    def hops(piece, chip, own):
        index, found = grid.chip(*chip), []
        for cross, wanted in grid.children(pieces[piece][3], chip):
            there, _ = grid.neighbour(cross)
            copy = pltpu.make_async_remote_copy(
                src_ref=source(piece, chip, own),
                dst_ref=target(piece, chip, grid.core),
                send_sem=send_sem.at[piece, index, grid.crosses.index(cross)],
                recv_sem=recv_sem.at[piece, index],
                device_id=grid.device(*there, grid.core),
                device_id_type=MESH,
            )
            found.append((wanted, copy))
        return found

    def pair(piece, chip, core, own=False, landing=False):
        index = grid.chip(*chip)
        return pltpu.make_async_remote_copy(
            src_ref=source(piece, chip, own),
            dst_ref=target(piece, chip, core),
            send_sem=pair_send.at[piece, index],
            recv_sem=(recv_sem if landing else pair_recv).at[piece, index],
            device_id=grid.partner(),
            device_id_type=MESH,
        )

    own_copies = [
        pltpu.make_async_copy(
            source(piece, grid.here(), True), target(piece, grid.here(), grid.core), own_sem.at[piece]
        )
        for piece in range(len(pieces))
    ]
    grid.greet_plane()

    def relay(chip, own):
        for piece in range(len(pieces)):
            if not own:
                pair(piece, chip, grid.core, landing=True).wait_recv()
            for wanted, copy in hops(piece, chip, own):
                under(wanted, copy.start)
            pair(piece, chip, grid.core, own).start()

    relay(grid.here(), True)
    for copy in own_copies:
        copy.start()

    def step(number, carry):
        relay(grid.entry(number), False)
        exchange.start(number - 1, grid.chips - 1)
        return carry

    lax.fori_loop(1, grid.chips, step, 0)

    def finish(number, carry):
        chip = grid.entry(number)
        for piece in range(len(pieces)):
            for wanted, copy in hops(piece, chip, False):
                under(wanted, copy.wait_send)
            pair(piece, chip, grid.core).wait_send()
            pair(piece, chip, 1 - grid.core).wait_recv()
        return carry

    lax.fori_loop(0, grid.chips, finish, 0)
    for copy in own_copies:
        copy.wait()
    exchange.finish()


def gather_call(fsdp_size, pieces, places, shards, shapes, collective_id, blocks, cut, sources, targets):
    count, chips = len(shards), fsdp_size // 2
    dma = pltpu.SemaphoreType.DMA
    moved = sum(s.size * s.dtype.itemsize for s in shapes)
    return pl.pallas_call(
        functools.partial(gather_kernel, fsdp_size, pieces, places, count, blocks, cut),
        out_shape=tuple(shapes) + tuple(targets),
        in_specs=[pl.BlockSpec(memory_space=pltpu.VMEM)] * count
        + [pl.BlockSpec(memory_space=pl.ANY)] * len(sources),
        out_specs=tuple([pl.BlockSpec(memory_space=pl.ANY)] * (count + len(targets))),
        scratch_shapes=[
            dma((len(pieces), chips, 4)),
            dma((len(pieces), chips)),
            dma((len(pieces), chips)),
            dma((len(pieces), chips)),
            dma((len(pieces),)),
            *exchange_sems(fsdp_size, len(sources)),
        ],
        compiler_params=pltpu.CompilerParams(collective_id=collective_id, has_side_effects=True),
        cost_estimate=pl.CostEstimate(flops=0, bytes_accessed=8 * moved, transcendentals=0),
    )(*shards, *sources)


def reduce_kernel(fsdp_size, dims, pieces, places, count, blocks, cut, side, *refs):
    moved, taken = len(cut), side.inputs if side else 0
    partials, sources = refs[:count], refs[count : count + moved]
    side_refs = refs[count + moved : count + moved + taken]
    refs = refs[count + moved + taken :]
    outs, targets = refs[:count], refs[count : count + moved]
    refs = refs[count + moved :]
    if side:
        side_refs, refs = side_refs + refs[: side.outputs], refs[side.outputs :]
    held, other, landed = (refs[i * count : (1 + i) * count] for i in range(3))
    send_sem, recv_sem, load_sem, pair_send, pair_recv = refs[3 * count : 3 * count + 5]
    refs = refs[3 * count + 5 :]
    grid = Grid(fsdp_size, dims)
    ways = len(grid.crosses)
    empty = grid.chips * ways
    exchange, job = None, None
    if moved:
        exchange = Exchange(fsdp_size, grid.x, blocks, sources, targets, cut, False, *refs[:3])
        refs = refs[3:]
    if side:
        job = side.make(*side_refs, *refs)

    def load(array, chip):
        index = grid.chip(*chip)
        return pltpu.make_async_copy(
            places[array](partials[array], chip, grid.core),
            held[array].at[index],
            load_sem.at[array, index],
        )

    def pair(array, chip):
        index = grid.chip(*chip)
        return pltpu.make_async_remote_copy(
            src_ref=places[array](partials[array], chip, 1 - grid.core),
            dst_ref=other[array].at[index],
            send_sem=pair_send.at[array, index],
            recv_sem=pair_recv.at[array, index],
            device_id=grid.partner(),
            device_id_type=MESH,
        )

    def hop(piece, chip, there, side_seen):
        array, first, rows, _ = pieces[piece]
        index = grid.chip(*chip)
        slot = index * ways + side_seen
        return pltpu.make_async_remote_copy(
            src_ref=held[array].at[index, pl.ds(first, rows)],
            dst_ref=landed[array].at[slot, pl.ds(first, rows)],
            send_sem=send_sem.at[piece, index],
            recv_sem=recv_sem.at[piece, slot],
            device_id=grid.device(*there, grid.core),
            device_id_type=MESH,
        )

    def add_up(piece, chip, root):
        array, first, rows, order = pieces[piece]
        index, slots, some = grid.chip(*chip), [], grid.z < 0
        for cross, wanted in grid.children(order, chip):
            way = grid.crosses.index(cross)
            under(wanted, hop(piece, chip, grid.here(), way).wait_recv)
            slot = index * ways + way
            slots.append(slot if wanted is None else jnp.where(wanted, slot, empty))
            some = None if wanted is None or some is None else jnp.logical_or(some, wanted)
        tile = 16 if rows % 16 == 0 else rows

        def add_all(used):
            def add(i, carry):
                span = pl.ds(pl.multiple_of(first + i * tile, tile), tile)
                total = held[array][index, span].astype(jnp.float32)
                total += other[array][index, span].astype(jnp.float32)
                for slot in used:
                    total += landed[array][slot, span].astype(jnp.float32)
                if root:
                    outs[array][span] = total
                else:
                    held[array][index, span] = total.astype(held[array].dtype)
                return carry

            lax.fori_loop(0, rows // tile, add, 0)

        if root or some is None:
            add_all(slots)
        else:
            pl.when(some)(lambda: add_all(slots))
            pl.when(jnp.logical_not(some))(lambda: add_all([]))

    def fetched(array, chip):
        load(array, chip).wait()
        pair(array, chip).wait_recv()

    firsts = [min(p for p, piece in enumerate(pieces) if piece[0] == a) for a in range(count)]
    for array in range(count):
        landed[array][empty] = jnp.zeros(landed[array].shape[1:], landed[array].dtype)
    if moved:
        grid.greet_plane()
    else:
        grid.greet()
    last = grid.chips - 1

    def begin(number, carry):
        chip = grid.entry(last - number)
        for array in range(count):
            load(array, chip).start()
            pair(array, chip).start()
        return carry

    lax.fori_loop(0, grid.chips, begin, 0)
    if job:
        job.begin()

    def step(number, carry):
        chip = grid.entry(last - number)
        for piece in range(len(pieces)):
            if piece in firsts:
                fetched(pieces[piece][0], chip)
            add_up(piece, chip, False)
            hop(piece, chip, *grid.parent(pieces[piece][3], chip)).start()
            if job:
                job.tick(number, piece)
        if exchange:
            exchange.start(number, last)
        return carry

    lax.fori_loop(0, last, step, 0)
    if job:
        job.finish()
    for piece in range(len(pieces)):
        if piece in firsts:
            fetched(pieces[piece][0], grid.here())
        add_up(piece, grid.here(), True)

    def finish(number, carry):
        chip = grid.entry(last - number)
        for array in range(count):
            pair(array, chip).wait_send()

        def sent():
            for piece in range(len(pieces)):
                hop(piece, chip, *grid.parent(pieces[piece][3], chip)).wait_send()

        pl.when(number < last)(sent)
        return carry

    lax.fori_loop(0, grid.chips, finish, 0)
    if exchange:
        exchange.finish()


def reduce_call(
    fsdp_size,
    dims,
    pieces,
    places,
    partials,
    shapes,
    collective_id,
    blocks=0,
    cut=(),
    sources=(),
    targets=(),
    side=None,
    extra=(),
):
    count = len(partials)
    ways = 4 if "x" in dims else 3
    chips = fsdp_size // 2 * (2 if "x" in dims else 1)
    dma = pltpu.SemaphoreType.DMA
    held = [pltpu.VMEM((chips, *s), p.dtype) for s, p in zip(shapes, partials)]
    landed = [pltpu.VMEM((chips * ways + 1, *s), p.dtype) for s, p in zip(shapes, partials)]
    moved = sum(p.size * p.dtype.itemsize for p in partials)
    side_outs = tuple(side.shapes) if side else ()
    return pl.pallas_call(
        functools.partial(reduce_kernel, fsdp_size, dims, pieces, places, count, blocks, cut, side),
        out_shape=tuple(jax.ShapeDtypeStruct(s, jnp.float32) for s in shapes)
        + tuple(targets)
        + side_outs,
        in_specs=[pl.BlockSpec(memory_space=pl.ANY)] * (count + len(sources) + len(extra)),
        out_specs=tuple(
            [pl.BlockSpec(memory_space=pltpu.VMEM)] * count
            + [pl.BlockSpec(memory_space=pl.ANY)] * (len(targets) + len(side_outs))
        ),
        scratch_shapes=[
            *held,
            *held,
            *landed,
            dma((len(pieces), chips)),
            dma((len(pieces), chips * ways)),
            dma((count, chips)),
            dma((count, chips)),
            dma((count, chips)),
            *exchange_sems(fsdp_size, len(sources)),
            *(side.scratch if side else ()),
        ],
        compiler_params=pltpu.CompilerParams(
            collective_id=collective_id, has_side_effects=True, vmem_limit_bytes=67043328
        ),
        cost_estimate=pl.CostEstimate(flops=0, bytes_accessed=16 * moved, transcendentals=0),
    )(*partials, *sources, *extra)


def token_row(chip, core, rows):
    x, y, z = chip
    return ((z * 4 + y * 2 + core) * 2 + x) * rows


def reduce_tokens(partials, collective_id):
    fsdp_size = lax.axis_size("fsdp")
    rows = partials[0].shape[0] // (2 * fsdp_size)
    unit = rows // 4

    def place(ref, chip, core):
        return ref.at[pl.ds(pl.multiple_of(token_row(chip, core, rows), 16), rows)]

    pieces = [(0, at * unit, unit, order) for at, order in enumerate(("xyz", "zyx", "zxy", "zyx"))]
    pieces += [(array, 0, rows, "zyx") for array in range(1, len(partials))]
    shapes = [(rows, p.shape[1]) for p in partials]
    return reduce_call(
        fsdp_size, "xyz", pieces, [place] * len(partials), partials, shapes, collective_id
    )


def plane_row(chip, core):
    return chip[2] * 4 + chip[1] * 2 + core


def row_place(rows):
    def place(ref, chip, core, first=0, count=rows):
        return ref.at[pl.ds(pl.multiple_of(plane_row(chip, core) * rows + first, 8), count)]

    return place


def column_place(columns, rows):
    def place(ref, chip, core, first=0, count=rows):
        start = pl.multiple_of(plane_row(chip, core) * columns, 128)
        return ref.at[pl.ds(first, count), pl.ds(start, columns)]

    return place


def weight_pieces(query, latent, expand, output, small):
    return [
        (4, 0, small, "zy"),
        (0, 0, query // 2, "zy"),
        (1, 0, latent, "zy"),
        (0, query // 2, query // 2, "zy"),
        (2, 0, expand, "yz"),
        (3, 0, output // 2, "zy"),
        (3, output // 2, output // 2, "zy"),
    ]


def block_span(block):
    return pl.ds(pl.multiple_of(block * BLOCK, BLOCK), BLOCK)


def cut_columns(rows):
    def to_owner(source, target, block, other):
        there = pl.ds(pl.multiple_of(other * rows, rows), rows)
        return source.at[:, block_span(block)], target.at[there]

    def from_owner(source, target, block, other):
        there = pl.ds(pl.multiple_of(other * rows, rows), rows)
        return source.at[there], target.at[:, block_span(block)]

    return to_owner, from_owner


def cut_rows(columns):
    def to_owner(source, target, block, other):
        there = pl.ds(pl.multiple_of(other * columns, columns), columns)
        return source.at[block_span(block)], target.at[:, there]

    def from_owner(source, target, block, other):
        there = pl.ds(pl.multiple_of(other * columns, columns), columns)
        return source.at[:, there], target.at[block_span(block)]

    return to_owner, from_owner


def gather_weights(query, latent, expand, output, small, gate, up, down, collective_id):
    size = lax.axis_size("fsdp")
    shards = [query, latent, expand, output, small]
    places = [row_place(query.shape[0]), row_place(latent.shape[0]), row_place(expand.shape[0])]
    places += [column_place(output.shape[1], output.shape[0]), row_place(small.shape[0])]
    shapes = [
        jax.ShapeDtypeStruct((s.shape[0] * size, s.shape[1]), s.dtype) for s in shards
    ]
    shapes[3] = jax.ShapeDtypeStruct((output.shape[0], output.shape[1] * size), output.dtype)
    columns, rows = cut_columns(gate.shape[0]), cut_rows(down.shape[1])
    tall = jax.ShapeDtypeStruct((gate.shape[0] * size, BLOCK), gate.dtype)
    flat = jax.ShapeDtypeStruct((BLOCK, down.shape[1] * size), down.dtype)
    return gather_call(
        size,
        weight_pieces(*[s.shape[0] for s in shards]),
        places,
        shards,
        shapes,
        collective_id,
        gate.shape[1] // BLOCK,
        (columns[0], columns[0], rows[0]),
        [gate, up, down],
        [tall, tall, flat],
    )


def reduce_weights(query, latent, expand, output, small, gate, up, down, blocks, collective_id):
    size = lax.axis_size("fsdp")
    partials = [query, latent, expand, output, small]
    shapes = [(p.shape[0] // size, p.shape[1]) for p in partials]
    shapes[3] = (output.shape[0], output.shape[1] // size)
    places = [row_place(shapes[i][0]) for i in range(5)]
    places[3] = column_place(shapes[3][1], shapes[3][0])
    columns, rows = cut_columns(gate.shape[0] // size), cut_rows(down.shape[1] // size)
    wide = jax.ShapeDtypeStruct((gate.shape[0] // size, blocks * BLOCK), gate.dtype)
    long = jax.ShapeDtypeStruct((blocks * BLOCK, down.shape[1] // size), down.dtype)
    return reduce_call(
        size,
        "zy",
        weight_pieces(*[s[0] for s in shapes]),
        places,
        partials,
        shapes,
        collective_id,
        blocks,
        (columns[1], columns[1], rows[1]),
        [gate, up, down],
        [wide, wide, long],
    )


class Spread:
    ORDERS = ("xyz", "zyx", "zxy", "zyx")
    LEAD = 3

    def __init__(self, fsdp_size, own, room, sems):
        self.grid = Grid(fsdp_size, "xyz", 1)
        self.own, self.room = own, room
        self.rows = own.shape[0]
        self.part = self.rows // len(self.ORDERS)
        self.send_sem, self.recv_sem, self.pair_send, self.pair_recv = sems
        self.units = fsdp_size // 2

    def unit(self, step):
        grid = self.grid
        flip = lax.rem(step, 2)
        return grid.y + flip - 2 * grid.y * flip, grid.level(lax.div(step, 2))

    def span(self, chip, piece):
        start = token_row(chip, self.grid.core, self.rows) + piece * self.part
        return self.room.at[pl.ds(pl.multiple_of(start, self.part), self.part)]

    def copies(self, chip, piece, own=False):
        grid, found = self.grid, []
        index, here = grid.chip(*chip), self.span(chip, piece)
        source = self.own.at[pl.ds(piece * self.part, self.part)] if own else here
        for cross, wanted in grid.children(self.ORDERS[piece], chip):
            there, _ = grid.neighbour(cross)
            copy = pltpu.make_async_remote_copy(
                src_ref=source,
                dst_ref=here,
                send_sem=self.send_sem.at[piece, index, grid.crosses.index(cross)],
                recv_sem=self.recv_sem.at[piece, index],
                device_id=grid.device(*there, grid.core),
                device_id_type=MESH,
            )
            found.append((wanted, copy))
        return found

    def pair(self, chip, piece, own=False, landing=False):
        grid = self.grid
        index, here = grid.chip(*chip), self.span(chip, piece)
        return pltpu.make_async_remote_copy(
            src_ref=self.own.at[pl.ds(piece * self.part, self.part)] if own else here,
            dst_ref=here,
            send_sem=self.pair_send.at[piece, index],
            recv_sem=(self.recv_sem if landing else self.pair_recv).at[piece, index],
            device_id=grid.partner(),
            device_id_type=MESH,
        )

    def relay(self, chip, piece, own=False):
        if not own:
            self.pair(chip, piece, landing=True).wait_recv()
        for wanted, copy in self.copies(chip, piece, own):
            under(wanted, copy.start)
        self.pair(chip, piece, own).start()

    def begin(self):
        grid = self.grid
        grid.greet()
        for piece in range(len(self.ORDERS)):
            self.relay(grid.here(), piece, own=True)
        start = token_row(grid.here(), grid.core, self.rows)
        self.room[pl.ds(pl.multiple_of(start, self.rows), self.rows)] = self.own[...]

        def early(number, carry):
            chip = grid.entry(number)
            for piece in range(len(self.ORDERS)):
                self.relay(chip, piece)
            return carry

        lax.fori_loop(1, self.LEAD, early, 0)

    def ahead(self, step):
        return [self.grid.entry(self.LEAD + 2 * step + one) for one in (0, 1)]

    def tick(self, step, chips, number):
        pieces = len(self.ORDERS)
        late = self.LEAD + 2 * step + number // pieces
        chip = chips[number // pieces]
        pl.when(late < 2 * self.units)(lambda: self.relay(chip, number % pieces))

    def arrived(self, step):
        y, z = self.unit(step)
        for x in (0, 1):
            for piece in range(len(self.ORDERS)):
                self.pair((x, y, z), piece).wait_recv()

    def drain(self):
        def finish(number, carry):
            chip = self.grid.entry(number)
            for piece in range(len(self.ORDERS)):
                for wanted, copy in self.copies(chip, piece):
                    under(wanted, copy.wait_send)
                self.pair(chip, piece).wait_send()
            return carry

        lax.fori_loop(0, 2 * self.units, finish, 0)


def spread_sems(fsdp_size):
    dma = pltpu.SemaphoreType.DMA
    return [dma((4, fsdp_size, 4)), dma((4, fsdp_size)), dma((4, fsdp_size)), dma((4, fsdp_size))]


class Stage:
    def __init__(self, buffers, results, sems):
        self.buffers, self.results, self.sems = buffers, results, sems

    def copy(self, number, step, unit):
        buffer = self.buffers[number]
        rows = buffer.shape[1]
        slot = lax.rem(step, 2)
        there = self.results[number].at[pl.ds(pl.multiple_of(unit * rows, rows), rows)]
        return pltpu.make_async_copy(buffer.at[slot], there, self.sems.at[number, slot])

    def reuse(self, step):
        def wait():
            for number in range(len(self.buffers)):
                self.copy(number, step, 0).wait()

        pl.when(step >= 2)(wait)

    def put(self, number, step, unit):
        self.copy(number, step, unit).start()

    def finish(self, steps):
        for step in (steps - 2, steps - 1):
            for number in range(len(self.buffers)):
                self.copy(number, step, 0).wait()


def dot(left, right):
    return jnp.dot(left, right, preferred_element_type=jnp.float32)


def dot_nt(left, right):
    return lax.dot_general(
        left, right, (((1,), (1,)), ((), ())), preferred_element_type=jnp.float32
    )


def dispatch_of(place_ref, sequence, capacity, seq_len):
    row = place_ref[pl.ds(sequence, 1), :]
    slot = lax.broadcasted_iota(jnp.int32, (capacity, seq_len), 0)
    return jnp.where(slot == row, 1.0, 0.0)


def forward_kernel(
    fsdp_size,
    experts,
    capacity,
    own,
    place_ref,
    gate_hbm,
    up_hbm,
    down_hbm,
    wide_hbm,
    block_hbm,
    tokens_out,
    received_out,
    gate_out,
    up_out,
    hidden_out,
    weight_out,
    shared_out,
    sh_out,
    part_out,
    room,
    picks,
    packs,
    chances,
    tall,
    received,
    gate_act,
    up_act,
    hidden,
    weight,
    shared,
    sh_act,
    part,
    gate_ref,
    up_ref,
    down_ref,
    wide_ref,
    block_ref,
    weight_sem,
    stage_sem,
    room_sem,
    *sems,
):
    f32, bf16 = jnp.float32, jnp.bfloat16
    seq_len = place_ref.shape[1]
    spread = Spread(fsdp_size, own, room, sems)
    expert = lax.axis_index("fsdp")
    stage = Stage(
        [received, gate_act, up_act, hidden, weight, shared, sh_act, part],
        [received_out, gate_out, up_out, hidden_out, weight_out, shared_out, sh_out, part_out],
        stage_sem,
    )
    lanes = lax.broadcasted_iota(jnp.int32, (2 * seq_len, BLOCK), 1)

    def tokens_copy(unit):
        span = pl.ds(pl.multiple_of(unit * 2 * seq_len, 2 * seq_len), 2 * seq_len)
        return pltpu.make_async_copy(room.at[span], tokens_out.at[span], room_sem.at[unit])

    weights = [
        pltpu.make_async_copy(source, target, weight_sem.at[number])
        for number, (source, target) in enumerate([(gate_hbm, gate_ref), (up_hbm, up_ref), (down_hbm, down_ref), (wide_hbm, wide_ref), (block_hbm, block_ref)])
    ]
    for copy in weights:
        copy.start()
    spread.begin()
    for copy in weights:
        copy.wait()
    for one in (0, 1):
        tall[one, capacity:] = block_ref[...]

    def body(step, carry):
        slot = lax.rem(step, 2)
        y, z = spread.unit(step)
        unit = z * 2 + y
        chips = spread.ahead(step)
        spread.arrived(step)
        tokens_copy(unit).start()
        stage.reuse(step)
        rows = [
            pl.ds(pl.multiple_of((2 * unit + one) * seq_len, seq_len), seq_len) for one in (0, 1)
        ]
        slots = [pl.ds(one * capacity, capacity) for one in (0, 1)]
        own_rows = [pl.ds(one * seq_len, seq_len) for one in (0, 1)]
        spread.tick(step, chips, 0)
        for one in (0, 1):
            pick = dispatch_of(place_ref, 2 * unit + one, capacity, seq_len)
            picks[one] = pick.astype(bf16)
            packs[one, :, :capacity] = jnp.transpose(pick).astype(bf16)
            received[slot, slots[one]] = dot(picks[one], room[rows[one]]).astype(bf16)
        stage.put(0, step, unit)
        spread.tick(step, chips, 1)
        both_rows = pl.ds(pl.multiple_of(unit * 2 * seq_len, 2 * seq_len), 2 * seq_len)
        wide = dot(room[both_rows], wide_ref[...])
        shared[slot] = wide[:, : 2 * BLOCK]
        gate_sh, up_sh = wide[:, :BLOCK], wide[:, BLOCK : 2 * BLOCK]
        act = (silu_parts(gate_sh)[0] * up_sh).astype(bf16)
        sh_act[slot] = act
        for one in (0, 1):
            packs[one, :, capacity:] = act[one * seq_len : (one + 1) * seq_len]
        logits = jnp.where(lanes < experts, wide[:, 2 * BLOCK :], MASKED)
        logit_exp = jnp.exp(logits - jnp.max(logits, axis=1, keepdims=True))
        chance = jnp.sum(jnp.where(lanes == expert, logit_exp, 0.0), axis=1, keepdims=True)
        chance = chance / jnp.sum(logit_exp, axis=1, keepdims=True)
        coarse = chance.astype(bf16).astype(f32)
        chances[...] = jnp.where(
            lanes == 0, coarse, jnp.where(lanes == 1, chance - coarse, 0.0)
        ).astype(bf16)
        stage.put(5, step, unit)
        stage.put(6, step, unit)
        spread.tick(step, chips, 2)
        gate_act[slot] = dot_nt(received[slot], gate_ref[...])
        stage.put(1, step, unit)
        spread.tick(step, chips, 3)
        up_act[slot] = dot_nt(received[slot], up_ref[...])
        stage.put(2, step, unit)
        spread.tick(step, chips, 4)
        for one in (0, 1):
            halves = dot(picks[one], chances[own_rows[one]])
            scale = halves[:, 0:1] + halves[:, 1:2]
            weight[slot, slots[one]] = jnp.broadcast_to(scale, (capacity, BLOCK))
            act = silu_parts(gate_act[slot, slots[one]])[0] * up_act[slot, slots[one]]
            hidden[slot, slots[one]] = (scale * act).astype(bf16)
        stage.put(3, step, unit)
        stage.put(4, step, unit)
        spread.tick(step, chips, 5)
        result = dot(hidden[slot], down_ref[...]).astype(bf16)
        for one in (0, 1):
            tall[one, :capacity] = result[one * capacity : (one + 1) * capacity]
        spread.tick(step, chips, 6)
        part[slot, own_rows[0]] = dot(packs[0], tall[0]).astype(bf16)
        spread.tick(step, chips, 7)
        part[slot, own_rows[1]] = dot(packs[1], tall[1]).astype(bf16)
        stage.put(7, step, unit)
        return carry

    lax.fori_loop(0, spread.units, body, 0)
    stage.finish(spread.units)
    for unit in range(spread.units):
        tokens_copy(unit).wait()
    spread.drain()


def experts_forward(own, place, gate, up, down, wide, block, capacity, experts, collective_id):
    fsdp_size = lax.axis_size("fsdp")
    f32, bf16 = jnp.float32, jnp.bfloat16
    seq_len, width, hidden = place.shape[1], own.shape[1], gate.shape[0]
    tokens, slots = fsdp_size * seq_len, fsdp_size * capacity
    shape = jax.ShapeDtypeStruct
    outs = [
        shape((tokens, width), bf16),
        shape((slots, width), bf16),
        shape((slots, hidden), f32),
        shape((slots, hidden), f32),
        shape((slots, hidden), bf16),
        shape((slots, BLOCK), f32),
        shape((tokens, 2 * BLOCK), f32),
        shape((tokens, BLOCK), bf16),
        shape((tokens, width), bf16),
    ]
    stages = [pltpu.VMEM((2, 2 * o.shape[0] // fsdp_size, o.shape[1]), o.dtype) for o in outs[1:]]
    dma = pltpu.SemaphoreType.DMA
    return pl.pallas_call(
        functools.partial(forward_kernel, fsdp_size, experts, capacity),
        out_shape=tuple(outs),
        in_specs=[pl.BlockSpec(memory_space=pltpu.VMEM)] * 2
        + [pl.BlockSpec(memory_space=pl.ANY)] * 5,
        out_specs=tuple([pl.BlockSpec(memory_space=pl.ANY)] * len(outs)),
        scratch_shapes=[
            pltpu.VMEM((tokens, width), bf16),
            pltpu.VMEM((2, capacity, seq_len), bf16),
            pltpu.VMEM((2, seq_len, capacity + BLOCK), bf16),
            pltpu.VMEM((2 * seq_len, BLOCK), bf16),
            pltpu.VMEM((2, capacity + BLOCK, width), bf16),
            *stages,
            *[pltpu.VMEM(w.shape, w.dtype) for w in (gate, up, down, wide, block)],
            dma((5,)),
            dma((len(stages), 2)),
            dma((fsdp_size // 2,)),
            *spread_sems(fsdp_size),
        ],
        compiler_params=pltpu.CompilerParams(
            collective_id=collective_id, has_side_effects=True, vmem_limit_bytes=67043328
        ),
        cost_estimate=pl.CostEstimate(
            flops=6 * slots * width * hidden, bytes_accessed=100_000_000, transcendentals=0
        ),
    )(own, place, gate, up, down, wide, block)


def backward_kernel(
    fsdp_size,
    capacity,
    own,
    place_ref,
    gate_hbm,
    up_hbm,
    down_hbm,
    pair_hbm,
    block_hbm,
    gate_in,
    up_in,
    weight_in,
    shared_in,
    grads_out,
    slots_out,
    gate_out,
    up_out,
    pair_out,
    chance_out,
    part_out,
    room,
    picks,
    packs,
    tall,
    gate_act,
    up_act,
    weight,
    shared,
    picked,
    gate_grad,
    up_grad,
    pair_grad,
    chance_grad,
    part,
    gate_ref,
    up_ref,
    down_ref,
    pair_ref,
    block_ref,
    weight_sem,
    load_sem,
    stage_sem,
    room_sem,
    *sems,
):
    f32, bf16 = jnp.float32, jnp.bfloat16
    seq_len = place_ref.shape[1]
    spread = Spread(fsdp_size, own, room, sems)
    expert = lax.axis_index("fsdp")
    stage = Stage(
        [picked, gate_grad, up_grad, pair_grad, chance_grad, part],
        [slots_out, gate_out, up_out, pair_out, chance_out, part_out],
        stage_sem,
    )
    saved = [gate_in, up_in, weight_in, shared_in]
    loads = [gate_act, up_act, weight, shared]

    def load(number, step):
        y, z = spread.unit(step)
        slot, rows = lax.rem(step, 2), loads[number].shape[1]
        span = pl.ds(pl.multiple_of((z * 2 + y) * rows, rows), rows)
        return pltpu.make_async_copy(
            saved[number].at[span], loads[number].at[slot], load_sem.at[number, slot]
        )

    def grads_copy(unit):
        span = pl.ds(pl.multiple_of(unit * 2 * seq_len, 2 * seq_len), 2 * seq_len)
        return pltpu.make_async_copy(room.at[span], grads_out.at[span], room_sem.at[unit])

    for number in range(len(saved)):
        load(number, 0).start()
    weights = [
        pltpu.make_async_copy(source, target, weight_sem.at[number])
        for number, (source, target) in enumerate([(gate_hbm, gate_ref), (up_hbm, up_ref), (down_hbm, down_ref), (pair_hbm, pair_ref), (block_hbm, block_ref)])
    ]
    for copy in weights:
        copy.start()
    spread.begin()
    for copy in weights:
        copy.wait()
    for one in (0, 1):
        tall[one, capacity:] = pair_ref[...]
    expert_lane = lax.broadcasted_iota(jnp.int32, (capacity, BLOCK), 1) == expert

    def body(step, carry):
        slot = lax.rem(step, 2)
        y, z = spread.unit(step)
        unit = z * 2 + y
        later = step + 1
        chips = spread.ahead(step)
        spread.arrived(step)
        grads_copy(unit).start()
        stage.reuse(step)
        rows = [
            pl.ds(pl.multiple_of((2 * unit + one) * seq_len, seq_len), seq_len) for one in (0, 1)
        ]
        both_rows = pl.ds(pl.multiple_of(unit * 2 * seq_len, 2 * seq_len), 2 * seq_len)
        slots = [pl.ds(one * capacity, capacity) for one in (0, 1)]
        own_rows = [pl.ds(one * seq_len, seq_len) for one in (0, 1)]
        for number in range(len(saved)):
            load(number, step).wait()

        def ahead():
            for number in range(len(saved)):
                load(number, later).start()

        pl.when(later < spread.units)(ahead)
        spread.tick(step, chips, 0)
        for one in (0, 1):
            pick = dispatch_of(place_ref, 2 * unit + one, capacity, seq_len)
            picks[one] = pick.astype(bf16)
            packs[one, :, :capacity] = jnp.transpose(pick).astype(bf16)
            picked[slot, slots[one]] = dot(picks[one], room[rows[one]]).astype(bf16)
        stage.put(0, step, unit)
        spread.tick(step, chips, 1)
        raw = dot_nt(picked[slot], down_ref[...])
        scale = weight[slot, :, 0:1]
        silu_gate, slope = silu_parts(gate_act[slot])
        up_value = up_act[slot]
        gate_sum = jnp.sum(raw * (silu_gate * up_value), axis=1, keepdims=True)
        scaled = scale * raw
        gate_grad[slot] = (scaled * up_value * slope).astype(bf16)
        up_grad[slot] = (scaled * silu_gate).astype(bf16)
        stage.put(1, step, unit)
        stage.put(2, step, unit)
        spread.tick(step, chips, 2)
        for one in (0, 1):
            column = gate_sum[one * capacity : (one + 1) * capacity]
            column = jnp.where(expert_lane, column, 0.0).astype(bf16)
            chance_grad[slot, own_rows[one]] = dot(packs[one, :, :capacity], column).astype(bf16)
        stage.put(4, step, unit)
        grad_sh = dot_nt(room[both_rows], block_ref[...])
        silu_sh, slope_sh = silu_parts(shared[slot, :, :BLOCK])
        gate_sh = (grad_sh * shared[slot, :, BLOCK:] * slope_sh).astype(bf16)
        up_sh = (grad_sh * silu_sh).astype(bf16)
        pair_grad[slot, :, :BLOCK] = gate_sh
        pair_grad[slot, :, BLOCK:] = up_sh
        for one in (0, 1):
            own_seq = slice(one * seq_len, (one + 1) * seq_len)
            packs[one, :, capacity : capacity + BLOCK] = gate_sh[own_seq]
            packs[one, :, capacity + BLOCK :] = up_sh[own_seq]
        stage.put(3, step, unit)
        spread.tick(step, chips, 3)
        back = dot(gate_grad[slot], gate_ref[...])
        spread.tick(step, chips, 4)
        back = (back + dot(up_grad[slot], up_ref[...])).astype(bf16)
        for one in (0, 1):
            tall[one, :capacity] = back[one * capacity : (one + 1) * capacity]
        spread.tick(step, chips, 5)
        part[slot, own_rows[0]] = dot(packs[0], tall[0]).astype(bf16)
        spread.tick(step, chips, 6)
        part[slot, own_rows[1]] = dot(packs[1], tall[1]).astype(bf16)
        stage.put(5, step, unit)
        spread.tick(step, chips, 7)
        return carry

    lax.fori_loop(0, spread.units, body, 0)
    stage.finish(spread.units)
    for unit in range(spread.units):
        grads_copy(unit).wait()
    spread.drain()


def experts_backward(
    own, place, gate, up, down, pair, block, gate_act, up_act, weight, shared, capacity, collective_id
):
    fsdp_size = lax.axis_size("fsdp")
    bf16 = jnp.bfloat16
    seq_len, width, hidden = place.shape[1], own.shape[1], gate.shape[0]
    tokens, slots = fsdp_size * seq_len, fsdp_size * capacity
    shape = jax.ShapeDtypeStruct
    outs = [
        shape((tokens, width), bf16),
        shape((slots, width), bf16),
        shape((slots, hidden), bf16),
        shape((slots, hidden), bf16),
        shape((tokens, 2 * BLOCK), bf16),
        shape((tokens, BLOCK), bf16),
        shape((tokens, width), bf16),
    ]

    def slots_of(arrays):
        return [pltpu.VMEM((2, 2 * a.shape[0] // fsdp_size, a.shape[1]), a.dtype) for a in arrays]

    saved = [gate_act, up_act, weight, shared]
    dma = pltpu.SemaphoreType.DMA
    return pl.pallas_call(
        functools.partial(backward_kernel, fsdp_size, capacity),
        out_shape=tuple(outs),
        in_specs=[pl.BlockSpec(memory_space=pltpu.VMEM)] * 2
        + [pl.BlockSpec(memory_space=pl.ANY)] * 9,
        out_specs=tuple([pl.BlockSpec(memory_space=pl.ANY)] * len(outs)),
        scratch_shapes=[
            pltpu.VMEM((tokens, width), bf16),
            pltpu.VMEM((2, capacity, seq_len), bf16),
            pltpu.VMEM((2, seq_len, capacity + 2 * BLOCK), bf16),
            pltpu.VMEM((2, capacity + 2 * BLOCK, width), bf16),
            *slots_of(saved),
            *slots_of(outs[1:]),
            *[pltpu.VMEM(w.shape, w.dtype) for w in (gate, up, down, pair, block)],
            dma((5,)),
            dma((4, 2)),
            dma((len(outs) - 1, 2)),
            dma((fsdp_size // 2,)),
            *spread_sems(fsdp_size),
        ],
        compiler_params=pltpu.CompilerParams(
            collective_id=collective_id, has_side_effects=True, vmem_limit_bytes=67043328
        ),
        cost_estimate=pl.CostEstimate(
            flops=6 * slots * width * hidden, bytes_accessed=100_000_000, transcendentals=0
        ),
    )(own, place, gate, up, down, pair, block, *saved)


def token_shards(
    inputs,
    teacher,
    valid_mask,
    prefix,
    routes,
    norm_gain,
    query_weight,
    latent_weight,
    latent_gain,
    expand_weight,
    output_weight,
    moe_gain,
    router_weight,
    shared_gate,
    shared_up,
    shared_down,
    expert_gate,
    expert_up,
    expert_down,
):
    f32 = jnp.float32
    bf16 = jnp.bfloat16
    tp_size = lax.axis_size("tp")
    fsdp_size = lax.axis_size("fsdp")
    own_tp = lax.axis_index("tp")
    own_expert = lax.axis_index("fsdp")
    local_heads = HEADS // tp_size
    own_rows = inputs.shape[0]
    width = inputs.shape[1]
    seq_len = own_rows * tp_size

    expert_count = router_weight.shape[1]
    route_rows = routes.shape[1] * seq_len // BLOCK
    valid_rows = seq_len // BLOCK
    parts = [
        routes.T.reshape(route_rows, BLOCK).astype(f32),
        valid_mask.reshape(valid_rows, BLOCK).astype(f32),
        norm_gain.reshape(1, BLOCK).astype(f32),
        moe_gain.reshape(1, BLOCK).astype(f32),
        jnp.pad(latent_gain, (0, BLOCK - latent_gain.shape[0])).reshape(1, BLOCK).astype(f32),
        router_weight.T.astype(f32),
    ]
    small = jnp.concatenate(parts, axis=0)
    small_rows = -(-small.shape[0] // 8) * 8
    small = jnp.pad(small, ((0, small_rows - small.shape[0]), (0, 0)))
    blocks = shared_gate.shape[1] // BLOCK
    (
        query_full,
        latent_full,
        expand_full,
        output_full,
        small_all,
        gate_block,
        up_block,
        down_block,
    ) = gather_weights(
        query_weight,
        latent_weight,
        expand_weight,
        output_weight,
        small,
        shared_gate,
        shared_up,
        shared_down,
        1,
    )
    small_all = small_all.reshape(fsdp_size, small_rows, BLOCK)
    routes_all = small_all[:, :route_rows].reshape(fsdp_size, routes.shape[1], seq_len)
    gain_row = route_rows + valid_rows
    valid_all = small_all[:, route_rows:gain_row]
    norm_gains = small_all[:, gain_row].reshape(width)
    moe_gains = small_all[:, gain_row + 1].reshape(width)
    latent_gains = small_all[:, gain_row + 2, : latent_gain.shape[0]].reshape(RANK)
    router_rows = small_all[:, gain_row + 3 : gain_row + 3 + expert_count]
    router_full = jnp.transpose(router_rows, (1, 0, 2)).reshape(expert_count, width).astype(bf16)
    own_block = (own_expert * blocks + fsdp_size - 1) // fsdp_size
    holds_block = (own_block < blocks) & (own_block * fsdp_size // blocks == own_expert)
    gate_block = jnp.where(holds_block, gate_block, 0)
    up_block = jnp.where(holds_block, up_block, 0)
    down_block = jnp.where(holds_block, down_block, 0)

    hidden = tp_gather(inputs, own_tp).astype(f32)
    cosine, sine_part = rope_tables(seq_len, ROPE)
    inverse_in = lax.rsqrt(jnp.mean(hidden * hidden, axis=-1, keepdims=True) + EPSILON)
    normal_in = hidden * inverse_in
    norm_scale = norm_gains.astype(f32)
    normed = (normal_in * norm_scale).astype(bf16)
    query_lin = jnp.dot(normed, query_full, preferred_element_type=f32).reshape(
        seq_len, local_heads, NOPE + ROPE
    )
    queries = jnp.concatenate(
        [
            query_lin[..., :NOPE],
            rotate(query_lin[..., NOPE:], cosine[:, None, :], sine_part[:, None, :]),
        ],
        axis=-1,
    ).astype(bf16)
    latent_lin = jnp.dot(normed, latent_full, preferred_element_type=f32)
    latent_raw = latent_lin[:, :RANK]
    inverse_lat = lax.rsqrt(jnp.mean(latent_raw * latent_raw, axis=-1, keepdims=True) + EPSILON)
    latent_unit = latent_raw * inverse_lat
    latent_scale = latent_gains.astype(f32)
    latent = (latent_unit * latent_scale).astype(bf16)
    key_rope = rotate(latent_lin[:, RANK:], cosine, sine_part).astype(bf16)
    keys_values = (
        jnp.dot(latent, expand_full, preferred_element_type=f32)
        .astype(bf16)
        .reshape(seq_len, local_heads, NOPE + VDIM)
    )
    key_nope = keys_values[..., :NOPE]
    values = keys_values[..., NOPE:]
    query_nope = queries[..., :NOPE]
    query_rope = queries[..., NOPE:]
    score_scale = 1.0 / math.sqrt(NOPE + ROPE)
    position = jnp.arange(seq_len, dtype=jnp.int32)
    visible = (position[None, :] <= position[:, None]) | (position[None, :] < prefix[0])
    raw_scores = jnp.einsum("ihd,jhd->hij", query_nope, key_nope, preferred_element_type=f32)
    raw_scores = raw_scores + jnp.einsum(
        "ihd,jd->hij", query_rope, key_rope, preferred_element_type=f32
    )
    scores = jnp.where(visible[None], raw_scores * score_scale, MASKED)
    row_max = jnp.max(scores, axis=-1, keepdims=True)
    shifted = jnp.exp(scores - row_max)
    attn_probs = shifted / jnp.sum(shifted, axis=-1, keepdims=True)
    probs_low = attn_probs.astype(bf16)
    heads_out = (
        jnp.einsum("hij,jhd->ihd", probs_low, values, preferred_element_type=f32)
        .astype(bf16)
        .reshape(seq_len, local_heads * VDIM)
    )
    attended = tp_scatter(
        jnp.dot(heads_out, output_full, preferred_element_type=f32), own_tp, own_rows
    )

    middle = inputs.astype(f32) + attended
    inverse_mid = lax.rsqrt(jnp.mean(middle * middle, axis=-1, keepdims=True) + EPSILON)
    normal_mid = middle * inverse_mid
    moe_scale = moe_gains.astype(f32)
    moe_in = (normal_mid * moe_scale).astype(bf16)

    def route(logits):
        logit_exp = jnp.exp(logits - jnp.max(logits, axis=-1, keepdims=True))
        return logit_exp / jnp.sum(logit_exp, axis=-1, keepdims=True)

    router_probs = route(jnp.einsum("td,ed->te", moe_in, router_full, preferred_element_type=f32))
    experts = expert_count
    top_count = routes.shape[1]
    capacity = top_count * seq_len * 4 // (3 * experts)

    named = jnp.any(routes_all == own_expert.astype(f32), axis=1)
    ahead = jnp.dot(
        named.astype(bf16),
        (position[:, None] < position[None, :]).astype(bf16),
        preferred_element_type=f32,
    ).astype(jnp.int32)
    place = jnp.where(named, ahead, -1)
    wide_block = jnp.concatenate(
        [gate_block, up_block, jnp.pad(router_full, ((0, BLOCK - experts), (0, 0))).T], axis=1
    )
    (
        tokens,
        received,
        gate_act,
        up_act,
        gated_hidden,
        gate_weight,
        shared_acts,
        shared_hidden,
        moe_part,
    ) = experts_forward(
        moe_in,
        place,
        expert_gate[0].T,
        expert_up[0].T,
        expert_down[0],
        wide_block,
        down_block,
        capacity,
        experts,
        2,
    )
    activations = middle + reduce_tokens([moe_part], 3)[0]

    own_mask = half_rows(valid_mask, own_tp, own_rows).astype(f32)
    offset = activations - half_rows(teacher, own_tp, own_rows).astype(f32)
    valid_total = jnp.maximum(jnp.sum(valid_all), 1.0)
    square_part = jnp.sum(own_mask[:, None] * offset * offset)
    grad_out = seq_len * fsdp_size / valid_total * own_mask[:, None] * offset
    grad_moe = grad_out.astype(bf16)

    (
        grads,
        grad_slots,
        grad_gate_act,
        grad_up_act,
        grad_sh_pair,
        grad_probs_part,
        grad_part,
    ) = experts_backward(
        grad_moe,
        place,
        expert_gate[0].T,
        expert_up[0].T,
        expert_down[0],
        jnp.concatenate([gate_block.T, up_block.T], axis=0),
        down_block,
        gate_act,
        up_act,
        gate_weight,
        shared_acts,
        capacity,
        4,
    )
    grad_moe_in, grad_router_probs = reduce_tokens([grad_part, grad_probs_part], 5)
    expert_down_grad = jnp.einsum(
        "cf,cd->fd", gated_hidden, grad_slots, preferred_element_type=f32
    )
    expert_gate_grad = jnp.einsum(
        "cd,cf->df", received, grad_gate_act, preferred_element_type=f32
    )
    expert_up_grad = jnp.einsum("cd,cf->df", received, grad_up_act, preferred_element_type=f32)
    down_shared_grad = jnp.einsum("tf,td->fd", shared_hidden, grads, preferred_element_type=f32)
    pair_grad = jnp.einsum("td,tf->df", tokens, grad_sh_pair, preferred_element_type=f32)
    gate_shared_grad = pair_grad[:, :BLOCK].astype(bf16)
    up_shared_grad = pair_grad[:, BLOCK:].astype(bf16)
    grad_router_probs = grad_router_probs[:, :experts]

    grad_logits = router_probs * (
        grad_router_probs - jnp.sum(router_probs * grad_router_probs, axis=-1, keepdims=True)
    )
    router_grad = jnp.einsum(
        "td,te->ed", moe_in.astype(f32), grad_logits, precision=HIGHEST, preferred_element_type=f32
    )
    grad_moe_in = grad_moe_in + jnp.einsum(
        "te,ed->td",
        grad_logits,
        router_full.astype(f32),
        precision=HIGHEST,
        preferred_element_type=f32,
    )
    moe_gain_grad = jnp.sum(grad_moe_in * normal_mid, axis=0)
    grad_middle = grad_out + norm_back(grad_moe_in * moe_scale, normal_mid, inverse_mid)
    grad_attended = tp_gather(grad_middle.astype(bf16), own_tp)

    output_grad = jnp.einsum("tf,td->fd", heads_out, grad_attended, preferred_element_type=f32)
    grad_heads = (
        jnp.einsum("td,fd->tf", grad_attended, output_full, preferred_element_type=f32)
        .astype(bf16)
        .reshape(seq_len, local_heads, VDIM)
    )
    grad_probs = jnp.einsum("ihd,jhd->hij", grad_heads, values, preferred_element_type=f32)
    grad_values = jnp.einsum("hij,ihd->jhd", probs_low, grad_heads, preferred_element_type=f32)
    grad_scores = (
        attn_probs * (grad_probs - jnp.sum(attn_probs * grad_probs, axis=-1, keepdims=True))
    ).astype(bf16)
    grad_q_nope = (
        jnp.einsum("hij,jhd->ihd", grad_scores, key_nope, preferred_element_type=f32) * score_scale
    )
    grad_q_rope = (
        jnp.einsum("hij,jd->ihd", grad_scores, key_rope, preferred_element_type=f32) * score_scale
    )
    grad_keys = (
        jnp.einsum("hij,ihd->jhd", grad_scores, query_nope, preferred_element_type=f32)
        * score_scale
    )
    grad_key_rope = (
        jnp.einsum("hij,ihd->jd", grad_scores, query_rope, preferred_element_type=f32) * score_scale
    )
    grad_query = (
        jnp.concatenate(
            [grad_q_nope, unrotate(grad_q_rope, cosine[:, None, :], sine_part[:, None, :])], axis=-1
        )
        .astype(bf16)
        .reshape(seq_len, local_heads * (NOPE + ROPE))
    )
    query_grad = jnp.einsum("td,tq->dq", normed, grad_query, preferred_element_type=f32)
    grad_normed = jnp.einsum("tq,dq->td", grad_query, query_full, preferred_element_type=f32)
    grad_kv = (
        jnp.concatenate([grad_keys, grad_values], axis=-1)
        .astype(bf16)
        .reshape(seq_len, local_heads * (NOPE + VDIM))
    )
    expand_grad = jnp.einsum("tr,tq->rq", latent, grad_kv, preferred_element_type=f32)
    grad_latent = jnp.einsum("tq,rq->tr", grad_kv, expand_full, preferred_element_type=f32)
    grad_both = tp_sum(jnp.concatenate([grad_latent, grad_key_rope], axis=1))
    grad_latent, grad_key_rope = grad_both[:, :RANK], grad_both[:, RANK:]
    latent_gain_grad = jnp.sum(grad_latent * latent_unit, axis=0)
    grad_latent_raw = norm_back(grad_latent * latent_scale, latent_unit, inverse_lat)
    grad_latent_lin = jnp.concatenate(
        [grad_latent_raw, unrotate(grad_key_rope, cosine, sine_part)], axis=-1
    ).astype(bf16)
    latent_grad = jnp.einsum("td,tr->dr", normed, grad_latent_lin, preferred_element_type=f32)
    grad_normed = tp_scatter(grad_normed, own_tp, own_rows) + jnp.einsum(
        "tr,dr->td",
        half_rows(grad_latent_lin, own_tp, own_rows),
        latent_full,
        preferred_element_type=f32,
    )
    own_normal = half_rows(normal_in, own_tp, own_rows)
    own_inverse = half_rows(inverse_in, own_tp, own_rows)
    norm_gain_grad = jnp.sum(grad_normed * own_normal, axis=0)
    input_grad = grad_middle + norm_back(grad_normed * norm_scale, own_normal, own_inverse)

    small = jnp.concatenate(
        [
            jnp.transpose(router_grad.reshape(experts, fsdp_size, BLOCK), (1, 0, 2)),
            norm_gain_grad.reshape(fsdp_size, 1, BLOCK),
            moe_gain_grad.reshape(fsdp_size, 1, BLOCK),
            jnp.pad(
                0.5 * latent_gain_grad.reshape(fsdp_size, 1, RANK // fsdp_size),
                ((0, 0), (0, 0), (0, BLOCK - RANK // fsdp_size)),
            ),
            jnp.full((fsdp_size, 1, BLOCK), square_part),
        ],
        axis=1,
    )
    small = jnp.pad(small, ((0, 0), (0, -(experts + 4) % 8), (0, 0))).reshape(-1, BLOCK)
    small = small + swap_tp(small)
    query_out, latent_out, expand_out, output_out, small_out, gate_out, up_out, down_out = (
        reduce_weights(
            query_grad.astype(bf16),
            latent_grad.astype(bf16),
            expand_grad.astype(bf16),
            output_grad.astype(bf16),
            small,
            gate_shared_grad,
            up_shared_grad,
            down_shared_grad.astype(bf16),
            blocks,
            6,
        )
    )
    return (
        small_out[experts + 3, 0] / (width * valid_total),
        activations,
        input_grad,
        small_out[experts],
        query_out,
        latent_out,
        small_out[experts + 2, : RANK // fsdp_size],
        expand_out,
        output_out,
        small_out[experts + 1],
        small_out[:experts].T,
        gate_out.astype(f32),
        up_out.astype(f32),
        down_out.astype(f32),
        expert_gate_grad[None],
        expert_up_grad[None],
        expert_down_grad[None],
    )


def slot_shards(
    inputs,
    teacher,
    valid_mask,
    prefix,
    routes,
    norm_gain,
    query_weight,
    latent_weight,
    latent_gain,
    expand_weight,
    output_weight,
    moe_gain,
    router_weight,
    shared_gate,
    shared_up,
    shared_down,
    expert_gate,
    expert_up,
    expert_down,
):
    f32 = jnp.float32
    bf16 = jnp.bfloat16
    tp_size = lax.axis_size("tp")
    fsdp_size = lax.axis_size("fsdp")
    local_heads = HEADS // tp_size
    (
        norm_gains,
        query_full,
        latent_full,
        latent_gains,
        expand_full,
        output_full,
        moe_gains,
        router_full,
        gate_full,
        up_full,
        down_full,
    ) = (
        lax.all_gather(norm_gain, "fsdp", axis=0, tiled=True),
        lax.all_gather(query_weight, "fsdp", axis=0, tiled=True),
        lax.all_gather(latent_weight, "fsdp", axis=0, tiled=True),
        lax.all_gather(latent_gain, "fsdp", axis=0, tiled=True),
        lax.all_gather(expand_weight, "fsdp", axis=0, tiled=True),
        lax.all_gather(output_weight, "fsdp", axis=1, tiled=True),
        lax.all_gather(moe_gain, "fsdp", axis=0, tiled=True),
        lax.all_gather(router_weight, "fsdp", axis=0, tiled=True),
        lax.all_gather(shared_gate, "fsdp", axis=0, tiled=True),
        lax.all_gather(shared_up, "fsdp", axis=0, tiled=True),
        lax.all_gather(shared_down, "fsdp", axis=1, tiled=True),
    )
    gathered = lax.all_gather(inputs, "tp", axis=0, tiled=True)
    seq_len = gathered.shape[0]
    width = gathered.shape[1]
    hidden = gathered.astype(f32)
    cosine, sine_part = rope_tables(seq_len, ROPE)
    inverse_in = lax.rsqrt(jnp.mean(hidden * hidden, axis=-1, keepdims=True) + EPSILON)
    normal_in = hidden * inverse_in
    norm_scale = norm_gains.astype(f32)
    normed = (normal_in * norm_scale).astype(bf16)
    query_lin = jnp.dot(normed, query_full, preferred_element_type=f32).reshape(
        seq_len, local_heads, NOPE + ROPE
    )
    queries = jnp.concatenate(
        [
            query_lin[..., :NOPE],
            rotate(query_lin[..., NOPE:], cosine[:, None, :], sine_part[:, None, :]),
        ],
        axis=-1,
    ).astype(bf16)
    latent_lin = jnp.dot(normed, latent_full, preferred_element_type=f32)
    latent_raw = latent_lin[:, :RANK]
    inverse_lat = lax.rsqrt(jnp.mean(latent_raw * latent_raw, axis=-1, keepdims=True) + EPSILON)
    latent_unit = latent_raw * inverse_lat
    latent_scale = latent_gains.astype(f32)
    latent = (latent_unit * latent_scale).astype(bf16)
    key_rope = rotate(latent_lin[:, RANK:], cosine, sine_part).astype(bf16)
    keys_values = (
        jnp.dot(latent, expand_full, preferred_element_type=f32)
        .astype(bf16)
        .reshape(seq_len, local_heads, NOPE + VDIM)
    )
    key_nope = keys_values[..., :NOPE]
    values = keys_values[..., NOPE:]
    query_nope = queries[..., :NOPE]
    query_rope = queries[..., NOPE:]
    score_scale = 1.0 / math.sqrt(NOPE + ROPE)
    position = jnp.arange(seq_len, dtype=jnp.int32)
    visible = (position[None, :] <= position[:, None]) | (position[None, :] < prefix[0])

    def scores_of():
        raw_scores = jnp.einsum("ihd,jhd->hij", query_nope, key_nope, preferred_element_type=f32)
        raw_scores = raw_scores + jnp.einsum(
            "ihd,jd->hij", query_rope, key_rope, preferred_element_type=f32
        )
        return jnp.where(visible[None], raw_scores * score_scale, MASKED)

    scores = scores_of()
    row_max = jnp.max(scores, axis=-1, keepdims=True)
    shifted = jnp.exp(scores - row_max)
    row_total = jnp.sum(shifted, axis=-1, keepdims=True)
    log_total = row_max + jnp.log(row_total)
    probs_low = (shifted / row_total).astype(bf16)
    heads_out = (
        jnp.einsum("hij,jhd->ihd", probs_low, values, preferred_element_type=f32)
        .astype(bf16)
        .reshape(seq_len, local_heads * VDIM)
    )
    attended = lax.psum(jnp.dot(heads_out, output_full, preferred_element_type=f32), "tp")
    middle = hidden + attended
    inverse_mid = lax.rsqrt(jnp.mean(middle * middle, axis=-1, keepdims=True) + EPSILON)
    normal_mid = middle * inverse_mid
    moe_scale = moe_gains.astype(f32)
    moe_in = (normal_mid * moe_scale).astype(bf16)
    logits = jnp.dot(moe_in, router_full, preferred_element_type=f32)
    logit_max = jnp.max(logits, axis=-1, keepdims=True)
    logit_exp = jnp.exp(logits - logit_max)
    router_probs = logit_exp / jnp.sum(logit_exp, axis=-1, keepdims=True)
    experts = router_full.shape[1]
    top_count = routes.shape[1]
    choose = routes[:, :, None] == jnp.arange(experts, dtype=jnp.int32)[None, None, :]
    gate_values = jnp.sum(jnp.where(choose, router_probs[:, None, :], 0.0), axis=-1)
    capacity = top_count * seq_len * 4 // (3 * experts)
    flat_routes = routes.reshape(seq_len * top_count)
    onehot = (flat_routes[:, None] == jnp.arange(experts, dtype=jnp.int32)[None, :]).astype(
        jnp.int32
    )
    earlier = jnp.cumsum(onehot, axis=0) - onehot
    slot_index = flat_routes * capacity + jnp.sum(earlier * onehot, axis=1)
    placed = jnp.arange(experts * capacity, dtype=jnp.int32)[:, None] == slot_index[None, :]
    dispatch = jnp.sum(
        placed.reshape(experts * capacity, seq_len, top_count).astype(f32), axis=2
    ).astype(bf16)
    gate_slot = jnp.sum(jnp.where(placed, gate_values.reshape(1, seq_len * top_count), 0.0), axis=1)

    def send_slots(slot_rows):
        return lax.all_to_all(slot_rows, "fsdp", split_axis=0, concat_axis=1, tiled=True)

    def return_slots(partials):
        return (
            lax.all_to_all(
                partials.astype(jnp.bfloat16), "fsdp", split_axis=1, concat_axis=0, tiled=True
            )
            .astype(partials.dtype)
            .reshape(experts * capacity, width)
        )

    expert_in = (
        jnp.dot(dispatch, moe_in, preferred_element_type=f32)
        .astype(bf16)
        .reshape(experts, capacity, width)
    )
    received = send_slots(expert_in)
    gate_act = jnp.einsum("ecd,edf->ecf", received, expert_gate, preferred_element_type=f32)
    up_act = jnp.einsum("ecd,edf->ecf", received, expert_up, preferred_element_type=f32)
    silu_gate, silu_slope = silu_parts(gate_act)
    expert_hidden = (silu_gate * up_act).astype(bf16)
    expert_out = jnp.einsum("ecf,efd->ecd", expert_hidden, expert_down, preferred_element_type=f32)
    returned = return_slots(expert_out)
    picked = jnp.take(returned, slot_index, axis=0).reshape(seq_len, top_count, width)
    routed = jnp.sum(gate_values[:, :, None] * picked, axis=1)
    gate_sh = jnp.dot(moe_in, gate_full, preferred_element_type=f32)
    up_sh = jnp.dot(moe_in, up_full, preferred_element_type=f32)
    silu_sh, slope_sh = silu_parts(gate_sh)
    shared_hidden = (silu_sh * up_sh).astype(bf16)
    moe_part = routed + jnp.dot(shared_hidden, down_full, preferred_element_type=f32)
    moe_out = lax.psum(moe_part.astype(jnp.bfloat16), "tp").astype(jnp.float32)
    activations = middle + moe_out
    mask_float = valid_mask.astype(f32)
    offset = activations - teacher.astype(f32)
    square_sum, valid_sum = lax.psum(
        (jnp.sum(mask_float[:, None] * offset * offset), jnp.sum(mask_float)), "fsdp"
    )
    valid_total = jnp.maximum(valid_sum, 1.0)
    loss_value = square_sum / (width * valid_total)
    grad_out = seq_len * fsdp_size / valid_total * mask_float[:, None] * offset
    grad_moe = grad_out.astype(bf16)
    down_shared_grad = jnp.einsum("tf,td->fd", shared_hidden, grad_moe, preferred_element_type=f32)
    grad_sh_hidden = jnp.einsum("td,fd->tf", grad_moe, down_full, preferred_element_type=f32)
    grad_gate_sh = (grad_sh_hidden * up_sh * slope_sh).astype(bf16)
    grad_up_sh = (grad_sh_hidden * silu_sh).astype(bf16)
    gate_shared_grad = jnp.einsum("td,tf->df", moe_in, grad_gate_sh, preferred_element_type=f32)
    up_shared_grad = jnp.einsum("td,tf->df", moe_in, grad_up_sh, preferred_element_type=f32)
    grad_moe_in = jnp.einsum("tf,df->td", grad_gate_sh, gate_full, preferred_element_type=f32)
    grad_moe_in = grad_moe_in + jnp.einsum(
        "tf,df->td", grad_up_sh, up_full, preferred_element_type=f32
    )
    grad_gates = jnp.sum(picked * grad_moe.astype(f32)[:, None, :], axis=-1)
    grad_slots = (
        (jnp.dot(dispatch, grad_moe, preferred_element_type=f32) * gate_slot[:, None])
        .astype(bf16)
        .reshape(experts, capacity, width)
    )
    grad_received = send_slots(grad_slots)
    expert_down_grad = jnp.einsum(
        "ecf,ecd->efd", expert_hidden, grad_received, preferred_element_type=f32
    )
    grad_expert_hidden = jnp.einsum(
        "ecd,efd->ecf", grad_received, expert_down, preferred_element_type=f32
    )
    grad_gate_act = (grad_expert_hidden * up_act * silu_slope).astype(bf16)
    grad_up_act = (grad_expert_hidden * silu_gate).astype(bf16)
    expert_gate_grad = jnp.einsum(
        "ecd,ecf->edf", received, grad_gate_act, preferred_element_type=f32
    )
    expert_up_grad = jnp.einsum("ecd,ecf->edf", received, grad_up_act, preferred_element_type=f32)
    grad_expert_in = jnp.einsum(
        "ecf,edf->ecd", grad_gate_act, expert_gate, preferred_element_type=f32
    )
    grad_expert_in = grad_expert_in + jnp.einsum(
        "ecf,edf->ecd", grad_up_act, expert_up, preferred_element_type=f32
    )
    grad_returned = return_slots(grad_expert_in)
    grad_moe_in = grad_moe_in + jnp.sum(
        jnp.take(grad_returned, slot_index, axis=0).reshape(seq_len, top_count, width), axis=1
    )
    grad_moe_in, grad_gates = (
        lax.psum(grad_moe_in.astype(jnp.bfloat16), "tp").astype(jnp.float32),
        lax.psum(grad_gates.astype(jnp.bfloat16), "tp").astype(jnp.float32),
    )
    grad_router_probs = jnp.sum(jnp.where(choose, grad_gates[:, :, None], 0.0), axis=1)
    grad_logits = router_probs * (
        grad_router_probs - jnp.sum(router_probs * grad_router_probs, axis=-1, keepdims=True)
    )
    router_grad = jnp.einsum(
        "td,te->de", moe_in.astype(f32), grad_logits, precision=HIGHEST, preferred_element_type=f32
    )
    grad_moe_in = grad_moe_in + jnp.einsum(
        "te,de->td",
        grad_logits,
        router_full.astype(f32),
        precision=HIGHEST,
        preferred_element_type=f32,
    )
    moe_gain_grad = jnp.sum(grad_moe_in * normal_mid, axis=0)
    grad_middle = grad_out + norm_back(grad_moe_in * moe_scale, normal_mid, inverse_mid)
    grad_attended = grad_middle.astype(bf16)
    output_grad = jnp.einsum("tf,td->fd", heads_out, grad_attended, preferred_element_type=f32)
    grad_heads = (
        jnp.einsum("td,fd->tf", grad_attended, output_full, preferred_element_type=f32)
        .astype(bf16)
        .reshape(seq_len, local_heads, VDIM)
    )
    attn_probs = jnp.exp(scores_of() - log_total)
    probs_again = attn_probs.astype(bf16)
    grad_probs = jnp.einsum("ihd,jhd->hij", grad_heads, values, preferred_element_type=f32)
    grad_values = jnp.einsum("hij,ihd->jhd", probs_again, grad_heads, preferred_element_type=f32)
    grad_scores = (
        attn_probs * (grad_probs - jnp.sum(attn_probs * grad_probs, axis=-1, keepdims=True))
    ).astype(bf16)
    grad_q_nope = (
        jnp.einsum("hij,jhd->ihd", grad_scores, key_nope, preferred_element_type=f32) * score_scale
    )
    grad_q_rope = (
        jnp.einsum("hij,jd->ihd", grad_scores, key_rope, preferred_element_type=f32) * score_scale
    )
    grad_keys = (
        jnp.einsum("hij,ihd->jhd", grad_scores, query_nope, preferred_element_type=f32)
        * score_scale
    )
    grad_key_rope = (
        jnp.einsum("hij,ihd->jd", grad_scores, query_rope, preferred_element_type=f32) * score_scale
    )
    grad_query = (
        jnp.concatenate(
            [grad_q_nope, unrotate(grad_q_rope, cosine[:, None, :], sine_part[:, None, :])], axis=-1
        )
        .astype(bf16)
        .reshape(seq_len, local_heads * (NOPE + ROPE))
    )
    query_grad = jnp.einsum("td,tq->dq", normed, grad_query, preferred_element_type=f32)
    grad_normed = jnp.einsum("tq,dq->td", grad_query, query_full, preferred_element_type=f32)
    grad_kv = (
        jnp.concatenate([grad_keys, grad_values], axis=-1)
        .astype(bf16)
        .reshape(seq_len, local_heads * (NOPE + VDIM))
    )
    expand_grad = jnp.einsum("tr,tq->rq", latent, grad_kv, preferred_element_type=f32)
    grad_latent = jnp.einsum("tq,rq->tr", grad_kv, expand_full, preferred_element_type=f32)
    grad_normed, grad_latent, grad_key_rope = (
        lax.psum(grad_normed.astype(jnp.bfloat16), "tp").astype(jnp.float32),
        lax.psum(grad_latent.astype(jnp.bfloat16), "tp").astype(jnp.float32),
        lax.psum(grad_key_rope.astype(jnp.bfloat16), "tp").astype(jnp.float32),
    )
    latent_gain_grad = jnp.sum(grad_latent * latent_unit, axis=0)
    grad_latent_raw = norm_back(grad_latent * latent_scale, latent_unit, inverse_lat)
    grad_latent_lin = jnp.concatenate(
        [grad_latent_raw, unrotate(grad_key_rope, cosine, sine_part)], axis=-1
    ).astype(bf16)
    latent_grad = jnp.einsum("td,tr->dr", normed, grad_latent_lin, preferred_element_type=f32)
    grad_normed = grad_normed + jnp.einsum(
        "tr,dr->td", grad_latent_lin, latent_full, preferred_element_type=f32
    )
    norm_gain_grad = jnp.sum(grad_normed * normal_in, axis=0)
    input_grad = grad_middle + norm_back(grad_normed * norm_scale, normal_in, inverse_in)
    (
        norm_out,
        query_out,
        latent_out,
        lgain_out,
        expand_out,
        output_out,
        mgain_out,
        router_out,
        gate_out,
        up_out,
        down_out,
    ) = (
        lax.psum_scatter(norm_gain_grad, "fsdp", scatter_dimension=0, tiled=True),
        lax.psum_scatter(query_grad, "fsdp", scatter_dimension=0, tiled=True),
        lax.psum_scatter(latent_grad, "fsdp", scatter_dimension=0, tiled=True),
        lax.psum_scatter(latent_gain_grad, "fsdp", scatter_dimension=0, tiled=True),
        lax.psum_scatter(expand_grad, "fsdp", scatter_dimension=0, tiled=True),
        lax.psum_scatter(output_grad, "fsdp", scatter_dimension=1, tiled=True),
        lax.psum_scatter(moe_gain_grad, "fsdp", scatter_dimension=0, tiled=True),
        lax.psum_scatter(router_grad, "fsdp", scatter_dimension=0, tiled=True),
        lax.psum_scatter(gate_shared_grad, "fsdp", scatter_dimension=0, tiled=True),
        lax.psum_scatter(up_shared_grad, "fsdp", scatter_dimension=0, tiled=True),
        lax.psum_scatter(down_shared_grad, "fsdp", scatter_dimension=1, tiled=True),
    )
    own_start = lax.axis_index("tp") * inputs.shape[0]
    own_activations = lax.dynamic_slice_in_dim(activations, own_start, inputs.shape[0], 0)
    own_input_grad = lax.dynamic_slice_in_dim(input_grad, own_start, inputs.shape[0], 0)
    return (
        loss_value,
        own_activations,
        own_input_grad,
        norm_out,
        query_out,
        latent_out,
        lgain_out,
        expand_out,
        output_out,
        mgain_out,
        router_out,
        gate_out,
        up_out,
        down_out,
        expert_gate_grad,
        expert_up_grad,
        expert_down_grad,
    )


def shards(*arrays):
    fsdp_size = lax.axis_size("fsdp")
    seq_len = arrays[4].shape[0]
    experts = arrays[12].shape[1]
    capacity = arrays[4].shape[1] * seq_len * 4 // (3 * experts)
    fits = fsdp_size * seq_len <= 2 * experts * capacity and fsdp_size == experts
    aligned = arrays[5].shape[0] == BLOCK and arrays[13].shape[1] % BLOCK == 0
    if fits and aligned and fsdp_size % 4 == 0:
        return token_shards(*arrays)
    return slot_shards(*arrays)


def solution(mesh):
    return jax.shard_map(
        shards,
        mesh=mesh,
        in_specs=(
            P(("fsdp", "tp"), None),
            P("fsdp", None),
            P("fsdp"),
            P("fsdp"),
            P("fsdp", None),
            P("fsdp"),
            P("fsdp", "tp"),
            P("fsdp", None),
            P("fsdp"),
            P("fsdp", "tp"),
            P("tp", "fsdp"),
            P("fsdp"),
            P("fsdp", None),
            P("fsdp", "tp"),
            P("fsdp", "tp"),
            P("tp", "fsdp"),
            P("fsdp", None, "tp"),
            P("fsdp", None, "tp"),
            P("fsdp", "tp", None),
        ),
        out_specs=(
            P(),
            P(("fsdp", "tp"), None),
            P(("fsdp", "tp"), None),
            P("fsdp"),
            P("fsdp", "tp"),
            P("fsdp", None),
            P("fsdp"),
            P("fsdp", "tp"),
            P("tp", "fsdp"),
            P("fsdp"),
            P("fsdp", None),
            P("fsdp", "tp"),
            P("fsdp", "tp"),
            P("tp", "fsdp"),
            P("fsdp", None, "tp"),
            P("fsdp", None, "tp"),
            P("fsdp", "tp", None),
        ),
        check_vma=False,
    )
```

```python
import functools
import math

import jax
import jax.numpy as jnp
from jax import lax
from jax.experimental import pallas as pl
from jax.experimental.pallas import tpu as pltpu
from jax.sharding import PartitionSpec as P

HEADS = 16
NOPE = 128
ROPE = 64
RANK = 512
VDIM = 128


EPSILON = 1e-06
HIGHEST = lax.Precision.HIGHEST
MASKED = -1e30


def rope_tables(length, dim_size):
    places = jnp.arange(length).astype(jnp.float32)
    exponent = jnp.arange(dim_size // 2).astype(jnp.float32) * (2.0 / dim_size)
    angles = places[:, None] * jnp.exp(exponent * -math.log(10000.0))[None, :]
    return (jnp.cos(angles), jnp.sin(angles))


def rotate(values, cosine, sine_part):
    half_width = values.shape[-1] // 2
    lower_half = values[..., :half_width]
    upper_half = values[..., half_width:]
    return jnp.concatenate(
        [
            lower_half * cosine - upper_half * sine_part,
            upper_half * cosine + lower_half * sine_part,
        ],
        axis=-1,
    )


def unrotate(gradient, cosine, sine_part):
    half_width = gradient.shape[-1] // 2
    lower_half = gradient[..., :half_width]
    upper_half = gradient[..., half_width:]
    return jnp.concatenate(
        [
            lower_half * cosine + upper_half * sine_part,
            upper_half * cosine - lower_half * sine_part,
        ],
        axis=-1,
    )


def silu_parts(gate_act):
    sigmoid_val = jax.nn.sigmoid(gate_act)
    return (gate_act * sigmoid_val, sigmoid_val * (1.0 + gate_act * (1.0 - sigmoid_val)))


def norm_back(grad_scaled, unit_rows, inverse):
    return inverse * (
        grad_scaled - unit_rows * jnp.mean(grad_scaled * unit_rows, axis=-1, keepdims=True)
    )


def swap_tp(value):
    return lax.ppermute(value, "tp", [(0, 1), (1, 0)])


def half_rows(value, which, rows):
    return lax.dynamic_slice_in_dim(value, which * rows, rows, 0)


def tp_scatter(partial, which, rows):
    other = half_rows(partial, 1 - which, rows).astype(jnp.bfloat16)
    return half_rows(partial, which, rows) + swap_tp(other).astype(jnp.float32)


def tp_sum(partial):
    low_partial = partial.astype(jnp.bfloat16)
    return low_partial.astype(jnp.float32) + swap_tp(low_partial).astype(jnp.float32)


def tp_gather(own, which):
    other = swap_tp(own)
    first = jnp.where(which == 0, own, other)
    second = jnp.where(which == 0, other, own)
    return jnp.concatenate([first, second], axis=0)


MESH = pl.DeviceIdType.MESH
CROSS = ("x", "y", "up", "down")
BLOCK = 128


def both(first, second):
    if first is None:
        return second
    if second is None:
        return first
    return jnp.logical_and(first, second)


def under(condition, body):
    if condition is None:
        body()
    else:
        pl.when(condition)(body)


class Grid:
    def __init__(self, fsdp_size, dims, tie=-1):
        self.tie = tie
        index = lax.axis_index("fsdp")
        self.core = lax.rem(index, 2)
        self.y = lax.rem(lax.div(index, 2), 2)
        self.z = lax.div(index, 4)
        self.x = lax.axis_index("tp")
        self.depth = fsdp_size // 4
        self.dims = dims
        self.crosses = CROSS if "x" in dims else CROSS[1:]
        self.chips = self.depth * 2 * (2 if "x" in dims else 1)

    def device(self, x, y, z, core):
        return {"fsdp": z * 4 + y * 2 + core, "tp": x}

    def chip(self, x, y, z):
        return (z * 2 + y) * 2 + x if "x" in self.dims else z * 2 + y

    def here(self):
        return self.x, self.y, self.z

    def partner(self):
        return self.device(self.x, self.y, self.z, 1 - self.core)

    def neighbour(self, cross):
        if cross == "x":
            return (1 - self.x, self.y, self.z), None
        if cross == "y":
            return (self.x, 1 - self.y, self.z), None
        if cross == "up":
            return (self.x, self.y, self.z + 1), self.z + 1 < self.depth
        return (self.x, self.y, self.z - 1), self.z >= 1

    def level(self, rank):
        inner = jnp.logical_or(self.z == 1, self.z == 2)
        rank = jnp.where(jnp.logical_and(inner, rank >= 2), 5 - rank, rank)
        high, low = lax.div(self.z, 2), lax.rem(self.z, 2)
        far, near = lax.div(rank, 2), lax.rem(rank, 2)
        return 2 * (high + far - 2 * high * far) + (low + near - 2 * low * near)

    def entry(self, number):
        steps = (0, 1) if "x" in self.dims else (0,)
        found = [(r, dy, dx) for r in range(self.depth) for dy in (0, 1) for dx in steps]
        codes = [4 * e[0] + 2 * e[1] + e[2] for e in sorted(found, key=lambda e: (sum(e), self.tie * e[0]))]
        code = jnp.int32(0) + (codes[number] if isinstance(number, int) else 0)
        if not isinstance(number, int):
            for at, value in enumerate(codes):
                code = jnp.where(number == at, value, code)
        dx, dy = lax.rem(code, 2), lax.rem(lax.div(code, 2), 2)
        x, y = self.x + dx - 2 * self.x * dx, self.y + dy - 2 * self.y * dy
        return x, y, self.level(lax.div(code, 4))

    def children(self, order, chip):
        zero = dict(x=chip[0] == self.x, y=chip[1] == self.y, z=chip[2] == self.z)
        found, rest = [], None
        for dim in reversed(order):
            if dim == "z":
                found.append(("up", both(rest, (chip[2] <= self.z) & (self.z + 1 < self.depth))))
                found.append(("down", both(rest, (chip[2] >= self.z) & (self.z >= 1))))
            else:
                found.append((dim, both(rest, zero[dim])))
            rest = both(rest, zero[dim])
        return found

    def parent(self, order, chip):
        zero = dict(x=chip[0] == self.x, y=chip[1] == self.y, z=chip[2] == self.z)
        rest, turned = None, {}
        for dim in reversed(order):
            turned[dim] = both(rest, jnp.logical_not(zero[dim]))
            rest = both(rest, zero[dim])
        x = jnp.where(turned["x"], 1 - self.x, self.x) if "x" in order else self.x
        y = jnp.where(turned["y"], 1 - self.y, self.y)
        above = chip[2] > self.z
        z = jnp.where(turned["z"], jnp.where(above, self.z + 1, self.z - 1), self.z)
        side = jnp.where(above, self.crosses.index("down"), self.crosses.index("up"))
        side = jnp.where(turned["y"], self.crosses.index("y"), side)
        if "x" in order:
            side = jnp.where(turned["x"], self.crosses.index("x"), side)
        return (x, y, z), side

    def greet(self):
        barrier = pltpu.get_barrier_semaphore()
        pl.semaphore_signal(barrier, inc=1, device_id=self.partner(), device_id_type=MESH)
        count = 1
        for cross in self.crosses:
            chip, exists = self.neighbour(cross)

            def send(chip=chip):
                there = self.device(*chip, self.core)
                pl.semaphore_signal(barrier, inc=1, device_id=there, device_id_type=MESH)

            under(exists, send)
            count = count + (1 if exists is None else jnp.where(exists, 1, 0))
        pl.semaphore_wait(barrier, count)

    def greet_plane(self):
        barrier = pltpu.get_barrier_semaphore()
        size = self.depth * 4
        me = lax.axis_index("fsdp")

        def send(step, carry):
            there = {"fsdp": lax.rem(me + step, size), "tp": self.x}
            pl.semaphore_signal(barrier, inc=1, device_id=there, device_id_type=MESH)
            return carry

        lax.fori_loop(1, size, send, 0)
        pl.semaphore_wait(barrier, size - 1)


def owner_of(block, chips):
    extra = 2 * lax.rem(3 * (block - chips) + 1 + 3 * chips, chips) + 1
    return jnp.where(block < chips, 2 * block, extra)


def block_of(device, chips):
    back = pow(3, -1, chips)
    chip, core = lax.div(device, 2), lax.rem(device, 2)
    return jnp.where(core == 0, chip, chips + lax.rem(back * (chip - 1 + chips), chips))


class Exchange:
    def __init__(self, fsdp_size, tp, blocks, sources, targets, cut, to_owner, send_sem, recv_sem, own_sem):
        self.size, self.tp, self.blocks = fsdp_size, tp, blocks
        self.sources, self.targets, self.cut, self.to_owner = sources, targets, cut, to_owner
        self.send_sem, self.recv_sem, self.own_sem = send_sem, recv_sem, own_sem
        self.me = lax.axis_index("fsdp")
        self.block = block_of(self.me, fsdp_size // 2)
        self.owns = self.block < blocks

    def remote(self, array, block, other, there, send, recv):
        source, target = self.cut[array](self.sources[array], self.targets[array], block, other)
        return pltpu.make_async_remote_copy(
            src_ref=source,
            dst_ref=target,
            send_sem=self.send_sem.at[array, send],
            recv_sem=self.recv_sem.at[array, recv],
            device_id={"fsdp": there, "tp": self.tp},
            device_id_type=MESH,
        )

    def local(self, array, block):
        source, target = self.cut[array](self.sources[array], self.targets[array], block, self.me)
        return pltpu.make_async_copy(source, target, self.own_sem.at[array])

    def by_block(self, act, act_local, low, high):
        def one(number, carry):
            block = lax.rem(number + lax.div(self.me * self.blocks, self.size), self.blocks)
            owner = owner_of(block, self.size // 2)
            for array in range(len(self.sources)):
                if self.to_owner:
                    copy = self.remote(array, block, self.me, owner, block, self.me)
                else:
                    copy = self.remote(array, block, self.me, owner, 0, block)
                pl.when(self.me != owner)(getattr(copy, act))
                if act_local:
                    pl.when(self.me == owner)(getattr(self.local(array, block), act_local))
            return carry

        lax.fori_loop(low, high, one, 0)

    def by_device(self, act, act_local, low, high):
        def one(number, carry):
            other = lax.rem(self.me + number, self.size)
            for array in range(len(self.sources)):
                if self.to_owner:
                    copy = self.remote(array, self.block, other, other, 0, other)
                else:
                    copy = self.remote(array, self.block, other, other, other, self.block)
                pl.when(self.me != other)(getattr(copy, act))
                if act_local:
                    pl.when(self.me == other)(getattr(self.local(array, self.block), act_local))
            return carry

        def every():
            lax.fori_loop(low, high, one, 0)

        pl.when(self.owns)(every)

    def start(self, step, steps):
        total = self.blocks if self.to_owner else self.size
        low, high = lax.div(step * total, steps), lax.div((step + 1) * total, steps)
        (self.by_block if self.to_owner else self.by_device)("start", "start", low, high)

    def finish(self):
        if self.to_owner:
            self.by_device("wait_recv", None, 0, self.size)
            self.by_block("wait_send", "wait", 0, self.blocks)
        else:
            self.by_block("wait_recv", None, 0, self.blocks)
            self.by_device("wait_send", "wait", 0, self.size)


def exchange_sems(fsdp_size, arrays):
    dma = pltpu.SemaphoreType.DMA
    return [dma((arrays, fsdp_size)), dma((arrays, fsdp_size)), dma((arrays,))] if arrays else []


def gather_kernel(fsdp_size, pieces, places, count, blocks, cut, *refs):
    moved = len(cut)
    shards, sources = refs[:count], refs[count : count + moved]
    refs = refs[count + moved :]
    outs, targets = refs[:count], refs[count : count + moved]
    send_sem, recv_sem, pair_send, pair_recv, own_sem = refs[count + moved : count + moved + 5]
    grid = Grid(fsdp_size, "zy")
    exchange = Exchange(
        fsdp_size, grid.x, blocks, sources, targets, cut, True, *refs[count + moved + 5 :]
    )

    def target(piece, chip, core):
        array, first, rows, _ = pieces[piece]
        return places[array](outs[array], chip, core, first, rows)

    def source(piece, chip, own):
        array, first, rows, _ = pieces[piece]
        return shards[array].at[pl.ds(first, rows)] if own else target(piece, chip, grid.core)

    def hops(piece, chip, own):
        index, found = grid.chip(*chip), []
        for cross, wanted in grid.children(pieces[piece][3], chip):
            there, _ = grid.neighbour(cross)
            copy = pltpu.make_async_remote_copy(
                src_ref=source(piece, chip, own),
                dst_ref=target(piece, chip, grid.core),
                send_sem=send_sem.at[piece, index, grid.crosses.index(cross)],
                recv_sem=recv_sem.at[piece, index],
                device_id=grid.device(*there, grid.core),
                device_id_type=MESH,
            )
            found.append((wanted, copy))
        return found

    def pair(piece, chip, core, own=False, landing=False):
        index = grid.chip(*chip)
        return pltpu.make_async_remote_copy(
            src_ref=source(piece, chip, own),
            dst_ref=target(piece, chip, core),
            send_sem=pair_send.at[piece, index],
            recv_sem=(recv_sem if landing else pair_recv).at[piece, index],
            device_id=grid.partner(),
            device_id_type=MESH,
        )

    own_copies = [
        pltpu.make_async_copy(
            source(piece, grid.here(), True), target(piece, grid.here(), grid.core), own_sem.at[piece]
        )
        for piece in range(len(pieces))
    ]
    grid.greet_plane()

    def relay(chip, own):
        for piece in range(len(pieces)):
            if not own:
                pair(piece, chip, grid.core, landing=True).wait_recv()
            for wanted, copy in hops(piece, chip, own):
                under(wanted, copy.start)
            pair(piece, chip, grid.core, own).start()

    relay(grid.here(), True)
    for copy in own_copies:
        copy.start()

    def step(number, carry):
        relay(grid.entry(number), False)
        exchange.start(number - 1, grid.chips - 1)
        return carry

    lax.fori_loop(1, grid.chips, step, 0)

    def finish(number, carry):
        chip = grid.entry(number)
        for piece in range(len(pieces)):
            for wanted, copy in hops(piece, chip, False):
                under(wanted, copy.wait_send)
            pair(piece, chip, grid.core).wait_send()
            pair(piece, chip, 1 - grid.core).wait_recv()
        return carry

    lax.fori_loop(0, grid.chips, finish, 0)
    for copy in own_copies:
        copy.wait()
    exchange.finish()


def gather_call(fsdp_size, pieces, places, shards, shapes, collective_id, blocks, cut, sources, targets):
    count, chips = len(shards), fsdp_size // 2
    dma = pltpu.SemaphoreType.DMA
    moved = sum(s.size * s.dtype.itemsize for s in shapes)
    return pl.pallas_call(
        functools.partial(gather_kernel, fsdp_size, pieces, places, count, blocks, cut),
        out_shape=tuple(shapes) + tuple(targets),
        in_specs=[pl.BlockSpec(memory_space=pltpu.VMEM)] * count
        + [pl.BlockSpec(memory_space=pl.ANY)] * len(sources),
        out_specs=tuple([pl.BlockSpec(memory_space=pl.ANY)] * (count + len(targets))),
        scratch_shapes=[
            dma((len(pieces), chips, 4)),
            dma((len(pieces), chips)),
            dma((len(pieces), chips)),
            dma((len(pieces), chips)),
            dma((len(pieces),)),
            *exchange_sems(fsdp_size, len(sources)),
        ],
        compiler_params=pltpu.CompilerParams(collective_id=collective_id, has_side_effects=True),
        cost_estimate=pl.CostEstimate(flops=0, bytes_accessed=8 * moved, transcendentals=0),
    )(*shards, *sources)


class WeightGrads:
    inputs, outputs = 5, 3
    PIECES = (1, 3, 5)

    def __init__(self, slots, hidden, width):
        bf16 = jnp.bfloat16
        dma = pltpu.SemaphoreType.DMA
        self.hidden = hidden
        self.shapes = [jax.ShapeDtypeStruct((hidden, width), bf16)] * self.outputs
        self.scratch = [
            pltpu.VMEM((2, slots, BLOCK), bf16),
            pltpu.VMEM((slots, width), bf16),
            pltpu.VMEM((2, BLOCK, width), bf16),
            dma((2,)),
            dma((1,)),
            dma((2,)),
        ]

    def make(self, *refs):
        return WeightGradsRun(self, refs)


class WeightGradsRun:
    def __init__(self, job, refs):
        self.lefts, self.rights, self.outs = refs[:3], refs[3:5], refs[5:8]
        self.left, self.right, self.result = refs[8:11]
        self.left_sem, self.right_sem, self.out_sem = refs[11:]
        self.blocks = -(-job.hidden // BLOCK)
        self.rest = job.hidden - (self.blocks - 1) * BLOCK
        self.total = 3 * self.blocks

    def left_copy(self, which, number):
        slot, block = lax.rem(number, 2), lax.rem(number, self.blocks)
        span = pl.ds(pl.multiple_of(block * BLOCK, BLOCK), BLOCK)
        return pltpu.make_async_copy(
            self.lefts[which].at[:, span], self.left.at[slot], self.left_sem.at[slot]
        )

    def left_start(self, number):
        for which in range(3):
            pl.when(lax.div(number, self.blocks) == which)(self.left_copy(which, number).start)

    def right_copy(self, which):
        return pltpu.make_async_copy(self.rights[which], self.right, self.right_sem.at[0])

    def out_copies(self, which, number):
        slot, block = lax.rem(number, 2), lax.rem(number, self.blocks)
        full = pl.ds(pl.multiple_of(block * BLOCK, BLOCK), BLOCK)
        part = pl.ds((self.blocks - 1) * BLOCK, self.rest)
        out, sem = self.outs[which], self.out_sem.at[slot]
        return [
            (
                block < self.blocks - 1,
                pltpu.make_async_copy(self.result.at[slot], out.at[full], sem),
            ),
            (
                block == self.blocks - 1,
                pltpu.make_async_copy(self.result.at[slot, pl.ds(0, self.rest)], out.at[part], sem),
            ),
        ]

    def begin(self):
        self.right_copy(0).start()
        self.left_copy(0, jnp.int32(0)).start()

    def out_wait(self, number):
        for wanted, copy in self.out_copies(0, number):
            pl.when(wanted)(copy.wait)

    def run(self, number):
        slot = lax.rem(number, 2)
        self.left_copy(0, number).wait()
        pl.when(number + 1 < self.total)(lambda: self.left_start(number + 1))
        pl.when(lax.rem(number, 2 * self.blocks) == 0)(self.right_copy(0).wait)
        pl.when(number >= 2)(lambda: self.out_wait(number - 2))
        self.result[slot] = lax.dot_general(
            self.left[slot],
            self.right[...],
            (((0,), (0,)), ((), ())),
            preferred_element_type=jnp.float32,
        ).astype(jnp.bfloat16)
        for which in range(3):
            for wanted, copy in self.out_copies(which, number):
                pl.when(wanted & (lax.div(number, self.blocks) == which))(copy.start)
        pl.when(number == 2 * self.blocks - 1)(self.right_copy(1).start)

    def tick(self, step, piece):
        if piece in WeightGrads.PIECES:
            number = step * len(WeightGrads.PIECES) + WeightGrads.PIECES.index(piece)
            pl.when(number < self.total)(lambda: self.run(number))

    def finish(self):
        for number in (self.total - 2, self.total - 1):
            self.out_wait(jnp.int32(0) + number)


def reduce_kernel(fsdp_size, dims, pieces, places, count, blocks, cut, side, *refs):
    moved, taken = len(cut), side.inputs if side else 0
    partials, sources = refs[:count], refs[count : count + moved]
    side_refs = refs[count + moved : count + moved + taken]
    refs = refs[count + moved + taken :]
    outs, targets = refs[:count], refs[count : count + moved]
    refs = refs[count + moved :]
    if side:
        side_refs, refs = side_refs + refs[: side.outputs], refs[side.outputs :]
    held, other, landed = (refs[i * count : (1 + i) * count] for i in range(3))
    send_sem, recv_sem, load_sem, pair_send, pair_recv = refs[3 * count : 3 * count + 5]
    refs = refs[3 * count + 5 :]
    grid = Grid(fsdp_size, dims)
    ways = len(grid.crosses)
    empty = grid.chips * ways
    exchange, job = None, None
    if moved:
        exchange = Exchange(fsdp_size, grid.x, blocks, sources, targets, cut, False, *refs[:3])
        refs = refs[3:]
    if side:
        job = side.make(*side_refs, *refs)

    def load(array, chip):
        index = grid.chip(*chip)
        return pltpu.make_async_copy(
            places[array](partials[array], chip, grid.core),
            held[array].at[index],
            load_sem.at[array, index],
        )

    def pair(array, chip):
        index = grid.chip(*chip)
        return pltpu.make_async_remote_copy(
            src_ref=places[array](partials[array], chip, 1 - grid.core),
            dst_ref=other[array].at[index],
            send_sem=pair_send.at[array, index],
            recv_sem=pair_recv.at[array, index],
            device_id=grid.partner(),
            device_id_type=MESH,
        )

    def hop(piece, chip, there, side_seen):
        array, first, rows, _ = pieces[piece]
        index = grid.chip(*chip)
        slot = index * ways + side_seen
        return pltpu.make_async_remote_copy(
            src_ref=held[array].at[index, pl.ds(first, rows)],
            dst_ref=landed[array].at[slot, pl.ds(first, rows)],
            send_sem=send_sem.at[piece, index],
            recv_sem=recv_sem.at[piece, slot],
            device_id=grid.device(*there, grid.core),
            device_id_type=MESH,
        )

    def add_up(piece, chip, root):
        array, first, rows, order = pieces[piece]
        index, slots, some = grid.chip(*chip), [], grid.z < 0
        for cross, wanted in grid.children(order, chip):
            way = grid.crosses.index(cross)
            under(wanted, hop(piece, chip, grid.here(), way).wait_recv)
            slot = index * ways + way
            slots.append(slot if wanted is None else jnp.where(wanted, slot, empty))
            some = None if wanted is None or some is None else jnp.logical_or(some, wanted)
        tile = 16 if rows % 16 == 0 else rows

        def add_all(used):
            def add(i, carry):
                span = pl.ds(pl.multiple_of(first + i * tile, tile), tile)
                total = held[array][index, span].astype(jnp.float32)
                total += other[array][index, span].astype(jnp.float32)
                for slot in used:
                    total += landed[array][slot, span].astype(jnp.float32)
                if root:
                    outs[array][span] = total
                else:
                    held[array][index, span] = total.astype(held[array].dtype)
                return carry

            lax.fori_loop(0, rows // tile, add, 0)

        if root or some is None:
            add_all(slots)
        else:
            pl.when(some)(lambda: add_all(slots))
            pl.when(jnp.logical_not(some))(lambda: add_all([]))

    def fetched(array, chip):
        load(array, chip).wait()
        pair(array, chip).wait_recv()

    firsts = [min(p for p, piece in enumerate(pieces) if piece[0] == a) for a in range(count)]
    for array in range(count):
        landed[array][empty] = jnp.zeros(landed[array].shape[1:], landed[array].dtype)
    if moved:
        grid.greet_plane()
    else:
        grid.greet()
    last = grid.chips - 1

    def begin(number, carry):
        chip = grid.entry(last - number)
        for array in range(count):
            load(array, chip).start()
            pair(array, chip).start()
        return carry

    lax.fori_loop(0, grid.chips, begin, 0)
    if job:
        job.begin()

    def step(number, carry):
        chip = grid.entry(last - number)
        for piece in range(len(pieces)):
            if piece in firsts:
                fetched(pieces[piece][0], chip)
            add_up(piece, chip, False)
            hop(piece, chip, *grid.parent(pieces[piece][3], chip)).start()
            if job:
                job.tick(number, piece)
        if exchange:
            exchange.start(number, last)
        return carry

    lax.fori_loop(0, last, step, 0)
    if job:
        job.finish()
    for piece in range(len(pieces)):
        if piece in firsts:
            fetched(pieces[piece][0], grid.here())
        add_up(piece, grid.here(), True)

    def finish(number, carry):
        chip = grid.entry(last - number)
        for array in range(count):
            pair(array, chip).wait_send()

        def sent():
            for piece in range(len(pieces)):
                hop(piece, chip, *grid.parent(pieces[piece][3], chip)).wait_send()

        pl.when(number < last)(sent)
        return carry

    lax.fori_loop(0, grid.chips, finish, 0)
    if exchange:
        exchange.finish()


def reduce_call(
    fsdp_size,
    dims,
    pieces,
    places,
    partials,
    shapes,
    collective_id,
    blocks=0,
    cut=(),
    sources=(),
    targets=(),
    side=None,
    extra=(),
):
    count = len(partials)
    ways = 4 if "x" in dims else 3
    chips = fsdp_size // 2 * (2 if "x" in dims else 1)
    dma = pltpu.SemaphoreType.DMA
    held = [pltpu.VMEM((chips, *s), p.dtype) for s, p in zip(shapes, partials)]
    landed = [pltpu.VMEM((chips * ways + 1, *s), p.dtype) for s, p in zip(shapes, partials)]
    moved = sum(p.size * p.dtype.itemsize for p in partials)
    side_outs = tuple(side.shapes) if side else ()
    return pl.pallas_call(
        functools.partial(reduce_kernel, fsdp_size, dims, pieces, places, count, blocks, cut, side),
        out_shape=tuple(jax.ShapeDtypeStruct(s, jnp.float32) for s in shapes)
        + tuple(targets)
        + side_outs,
        in_specs=[pl.BlockSpec(memory_space=pl.ANY)] * (count + len(sources) + len(extra)),
        out_specs=tuple(
            [pl.BlockSpec(memory_space=pltpu.VMEM)] * count
            + [pl.BlockSpec(memory_space=pl.ANY)] * (len(targets) + len(side_outs))
        ),
        scratch_shapes=[
            *held,
            *held,
            *landed,
            dma((len(pieces), chips)),
            dma((len(pieces), chips * ways)),
            dma((count, chips)),
            dma((count, chips)),
            dma((count, chips)),
            *exchange_sems(fsdp_size, len(sources)),
            *(side.scratch if side else ()),
        ],
        compiler_params=pltpu.CompilerParams(
            collective_id=collective_id, has_side_effects=True, vmem_limit_bytes=67043328
        ),
        cost_estimate=pl.CostEstimate(flops=0, bytes_accessed=16 * moved, transcendentals=0),
    )(*partials, *sources, *extra)


def token_row(chip, core, rows):
    x, y, z = chip
    return ((z * 4 + y * 2 + core) * 2 + x) * rows


def reduce_tokens(partials, collective_id):
    fsdp_size = lax.axis_size("fsdp")
    rows = partials[0].shape[0] // (2 * fsdp_size)
    unit = rows // 4

    def place(ref, chip, core):
        return ref.at[pl.ds(pl.multiple_of(token_row(chip, core, rows), 16), rows)]

    pieces = [(0, at * unit, unit, order) for at, order in enumerate(("xyz", "zyx", "zxy", "zyx"))]
    pieces += [(array, 0, rows, "zyx") for array in range(1, len(partials))]
    shapes = [(rows, p.shape[1]) for p in partials]
    return reduce_call(
        fsdp_size, "xyz", pieces, [place] * len(partials), partials, shapes, collective_id
    )


def plane_row(chip, core):
    return chip[2] * 4 + chip[1] * 2 + core


def row_place(rows):
    def place(ref, chip, core, first=0, count=rows):
        return ref.at[pl.ds(pl.multiple_of(plane_row(chip, core) * rows + first, 8), count)]

    return place


def column_place(columns, rows):
    def place(ref, chip, core, first=0, count=rows):
        start = pl.multiple_of(plane_row(chip, core) * columns, 128)
        return ref.at[pl.ds(first, count), pl.ds(start, columns)]

    return place


def weight_pieces(query, latent, expand, output, small):
    return [
        (4, 0, small, "zy"),
        (0, 0, query // 2, "zy"),
        (1, 0, latent, "zy"),
        (0, query // 2, query // 2, "zy"),
        (2, 0, expand, "yz"),
        (3, 0, output // 2, "zy"),
        (3, output // 2, output // 2, "zy"),
    ]


def block_span(block):
    return pl.ds(pl.multiple_of(block * BLOCK, BLOCK), BLOCK)


def cut_columns(rows):
    def to_owner(source, target, block, other):
        there = pl.ds(pl.multiple_of(other * rows, rows), rows)
        return source.at[:, block_span(block)], target.at[there]

    def from_owner(source, target, block, other):
        there = pl.ds(pl.multiple_of(other * rows, rows), rows)
        return source.at[there], target.at[:, block_span(block)]

    return to_owner, from_owner


def cut_rows(columns):
    def to_owner(source, target, block, other):
        there = pl.ds(pl.multiple_of(other * columns, columns), columns)
        return source.at[block_span(block)], target.at[:, there]

    def from_owner(source, target, block, other):
        there = pl.ds(pl.multiple_of(other * columns, columns), columns)
        return source.at[:, there], target.at[block_span(block)]

    return to_owner, from_owner


def gather_weights(query, latent, expand, output, small, gate, up, down, collective_id):
    size = lax.axis_size("fsdp")
    shards = [query, latent, expand, output, small]
    places = [row_place(s.shape[0]) for s in shards]
    shapes = [
        jax.ShapeDtypeStruct((s.shape[0] * size, s.shape[1]), s.dtype) for s in shards
    ]
    for at in (1, 3):
        rows, columns = shards[at].shape
        places[at] = column_place(columns, rows)
        shapes[at] = jax.ShapeDtypeStruct((rows, columns * size), shards[at].dtype)
    columns, rows = cut_columns(gate.shape[0]), cut_rows(down.shape[1])
    tall = jax.ShapeDtypeStruct((gate.shape[0] * size, BLOCK), gate.dtype)
    flat = jax.ShapeDtypeStruct((BLOCK, down.shape[1] * size), down.dtype)
    return gather_call(
        size,
        weight_pieces(*[s.shape[0] for s in shards]),
        places,
        shards,
        shapes,
        collective_id,
        gate.shape[1] // BLOCK,
        (columns[0], columns[0], rows[0]),
        [gate, up, down],
        [tall, tall, flat],
    )


def reduce_weights(
    query, latent, expand, output, small, gate, up, down, blocks, collective_id, side, extra
):
    size = lax.axis_size("fsdp")
    partials = [query, latent, expand, output, small]
    shapes = [(p.shape[0] // size, p.shape[1]) for p in partials]
    places = [row_place(s[0]) for s in shapes]
    for at in (1, 3):
        rows, columns = partials[at].shape
        shapes[at] = (rows, columns // size)
        places[at] = column_place(columns // size, rows)
    columns, rows = cut_columns(gate.shape[0] // size), cut_rows(down.shape[1] // size)
    wide = jax.ShapeDtypeStruct((gate.shape[0] // size, blocks * BLOCK), gate.dtype)
    long = jax.ShapeDtypeStruct((blocks * BLOCK, down.shape[1] // size), down.dtype)
    return reduce_call(
        size,
        "zy",
        weight_pieces(*[s[0] for s in shapes]),
        places,
        partials,
        shapes,
        collective_id,
        blocks,
        (columns[1], columns[1], rows[1]),
        [gate, up, down],
        [wide, wide, long],
        side,
        extra,
    )


class Spread:
    ORDERS = ("xyz", "zyx", "zxy", "zyx")
    LEAD = 3

    def __init__(self, fsdp_size, own, room, sems):
        self.grid = Grid(fsdp_size, "xyz", 1)
        self.own, self.room = own, room
        self.rows = own.shape[0]
        self.part = self.rows // len(self.ORDERS)
        self.send_sem, self.recv_sem, self.pair_send, self.pair_recv = sems
        self.units = fsdp_size // 2

    def unit(self, step):
        grid = self.grid
        flip = lax.rem(step, 2)
        return grid.y + flip - 2 * grid.y * flip, grid.level(lax.div(step, 2))

    def span(self, chip, piece):
        start = token_row(chip, self.grid.core, self.rows) + piece * self.part
        return self.room.at[pl.ds(pl.multiple_of(start, self.part), self.part)]

    def copies(self, chip, piece, own=False):
        grid, found = self.grid, []
        index, here = grid.chip(*chip), self.span(chip, piece)
        source = self.own.at[pl.ds(piece * self.part, self.part)] if own else here
        for cross, wanted in grid.children(self.ORDERS[piece], chip):
            there, _ = grid.neighbour(cross)
            copy = pltpu.make_async_remote_copy(
                src_ref=source,
                dst_ref=here,
                send_sem=self.send_sem.at[piece, index, grid.crosses.index(cross)],
                recv_sem=self.recv_sem.at[piece, index],
                device_id=grid.device(*there, grid.core),
                device_id_type=MESH,
            )
            found.append((wanted, copy))
        return found

    def pair(self, chip, piece, own=False, landing=False):
        grid = self.grid
        index, here = grid.chip(*chip), self.span(chip, piece)
        return pltpu.make_async_remote_copy(
            src_ref=self.own.at[pl.ds(piece * self.part, self.part)] if own else here,
            dst_ref=here,
            send_sem=self.pair_send.at[piece, index],
            recv_sem=(self.recv_sem if landing else self.pair_recv).at[piece, index],
            device_id=grid.partner(),
            device_id_type=MESH,
        )

    def relay(self, chip, piece, own=False):
        if not own:
            self.pair(chip, piece, landing=True).wait_recv()
        for wanted, copy in self.copies(chip, piece, own):
            under(wanted, copy.start)
        self.pair(chip, piece, own).start()

    def begin(self):
        grid = self.grid
        grid.greet()
        for piece in range(len(self.ORDERS)):
            self.relay(grid.here(), piece, own=True)
        start = token_row(grid.here(), grid.core, self.rows)
        self.room[pl.ds(pl.multiple_of(start, self.rows), self.rows)] = self.own[...]

        def early(number, carry):
            chip = grid.entry(number)
            for piece in range(len(self.ORDERS)):
                self.relay(chip, piece)
            return carry

        lax.fori_loop(1, self.LEAD, early, 0)

    def ahead(self, step):
        return [self.grid.entry(self.LEAD + 2 * step + one) for one in (0, 1)]

    def tick(self, step, chips, number):
        pieces = len(self.ORDERS)
        late = self.LEAD + 2 * step + number // pieces
        chip = chips[number // pieces]
        pl.when(late < 2 * self.units)(lambda: self.relay(chip, number % pieces))

    def arrived(self, step):
        y, z = self.unit(step)
        for x in (0, 1):
            for piece in range(len(self.ORDERS)):
                self.pair((x, y, z), piece).wait_recv()

    def drain(self):
        def finish(number, carry):
            chip = self.grid.entry(number)
            for piece in range(len(self.ORDERS)):
                for wanted, copy in self.copies(chip, piece):
                    under(wanted, copy.wait_send)
                self.pair(chip, piece).wait_send()
            return carry

        lax.fori_loop(0, 2 * self.units, finish, 0)


def spread_sems(fsdp_size):
    dma = pltpu.SemaphoreType.DMA
    return [dma((4, fsdp_size, 4)), dma((4, fsdp_size)), dma((4, fsdp_size)), dma((4, fsdp_size))]


class Stage:
    def __init__(self, buffers, results, sems):
        self.buffers, self.results, self.sems = buffers, results, sems

    def copy(self, number, step, unit):
        buffer = self.buffers[number]
        rows = buffer.shape[1]
        slot = lax.rem(step, 2)
        there = self.results[number].at[pl.ds(pl.multiple_of(unit * rows, rows), rows)]
        return pltpu.make_async_copy(buffer.at[slot], there, self.sems.at[number, slot])

    def reuse(self, step):
        def wait():
            for number in range(len(self.buffers)):
                self.copy(number, step, 0).wait()

        pl.when(step >= 2)(wait)

    def put(self, number, step, unit):
        self.copy(number, step, unit).start()

    def finish(self, steps):
        for step in (steps - 2, steps - 1):
            for number in range(len(self.buffers)):
                self.copy(number, step, 0).wait()


def dot(left, right):
    return jnp.dot(left, right, preferred_element_type=jnp.float32)


def dot_nt(left, right):
    return lax.dot_general(
        left, right, (((1,), (1,)), ((), ())), preferred_element_type=jnp.float32
    )


def dispatch_of(place_ref, sequence, capacity, seq_len):
    row = place_ref[pl.ds(sequence, 1), :]
    slot = lax.broadcasted_iota(jnp.int32, (capacity, seq_len), 0)
    return jnp.where(slot == row, 1.0, 0.0)


def forward_kernel(
    fsdp_size,
    experts,
    capacity,
    own,
    place_ref,
    gate_hbm,
    up_hbm,
    down_hbm,
    wide_hbm,
    block_hbm,
    tokens_out,
    received_out,
    gate_out,
    up_out,
    hidden_out,
    weight_out,
    shared_out,
    sh_out,
    part_out,
    room,
    picks,
    packs,
    chances,
    tall,
    received,
    gate_act,
    up_act,
    hidden,
    weight,
    shared,
    sh_act,
    part,
    gate_ref,
    up_ref,
    down_ref,
    wide_ref,
    block_ref,
    weight_sem,
    stage_sem,
    room_sem,
    *sems,
):
    f32, bf16 = jnp.float32, jnp.bfloat16
    seq_len = place_ref.shape[1]
    spread = Spread(fsdp_size, own, room, sems)
    expert = lax.axis_index("fsdp")
    stage = Stage(
        [received, gate_act, up_act, hidden, weight, shared, sh_act, part],
        [received_out, gate_out, up_out, hidden_out, weight_out, shared_out, sh_out, part_out],
        stage_sem,
    )
    lanes = lax.broadcasted_iota(jnp.int32, (2 * seq_len, BLOCK), 1)

    def tokens_copy(unit):
        span = pl.ds(pl.multiple_of(unit * 2 * seq_len, 2 * seq_len), 2 * seq_len)
        return pltpu.make_async_copy(room.at[span], tokens_out.at[span], room_sem.at[unit])

    weights = [
        pltpu.make_async_copy(source, target, weight_sem.at[number])
        for number, (source, target) in enumerate([(gate_hbm, gate_ref), (up_hbm, up_ref), (down_hbm, down_ref), (wide_hbm, wide_ref), (block_hbm, block_ref)])
    ]
    for copy in weights:
        copy.start()
    spread.begin()
    for copy in weights:
        copy.wait()
    units = down_ref.shape[0]
    if units < hidden.shape[2]:
        hidden[:, :, units:] = jnp.zeros((2, 2 * capacity, hidden.shape[2] - units), bf16)
    for one in (0, 1):
        tall[one, capacity:] = block_ref[...]

    def body(step, carry):
        slot = lax.rem(step, 2)
        y, z = spread.unit(step)
        unit = z * 2 + y
        chips = spread.ahead(step)
        spread.arrived(step)
        tokens_copy(unit).start()
        stage.reuse(step)
        rows = [
            pl.ds(pl.multiple_of((2 * unit + one) * seq_len, seq_len), seq_len) for one in (0, 1)
        ]
        slots = [pl.ds(one * capacity, capacity) for one in (0, 1)]
        own_rows = [pl.ds(one * seq_len, seq_len) for one in (0, 1)]
        spread.tick(step, chips, 0)
        for one in (0, 1):
            pick = dispatch_of(place_ref, 2 * unit + one, capacity, seq_len)
            picks[one] = pick.astype(bf16)
            packs[one, :, :capacity] = jnp.transpose(pick).astype(bf16)
            received[slot, slots[one]] = dot(picks[one], room[rows[one]]).astype(bf16)
        stage.put(0, step, unit)
        spread.tick(step, chips, 1)
        both_rows = pl.ds(pl.multiple_of(unit * 2 * seq_len, 2 * seq_len), 2 * seq_len)
        wide = dot(room[both_rows], wide_ref[...])
        shared[slot] = wide[:, : 2 * BLOCK]
        gate_sh, up_sh = wide[:, :BLOCK], wide[:, BLOCK : 2 * BLOCK]
        act = (silu_parts(gate_sh)[0] * up_sh).astype(bf16)
        sh_act[slot] = act
        for one in (0, 1):
            packs[one, :, capacity:] = act[one * seq_len : (one + 1) * seq_len]
        logits = jnp.where(lanes < experts, wide[:, 2 * BLOCK :], MASKED)
        logit_exp = jnp.exp(logits - jnp.max(logits, axis=1, keepdims=True))
        chance = jnp.sum(jnp.where(lanes == expert, logit_exp, 0.0), axis=1, keepdims=True)
        chance = chance / jnp.sum(logit_exp, axis=1, keepdims=True)
        coarse = chance.astype(bf16).astype(f32)
        chances[...] = jnp.where(
            lanes == 0, coarse, jnp.where(lanes == 1, chance - coarse, 0.0)
        ).astype(bf16)
        stage.put(5, step, unit)
        stage.put(6, step, unit)
        spread.tick(step, chips, 2)
        gate_act[slot] = dot_nt(received[slot], gate_ref[...])
        stage.put(1, step, unit)
        spread.tick(step, chips, 3)
        up_act[slot] = dot_nt(received[slot], up_ref[...])
        stage.put(2, step, unit)
        spread.tick(step, chips, 4)
        for one in (0, 1):
            halves = dot(picks[one], chances[own_rows[one]])
            scale = halves[:, 0:1] + halves[:, 1:2]
            weight[slot, slots[one]] = jnp.broadcast_to(scale, (capacity, BLOCK))
            act = silu_parts(gate_act[slot, slots[one]])[0] * up_act[slot, slots[one]]
            hidden[slot, slots[one], :units] = (scale * act).astype(bf16)
        stage.put(3, step, unit)
        stage.put(4, step, unit)
        spread.tick(step, chips, 5)
        result = dot(hidden[slot, :, :units], down_ref[...]).astype(bf16)
        for one in (0, 1):
            tall[one, :capacity] = result[one * capacity : (one + 1) * capacity]
        spread.tick(step, chips, 6)
        part[slot, own_rows[0]] = dot(packs[0], tall[0]).astype(bf16)
        spread.tick(step, chips, 7)
        part[slot, own_rows[1]] = dot(packs[1], tall[1]).astype(bf16)
        stage.put(7, step, unit)
        return carry

    lax.fori_loop(0, spread.units, body, 0)
    stage.finish(spread.units)
    for unit in range(spread.units):
        tokens_copy(unit).wait()
    spread.drain()


def experts_forward(own, place, gate, up, down, wide, block, capacity, experts, collective_id):
    fsdp_size = lax.axis_size("fsdp")
    f32, bf16 = jnp.float32, jnp.bfloat16
    seq_len, width, hidden = place.shape[1], own.shape[1], gate.shape[0]
    tokens, slots = fsdp_size * seq_len, fsdp_size * capacity
    padded = -(-hidden // BLOCK) * BLOCK
    shape = jax.ShapeDtypeStruct
    outs = [
        shape((tokens, width), bf16),
        shape((slots, width), bf16),
        shape((slots, hidden), f32),
        shape((slots, hidden), f32),
        shape((slots, padded), bf16),
        shape((slots, BLOCK), f32),
        shape((tokens, 2 * BLOCK), f32),
        shape((tokens, BLOCK), bf16),
        shape((tokens, width), bf16),
    ]
    stages = [pltpu.VMEM((2, 2 * o.shape[0] // fsdp_size, o.shape[1]), o.dtype) for o in outs[1:]]
    dma = pltpu.SemaphoreType.DMA
    return pl.pallas_call(
        functools.partial(forward_kernel, fsdp_size, experts, capacity),
        out_shape=tuple(outs),
        in_specs=[pl.BlockSpec(memory_space=pltpu.VMEM)] * 2
        + [pl.BlockSpec(memory_space=pl.ANY)] * 5,
        out_specs=tuple([pl.BlockSpec(memory_space=pl.ANY)] * len(outs)),
        scratch_shapes=[
            pltpu.VMEM((tokens, width), bf16),
            pltpu.VMEM((2, capacity, seq_len), bf16),
            pltpu.VMEM((2, seq_len, capacity + BLOCK), bf16),
            pltpu.VMEM((2 * seq_len, BLOCK), bf16),
            pltpu.VMEM((2, capacity + BLOCK, width), bf16),
            *stages,
            *[pltpu.VMEM(w.shape, w.dtype) for w in (gate, up, down, wide, block)],
            dma((5,)),
            dma((len(stages), 2)),
            dma((fsdp_size // 2,)),
            *spread_sems(fsdp_size),
        ],
        compiler_params=pltpu.CompilerParams(
            collective_id=collective_id, has_side_effects=True, vmem_limit_bytes=67043328
        ),
        cost_estimate=pl.CostEstimate(
            flops=6 * slots * width * hidden, bytes_accessed=100_000_000, transcendentals=0
        ),
    )(own, place, gate, up, down, wide, block)


def backward_kernel(
    fsdp_size,
    capacity,
    own,
    place_ref,
    gate_hbm,
    up_hbm,
    down_hbm,
    pair_hbm,
    block_hbm,
    gate_in,
    up_in,
    weight_in,
    shared_in,
    grads_out,
    slots_out,
    gate_out,
    up_out,
    pair_out,
    chance_out,
    part_out,
    room,
    picks,
    packs,
    tall,
    gate_act,
    up_act,
    weight,
    shared,
    picked,
    gate_grad,
    up_grad,
    pair_grad,
    chance_grad,
    part,
    gate_ref,
    up_ref,
    down_ref,
    pair_ref,
    block_ref,
    weight_sem,
    load_sem,
    stage_sem,
    room_sem,
    *sems,
):
    f32, bf16 = jnp.float32, jnp.bfloat16
    seq_len = place_ref.shape[1]
    spread = Spread(fsdp_size, own, room, sems)
    expert = lax.axis_index("fsdp")
    stage = Stage(
        [picked, gate_grad, up_grad, pair_grad, chance_grad, part],
        [slots_out, gate_out, up_out, pair_out, chance_out, part_out],
        stage_sem,
    )
    saved = [gate_in, up_in, weight_in, shared_in]
    loads = [gate_act, up_act, weight, shared]

    def load(number, step):
        y, z = spread.unit(step)
        slot, rows = lax.rem(step, 2), loads[number].shape[1]
        span = pl.ds(pl.multiple_of((z * 2 + y) * rows, rows), rows)
        return pltpu.make_async_copy(
            saved[number].at[span], loads[number].at[slot], load_sem.at[number, slot]
        )

    def grads_copy(unit):
        span = pl.ds(pl.multiple_of(unit * 2 * seq_len, 2 * seq_len), 2 * seq_len)
        return pltpu.make_async_copy(room.at[span], grads_out.at[span], room_sem.at[unit])

    for number in range(len(saved)):
        load(number, 0).start()
    weights = [
        pltpu.make_async_copy(source, target, weight_sem.at[number])
        for number, (source, target) in enumerate([(gate_hbm, gate_ref), (up_hbm, up_ref), (down_hbm, down_ref), (pair_hbm, pair_ref), (block_hbm, block_ref)])
    ]
    for copy in weights:
        copy.start()
    spread.begin()
    for copy in weights:
        copy.wait()
    units = down_ref.shape[0]
    if units < gate_grad.shape[2]:
        for grad in (gate_grad, up_grad):
            grad[:, :, units:] = jnp.zeros((2, 2 * capacity, grad.shape[2] - units), bf16)
    for one in (0, 1):
        tall[one, capacity:] = pair_ref[...]
    expert_lane = lax.broadcasted_iota(jnp.int32, (capacity, BLOCK), 1) == expert

    def body(step, carry):
        slot = lax.rem(step, 2)
        y, z = spread.unit(step)
        unit = z * 2 + y
        later = step + 1
        chips = spread.ahead(step)
        spread.arrived(step)
        grads_copy(unit).start()
        stage.reuse(step)
        rows = [
            pl.ds(pl.multiple_of((2 * unit + one) * seq_len, seq_len), seq_len) for one in (0, 1)
        ]
        both_rows = pl.ds(pl.multiple_of(unit * 2 * seq_len, 2 * seq_len), 2 * seq_len)
        slots = [pl.ds(one * capacity, capacity) for one in (0, 1)]
        own_rows = [pl.ds(one * seq_len, seq_len) for one in (0, 1)]
        for number in range(len(saved)):
            load(number, step).wait()

        def ahead():
            for number in range(len(saved)):
                load(number, later).start()

        pl.when(later < spread.units)(ahead)
        spread.tick(step, chips, 0)
        for one in (0, 1):
            pick = dispatch_of(place_ref, 2 * unit + one, capacity, seq_len)
            picks[one] = pick.astype(bf16)
            packs[one, :, :capacity] = jnp.transpose(pick).astype(bf16)
            picked[slot, slots[one]] = dot(picks[one], room[rows[one]]).astype(bf16)
        stage.put(0, step, unit)
        spread.tick(step, chips, 1)
        raw = dot_nt(picked[slot], down_ref[...])
        scale = weight[slot, :, 0:1]
        silu_gate, slope = silu_parts(gate_act[slot])
        up_value = up_act[slot]
        gate_sum = jnp.sum(raw * (silu_gate * up_value), axis=1, keepdims=True)
        scaled = scale * raw
        gate_grad[slot, :, :units] = (scaled * up_value * slope).astype(bf16)
        up_grad[slot, :, :units] = (scaled * silu_gate).astype(bf16)
        stage.put(1, step, unit)
        stage.put(2, step, unit)
        spread.tick(step, chips, 2)
        for one in (0, 1):
            column = gate_sum[one * capacity : (one + 1) * capacity]
            column = jnp.where(expert_lane, column, 0.0).astype(bf16)
            chance_grad[slot, own_rows[one]] = dot(packs[one, :, :capacity], column).astype(bf16)
        stage.put(4, step, unit)
        grad_sh = dot_nt(room[both_rows], block_ref[...])
        silu_sh, slope_sh = silu_parts(shared[slot, :, :BLOCK])
        gate_sh = (grad_sh * shared[slot, :, BLOCK:] * slope_sh).astype(bf16)
        up_sh = (grad_sh * silu_sh).astype(bf16)
        pair_grad[slot, :, :BLOCK] = gate_sh
        pair_grad[slot, :, BLOCK:] = up_sh
        for one in (0, 1):
            own_seq = slice(one * seq_len, (one + 1) * seq_len)
            packs[one, :, capacity : capacity + BLOCK] = gate_sh[own_seq]
            packs[one, :, capacity + BLOCK :] = up_sh[own_seq]
        stage.put(3, step, unit)
        spread.tick(step, chips, 3)
        back = dot(gate_grad[slot, :, :units], gate_ref[...])
        spread.tick(step, chips, 4)
        back = (back + dot(up_grad[slot, :, :units], up_ref[...])).astype(bf16)
        for one in (0, 1):
            tall[one, :capacity] = back[one * capacity : (one + 1) * capacity]
        spread.tick(step, chips, 5)
        part[slot, own_rows[0]] = dot(packs[0], tall[0]).astype(bf16)
        spread.tick(step, chips, 6)
        part[slot, own_rows[1]] = dot(packs[1], tall[1]).astype(bf16)
        stage.put(5, step, unit)
        spread.tick(step, chips, 7)
        return carry

    lax.fori_loop(0, spread.units, body, 0)
    stage.finish(spread.units)
    for unit in range(spread.units):
        grads_copy(unit).wait()
    spread.drain()


def experts_backward(
    own, place, gate, up, down, pair, block, gate_act, up_act, weight, shared, capacity, collective_id
):
    fsdp_size = lax.axis_size("fsdp")
    bf16 = jnp.bfloat16
    seq_len, width, hidden = place.shape[1], own.shape[1], gate.shape[0]
    tokens, slots = fsdp_size * seq_len, fsdp_size * capacity
    padded = -(-hidden // BLOCK) * BLOCK
    shape = jax.ShapeDtypeStruct
    outs = [
        shape((tokens, width), bf16),
        shape((slots, width), bf16),
        shape((slots, padded), bf16),
        shape((slots, padded), bf16),
        shape((tokens, 2 * BLOCK), bf16),
        shape((tokens, BLOCK), bf16),
        shape((tokens, width), bf16),
    ]

    def slots_of(arrays):
        return [pltpu.VMEM((2, 2 * a.shape[0] // fsdp_size, a.shape[1]), a.dtype) for a in arrays]

    saved = [gate_act, up_act, weight, shared]
    dma = pltpu.SemaphoreType.DMA
    return pl.pallas_call(
        functools.partial(backward_kernel, fsdp_size, capacity),
        out_shape=tuple(outs),
        in_specs=[pl.BlockSpec(memory_space=pltpu.VMEM)] * 2
        + [pl.BlockSpec(memory_space=pl.ANY)] * 9,
        out_specs=tuple([pl.BlockSpec(memory_space=pl.ANY)] * len(outs)),
        scratch_shapes=[
            pltpu.VMEM((tokens, width), bf16),
            pltpu.VMEM((2, capacity, seq_len), bf16),
            pltpu.VMEM((2, seq_len, capacity + 2 * BLOCK), bf16),
            pltpu.VMEM((2, capacity + 2 * BLOCK, width), bf16),
            *slots_of(saved),
            *slots_of(outs[1:]),
            *[pltpu.VMEM(w.shape, w.dtype) for w in (gate, up, down, pair, block)],
            dma((5,)),
            dma((4, 2)),
            dma((len(outs) - 1, 2)),
            dma((fsdp_size // 2,)),
            *spread_sems(fsdp_size),
        ],
        compiler_params=pltpu.CompilerParams(
            collective_id=collective_id, has_side_effects=True, vmem_limit_bytes=67043328
        ),
        cost_estimate=pl.CostEstimate(
            flops=6 * slots * width * hidden, bytes_accessed=100_000_000, transcendentals=0
        ),
    )(own, place, gate, up, down, pair, block, *saved)


def token_shards(
    inputs,
    teacher,
    valid_mask,
    prefix,
    routes,
    norm_gain,
    query_weight,
    latent_weight,
    latent_gain,
    expand_weight,
    output_weight,
    moe_gain,
    router_weight,
    shared_gate,
    shared_up,
    shared_down,
    expert_gate,
    expert_up,
    expert_down,
):
    f32 = jnp.float32
    bf16 = jnp.bfloat16
    tp_size = lax.axis_size("tp")
    fsdp_size = lax.axis_size("fsdp")
    own_tp = lax.axis_index("tp")
    own_expert = lax.axis_index("fsdp")
    local_heads = HEADS // tp_size
    own_rows = inputs.shape[0]
    width = inputs.shape[1]
    seq_len = own_rows * tp_size

    expert_count = router_weight.shape[1]
    route_rows = routes.shape[1] * seq_len // BLOCK
    valid_rows = seq_len // BLOCK
    parts = [
        routes.T.reshape(route_rows, BLOCK).astype(f32),
        valid_mask.reshape(valid_rows, BLOCK).astype(f32),
        norm_gain.reshape(1, BLOCK).astype(f32),
        moe_gain.reshape(1, BLOCK).astype(f32),
        jnp.pad(latent_gain, (0, BLOCK - latent_gain.shape[0])).reshape(1, BLOCK).astype(f32),
        router_weight.T.astype(f32),
    ]
    small = jnp.concatenate(parts, axis=0)
    small_rows = -(-small.shape[0] // 8) * 8
    small = jnp.pad(small, ((0, small_rows - small.shape[0]), (0, 0)))
    blocks = shared_gate.shape[1] // BLOCK
    (
        query_full,
        latent_full,
        expand_full,
        output_full,
        small_all,
        gate_block,
        up_block,
        down_block,
    ) = gather_weights(
        query_weight,
        latent_weight.T,
        expand_weight,
        output_weight,
        small,
        shared_gate,
        shared_up,
        shared_down,
        1,
    )
    small_all = small_all.reshape(fsdp_size, small_rows, BLOCK)
    gain_row = route_rows + valid_rows
    norm_gains = small_all[:, gain_row].reshape(width)
    latent_gains = small_all[:, gain_row + 2, : latent_gain.shape[0]].reshape(RANK)

    hidden = tp_gather(inputs, own_tp).astype(f32)
    cosine, sine_part = rope_tables(seq_len, ROPE)
    inverse_in = lax.rsqrt(jnp.mean(hidden * hidden, axis=-1, keepdims=True) + EPSILON)
    normal_in = hidden * inverse_in
    norm_scale = norm_gains.astype(f32)
    normed = (normal_in * norm_scale).astype(bf16)
    query_lin = jnp.dot(normed, query_full, preferred_element_type=f32).reshape(
        seq_len, local_heads, NOPE + ROPE
    )
    queries = jnp.concatenate(
        [
            query_lin[..., :NOPE],
            rotate(query_lin[..., NOPE:], cosine[:, None, :], sine_part[:, None, :]),
        ],
        axis=-1,
    ).astype(bf16)
    latent_lin = jnp.einsum("td,rd->tr", normed, latent_full, preferred_element_type=f32)
    latent_raw = latent_lin[:, :RANK]
    inverse_lat = lax.rsqrt(jnp.mean(latent_raw * latent_raw, axis=-1, keepdims=True) + EPSILON)
    latent_unit = latent_raw * inverse_lat
    latent_scale = latent_gains.astype(f32)
    latent = (latent_unit * latent_scale).astype(bf16)
    key_rope = rotate(latent_lin[:, RANK:], cosine, sine_part).astype(bf16)
    keys_values = (
        jnp.dot(latent, expand_full, preferred_element_type=f32)
        .astype(bf16)
        .reshape(seq_len, local_heads, NOPE + VDIM)
    )
    key_nope = keys_values[..., :NOPE]
    values = keys_values[..., NOPE:]
    query_nope = queries[..., :NOPE]
    query_rope = queries[..., NOPE:]
    score_scale = 1.0 / math.sqrt(NOPE + ROPE)
    position = jnp.arange(seq_len, dtype=jnp.int32)
    visible = (position[None, :] <= position[:, None]) | (position[None, :] < prefix[0])
    raw_scores = jnp.einsum("ihd,jhd->hij", query_nope, key_nope, preferred_element_type=f32)
    raw_scores = raw_scores + jnp.einsum(
        "ihd,jd->hij", query_rope, key_rope, preferred_element_type=f32
    )
    scores = jnp.where(visible[None], raw_scores * score_scale, MASKED)
    row_max = jnp.max(scores, axis=-1, keepdims=True)
    shifted = jnp.exp(scores - row_max)
    attn_probs = shifted / jnp.sum(shifted, axis=-1, keepdims=True)
    probs_low = attn_probs.astype(bf16)
    heads_out = (
        jnp.einsum("hij,jhd->ihd", probs_low, values, preferred_element_type=f32)
        .astype(bf16)
        .reshape(seq_len, local_heads * VDIM)
    )
    attended = jnp.dot(heads_out, output_full, preferred_element_type=f32)
    small_all, gate_block, up_block, down_block, attended = lax.optimization_barrier(
        (small_all, gate_block, up_block, down_block, attended)
    )
    attended = tp_scatter(attended, own_tp, own_rows)

    routes_all = small_all[:, :route_rows].reshape(fsdp_size, routes.shape[1], seq_len)
    valid_all = small_all[:, route_rows:gain_row]
    moe_gains = small_all[:, gain_row + 1].reshape(width)
    router_rows = small_all[:, gain_row + 3 : gain_row + 3 + expert_count]
    router_full = jnp.transpose(router_rows, (1, 0, 2)).reshape(expert_count, width).astype(bf16)
    holds_block = block_of(own_expert, fsdp_size // 2) < blocks
    gate_block = jnp.where(holds_block, gate_block, 0)
    up_block = jnp.where(holds_block, up_block, 0)
    down_block = jnp.where(holds_block, down_block, 0)

    middle = inputs.astype(f32) + attended
    inverse_mid = lax.rsqrt(jnp.mean(middle * middle, axis=-1, keepdims=True) + EPSILON)
    normal_mid = middle * inverse_mid
    moe_scale = moe_gains.astype(f32)
    moe_in = (normal_mid * moe_scale).astype(bf16)

    def route(logits):
        logit_exp = jnp.exp(logits - jnp.max(logits, axis=-1, keepdims=True))
        return logit_exp / jnp.sum(logit_exp, axis=-1, keepdims=True)

    router_probs = route(jnp.einsum("td,ed->te", moe_in, router_full, preferred_element_type=f32))
    experts = expert_count
    top_count = routes.shape[1]
    capacity = top_count * seq_len * 4 // (3 * experts)

    named = jnp.any(routes_all == own_expert.astype(f32), axis=1)
    ahead = jnp.dot(
        named.astype(bf16),
        (position[:, None] < position[None, :]).astype(bf16),
        preferred_element_type=f32,
    ).astype(jnp.int32)
    place = jnp.where(named, ahead, -1)
    wide_block = jnp.concatenate(
        [gate_block, up_block, jnp.pad(router_full, ((0, BLOCK - experts), (0, 0))).T], axis=1
    )
    (
        tokens,
        received,
        gate_act,
        up_act,
        gated_hidden,
        gate_weight,
        shared_acts,
        shared_hidden,
        moe_part,
    ) = experts_forward(
        moe_in,
        place,
        expert_gate[0].T,
        expert_up[0].T,
        expert_down[0],
        wide_block,
        down_block,
        capacity,
        experts,
        2,
    )
    activations = middle + reduce_tokens([moe_part], 3)[0]

    own_mask = half_rows(valid_mask, own_tp, own_rows).astype(f32)
    offset = activations - half_rows(teacher, own_tp, own_rows).astype(f32)
    valid_total = jnp.maximum(jnp.sum(valid_all), 1.0)
    square_part = jnp.sum(own_mask[:, None] * offset * offset)
    grad_out = seq_len * fsdp_size / valid_total * own_mask[:, None] * offset
    grad_moe = grad_out.astype(bf16)

    (
        grads,
        grad_slots,
        grad_gate_act,
        grad_up_act,
        grad_sh_pair,
        grad_probs_part,
        grad_part,
    ) = experts_backward(
        grad_moe,
        place,
        expert_gate[0].T,
        expert_up[0].T,
        expert_down[0],
        jnp.concatenate([gate_block.T, up_block.T], axis=0),
        down_block,
        gate_act,
        up_act,
        gate_weight,
        shared_acts,
        capacity,
        4,
    )
    grad_moe_in, grad_router_probs = reduce_tokens([grad_part, grad_probs_part], 5)
    down_shared_grad = jnp.einsum("tf,td->fd", shared_hidden, grads, preferred_element_type=f32)
    pair_grad = jnp.einsum("td,tf->df", tokens, grad_sh_pair, preferred_element_type=f32)
    gate_shared_grad = pair_grad[:, :BLOCK].astype(bf16)
    up_shared_grad = pair_grad[:, BLOCK:].astype(bf16)
    grad_router_probs = grad_router_probs[:, :experts]

    grad_logits = router_probs * (
        grad_router_probs - jnp.sum(router_probs * grad_router_probs, axis=-1, keepdims=True)
    )
    router_grad = jnp.einsum(
        "td,te->ed", moe_in.astype(f32), grad_logits, precision=HIGHEST, preferred_element_type=f32
    )
    grad_moe_in = grad_moe_in + jnp.einsum(
        "te,ed->td",
        grad_logits,
        router_full.astype(f32),
        precision=HIGHEST,
        preferred_element_type=f32,
    )
    moe_gain_grad = jnp.sum(grad_moe_in * normal_mid, axis=0)
    grad_middle = grad_out + norm_back(grad_moe_in * moe_scale, normal_mid, inverse_mid)
    grad_attended = tp_gather(grad_middle.astype(bf16), own_tp)

    output_grad = jnp.einsum("tf,td->fd", heads_out, grad_attended, preferred_element_type=f32)
    grad_heads = (
        jnp.einsum("td,fd->tf", grad_attended, output_full, preferred_element_type=f32)
        .astype(bf16)
        .reshape(seq_len, local_heads, VDIM)
    )
    grad_probs = jnp.einsum("ihd,jhd->hij", grad_heads, values, preferred_element_type=f32)
    grad_values = jnp.einsum("hij,ihd->jhd", probs_low, grad_heads, preferred_element_type=f32)
    grad_scores = (
        attn_probs * (grad_probs - jnp.sum(attn_probs * grad_probs, axis=-1, keepdims=True))
    ).astype(bf16)
    grad_q_nope = (
        jnp.einsum("hij,jhd->ihd", grad_scores, key_nope, preferred_element_type=f32) * score_scale
    )
    grad_q_rope = (
        jnp.einsum("hij,jd->ihd", grad_scores, key_rope, preferred_element_type=f32) * score_scale
    )
    grad_keys = (
        jnp.einsum("hij,ihd->jhd", grad_scores, query_nope, preferred_element_type=f32)
        * score_scale
    )
    grad_key_rope = (
        jnp.einsum("hij,ihd->jd", grad_scores, query_rope, preferred_element_type=f32) * score_scale
    )
    grad_query = (
        jnp.concatenate(
            [grad_q_nope, unrotate(grad_q_rope, cosine[:, None, :], sine_part[:, None, :])], axis=-1
        )
        .astype(bf16)
        .reshape(seq_len, local_heads * (NOPE + ROPE))
    )
    query_grad = jnp.einsum("td,tq->dq", normed, grad_query, preferred_element_type=f32)
    grad_normed = jnp.einsum("tq,dq->td", grad_query, query_full, preferred_element_type=f32)
    grad_kv = (
        jnp.concatenate([grad_keys, grad_values], axis=-1)
        .astype(bf16)
        .reshape(seq_len, local_heads * (NOPE + VDIM))
    )
    expand_grad = jnp.einsum("tr,tq->rq", latent, grad_kv, preferred_element_type=f32)
    grad_latent = jnp.einsum("tq,rq->tr", grad_kv, expand_full, preferred_element_type=f32)
    grad_both = tp_sum(jnp.concatenate([grad_latent, grad_key_rope], axis=1))
    grad_latent, grad_key_rope = grad_both[:, :RANK], grad_both[:, RANK:]
    latent_gain_grad = jnp.sum(grad_latent * latent_unit, axis=0)
    grad_latent_raw = norm_back(grad_latent * latent_scale, latent_unit, inverse_lat)
    grad_latent_lin = jnp.concatenate(
        [grad_latent_raw, unrotate(grad_key_rope, cosine, sine_part)], axis=-1
    ).astype(bf16)
    latent_grad = jnp.einsum("tr,td->rd", grad_latent_lin, normed, preferred_element_type=f32)
    grad_normed = tp_scatter(grad_normed, own_tp, own_rows) + jnp.einsum(
        "tr,rd->td",
        half_rows(grad_latent_lin, own_tp, own_rows),
        latent_full,
        preferred_element_type=f32,
    )
    own_normal = half_rows(normal_in, own_tp, own_rows)
    own_inverse = half_rows(inverse_in, own_tp, own_rows)
    norm_gain_grad = jnp.sum(grad_normed * own_normal, axis=0)
    input_grad = grad_middle + norm_back(grad_normed * norm_scale, own_normal, own_inverse)

    small = jnp.concatenate(
        [
            jnp.transpose(router_grad.reshape(experts, fsdp_size, BLOCK), (1, 0, 2)),
            norm_gain_grad.reshape(fsdp_size, 1, BLOCK),
            moe_gain_grad.reshape(fsdp_size, 1, BLOCK),
            jnp.pad(
                0.5 * latent_gain_grad.reshape(fsdp_size, 1, RANK // fsdp_size),
                ((0, 0), (0, 0), (0, BLOCK - RANK // fsdp_size)),
            ),
            jnp.full((fsdp_size, 1, BLOCK), square_part),
        ],
        axis=1,
    )
    small = jnp.pad(small, ((0, 0), (0, -(experts + 4) % 8), (0, 0))).reshape(-1, BLOCK)
    small = small + swap_tp(small)
    query_out, latent_out, expand_out, output_out, small_out, gate_out, up_out, down_out, *expert_grads = (
        reduce_weights(
            query_grad.astype(bf16),
            latent_grad.astype(bf16),
            expand_grad.astype(bf16),
            output_grad.astype(bf16),
            small,
            gate_shared_grad,
            up_shared_grad,
            down_shared_grad.astype(bf16),
            blocks,
            6,
            WeightGrads(received.shape[0], expert_down.shape[1], width),
            [grad_gate_act, grad_up_act, gated_hidden, received, grad_slots],
        )
    )
    return (
        small_out[experts + 3, 0] / (width * valid_total),
        activations,
        input_grad,
        small_out[experts],
        query_out,
        latent_out.T,
        small_out[experts + 2, : RANK // fsdp_size],
        expand_out,
        output_out,
        small_out[experts + 1],
        small_out[:experts].T,
        gate_out.astype(f32),
        up_out.astype(f32),
        down_out.astype(f32),
        expert_grads[0].T.astype(f32)[None],
        expert_grads[1].T.astype(f32)[None],
        expert_grads[2].astype(f32)[None],
    )


def slot_shards(
    inputs,
    teacher,
    valid_mask,
    prefix,
    routes,
    norm_gain,
    query_weight,
    latent_weight,
    latent_gain,
    expand_weight,
    output_weight,
    moe_gain,
    router_weight,
    shared_gate,
    shared_up,
    shared_down,
    expert_gate,
    expert_up,
    expert_down,
):
    f32 = jnp.float32
    bf16 = jnp.bfloat16
    tp_size = lax.axis_size("tp")
    fsdp_size = lax.axis_size("fsdp")
    local_heads = HEADS // tp_size
    (
        norm_gains,
        query_full,
        latent_full,
        latent_gains,
        expand_full,
        output_full,
        moe_gains,
        router_full,
        gate_full,
        up_full,
        down_full,
    ) = (
        lax.all_gather(norm_gain, "fsdp", axis=0, tiled=True),
        lax.all_gather(query_weight, "fsdp", axis=0, tiled=True),
        lax.all_gather(latent_weight, "fsdp", axis=0, tiled=True),
        lax.all_gather(latent_gain, "fsdp", axis=0, tiled=True),
        lax.all_gather(expand_weight, "fsdp", axis=0, tiled=True),
        lax.all_gather(output_weight, "fsdp", axis=1, tiled=True),
        lax.all_gather(moe_gain, "fsdp", axis=0, tiled=True),
        lax.all_gather(router_weight, "fsdp", axis=0, tiled=True),
        lax.all_gather(shared_gate, "fsdp", axis=0, tiled=True),
        lax.all_gather(shared_up, "fsdp", axis=0, tiled=True),
        lax.all_gather(shared_down, "fsdp", axis=1, tiled=True),
    )
    gathered = lax.all_gather(inputs, "tp", axis=0, tiled=True)
    seq_len = gathered.shape[0]
    width = gathered.shape[1]
    hidden = gathered.astype(f32)
    cosine, sine_part = rope_tables(seq_len, ROPE)
    inverse_in = lax.rsqrt(jnp.mean(hidden * hidden, axis=-1, keepdims=True) + EPSILON)
    normal_in = hidden * inverse_in
    norm_scale = norm_gains.astype(f32)
    normed = (normal_in * norm_scale).astype(bf16)
    query_lin = jnp.dot(normed, query_full, preferred_element_type=f32).reshape(
        seq_len, local_heads, NOPE + ROPE
    )
    queries = jnp.concatenate(
        [
            query_lin[..., :NOPE],
            rotate(query_lin[..., NOPE:], cosine[:, None, :], sine_part[:, None, :]),
        ],
        axis=-1,
    ).astype(bf16)
    latent_lin = jnp.dot(normed, latent_full, preferred_element_type=f32)
    latent_raw = latent_lin[:, :RANK]
    inverse_lat = lax.rsqrt(jnp.mean(latent_raw * latent_raw, axis=-1, keepdims=True) + EPSILON)
    latent_unit = latent_raw * inverse_lat
    latent_scale = latent_gains.astype(f32)
    latent = (latent_unit * latent_scale).astype(bf16)
    key_rope = rotate(latent_lin[:, RANK:], cosine, sine_part).astype(bf16)
    keys_values = (
        jnp.dot(latent, expand_full, preferred_element_type=f32)
        .astype(bf16)
        .reshape(seq_len, local_heads, NOPE + VDIM)
    )
    key_nope = keys_values[..., :NOPE]
    values = keys_values[..., NOPE:]
    query_nope = queries[..., :NOPE]
    query_rope = queries[..., NOPE:]
    score_scale = 1.0 / math.sqrt(NOPE + ROPE)
    position = jnp.arange(seq_len, dtype=jnp.int32)
    visible = (position[None, :] <= position[:, None]) | (position[None, :] < prefix[0])

    def scores_of():
        raw_scores = jnp.einsum("ihd,jhd->hij", query_nope, key_nope, preferred_element_type=f32)
        raw_scores = raw_scores + jnp.einsum(
            "ihd,jd->hij", query_rope, key_rope, preferred_element_type=f32
        )
        return jnp.where(visible[None], raw_scores * score_scale, MASKED)

    scores = scores_of()
    row_max = jnp.max(scores, axis=-1, keepdims=True)
    shifted = jnp.exp(scores - row_max)
    row_total = jnp.sum(shifted, axis=-1, keepdims=True)
    log_total = row_max + jnp.log(row_total)
    probs_low = (shifted / row_total).astype(bf16)
    heads_out = (
        jnp.einsum("hij,jhd->ihd", probs_low, values, preferred_element_type=f32)
        .astype(bf16)
        .reshape(seq_len, local_heads * VDIM)
    )
    attended = lax.psum(jnp.dot(heads_out, output_full, preferred_element_type=f32), "tp")
    middle = hidden + attended
    inverse_mid = lax.rsqrt(jnp.mean(middle * middle, axis=-1, keepdims=True) + EPSILON)
    normal_mid = middle * inverse_mid
    moe_scale = moe_gains.astype(f32)
    moe_in = (normal_mid * moe_scale).astype(bf16)
    logits = jnp.dot(moe_in, router_full, preferred_element_type=f32)
    logit_max = jnp.max(logits, axis=-1, keepdims=True)
    logit_exp = jnp.exp(logits - logit_max)
    router_probs = logit_exp / jnp.sum(logit_exp, axis=-1, keepdims=True)
    experts = router_full.shape[1]
    top_count = routes.shape[1]
    choose = routes[:, :, None] == jnp.arange(experts, dtype=jnp.int32)[None, None, :]
    gate_values = jnp.sum(jnp.where(choose, router_probs[:, None, :], 0.0), axis=-1)
    capacity = top_count * seq_len * 4 // (3 * experts)
    flat_routes = routes.reshape(seq_len * top_count)
    onehot = (flat_routes[:, None] == jnp.arange(experts, dtype=jnp.int32)[None, :]).astype(
        jnp.int32
    )
    earlier = jnp.cumsum(onehot, axis=0) - onehot
    slot_index = flat_routes * capacity + jnp.sum(earlier * onehot, axis=1)
    placed = jnp.arange(experts * capacity, dtype=jnp.int32)[:, None] == slot_index[None, :]
    dispatch = jnp.sum(
        placed.reshape(experts * capacity, seq_len, top_count).astype(f32), axis=2
    ).astype(bf16)
    gate_slot = jnp.sum(jnp.where(placed, gate_values.reshape(1, seq_len * top_count), 0.0), axis=1)

    def send_slots(slot_rows):
        return lax.all_to_all(slot_rows, "fsdp", split_axis=0, concat_axis=1, tiled=True)

    def return_slots(partials):
        return (
            lax.all_to_all(
                partials.astype(jnp.bfloat16), "fsdp", split_axis=1, concat_axis=0, tiled=True
            )
            .astype(partials.dtype)
            .reshape(experts * capacity, width)
        )

    expert_in = (
        jnp.dot(dispatch, moe_in, preferred_element_type=f32)
        .astype(bf16)
        .reshape(experts, capacity, width)
    )
    received = send_slots(expert_in)
    gate_act = jnp.einsum("ecd,edf->ecf", received, expert_gate, preferred_element_type=f32)
    up_act = jnp.einsum("ecd,edf->ecf", received, expert_up, preferred_element_type=f32)
    silu_gate, silu_slope = silu_parts(gate_act)
    expert_hidden = (silu_gate * up_act).astype(bf16)
    expert_out = jnp.einsum("ecf,efd->ecd", expert_hidden, expert_down, preferred_element_type=f32)
    returned = return_slots(expert_out)
    picked = jnp.take(returned, slot_index, axis=0).reshape(seq_len, top_count, width)
    routed = jnp.sum(gate_values[:, :, None] * picked, axis=1)
    gate_sh = jnp.dot(moe_in, gate_full, preferred_element_type=f32)
    up_sh = jnp.dot(moe_in, up_full, preferred_element_type=f32)
    silu_sh, slope_sh = silu_parts(gate_sh)
    shared_hidden = (silu_sh * up_sh).astype(bf16)
    moe_part = routed + jnp.dot(shared_hidden, down_full, preferred_element_type=f32)
    moe_out = lax.psum(moe_part.astype(jnp.bfloat16), "tp").astype(jnp.float32)
    activations = middle + moe_out
    mask_float = valid_mask.astype(f32)
    offset = activations - teacher.astype(f32)
    square_sum, valid_sum = lax.psum(
        (jnp.sum(mask_float[:, None] * offset * offset), jnp.sum(mask_float)), "fsdp"
    )
    valid_total = jnp.maximum(valid_sum, 1.0)
    loss_value = square_sum / (width * valid_total)
    grad_out = seq_len * fsdp_size / valid_total * mask_float[:, None] * offset
    grad_moe = grad_out.astype(bf16)
    down_shared_grad = jnp.einsum("tf,td->fd", shared_hidden, grad_moe, preferred_element_type=f32)
    grad_sh_hidden = jnp.einsum("td,fd->tf", grad_moe, down_full, preferred_element_type=f32)
    grad_gate_sh = (grad_sh_hidden * up_sh * slope_sh).astype(bf16)
    grad_up_sh = (grad_sh_hidden * silu_sh).astype(bf16)
    gate_shared_grad = jnp.einsum("td,tf->df", moe_in, grad_gate_sh, preferred_element_type=f32)
    up_shared_grad = jnp.einsum("td,tf->df", moe_in, grad_up_sh, preferred_element_type=f32)
    grad_moe_in = jnp.einsum("tf,df->td", grad_gate_sh, gate_full, preferred_element_type=f32)
    grad_moe_in = grad_moe_in + jnp.einsum(
        "tf,df->td", grad_up_sh, up_full, preferred_element_type=f32
    )
    grad_gates = jnp.sum(picked * grad_moe.astype(f32)[:, None, :], axis=-1)
    grad_slots = (
        (jnp.dot(dispatch, grad_moe, preferred_element_type=f32) * gate_slot[:, None])
        .astype(bf16)
        .reshape(experts, capacity, width)
    )
    grad_received = send_slots(grad_slots)
    expert_down_grad = jnp.einsum(
        "ecf,ecd->efd", expert_hidden, grad_received, preferred_element_type=f32
    )
    grad_expert_hidden = jnp.einsum(
        "ecd,efd->ecf", grad_received, expert_down, preferred_element_type=f32
    )
    grad_gate_act = (grad_expert_hidden * up_act * silu_slope).astype(bf16)
    grad_up_act = (grad_expert_hidden * silu_gate).astype(bf16)
    expert_gate_grad = jnp.einsum(
        "ecd,ecf->edf", received, grad_gate_act, preferred_element_type=f32
    )
    expert_up_grad = jnp.einsum("ecd,ecf->edf", received, grad_up_act, preferred_element_type=f32)
    grad_expert_in = jnp.einsum(
        "ecf,edf->ecd", grad_gate_act, expert_gate, preferred_element_type=f32
    )
    grad_expert_in = grad_expert_in + jnp.einsum(
        "ecf,edf->ecd", grad_up_act, expert_up, preferred_element_type=f32
    )
    grad_returned = return_slots(grad_expert_in)
    grad_moe_in = grad_moe_in + jnp.sum(
        jnp.take(grad_returned, slot_index, axis=0).reshape(seq_len, top_count, width), axis=1
    )
    grad_moe_in, grad_gates = (
        lax.psum(grad_moe_in.astype(jnp.bfloat16), "tp").astype(jnp.float32),
        lax.psum(grad_gates.astype(jnp.bfloat16), "tp").astype(jnp.float32),
    )
    grad_router_probs = jnp.sum(jnp.where(choose, grad_gates[:, :, None], 0.0), axis=1)
    grad_logits = router_probs * (
        grad_router_probs - jnp.sum(router_probs * grad_router_probs, axis=-1, keepdims=True)
    )
    router_grad = jnp.einsum(
        "td,te->de", moe_in.astype(f32), grad_logits, precision=HIGHEST, preferred_element_type=f32
    )
    grad_moe_in = grad_moe_in + jnp.einsum(
        "te,de->td",
        grad_logits,
        router_full.astype(f32),
        precision=HIGHEST,
        preferred_element_type=f32,
    )
    moe_gain_grad = jnp.sum(grad_moe_in * normal_mid, axis=0)
    grad_middle = grad_out + norm_back(grad_moe_in * moe_scale, normal_mid, inverse_mid)
    grad_attended = grad_middle.astype(bf16)
    output_grad = jnp.einsum("tf,td->fd", heads_out, grad_attended, preferred_element_type=f32)
    grad_heads = (
        jnp.einsum("td,fd->tf", grad_attended, output_full, preferred_element_type=f32)
        .astype(bf16)
        .reshape(seq_len, local_heads, VDIM)
    )
    attn_probs = jnp.exp(scores_of() - log_total)
    probs_again = attn_probs.astype(bf16)
    grad_probs = jnp.einsum("ihd,jhd->hij", grad_heads, values, preferred_element_type=f32)
    grad_values = jnp.einsum("hij,ihd->jhd", probs_again, grad_heads, preferred_element_type=f32)
    grad_scores = (
        attn_probs * (grad_probs - jnp.sum(attn_probs * grad_probs, axis=-1, keepdims=True))
    ).astype(bf16)
    grad_q_nope = (
        jnp.einsum("hij,jhd->ihd", grad_scores, key_nope, preferred_element_type=f32) * score_scale
    )
    grad_q_rope = (
        jnp.einsum("hij,jd->ihd", grad_scores, key_rope, preferred_element_type=f32) * score_scale
    )
    grad_keys = (
        jnp.einsum("hij,ihd->jhd", grad_scores, query_nope, preferred_element_type=f32)
        * score_scale
    )
    grad_key_rope = (
        jnp.einsum("hij,ihd->jd", grad_scores, query_rope, preferred_element_type=f32) * score_scale
    )
    grad_query = (
        jnp.concatenate(
            [grad_q_nope, unrotate(grad_q_rope, cosine[:, None, :], sine_part[:, None, :])], axis=-1
        )
        .astype(bf16)
        .reshape(seq_len, local_heads * (NOPE + ROPE))
    )
    query_grad = jnp.einsum("td,tq->dq", normed, grad_query, preferred_element_type=f32)
    grad_normed = jnp.einsum("tq,dq->td", grad_query, query_full, preferred_element_type=f32)
    grad_kv = (
        jnp.concatenate([grad_keys, grad_values], axis=-1)
        .astype(bf16)
        .reshape(seq_len, local_heads * (NOPE + VDIM))
    )
    expand_grad = jnp.einsum("tr,tq->rq", latent, grad_kv, preferred_element_type=f32)
    grad_latent = jnp.einsum("tq,rq->tr", grad_kv, expand_full, preferred_element_type=f32)
    grad_normed, grad_latent, grad_key_rope = (
        lax.psum(grad_normed.astype(jnp.bfloat16), "tp").astype(jnp.float32),
        lax.psum(grad_latent.astype(jnp.bfloat16), "tp").astype(jnp.float32),
        lax.psum(grad_key_rope.astype(jnp.bfloat16), "tp").astype(jnp.float32),
    )
    latent_gain_grad = jnp.sum(grad_latent * latent_unit, axis=0)
    grad_latent_raw = norm_back(grad_latent * latent_scale, latent_unit, inverse_lat)
    grad_latent_lin = jnp.concatenate(
        [grad_latent_raw, unrotate(grad_key_rope, cosine, sine_part)], axis=-1
    ).astype(bf16)
    latent_grad = jnp.einsum("td,tr->dr", normed, grad_latent_lin, preferred_element_type=f32)
    grad_normed = grad_normed + jnp.einsum(
        "tr,dr->td", grad_latent_lin, latent_full, preferred_element_type=f32
    )
    norm_gain_grad = jnp.sum(grad_normed * normal_in, axis=0)
    input_grad = grad_middle + norm_back(grad_normed * norm_scale, normal_in, inverse_in)
    (
        norm_out,
        query_out,
        latent_out,
        lgain_out,
        expand_out,
        output_out,
        mgain_out,
        router_out,
        gate_out,
        up_out,
        down_out,
    ) = (
        lax.psum_scatter(norm_gain_grad, "fsdp", scatter_dimension=0, tiled=True),
        lax.psum_scatter(query_grad, "fsdp", scatter_dimension=0, tiled=True),
        lax.psum_scatter(latent_grad, "fsdp", scatter_dimension=0, tiled=True),
        lax.psum_scatter(latent_gain_grad, "fsdp", scatter_dimension=0, tiled=True),
        lax.psum_scatter(expand_grad, "fsdp", scatter_dimension=0, tiled=True),
        lax.psum_scatter(output_grad, "fsdp", scatter_dimension=1, tiled=True),
        lax.psum_scatter(moe_gain_grad, "fsdp", scatter_dimension=0, tiled=True),
        lax.psum_scatter(router_grad, "fsdp", scatter_dimension=0, tiled=True),
        lax.psum_scatter(gate_shared_grad, "fsdp", scatter_dimension=0, tiled=True),
        lax.psum_scatter(up_shared_grad, "fsdp", scatter_dimension=0, tiled=True),
        lax.psum_scatter(down_shared_grad, "fsdp", scatter_dimension=1, tiled=True),
    )
    own_start = lax.axis_index("tp") * inputs.shape[0]
    own_activations = lax.dynamic_slice_in_dim(activations, own_start, inputs.shape[0], 0)
    own_input_grad = lax.dynamic_slice_in_dim(input_grad, own_start, inputs.shape[0], 0)
    return (
        loss_value,
        own_activations,
        own_input_grad,
        norm_out,
        query_out,
        latent_out,
        lgain_out,
        expand_out,
        output_out,
        mgain_out,
        router_out,
        gate_out,
        up_out,
        down_out,
        expert_gate_grad,
        expert_up_grad,
        expert_down_grad,
    )


def shards(*arrays):
    fsdp_size = lax.axis_size("fsdp")
    seq_len = arrays[4].shape[0]
    experts = arrays[12].shape[1]
    capacity = arrays[4].shape[1] * seq_len * 4 // (3 * experts)
    fits = fsdp_size * seq_len <= 2 * experts * capacity and fsdp_size == experts
    aligned = arrays[5].shape[0] == BLOCK and arrays[13].shape[1] % BLOCK == 0 and arrays[13].shape[1] <= fsdp_size * BLOCK
    if fits and aligned and fsdp_size % 4 == 0:
        return token_shards(*arrays)
    return slot_shards(*arrays)


def solution(mesh):
    return jax.shard_map(
        shards,
        mesh=mesh,
        in_specs=(
            P(("fsdp", "tp"), None),
            P("fsdp", None),
            P("fsdp"),
            P("fsdp"),
            P("fsdp", None),
            P("fsdp"),
            P("fsdp", "tp"),
            P("fsdp", None),
            P("fsdp"),
            P("fsdp", "tp"),
            P("tp", "fsdp"),
            P("fsdp"),
            P("fsdp", None),
            P("fsdp", "tp"),
            P("fsdp", "tp"),
            P("tp", "fsdp"),
            P("fsdp", None, "tp"),
            P("fsdp", None, "tp"),
            P("fsdp", "tp", None),
        ),
        out_specs=(
            P(),
            P(("fsdp", "tp"), None),
            P(("fsdp", "tp"), None),
            P("fsdp"),
            P("fsdp", "tp"),
            P("fsdp", None),
            P("fsdp"),
            P("fsdp", "tp"),
            P("tp", "fsdp"),
            P("fsdp"),
            P("fsdp", None),
            P("fsdp", "tp"),
            P("fsdp", "tp"),
            P("tp", "fsdp"),
            P("fsdp", None, "tp"),
            P("fsdp", None, "tp"),
            P("fsdp", "tp", None),
        ),
        check_vma=False,
    )
```

```python
import functools
import math

import jax
import jax.numpy as jnp
from jax import lax
from jax.experimental import pallas as pl
from jax.experimental.pallas import tpu as pltpu
from jax.sharding import PartitionSpec as P

HEADS = 16
NOPE = 128
ROPE = 64
RANK = 512
VDIM = 128


EPSILON = 1e-06
HIGHEST = lax.Precision.HIGHEST
MASKED = -1e30


def rope_tables(length, dim_size):
    places = jnp.arange(length).astype(jnp.float32)
    exponent = jnp.arange(dim_size // 2).astype(jnp.float32) * (2.0 / dim_size)
    angles = places[:, None] * jnp.exp(exponent * -math.log(10000.0))[None, :]
    return (jnp.cos(angles), jnp.sin(angles))


def rotate(values, cosine, sine_part):
    half_width = values.shape[-1] // 2
    lower_half = values[..., :half_width]
    upper_half = values[..., half_width:]
    return jnp.concatenate(
        [
            lower_half * cosine - upper_half * sine_part,
            upper_half * cosine + lower_half * sine_part,
        ],
        axis=-1,
    )


def unrotate(gradient, cosine, sine_part):
    half_width = gradient.shape[-1] // 2
    lower_half = gradient[..., :half_width]
    upper_half = gradient[..., half_width:]
    return jnp.concatenate(
        [
            lower_half * cosine + upper_half * sine_part,
            upper_half * cosine - lower_half * sine_part,
        ],
        axis=-1,
    )


def silu_parts(gate_act):
    sigmoid_val = jax.nn.sigmoid(gate_act)
    return (gate_act * sigmoid_val, sigmoid_val * (1.0 + gate_act * (1.0 - sigmoid_val)))


def norm_back(grad_scaled, unit_rows, inverse):
    return inverse * (
        grad_scaled - unit_rows * jnp.mean(grad_scaled * unit_rows, axis=-1, keepdims=True)
    )


def swap_tp(value):
    return lax.ppermute(value, "tp", [(0, 1), (1, 0)])


def half_rows(value, which, rows):
    return lax.dynamic_slice_in_dim(value, which * rows, rows, 0)


def tp_scatter(partial, which, rows):
    other = half_rows(partial, 1 - which, rows).astype(jnp.bfloat16)
    return half_rows(partial, which, rows) + swap_tp(other).astype(jnp.float32)


def tp_sum(partial):
    low_partial = partial.astype(jnp.bfloat16)
    return low_partial.astype(jnp.float32) + swap_tp(low_partial).astype(jnp.float32)


def tp_gather(own, which):
    other = swap_tp(own)
    first = jnp.where(which == 0, own, other)
    second = jnp.where(which == 0, other, own)
    return jnp.concatenate([first, second], axis=0)


MESH = pl.DeviceIdType.MESH
CROSS = ("x", "y", "up", "down")
BLOCK = 128


def both(first, second):
    if first is None:
        return second
    if second is None:
        return first
    return jnp.logical_and(first, second)


def under(condition, body):
    if condition is None:
        body()
    else:
        pl.when(condition)(body)


class Grid:
    def __init__(self, fsdp_size, dims, tie=-1):
        self.tie = tie
        index = lax.axis_index("fsdp")
        self.core = lax.rem(index, 2)
        self.y = lax.rem(lax.div(index, 2), 2)
        self.z = lax.div(index, 4)
        self.x = lax.axis_index("tp")
        self.depth = fsdp_size // 4
        self.dims = dims
        self.crosses = CROSS if "x" in dims else CROSS[1:]
        self.chips = self.depth * 2 * (2 if "x" in dims else 1)

    def device(self, x, y, z, core):
        return {"fsdp": z * 4 + y * 2 + core, "tp": x}

    def chip(self, x, y, z):
        return (z * 2 + y) * 2 + x if "x" in self.dims else z * 2 + y

    def here(self):
        return self.x, self.y, self.z

    def partner(self):
        return self.device(self.x, self.y, self.z, 1 - self.core)

    def neighbour(self, cross):
        if cross == "x":
            return (1 - self.x, self.y, self.z), None
        if cross == "y":
            return (self.x, 1 - self.y, self.z), None
        if cross == "up":
            return (self.x, self.y, self.z + 1), self.z + 1 < self.depth
        return (self.x, self.y, self.z - 1), self.z >= 1

    def level(self, rank):
        inner = jnp.logical_or(self.z == 1, self.z == 2)
        rank = jnp.where(jnp.logical_and(inner, rank >= 2), 5 - rank, rank)
        high, low = lax.div(self.z, 2), lax.rem(self.z, 2)
        far, near = lax.div(rank, 2), lax.rem(rank, 2)
        return 2 * (high + far - 2 * high * far) + (low + near - 2 * low * near)

    def entry(self, number):
        steps = (0, 1) if "x" in self.dims else (0,)
        found = [(r, dy, dx) for r in range(self.depth) for dy in (0, 1) for dx in steps]
        if "x" in self.dims:
            found.sort(key=lambda e: (sum(e), self.tie * e[0]))
        else:
            found.sort(key=lambda e: e[0] + 2.1 * e[1])
        codes = [4 * e[0] + 2 * e[1] + e[2] for e in found]
        code = jnp.int32(0) + (codes[number] if isinstance(number, int) else 0)
        if not isinstance(number, int):
            for at, value in enumerate(codes):
                code = jnp.where(number == at, value, code)
        dx, dy = lax.rem(code, 2), lax.rem(lax.div(code, 2), 2)
        x, y = self.x + dx - 2 * self.x * dx, self.y + dy - 2 * self.y * dy
        return x, y, self.level(lax.div(code, 4))

    def children(self, order, chip):
        zero = dict(x=chip[0] == self.x, y=chip[1] == self.y, z=chip[2] == self.z)
        found, rest = [], None
        for dim in reversed(order):
            if dim == "z":
                found.append(("up", both(rest, (chip[2] <= self.z) & (self.z + 1 < self.depth))))
                found.append(("down", both(rest, (chip[2] >= self.z) & (self.z >= 1))))
            else:
                found.append((dim, both(rest, zero[dim])))
            rest = both(rest, zero[dim])
        return found

    def parent(self, order, chip):
        zero = dict(x=chip[0] == self.x, y=chip[1] == self.y, z=chip[2] == self.z)
        rest, turned = None, {}
        for dim in reversed(order):
            turned[dim] = both(rest, jnp.logical_not(zero[dim]))
            rest = both(rest, zero[dim])
        x = jnp.where(turned["x"], 1 - self.x, self.x) if "x" in order else self.x
        y = jnp.where(turned["y"], 1 - self.y, self.y)
        above = chip[2] > self.z
        z = jnp.where(turned["z"], jnp.where(above, self.z + 1, self.z - 1), self.z)
        side = jnp.where(above, self.crosses.index("down"), self.crosses.index("up"))
        side = jnp.where(turned["y"], self.crosses.index("y"), side)
        if "x" in order:
            side = jnp.where(turned["x"], self.crosses.index("x"), side)
        return (x, y, z), side

    def greet(self):
        barrier = pltpu.get_barrier_semaphore()
        pl.semaphore_signal(barrier, inc=1, device_id=self.partner(), device_id_type=MESH)
        count = 1
        for cross in self.crosses:
            chip, exists = self.neighbour(cross)

            def send(chip=chip):
                there = self.device(*chip, self.core)
                pl.semaphore_signal(barrier, inc=1, device_id=there, device_id_type=MESH)

            under(exists, send)
            count = count + (1 if exists is None else jnp.where(exists, 1, 0))
        pl.semaphore_wait(barrier, count)

    def greet_plane(self):
        barrier = pltpu.get_barrier_semaphore()
        size = self.depth * 4
        me = lax.axis_index("fsdp")

        def send(step, carry):
            there = {"fsdp": lax.rem(me + step, size), "tp": self.x}
            pl.semaphore_signal(barrier, inc=1, device_id=there, device_id_type=MESH)
            return carry

        lax.fori_loop(1, size, send, 0)
        pl.semaphore_wait(barrier, size - 1)


def owner_of(block, chips):
    extra = 2 * lax.rem(3 * (block - chips) + 1 + 3 * chips, chips) + 1
    return jnp.where(block < chips, 2 * block, extra)


def block_of(device, chips):
    back = pow(3, -1, chips)
    chip, core = lax.div(device, 2), lax.rem(device, 2)
    return jnp.where(core == 0, chip, chips + lax.rem(back * (chip - 1 + chips), chips))


class Exchange:
    def __init__(self, fsdp_size, tp, blocks, sources, targets, cut, to_owner, send_sem, recv_sem, own_sem):
        self.size, self.tp, self.blocks = fsdp_size, tp, blocks
        self.sources, self.targets, self.cut, self.to_owner = sources, targets, cut, to_owner
        self.send_sem, self.recv_sem, self.own_sem = send_sem, recv_sem, own_sem
        self.me = lax.axis_index("fsdp")
        self.block = block_of(self.me, fsdp_size // 2)
        self.owns = self.block < blocks

    def remote(self, array, block, other, there, send, recv):
        source, target = self.cut[array](self.sources[array], self.targets[array], block, other)
        return pltpu.make_async_remote_copy(
            src_ref=source,
            dst_ref=target,
            send_sem=self.send_sem.at[array, send],
            recv_sem=self.recv_sem.at[array, recv],
            device_id={"fsdp": there, "tp": self.tp},
            device_id_type=MESH,
        )

    def local(self, array, block):
        source, target = self.cut[array](self.sources[array], self.targets[array], block, self.me)
        return pltpu.make_async_copy(source, target, self.own_sem.at[array])

    def by_block(self, act, act_local, low, high):
        def one(number, carry):
            block = lax.rem(number + lax.div(self.me * self.blocks, self.size), self.blocks)
            owner = owner_of(block, self.size // 2)
            for array in range(len(self.sources)):
                if self.to_owner:
                    copy = self.remote(array, block, self.me, owner, block, self.me)
                else:
                    copy = self.remote(array, block, self.me, owner, 0, block)
                pl.when(self.me != owner)(getattr(copy, act))
                if act_local:
                    pl.when(self.me == owner)(getattr(self.local(array, block), act_local))
            return carry

        lax.fori_loop(low, high, one, 0)

    def by_device(self, act, act_local, low, high):
        def one(number, carry):
            other = lax.rem(self.me + number, self.size)
            for array in range(len(self.sources)):
                if self.to_owner:
                    copy = self.remote(array, self.block, other, other, 0, other)
                else:
                    copy = self.remote(array, self.block, other, other, other, self.block)
                pl.when(self.me != other)(getattr(copy, act))
                if act_local:
                    pl.when(self.me == other)(getattr(self.local(array, self.block), act_local))
            return carry

        def every():
            lax.fori_loop(low, high, one, 0)

        pl.when(self.owns)(every)

    def start(self, step, steps):
        total = self.blocks if self.to_owner else self.size
        low, high = lax.div(step * total, steps), lax.div((step + 1) * total, steps)
        (self.by_block if self.to_owner else self.by_device)("start", "start", low, high)

    def finish(self):
        if self.to_owner:
            self.by_device("wait_recv", None, 0, self.size)
            self.by_block("wait_send", "wait", 0, self.blocks)
        else:
            self.by_block("wait_recv", None, 0, self.blocks)
            self.by_device("wait_send", "wait", 0, self.size)


def exchange_sems(fsdp_size, arrays):
    dma = pltpu.SemaphoreType.DMA
    return [dma((arrays, fsdp_size)), dma((arrays, fsdp_size)), dma((arrays,))] if arrays else []


def gather_kernel(fsdp_size, pieces, places, count, blocks, cut, *refs):
    moved = len(cut)
    shards, sources = refs[:count], refs[count : count + moved]
    refs = refs[count + moved :]
    outs, targets = refs[:count], refs[count : count + moved]
    send_sem, recv_sem, pair_send, pair_recv, own_sem = refs[count + moved : count + moved + 5]
    grid = Grid(fsdp_size, "zy")
    exchange = Exchange(
        fsdp_size, grid.x, blocks, sources, targets, cut, True, *refs[count + moved + 5 :]
    )

    def target(piece, chip, core):
        array, first, rows, _ = pieces[piece]
        return places[array](outs[array], chip, core, first, rows)

    def source(piece, chip, own):
        array, first, rows, _ = pieces[piece]
        return shards[array].at[pl.ds(first, rows)] if own else target(piece, chip, grid.core)

    def hops(piece, chip, own):
        index, found = grid.chip(*chip), []
        for cross, wanted in grid.children(pieces[piece][3], chip):
            there, _ = grid.neighbour(cross)
            copy = pltpu.make_async_remote_copy(
                src_ref=source(piece, chip, own),
                dst_ref=target(piece, chip, grid.core),
                send_sem=send_sem.at[piece, index, grid.crosses.index(cross)],
                recv_sem=recv_sem.at[piece, index],
                device_id=grid.device(*there, grid.core),
                device_id_type=MESH,
            )
            found.append((wanted, copy))
        return found

    def pair(piece, chip, core, own=False, landing=False):
        index = grid.chip(*chip)
        return pltpu.make_async_remote_copy(
            src_ref=source(piece, chip, own),
            dst_ref=target(piece, chip, core),
            send_sem=pair_send.at[piece, index],
            recv_sem=(recv_sem if landing else pair_recv).at[piece, index],
            device_id=grid.partner(),
            device_id_type=MESH,
        )

    own_copies = [
        pltpu.make_async_copy(
            source(piece, grid.here(), True), target(piece, grid.here(), grid.core), own_sem.at[piece]
        )
        for piece in range(len(pieces))
    ]
    grid.greet_plane()

    def relay(chip, own):
        for piece in range(len(pieces)):
            if not own:
                pair(piece, chip, grid.core, landing=True).wait_recv()
            for wanted, copy in hops(piece, chip, own):
                under(wanted, copy.start)
            pair(piece, chip, grid.core, own).start()

    relay(grid.here(), True)
    for copy in own_copies:
        copy.start()

    def step(number, carry):
        relay(grid.entry(number), False)
        exchange.start(number - 1, grid.chips - 1)
        return carry

    lax.fori_loop(1, grid.chips, step, 0)

    def finish(number, carry):
        chip = grid.entry(number)
        for piece in range(len(pieces)):
            for wanted, copy in hops(piece, chip, False):
                under(wanted, copy.wait_send)
            pair(piece, chip, grid.core).wait_send()
            pair(piece, chip, 1 - grid.core).wait_recv()
        return carry

    lax.fori_loop(0, grid.chips, finish, 0)
    for copy in own_copies:
        copy.wait()
    exchange.finish()


def gather_call(fsdp_size, pieces, places, shards, shapes, collective_id, blocks, cut, sources, targets):
    count, chips = len(shards), fsdp_size // 2
    dma = pltpu.SemaphoreType.DMA
    moved = sum(s.size * s.dtype.itemsize for s in shapes)
    return pl.pallas_call(
        functools.partial(gather_kernel, fsdp_size, pieces, places, count, blocks, cut),
        out_shape=tuple(shapes) + tuple(targets),
        in_specs=[pl.BlockSpec(memory_space=pltpu.VMEM)] * count
        + [pl.BlockSpec(memory_space=pl.ANY)] * len(sources),
        out_specs=tuple([pl.BlockSpec(memory_space=pl.ANY)] * (count + len(targets))),
        scratch_shapes=[
            dma((len(pieces), chips, 4)),
            dma((len(pieces), chips)),
            dma((len(pieces), chips)),
            dma((len(pieces), chips)),
            dma((len(pieces),)),
            *exchange_sems(fsdp_size, len(sources)),
        ],
        compiler_params=pltpu.CompilerParams(collective_id=collective_id, has_side_effects=True),
        cost_estimate=pl.CostEstimate(flops=0, bytes_accessed=8 * moved, transcendentals=0),
    )(*shards, *sources)


class WeightGrads:
    inputs, outputs = 5, 3
    PIECES = (1, 3, 5)

    def __init__(self, slots, hidden, width):
        bf16 = jnp.bfloat16
        dma = pltpu.SemaphoreType.DMA
        self.hidden = hidden
        self.shapes = [jax.ShapeDtypeStruct((hidden, width), bf16)] * self.outputs
        self.scratch = [
            pltpu.VMEM((2, slots, BLOCK), bf16),
            pltpu.VMEM((slots, width), bf16),
            pltpu.VMEM((2, BLOCK, width), bf16),
            dma((2,)),
            dma((1,)),
            dma((2,)),
        ]

    def make(self, *refs):
        return WeightGradsRun(self, refs)


class WeightGradsRun:
    def __init__(self, job, refs):
        self.lefts, self.rights, self.outs = refs[:3], refs[3:5], refs[5:8]
        self.left, self.right, self.result = refs[8:11]
        self.left_sem, self.right_sem, self.out_sem = refs[11:]
        self.blocks = -(-job.hidden // BLOCK)
        self.rest = job.hidden - (self.blocks - 1) * BLOCK
        self.total = 3 * self.blocks

    def left_copy(self, which, number):
        slot, block = lax.rem(number, 2), lax.rem(number, self.blocks)
        span = pl.ds(pl.multiple_of(block * BLOCK, BLOCK), BLOCK)
        return pltpu.make_async_copy(
            self.lefts[which].at[:, span], self.left.at[slot], self.left_sem.at[slot]
        )

    def left_start(self, number):
        for which in range(3):
            pl.when(lax.div(number, self.blocks) == which)(self.left_copy(which, number).start)

    def right_copy(self, which):
        return pltpu.make_async_copy(self.rights[which], self.right, self.right_sem.at[0])

    def out_copies(self, which, number):
        slot, block = lax.rem(number, 2), lax.rem(number, self.blocks)
        full = pl.ds(pl.multiple_of(block * BLOCK, BLOCK), BLOCK)
        part = pl.ds((self.blocks - 1) * BLOCK, self.rest)
        out, sem = self.outs[which], self.out_sem.at[slot]
        return [
            (
                block < self.blocks - 1,
                pltpu.make_async_copy(self.result.at[slot], out.at[full], sem),
            ),
            (
                block == self.blocks - 1,
                pltpu.make_async_copy(self.result.at[slot, pl.ds(0, self.rest)], out.at[part], sem),
            ),
        ]

    def begin(self):
        self.right_copy(0).start()
        self.left_copy(0, jnp.int32(0)).start()

    def out_wait(self, number):
        for wanted, copy in self.out_copies(0, number):
            pl.when(wanted)(copy.wait)

    def run(self, number):
        slot = lax.rem(number, 2)
        self.left_copy(0, number).wait()
        pl.when(number + 1 < self.total)(lambda: self.left_start(number + 1))
        pl.when(lax.rem(number, 2 * self.blocks) == 0)(self.right_copy(0).wait)
        pl.when(number >= 2)(lambda: self.out_wait(number - 2))
        self.result[slot] = lax.dot_general(
            self.left[slot],
            self.right[...],
            (((0,), (0,)), ((), ())),
            preferred_element_type=jnp.float32,
        ).astype(jnp.bfloat16)
        for which in range(3):
            for wanted, copy in self.out_copies(which, number):
                pl.when(wanted & (lax.div(number, self.blocks) == which))(copy.start)
        pl.when(number == 2 * self.blocks - 1)(self.right_copy(1).start)

    def tick(self, step, piece):
        if piece in WeightGrads.PIECES:
            number = (step - 1) * len(WeightGrads.PIECES) + WeightGrads.PIECES.index(piece)
            pl.when((number >= 0) & (number < self.total))(lambda: self.run(number))

    def finish(self, steps):
        for number in range(len(WeightGrads.PIECES) * (steps - 1), self.total):
            self.run(jnp.int32(0) + number)
        for number in (self.total - 2, self.total - 1):
            self.out_wait(jnp.int32(0) + number)


def reduce_kernel(fsdp_size, dims, pieces, places, count, blocks, cut, side, *refs):
    moved, taken = len(cut), side.inputs if side else 0
    partials, sources = refs[:count], refs[count : count + moved]
    side_refs = refs[count + moved : count + moved + taken]
    refs = refs[count + moved + taken :]
    outs, targets = refs[:count], refs[count : count + moved]
    refs = refs[count + moved :]
    if side:
        side_refs, refs = side_refs + refs[: side.outputs], refs[side.outputs :]
    held, other, landed = (refs[i * count : (1 + i) * count] for i in range(3))
    send_sem, recv_sem, load_sem, pair_send, pair_recv = refs[3 * count : 3 * count + 5]
    refs = refs[3 * count + 5 :]
    grid = Grid(fsdp_size, dims)
    ways = len(grid.crosses)
    empty = grid.chips * ways
    exchange, job = None, None
    if moved:
        exchange = Exchange(fsdp_size, grid.x, blocks, sources, targets, cut, False, *refs[:3])
        refs = refs[3:]
    if side:
        job = side.make(*side_refs, *refs)

    def load(array, chip):
        index = grid.chip(*chip)
        return pltpu.make_async_copy(
            places[array](partials[array], chip, grid.core),
            held[array].at[index],
            load_sem.at[array, index],
        )

    def pair(array, chip):
        index = grid.chip(*chip)
        return pltpu.make_async_remote_copy(
            src_ref=places[array](partials[array], chip, 1 - grid.core),
            dst_ref=other[array].at[index],
            send_sem=pair_send.at[array, index],
            recv_sem=pair_recv.at[array, index],
            device_id=grid.partner(),
            device_id_type=MESH,
        )

    def hop(piece, chip, there, side_seen):
        array, first, rows, _ = pieces[piece]
        index = grid.chip(*chip)
        slot = index * ways + side_seen
        return pltpu.make_async_remote_copy(
            src_ref=held[array].at[index, pl.ds(first, rows)],
            dst_ref=landed[array].at[slot, pl.ds(first, rows)],
            send_sem=send_sem.at[piece, index],
            recv_sem=recv_sem.at[piece, slot],
            device_id=grid.device(*there, grid.core),
            device_id_type=MESH,
        )

    def add_up(piece, chip, root):
        array, first, rows, order = pieces[piece]
        index, slots, some = grid.chip(*chip), [], grid.z < 0
        for cross, wanted in grid.children(order, chip):
            way = grid.crosses.index(cross)
            under(wanted, hop(piece, chip, grid.here(), way).wait_recv)
            slot = index * ways + way
            slots.append(slot if wanted is None else jnp.where(wanted, slot, empty))
            some = None if wanted is None or some is None else jnp.logical_or(some, wanted)
        tile = 16 if rows % 16 == 0 else rows

        def add_all(used):
            def add(i, carry):
                span = pl.ds(pl.multiple_of(first + i * tile, tile), tile)
                total = held[array][index, span].astype(jnp.float32)
                total += other[array][index, span].astype(jnp.float32)
                for slot in used:
                    total += landed[array][slot, span].astype(jnp.float32)
                if root:
                    outs[array][span] = total
                else:
                    held[array][index, span] = total.astype(held[array].dtype)
                return carry

            lax.fori_loop(0, rows // tile, add, 0)

        if root or some is None:
            add_all(slots)
        else:
            pl.when(some)(lambda: add_all(slots))
            pl.when(jnp.logical_not(some))(lambda: add_all([]))

    def fetched(array, chip):
        load(array, chip).wait()
        pair(array, chip).wait_recv()

    firsts = [min(p for p, piece in enumerate(pieces) if piece[0] == a) for a in range(count)]
    for array in range(count):
        landed[array][empty] = jnp.zeros(landed[array].shape[1:], landed[array].dtype)
    if moved:
        grid.greet_plane()
    else:
        grid.greet()
    last = grid.chips - 1

    def begin(number, carry):
        chip = grid.entry(last - number)
        for array in range(count):
            load(array, chip).start()
            pair(array, chip).start()
        return carry

    lax.fori_loop(0, grid.chips, begin, 0)
    if job:
        job.begin()

    def step(number, carry):
        chip = grid.entry(last - number)
        for piece in range(len(pieces)):
            if piece in firsts:
                fetched(pieces[piece][0], chip)
            add_up(piece, chip, False)
            hop(piece, chip, *grid.parent(pieces[piece][3], chip)).start()
            if job:
                job.tick(number, piece)
        if exchange:
            exchange.start(number, last)
        return carry

    lax.fori_loop(0, last, step, 0)
    if job:
        job.finish(last)
    for piece in range(len(pieces)):
        if piece in firsts:
            fetched(pieces[piece][0], grid.here())
        add_up(piece, grid.here(), True)

    def finish(number, carry):
        chip = grid.entry(last - number)
        for array in range(count):
            pair(array, chip).wait_send()

        def sent():
            for piece in range(len(pieces)):
                hop(piece, chip, *grid.parent(pieces[piece][3], chip)).wait_send()

        pl.when(number < last)(sent)
        return carry

    lax.fori_loop(0, grid.chips, finish, 0)
    if exchange:
        exchange.finish()


def reduce_call(
    fsdp_size,
    dims,
    pieces,
    places,
    partials,
    shapes,
    collective_id,
    blocks=0,
    cut=(),
    sources=(),
    targets=(),
    side=None,
    extra=(),
):
    count = len(partials)
    ways = 4 if "x" in dims else 3
    chips = fsdp_size // 2 * (2 if "x" in dims else 1)
    dma = pltpu.SemaphoreType.DMA
    held = [pltpu.VMEM((chips, *s), p.dtype) for s, p in zip(shapes, partials)]
    landed = [pltpu.VMEM((chips * ways + 1, *s), p.dtype) for s, p in zip(shapes, partials)]
    moved = sum(p.size * p.dtype.itemsize for p in partials)
    side_outs = tuple(side.shapes) if side else ()
    return pl.pallas_call(
        functools.partial(reduce_kernel, fsdp_size, dims, pieces, places, count, blocks, cut, side),
        out_shape=tuple(jax.ShapeDtypeStruct(s, jnp.float32) for s in shapes)
        + tuple(targets)
        + side_outs,
        in_specs=[pl.BlockSpec(memory_space=pl.ANY)] * (count + len(sources) + len(extra)),
        out_specs=tuple(
            [pl.BlockSpec(memory_space=pltpu.VMEM)] * count
            + [pl.BlockSpec(memory_space=pl.ANY)] * (len(targets) + len(side_outs))
        ),
        scratch_shapes=[
            *held,
            *held,
            *landed,
            dma((len(pieces), chips)),
            dma((len(pieces), chips * ways)),
            dma((count, chips)),
            dma((count, chips)),
            dma((count, chips)),
            *exchange_sems(fsdp_size, len(sources)),
            *(side.scratch if side else ()),
        ],
        compiler_params=pltpu.CompilerParams(
            collective_id=collective_id, has_side_effects=True, vmem_limit_bytes=67043328
        ),
        cost_estimate=pl.CostEstimate(flops=0, bytes_accessed=16 * moved, transcendentals=0),
    )(*partials, *sources, *extra)


def token_row(chip, core, rows):
    x, y, z = chip
    return ((z * 4 + y * 2 + core) * 2 + x) * rows


def reduce_tokens(partials, collective_id):
    fsdp_size = lax.axis_size("fsdp")
    rows = partials[0].shape[0] // (2 * fsdp_size)
    unit = rows // 4

    def place(ref, chip, core):
        return ref.at[pl.ds(pl.multiple_of(token_row(chip, core, rows), 16), rows)]

    pieces = [(0, at * unit, unit, order) for at, order in enumerate(("xyz", "zyx", "zxy", "zyx"))]
    pieces += [(array, 0, rows, "zyx") for array in range(1, len(partials))]
    shapes = [(rows, p.shape[1]) for p in partials]
    return reduce_call(
        fsdp_size, "xyz", pieces, [place] * len(partials), partials, shapes, collective_id
    )


def plane_row(chip, core):
    return chip[2] * 4 + chip[1] * 2 + core


def row_place(rows):
    def place(ref, chip, core, first=0, count=rows):
        return ref.at[pl.ds(pl.multiple_of(plane_row(chip, core) * rows + first, 8), count)]

    return place


def column_place(columns, rows):
    def place(ref, chip, core, first=0, count=rows):
        start = pl.multiple_of(plane_row(chip, core) * columns, 128)
        return ref.at[pl.ds(first, count), pl.ds(start, columns)]

    return place


def weight_pieces(query, latent, expand, output, small):
    return [
        (4, 0, small, "zy"),
        (0, 0, query // 2, "zy"),
        (1, 0, latent, "zy"),
        (0, query // 2, query // 2, "zy"),
        (2, 0, expand, "yz"),
        (3, 0, output // 2, "zy"),
        (3, output // 2, output // 2, "zy"),
    ]


def block_span(block):
    return pl.ds(pl.multiple_of(block * BLOCK, BLOCK), BLOCK)


def cut_columns(rows):
    def to_owner(source, target, block, other):
        there = pl.ds(pl.multiple_of(other * rows, rows), rows)
        return source.at[:, block_span(block)], target.at[there]

    def from_owner(source, target, block, other):
        there = pl.ds(pl.multiple_of(other * rows, rows), rows)
        return source.at[there], target.at[:, block_span(block)]

    return to_owner, from_owner


def cut_rows(columns):
    def to_owner(source, target, block, other):
        there = pl.ds(pl.multiple_of(other * columns, columns), columns)
        return source.at[block_span(block)], target.at[:, there]

    def from_owner(source, target, block, other):
        there = pl.ds(pl.multiple_of(other * columns, columns), columns)
        return source.at[:, there], target.at[block_span(block)]

    return to_owner, from_owner


def gather_weights(query, latent, expand, output, small, gate, up, down, collective_id):
    size = lax.axis_size("fsdp")
    shards = [query, latent, expand, output, small]
    places = [row_place(s.shape[0]) for s in shards]
    shapes = [
        jax.ShapeDtypeStruct((s.shape[0] * size, s.shape[1]), s.dtype) for s in shards
    ]
    for at in (1, 3):
        rows, columns = shards[at].shape
        places[at] = column_place(columns, rows)
        shapes[at] = jax.ShapeDtypeStruct((rows, columns * size), shards[at].dtype)
    columns, rows = cut_columns(gate.shape[0]), cut_rows(down.shape[1])
    tall = jax.ShapeDtypeStruct((gate.shape[0] * size, BLOCK), gate.dtype)
    flat = jax.ShapeDtypeStruct((BLOCK, down.shape[1] * size), down.dtype)
    return gather_call(
        size,
        weight_pieces(*[s.shape[0] for s in shards]),
        places,
        shards,
        shapes,
        collective_id,
        gate.shape[1] // BLOCK,
        (columns[0], columns[0], rows[0]),
        [gate, up, down],
        [tall, tall, flat],
    )


def reduce_weights(
    query, latent, expand, output, small, gate, up, down, blocks, collective_id, side, extra
):
    size = lax.axis_size("fsdp")
    partials = [query, latent, expand, output, small]
    shapes = [(p.shape[0] // size, p.shape[1]) for p in partials]
    places = [row_place(s[0]) for s in shapes]
    for at in (1, 3):
        rows, columns = partials[at].shape
        shapes[at] = (rows, columns // size)
        places[at] = column_place(columns // size, rows)
    columns, rows = cut_columns(gate.shape[0] // size), cut_rows(down.shape[1] // size)
    wide = jax.ShapeDtypeStruct((gate.shape[0] // size, blocks * BLOCK), gate.dtype)
    long = jax.ShapeDtypeStruct((blocks * BLOCK, down.shape[1] // size), down.dtype)
    return reduce_call(
        size,
        "zy",
        weight_pieces(*[s[0] for s in shapes]),
        places,
        partials,
        shapes,
        collective_id,
        blocks,
        (columns[1], columns[1], rows[1]),
        [gate, up, down],
        [wide, wide, long],
        side,
        extra,
    )


class Spread:
    ORDERS = ("xyz", "zyx", "zxy", "zyx")

    def __init__(self, fsdp_size, own, room, lead, sems):
        self.lead = lead
        self.grid = Grid(fsdp_size, "xyz", 1)
        self.own, self.room = own, room
        self.rows = own.shape[0]
        self.part = self.rows // len(self.ORDERS)
        self.send_sem, self.recv_sem, self.pair_send, self.pair_recv = sems
        self.units = fsdp_size // 2

    def unit(self, step):
        grid = self.grid
        flip = lax.rem(step, 2)
        return grid.y + flip - 2 * grid.y * flip, grid.level(lax.div(step, 2))

    def span(self, chip, piece):
        start = token_row(chip, self.grid.core, self.rows) + piece * self.part
        return self.room.at[pl.ds(pl.multiple_of(start, self.part), self.part)]

    def copies(self, chip, piece, own=False):
        grid, found = self.grid, []
        index, here = grid.chip(*chip), self.span(chip, piece)
        source = self.own.at[pl.ds(piece * self.part, self.part)] if own else here
        for cross, wanted in grid.children(self.ORDERS[piece], chip):
            there, _ = grid.neighbour(cross)
            copy = pltpu.make_async_remote_copy(
                src_ref=source,
                dst_ref=here,
                send_sem=self.send_sem.at[piece, index, grid.crosses.index(cross)],
                recv_sem=self.recv_sem.at[piece, index],
                device_id=grid.device(*there, grid.core),
                device_id_type=MESH,
            )
            found.append((wanted, copy))
        return found

    def pair(self, chip, piece, own=False, landing=False):
        grid = self.grid
        index, here = grid.chip(*chip), self.span(chip, piece)
        return pltpu.make_async_remote_copy(
            src_ref=self.own.at[pl.ds(piece * self.part, self.part)] if own else here,
            dst_ref=here,
            send_sem=self.pair_send.at[piece, index],
            recv_sem=(self.recv_sem if landing else self.pair_recv).at[piece, index],
            device_id=grid.partner(),
            device_id_type=MESH,
        )

    def relay(self, chip, piece, own=False):
        if not own:
            self.pair(chip, piece, landing=True).wait_recv()
        for wanted, copy in self.copies(chip, piece, own):
            under(wanted, copy.start)
        self.pair(chip, piece, own).start()

    def begin(self):
        grid = self.grid
        grid.greet()
        for piece in range(len(self.ORDERS)):
            self.relay(grid.here(), piece, own=True)
        start = token_row(grid.here(), grid.core, self.rows)
        self.room[pl.ds(pl.multiple_of(start, self.rows), self.rows)] = self.own[...]

        def early(number, carry):
            chip = grid.entry(number)
            for piece in range(len(self.ORDERS)):
                self.relay(chip, piece)
            return carry

        lax.fori_loop(1, self.lead, early, 0)

    def ahead(self, step):
        return [self.grid.entry(self.lead + 2 * step + one) for one in (0, 1)]

    def tick(self, step, chips, number):
        pieces = len(self.ORDERS)
        late = self.lead + 2 * step + number // pieces
        chip = chips[number // pieces]
        pl.when(late < 2 * self.units)(lambda: self.relay(chip, number % pieces))

    def arrived(self, step):
        y, z = self.unit(step)
        for x in (0, 1):
            for piece in range(len(self.ORDERS)):
                self.pair((x, y, z), piece).wait_recv()

    def drain(self):
        def finish(number, carry):
            chip = self.grid.entry(number)
            for piece in range(len(self.ORDERS)):
                for wanted, copy in self.copies(chip, piece):
                    under(wanted, copy.wait_send)
                self.pair(chip, piece).wait_send()
            return carry

        lax.fori_loop(0, 2 * self.units, finish, 0)


def spread_sems(fsdp_size):
    dma = pltpu.SemaphoreType.DMA
    return [dma((4, fsdp_size, 4)), dma((4, fsdp_size)), dma((4, fsdp_size)), dma((4, fsdp_size))]


class Stage:
    def __init__(self, buffers, results, sems):
        self.buffers, self.results, self.sems = buffers, results, sems

    def copy(self, number, step, unit):
        buffer = self.buffers[number]
        rows = buffer.shape[1]
        slot = lax.rem(step, 2)
        there = self.results[number].at[pl.ds(pl.multiple_of(unit * rows, rows), rows)]
        return pltpu.make_async_copy(buffer.at[slot], there, self.sems.at[number, slot])

    def reuse(self, step):
        def wait():
            for number in range(len(self.buffers)):
                self.copy(number, step, 0).wait()

        pl.when(step >= 2)(wait)

    def put(self, number, step, unit):
        self.copy(number, step, unit).start()

    def finish(self, steps):
        for step in (steps - 2, steps - 1):
            for number in range(len(self.buffers)):
                self.copy(number, step, 0).wait()


def dot(left, right):
    return jnp.dot(left, right, preferred_element_type=jnp.float32)


def dot_nt(left, right):
    return lax.dot_general(
        left, right, (((1,), (1,)), ((), ())), preferred_element_type=jnp.float32
    )


def dispatch_of(place_ref, sequence, capacity, seq_len):
    row = place_ref[pl.ds(sequence, 1), :]
    slot = lax.broadcasted_iota(jnp.int32, (capacity, seq_len), 0)
    return jnp.where(slot == row, 1.0, 0.0)


def forward_kernel(
    fsdp_size,
    experts,
    capacity,
    own,
    place_ref,
    gate_hbm,
    up_hbm,
    down_hbm,
    wide_hbm,
    block_hbm,
    tokens_out,
    received_out,
    gate_out,
    up_out,
    hidden_out,
    weight_out,
    shared_out,
    sh_out,
    part_out,
    room,
    picks,
    packs,
    chances,
    tall,
    received,
    gate_act,
    up_act,
    hidden,
    weight,
    shared,
    sh_act,
    part,
    gate_ref,
    up_ref,
    down_ref,
    wide_ref,
    block_ref,
    weight_sem,
    stage_sem,
    room_sem,
    *sems,
):
    f32, bf16 = jnp.float32, jnp.bfloat16
    seq_len = place_ref.shape[1]
    spread = Spread(fsdp_size, own, room, 3, sems)
    expert = lax.axis_index("fsdp")
    stage = Stage(
        [received, gate_act, up_act, hidden, weight, shared, sh_act, part],
        [received_out, gate_out, up_out, hidden_out, weight_out, shared_out, sh_out, part_out],
        stage_sem,
    )
    lanes = lax.broadcasted_iota(jnp.int32, (2 * seq_len, BLOCK), 1)

    def tokens_copy(unit):
        span = pl.ds(pl.multiple_of(unit * 2 * seq_len, 2 * seq_len), 2 * seq_len)
        return pltpu.make_async_copy(room.at[span], tokens_out.at[span], room_sem.at[unit])

    weights = [
        pltpu.make_async_copy(source, target, weight_sem.at[number])
        for number, (source, target) in enumerate([(gate_hbm, gate_ref), (up_hbm, up_ref), (down_hbm, down_ref), (wide_hbm, wide_ref), (block_hbm, block_ref)])
    ]
    for copy in weights:
        copy.start()
    spread.begin()
    for copy in weights:
        copy.wait()
    units = down_ref.shape[0]
    if units < hidden.shape[2]:
        hidden[:, :, units:] = jnp.zeros((2, 2 * capacity, hidden.shape[2] - units), bf16)
    for one in (0, 1):
        tall[one, capacity:] = block_ref[...]

    def body(step, carry):
        slot = lax.rem(step, 2)
        y, z = spread.unit(step)
        unit = z * 2 + y
        chips = spread.ahead(step)
        spread.arrived(step)
        tokens_copy(unit).start()
        stage.reuse(step)
        rows = [
            pl.ds(pl.multiple_of((2 * unit + one) * seq_len, seq_len), seq_len) for one in (0, 1)
        ]
        slots = [pl.ds(one * capacity, capacity) for one in (0, 1)]
        own_rows = [pl.ds(one * seq_len, seq_len) for one in (0, 1)]
        spread.tick(step, chips, 0)
        for one in (0, 1):
            pick = dispatch_of(place_ref, 2 * unit + one, capacity, seq_len)
            picks[one] = pick.astype(bf16)
            packs[one, :, :capacity] = jnp.transpose(pick).astype(bf16)
            received[slot, slots[one]] = dot(picks[one], room[rows[one]]).astype(bf16)
        stage.put(0, step, unit)
        spread.tick(step, chips, 1)
        both_rows = pl.ds(pl.multiple_of(unit * 2 * seq_len, 2 * seq_len), 2 * seq_len)
        wide = dot(room[both_rows], wide_ref[...])
        shared[slot] = wide[:, : 2 * BLOCK]
        gate_sh, up_sh = wide[:, :BLOCK], wide[:, BLOCK : 2 * BLOCK]
        act = (silu_parts(gate_sh)[0] * up_sh).astype(bf16)
        sh_act[slot] = act
        for one in (0, 1):
            packs[one, :, capacity:] = act[one * seq_len : (one + 1) * seq_len]
        logits = jnp.where(lanes < experts, wide[:, 2 * BLOCK :], MASKED)
        logit_exp = jnp.exp(logits - jnp.max(logits, axis=1, keepdims=True))
        chance = jnp.sum(jnp.where(lanes == expert, logit_exp, 0.0), axis=1, keepdims=True)
        chance = chance / jnp.sum(logit_exp, axis=1, keepdims=True)
        coarse = chance.astype(bf16).astype(f32)
        chances[...] = jnp.where(
            lanes == 0, coarse, jnp.where(lanes == 1, chance - coarse, 0.0)
        ).astype(bf16)
        stage.put(5, step, unit)
        stage.put(6, step, unit)
        spread.tick(step, chips, 2)
        gate_act[slot] = dot_nt(received[slot], gate_ref[...])
        stage.put(1, step, unit)
        spread.tick(step, chips, 3)
        up_act[slot] = dot_nt(received[slot], up_ref[...])
        stage.put(2, step, unit)
        spread.tick(step, chips, 4)
        for one in (0, 1):
            halves = dot(picks[one], chances[own_rows[one]])
            scale = halves[:, 0:1] + halves[:, 1:2]
            weight[slot, slots[one]] = jnp.broadcast_to(scale, (capacity, BLOCK))
            act = silu_parts(gate_act[slot, slots[one]])[0] * up_act[slot, slots[one]]
            hidden[slot, slots[one], :units] = (scale * act).astype(bf16)
        stage.put(3, step, unit)
        stage.put(4, step, unit)
        spread.tick(step, chips, 5)
        result = dot(hidden[slot, :, :units], down_ref[...]).astype(bf16)
        for one in (0, 1):
            tall[one, :capacity] = result[one * capacity : (one + 1) * capacity]
        spread.tick(step, chips, 6)
        part[slot, own_rows[0]] = dot(packs[0], tall[0]).astype(bf16)
        spread.tick(step, chips, 7)
        part[slot, own_rows[1]] = dot(packs[1], tall[1]).astype(bf16)
        stage.put(7, step, unit)
        return carry

    lax.fori_loop(0, spread.units, body, 0)
    stage.finish(spread.units)
    for unit in range(spread.units):
        tokens_copy(unit).wait()
    spread.drain()


def experts_forward(own, place, gate, up, down, wide, block, capacity, experts, collective_id):
    fsdp_size = lax.axis_size("fsdp")
    f32, bf16 = jnp.float32, jnp.bfloat16
    seq_len, width, hidden = place.shape[1], own.shape[1], gate.shape[0]
    tokens, slots = fsdp_size * seq_len, fsdp_size * capacity
    padded = -(-hidden // BLOCK) * BLOCK
    shape = jax.ShapeDtypeStruct
    outs = [
        shape((tokens, width), bf16),
        shape((slots, width), bf16),
        shape((slots, hidden), f32),
        shape((slots, hidden), f32),
        shape((slots, padded), bf16),
        shape((slots, BLOCK), f32),
        shape((tokens, 2 * BLOCK), f32),
        shape((tokens, BLOCK), bf16),
        shape((tokens, width), bf16),
    ]
    stages = [pltpu.VMEM((2, 2 * o.shape[0] // fsdp_size, o.shape[1]), o.dtype) for o in outs[1:]]
    dma = pltpu.SemaphoreType.DMA
    return pl.pallas_call(
        functools.partial(forward_kernel, fsdp_size, experts, capacity),
        out_shape=tuple(outs),
        in_specs=[pl.BlockSpec(memory_space=pltpu.VMEM)] * 2
        + [pl.BlockSpec(memory_space=pl.ANY)] * 5,
        out_specs=tuple([pl.BlockSpec(memory_space=pl.ANY)] * len(outs)),
        scratch_shapes=[
            pltpu.VMEM((tokens, width), bf16),
            pltpu.VMEM((2, capacity, seq_len), bf16),
            pltpu.VMEM((2, seq_len, capacity + BLOCK), bf16),
            pltpu.VMEM((2 * seq_len, BLOCK), bf16),
            pltpu.VMEM((2, capacity + BLOCK, width), bf16),
            *stages,
            *[pltpu.VMEM(w.shape, w.dtype) for w in (gate, up, down, wide, block)],
            dma((5,)),
            dma((len(stages), 2)),
            dma((fsdp_size // 2,)),
            *spread_sems(fsdp_size),
        ],
        compiler_params=pltpu.CompilerParams(
            collective_id=collective_id, has_side_effects=True, vmem_limit_bytes=67043328
        ),
        cost_estimate=pl.CostEstimate(
            flops=6 * slots * width * hidden, bytes_accessed=100_000_000, transcendentals=0
        ),
    )(own, place, gate, up, down, wide, block)


def backward_kernel(
    fsdp_size,
    capacity,
    own,
    place_ref,
    gate_hbm,
    up_hbm,
    down_hbm,
    pair_hbm,
    block_hbm,
    gate_in,
    up_in,
    weight_in,
    shared_in,
    grads_out,
    slots_out,
    gate_out,
    up_out,
    pair_out,
    chance_out,
    part_out,
    room,
    picks,
    packs,
    tall,
    gate_act,
    up_act,
    weight,
    shared,
    picked,
    gate_grad,
    up_grad,
    pair_grad,
    chance_grad,
    part,
    gate_ref,
    up_ref,
    down_ref,
    pair_ref,
    block_ref,
    weight_sem,
    load_sem,
    stage_sem,
    room_sem,
    *sems,
):
    f32, bf16 = jnp.float32, jnp.bfloat16
    seq_len = place_ref.shape[1]
    spread = Spread(fsdp_size, own, room, 4, sems)
    expert = lax.axis_index("fsdp")
    stage = Stage(
        [picked, gate_grad, up_grad, pair_grad, chance_grad, part],
        [slots_out, gate_out, up_out, pair_out, chance_out, part_out],
        stage_sem,
    )
    saved = [gate_in, up_in, weight_in, shared_in]
    loads = [gate_act, up_act, weight, shared]

    def load(number, step):
        y, z = spread.unit(step)
        slot, rows = lax.rem(step, 2), loads[number].shape[1]
        span = pl.ds(pl.multiple_of((z * 2 + y) * rows, rows), rows)
        return pltpu.make_async_copy(
            saved[number].at[span], loads[number].at[slot], load_sem.at[number, slot]
        )

    def grads_copy(unit):
        span = pl.ds(pl.multiple_of(unit * 2 * seq_len, 2 * seq_len), 2 * seq_len)
        return pltpu.make_async_copy(room.at[span], grads_out.at[span], room_sem.at[unit])

    for number in range(len(saved)):
        load(number, 0).start()
    weights = [
        pltpu.make_async_copy(source, target, weight_sem.at[number])
        for number, (source, target) in enumerate([(gate_hbm, gate_ref), (up_hbm, up_ref), (down_hbm, down_ref), (pair_hbm, pair_ref), (block_hbm, block_ref)])
    ]
    for copy in weights:
        copy.start()
    spread.begin()
    for copy in weights:
        copy.wait()
    units = down_ref.shape[0]
    if units < gate_grad.shape[2]:
        for grad in (gate_grad, up_grad):
            grad[:, :, units:] = jnp.zeros((2, 2 * capacity, grad.shape[2] - units), bf16)
    for one in (0, 1):
        tall[one, capacity:] = pair_ref[...]
    expert_lane = lax.broadcasted_iota(jnp.int32, (capacity, BLOCK), 1) == expert

    def body(step, carry):
        slot = lax.rem(step, 2)
        y, z = spread.unit(step)
        unit = z * 2 + y
        later = step + 1
        chips = spread.ahead(step)
        spread.arrived(step)
        grads_copy(unit).start()
        stage.reuse(step)
        rows = [
            pl.ds(pl.multiple_of((2 * unit + one) * seq_len, seq_len), seq_len) for one in (0, 1)
        ]
        both_rows = pl.ds(pl.multiple_of(unit * 2 * seq_len, 2 * seq_len), 2 * seq_len)
        slots = [pl.ds(one * capacity, capacity) for one in (0, 1)]
        own_rows = [pl.ds(one * seq_len, seq_len) for one in (0, 1)]
        for number in range(len(saved)):
            load(number, step).wait()

        def ahead():
            for number in range(len(saved)):
                load(number, later).start()

        pl.when(later < spread.units)(ahead)
        spread.tick(step, chips, 0)
        for one in (0, 1):
            pick = dispatch_of(place_ref, 2 * unit + one, capacity, seq_len)
            picks[one] = pick.astype(bf16)
            packs[one, :, :capacity] = jnp.transpose(pick).astype(bf16)
            picked[slot, slots[one]] = dot(picks[one], room[rows[one]]).astype(bf16)
        stage.put(0, step, unit)
        spread.tick(step, chips, 1)
        raw = dot_nt(picked[slot], down_ref[...])
        scale = weight[slot, :, 0:1]
        silu_gate, slope = silu_parts(gate_act[slot])
        up_value = up_act[slot]
        gate_sum = jnp.sum(raw * (silu_gate * up_value), axis=1, keepdims=True)
        scaled = scale * raw
        gate_grad[slot, :, :units] = (scaled * up_value * slope).astype(bf16)
        up_grad[slot, :, :units] = (scaled * silu_gate).astype(bf16)
        stage.put(1, step, unit)
        stage.put(2, step, unit)
        spread.tick(step, chips, 2)
        for one in (0, 1):
            column = gate_sum[one * capacity : (one + 1) * capacity]
            column = jnp.where(expert_lane, column, 0.0).astype(bf16)
            chance_grad[slot, own_rows[one]] = dot(packs[one, :, :capacity], column).astype(bf16)
        stage.put(4, step, unit)
        grad_sh = dot_nt(room[both_rows], block_ref[...])
        silu_sh, slope_sh = silu_parts(shared[slot, :, :BLOCK])
        gate_sh = (grad_sh * shared[slot, :, BLOCK:] * slope_sh).astype(bf16)
        up_sh = (grad_sh * silu_sh).astype(bf16)
        pair_grad[slot, :, :BLOCK] = gate_sh
        pair_grad[slot, :, BLOCK:] = up_sh
        for one in (0, 1):
            own_seq = slice(one * seq_len, (one + 1) * seq_len)
            packs[one, :, capacity : capacity + BLOCK] = gate_sh[own_seq]
            packs[one, :, capacity + BLOCK :] = up_sh[own_seq]
        stage.put(3, step, unit)
        spread.tick(step, chips, 3)
        back = dot(gate_grad[slot, :, :units], gate_ref[...])
        spread.tick(step, chips, 4)
        back = (back + dot(up_grad[slot, :, :units], up_ref[...])).astype(bf16)
        for one in (0, 1):
            tall[one, :capacity] = back[one * capacity : (one + 1) * capacity]
        spread.tick(step, chips, 5)
        part[slot, own_rows[0]] = dot(packs[0], tall[0]).astype(bf16)
        spread.tick(step, chips, 6)
        part[slot, own_rows[1]] = dot(packs[1], tall[1]).astype(bf16)
        stage.put(5, step, unit)
        spread.tick(step, chips, 7)
        return carry

    lax.fori_loop(0, spread.units, body, 0)
    stage.finish(spread.units)
    for unit in range(spread.units):
        grads_copy(unit).wait()
    spread.drain()


def experts_backward(
    own, place, gate, up, down, pair, block, gate_act, up_act, weight, shared, capacity, collective_id
):
    fsdp_size = lax.axis_size("fsdp")
    bf16 = jnp.bfloat16
    seq_len, width, hidden = place.shape[1], own.shape[1], gate.shape[0]
    tokens, slots = fsdp_size * seq_len, fsdp_size * capacity
    padded = -(-hidden // BLOCK) * BLOCK
    shape = jax.ShapeDtypeStruct
    outs = [
        shape((tokens, width), bf16),
        shape((slots, width), bf16),
        shape((slots, padded), bf16),
        shape((slots, padded), bf16),
        shape((tokens, 2 * BLOCK), bf16),
        shape((tokens, BLOCK), bf16),
        shape((tokens, width), bf16),
    ]

    def slots_of(arrays):
        return [pltpu.VMEM((2, 2 * a.shape[0] // fsdp_size, a.shape[1]), a.dtype) for a in arrays]

    saved = [gate_act, up_act, weight, shared]
    dma = pltpu.SemaphoreType.DMA
    return pl.pallas_call(
        functools.partial(backward_kernel, fsdp_size, capacity),
        out_shape=tuple(outs),
        in_specs=[pl.BlockSpec(memory_space=pltpu.VMEM)] * 2
        + [pl.BlockSpec(memory_space=pl.ANY)] * 9,
        out_specs=tuple([pl.BlockSpec(memory_space=pl.ANY)] * len(outs)),
        scratch_shapes=[
            pltpu.VMEM((tokens, width), bf16),
            pltpu.VMEM((2, capacity, seq_len), bf16),
            pltpu.VMEM((2, seq_len, capacity + 2 * BLOCK), bf16),
            pltpu.VMEM((2, capacity + 2 * BLOCK, width), bf16),
            *slots_of(saved),
            *slots_of(outs[1:]),
            *[pltpu.VMEM(w.shape, w.dtype) for w in (gate, up, down, pair, block)],
            dma((5,)),
            dma((4, 2)),
            dma((len(outs) - 1, 2)),
            dma((fsdp_size // 2,)),
            *spread_sems(fsdp_size),
        ],
        compiler_params=pltpu.CompilerParams(
            collective_id=collective_id, has_side_effects=True, vmem_limit_bytes=67043328
        ),
        cost_estimate=pl.CostEstimate(
            flops=6 * slots * width * hidden, bytes_accessed=100_000_000, transcendentals=0
        ),
    )(own, place, gate, up, down, pair, block, *saved)


def token_shards(
    inputs,
    teacher,
    valid_mask,
    prefix,
    routes,
    norm_gain,
    query_weight,
    latent_weight,
    latent_gain,
    expand_weight,
    output_weight,
    moe_gain,
    router_weight,
    shared_gate,
    shared_up,
    shared_down,
    expert_gate,
    expert_up,
    expert_down,
):
    f32 = jnp.float32
    bf16 = jnp.bfloat16
    tp_size = lax.axis_size("tp")
    fsdp_size = lax.axis_size("fsdp")
    own_tp = lax.axis_index("tp")
    own_expert = lax.axis_index("fsdp")
    local_heads = HEADS // tp_size
    own_rows = inputs.shape[0]
    width = inputs.shape[1]
    seq_len = own_rows * tp_size

    expert_count = router_weight.shape[1]
    route_rows = routes.shape[1] * seq_len // BLOCK
    valid_rows = seq_len // BLOCK
    parts = [
        routes.T.reshape(route_rows, BLOCK).astype(f32),
        valid_mask.reshape(valid_rows, BLOCK).astype(f32),
        norm_gain.reshape(1, BLOCK).astype(f32),
        moe_gain.reshape(1, BLOCK).astype(f32),
        jnp.pad(latent_gain, (0, BLOCK - latent_gain.shape[0])).reshape(1, BLOCK).astype(f32),
        router_weight.T.astype(f32),
    ]
    small = jnp.concatenate(parts, axis=0)
    small_rows = -(-small.shape[0] // 8) * 8
    small = jnp.pad(small, ((0, small_rows - small.shape[0]), (0, 0)))
    blocks = shared_gate.shape[1] // BLOCK
    (
        query_full,
        latent_full,
        expand_full,
        output_full,
        small_all,
        gate_block,
        up_block,
        down_block,
    ) = gather_weights(
        query_weight,
        latent_weight.T,
        expand_weight,
        output_weight,
        small,
        shared_gate,
        shared_up,
        shared_down,
        1,
    )
    small_all = small_all.reshape(fsdp_size, small_rows, BLOCK)
    gain_row = route_rows + valid_rows
    norm_gains = small_all[:, gain_row].reshape(width)
    latent_gains = small_all[:, gain_row + 2, : latent_gain.shape[0]].reshape(RANK)

    hidden = tp_gather(inputs, own_tp).astype(f32)
    cosine, sine_part = rope_tables(seq_len, ROPE)
    inverse_in = lax.rsqrt(jnp.mean(hidden * hidden, axis=-1, keepdims=True) + EPSILON)
    normal_in = hidden * inverse_in
    norm_scale = norm_gains.astype(f32)
    normed = (normal_in * norm_scale).astype(bf16)
    query_lin = jnp.dot(normed, query_full, preferred_element_type=f32).reshape(
        seq_len, local_heads, NOPE + ROPE
    )
    queries = jnp.concatenate(
        [
            query_lin[..., :NOPE],
            rotate(query_lin[..., NOPE:], cosine[:, None, :], sine_part[:, None, :]),
        ],
        axis=-1,
    ).astype(bf16)
    latent_lin = jnp.einsum("td,rd->tr", normed, latent_full, preferred_element_type=f32)
    latent_raw = latent_lin[:, :RANK]
    inverse_lat = lax.rsqrt(jnp.mean(latent_raw * latent_raw, axis=-1, keepdims=True) + EPSILON)
    latent_unit = latent_raw * inverse_lat
    latent_scale = latent_gains.astype(f32)
    latent = (latent_unit * latent_scale).astype(bf16)
    key_rope = rotate(latent_lin[:, RANK:], cosine, sine_part).astype(bf16)
    keys_values = (
        jnp.dot(latent, expand_full, preferred_element_type=f32)
        .astype(bf16)
        .reshape(seq_len, local_heads, NOPE + VDIM)
    )
    key_nope = keys_values[..., :NOPE]
    values = keys_values[..., NOPE:]
    query_nope = queries[..., :NOPE]
    query_rope = queries[..., NOPE:]
    score_scale = 1.0 / math.sqrt(NOPE + ROPE)
    position = jnp.arange(seq_len, dtype=jnp.int32)
    visible = (position[None, :] <= position[:, None]) | (position[None, :] < prefix[0])
    raw_scores = jnp.einsum("ihd,jhd->hij", query_nope, key_nope, preferred_element_type=f32)
    raw_scores = raw_scores + jnp.einsum(
        "ihd,jd->hij", query_rope, key_rope, preferred_element_type=f32
    )
    scores = jnp.where(visible[None], raw_scores * score_scale, MASKED)
    row_max = jnp.max(scores, axis=-1, keepdims=True)
    shifted = jnp.exp(scores - row_max)
    attn_probs = shifted / jnp.sum(shifted, axis=-1, keepdims=True)
    probs_low = attn_probs.astype(bf16)
    heads_out = (
        jnp.einsum("hij,jhd->ihd", probs_low, values, preferred_element_type=f32)
        .astype(bf16)
        .reshape(seq_len, local_heads * VDIM)
    )
    attended = jnp.dot(heads_out, output_full, preferred_element_type=f32)
    small_all, gate_block, up_block, down_block, attended = lax.optimization_barrier(
        (small_all, gate_block, up_block, down_block, attended)
    )
    attended = tp_scatter(attended, own_tp, own_rows)

    routes_all = small_all[:, :route_rows].reshape(fsdp_size, routes.shape[1], seq_len)
    valid_all = small_all[:, route_rows:gain_row]
    moe_gains = small_all[:, gain_row + 1].reshape(width)
    router_rows = small_all[:, gain_row + 3 : gain_row + 3 + expert_count]
    router_full = jnp.transpose(router_rows, (1, 0, 2)).reshape(expert_count, width).astype(bf16)
    holds_block = block_of(own_expert, fsdp_size // 2) < blocks
    gate_block = jnp.where(holds_block, gate_block, 0)
    up_block = jnp.where(holds_block, up_block, 0)
    down_block = jnp.where(holds_block, down_block, 0)

    middle = inputs.astype(f32) + attended
    inverse_mid = lax.rsqrt(jnp.mean(middle * middle, axis=-1, keepdims=True) + EPSILON)
    normal_mid = middle * inverse_mid
    moe_scale = moe_gains.astype(f32)
    moe_in = (normal_mid * moe_scale).astype(bf16)

    def route(logits):
        logit_exp = jnp.exp(logits - jnp.max(logits, axis=-1, keepdims=True))
        return logit_exp / jnp.sum(logit_exp, axis=-1, keepdims=True)

    router_probs = route(jnp.einsum("td,ed->te", moe_in, router_full, preferred_element_type=f32))
    experts = expert_count
    top_count = routes.shape[1]
    capacity = top_count * seq_len * 4 // (3 * experts)

    named = jnp.any(routes_all == own_expert.astype(f32), axis=1)
    ahead = jnp.dot(
        named.astype(bf16),
        (position[:, None] < position[None, :]).astype(bf16),
        preferred_element_type=f32,
    ).astype(jnp.int32)
    place = jnp.where(named, ahead, -1)
    wide_block = jnp.concatenate(
        [gate_block, up_block, jnp.pad(router_full, ((0, BLOCK - experts), (0, 0))).T], axis=1
    )
    (
        tokens,
        received,
        gate_act,
        up_act,
        gated_hidden,
        gate_weight,
        shared_acts,
        shared_hidden,
        moe_part,
    ) = experts_forward(
        moe_in,
        place,
        expert_gate[0].T,
        expert_up[0].T,
        expert_down[0],
        wide_block,
        down_block,
        capacity,
        experts,
        2,
    )
    activations = middle + reduce_tokens([moe_part], 3)[0]

    own_mask = half_rows(valid_mask, own_tp, own_rows).astype(f32)
    offset = activations - half_rows(teacher, own_tp, own_rows).astype(f32)
    valid_total = jnp.maximum(jnp.sum(valid_all), 1.0)
    square_part = jnp.sum(own_mask[:, None] * offset * offset)
    grad_out = seq_len * fsdp_size / valid_total * own_mask[:, None] * offset
    grad_moe = grad_out.astype(bf16)

    (
        grads,
        grad_slots,
        grad_gate_act,
        grad_up_act,
        grad_sh_pair,
        grad_probs_part,
        grad_part,
    ) = experts_backward(
        grad_moe,
        place,
        expert_gate[0].T,
        expert_up[0].T,
        expert_down[0],
        jnp.concatenate([gate_block.T, up_block.T], axis=0),
        down_block,
        gate_act,
        up_act,
        gate_weight,
        shared_acts,
        capacity,
        4,
    )
    grad_moe_in, grad_router_probs = reduce_tokens([grad_part, grad_probs_part], 5)
    down_shared_grad = jnp.einsum("tf,td->fd", shared_hidden, grads, preferred_element_type=f32)
    pair_grad = jnp.einsum("td,tf->df", tokens, grad_sh_pair, preferred_element_type=f32)
    gate_shared_grad = pair_grad[:, :BLOCK].astype(bf16)
    up_shared_grad = pair_grad[:, BLOCK:].astype(bf16)
    grad_router_probs = grad_router_probs[:, :experts]

    grad_logits = router_probs * (
        grad_router_probs - jnp.sum(router_probs * grad_router_probs, axis=-1, keepdims=True)
    )
    router_grad = jnp.einsum(
        "td,te->ed", moe_in.astype(f32), grad_logits, precision=HIGHEST, preferred_element_type=f32
    )
    grad_moe_in = grad_moe_in + jnp.einsum(
        "te,ed->td",
        grad_logits,
        router_full.astype(f32),
        precision=HIGHEST,
        preferred_element_type=f32,
    )
    moe_gain_grad = jnp.sum(grad_moe_in * normal_mid, axis=0)
    grad_middle = grad_out + norm_back(grad_moe_in * moe_scale, normal_mid, inverse_mid)
    grad_attended = tp_gather(grad_middle.astype(bf16), own_tp)

    output_grad = jnp.einsum("tf,td->fd", heads_out, grad_attended, preferred_element_type=f32)
    grad_heads = (
        jnp.einsum("td,fd->tf", grad_attended, output_full, preferred_element_type=f32)
        .astype(bf16)
        .reshape(seq_len, local_heads, VDIM)
    )
    grad_probs = jnp.einsum("ihd,jhd->hij", grad_heads, values, preferred_element_type=f32)
    grad_values = jnp.einsum("hij,ihd->jhd", probs_low, grad_heads, preferred_element_type=f32)
    grad_scores = (
        attn_probs * (grad_probs - jnp.sum(attn_probs * grad_probs, axis=-1, keepdims=True))
    ).astype(bf16)
    grad_q_nope = (
        jnp.einsum("hij,jhd->ihd", grad_scores, key_nope, preferred_element_type=f32) * score_scale
    )
    grad_q_rope = (
        jnp.einsum("hij,jd->ihd", grad_scores, key_rope, preferred_element_type=f32) * score_scale
    )
    grad_keys = (
        jnp.einsum("hij,ihd->jhd", grad_scores, query_nope, preferred_element_type=f32)
        * score_scale
    )
    grad_key_rope = (
        jnp.einsum("hij,ihd->jd", grad_scores, query_rope, preferred_element_type=f32) * score_scale
    )
    grad_query = (
        jnp.concatenate(
            [grad_q_nope, unrotate(grad_q_rope, cosine[:, None, :], sine_part[:, None, :])], axis=-1
        )
        .astype(bf16)
        .reshape(seq_len, local_heads * (NOPE + ROPE))
    )
    query_grad = jnp.einsum("td,tq->dq", normed, grad_query, preferred_element_type=f32)
    grad_normed = jnp.einsum("tq,dq->td", grad_query, query_full, preferred_element_type=f32)
    grad_kv = (
        jnp.concatenate([grad_keys, grad_values], axis=-1)
        .astype(bf16)
        .reshape(seq_len, local_heads * (NOPE + VDIM))
    )
    expand_grad = jnp.einsum("tr,tq->rq", latent, grad_kv, preferred_element_type=f32)
    grad_latent = jnp.einsum("tq,rq->tr", grad_kv, expand_full, preferred_element_type=f32)
    grad_both = tp_sum(jnp.concatenate([grad_latent, grad_key_rope], axis=1))
    grad_latent, grad_key_rope = grad_both[:, :RANK], grad_both[:, RANK:]
    latent_gain_grad = jnp.sum(grad_latent * latent_unit, axis=0)
    grad_latent_raw = norm_back(grad_latent * latent_scale, latent_unit, inverse_lat)
    grad_latent_lin = jnp.concatenate(
        [grad_latent_raw, unrotate(grad_key_rope, cosine, sine_part)], axis=-1
    ).astype(bf16)
    latent_grad = jnp.einsum("tr,td->rd", grad_latent_lin, normed, preferred_element_type=f32)
    grad_normed = tp_scatter(grad_normed, own_tp, own_rows) + jnp.einsum(
        "tr,rd->td",
        half_rows(grad_latent_lin, own_tp, own_rows),
        latent_full,
        preferred_element_type=f32,
    )
    own_normal = half_rows(normal_in, own_tp, own_rows)
    own_inverse = half_rows(inverse_in, own_tp, own_rows)
    norm_gain_grad = jnp.sum(grad_normed * own_normal, axis=0)
    input_grad = grad_middle + norm_back(grad_normed * norm_scale, own_normal, own_inverse)

    small = jnp.concatenate(
        [
            jnp.transpose(router_grad.reshape(experts, fsdp_size, BLOCK), (1, 0, 2)),
            norm_gain_grad.reshape(fsdp_size, 1, BLOCK),
            moe_gain_grad.reshape(fsdp_size, 1, BLOCK),
            jnp.pad(
                0.5 * latent_gain_grad.reshape(fsdp_size, 1, RANK // fsdp_size),
                ((0, 0), (0, 0), (0, BLOCK - RANK // fsdp_size)),
            ),
            jnp.full((fsdp_size, 1, BLOCK), square_part),
        ],
        axis=1,
    )
    small = jnp.pad(small, ((0, 0), (0, -(experts + 4) % 8), (0, 0))).reshape(-1, BLOCK)
    small = small + swap_tp(small)
    query_out, latent_out, expand_out, output_out, small_out, gate_out, up_out, down_out, *expert_grads = (
        reduce_weights(
            query_grad.astype(bf16),
            latent_grad.astype(bf16),
            expand_grad.astype(bf16),
            output_grad.astype(bf16),
            small,
            gate_shared_grad,
            up_shared_grad,
            down_shared_grad.astype(bf16),
            blocks,
            6,
            WeightGrads(received.shape[0], expert_down.shape[1], width),
            [grad_gate_act, grad_up_act, gated_hidden, received, grad_slots],
        )
    )
    return (
        small_out[experts + 3, 0] / (width * valid_total),
        activations,
        input_grad,
        small_out[experts],
        query_out,
        latent_out.T,
        small_out[experts + 2, : RANK // fsdp_size],
        expand_out,
        output_out,
        small_out[experts + 1],
        small_out[:experts].T,
        gate_out.astype(f32),
        up_out.astype(f32),
        down_out.astype(f32),
        expert_grads[0].T.astype(f32)[None],
        expert_grads[1].T.astype(f32)[None],
        expert_grads[2].astype(f32)[None],
    )


def slot_shards(
    inputs,
    teacher,
    valid_mask,
    prefix,
    routes,
    norm_gain,
    query_weight,
    latent_weight,
    latent_gain,
    expand_weight,
    output_weight,
    moe_gain,
    router_weight,
    shared_gate,
    shared_up,
    shared_down,
    expert_gate,
    expert_up,
    expert_down,
):
    f32 = jnp.float32
    bf16 = jnp.bfloat16
    tp_size = lax.axis_size("tp")
    fsdp_size = lax.axis_size("fsdp")
    local_heads = HEADS // tp_size
    (
        norm_gains,
        query_full,
        latent_full,
        latent_gains,
        expand_full,
        output_full,
        moe_gains,
        router_full,
        gate_full,
        up_full,
        down_full,
    ) = (
        lax.all_gather(norm_gain, "fsdp", axis=0, tiled=True),
        lax.all_gather(query_weight, "fsdp", axis=0, tiled=True),
        lax.all_gather(latent_weight, "fsdp", axis=0, tiled=True),
        lax.all_gather(latent_gain, "fsdp", axis=0, tiled=True),
        lax.all_gather(expand_weight, "fsdp", axis=0, tiled=True),
        lax.all_gather(output_weight, "fsdp", axis=1, tiled=True),
        lax.all_gather(moe_gain, "fsdp", axis=0, tiled=True),
        lax.all_gather(router_weight, "fsdp", axis=0, tiled=True),
        lax.all_gather(shared_gate, "fsdp", axis=0, tiled=True),
        lax.all_gather(shared_up, "fsdp", axis=0, tiled=True),
        lax.all_gather(shared_down, "fsdp", axis=1, tiled=True),
    )
    gathered = lax.all_gather(inputs, "tp", axis=0, tiled=True)
    seq_len = gathered.shape[0]
    width = gathered.shape[1]
    hidden = gathered.astype(f32)
    cosine, sine_part = rope_tables(seq_len, ROPE)
    inverse_in = lax.rsqrt(jnp.mean(hidden * hidden, axis=-1, keepdims=True) + EPSILON)
    normal_in = hidden * inverse_in
    norm_scale = norm_gains.astype(f32)
    normed = (normal_in * norm_scale).astype(bf16)
    query_lin = jnp.dot(normed, query_full, preferred_element_type=f32).reshape(
        seq_len, local_heads, NOPE + ROPE
    )
    queries = jnp.concatenate(
        [
            query_lin[..., :NOPE],
            rotate(query_lin[..., NOPE:], cosine[:, None, :], sine_part[:, None, :]),
        ],
        axis=-1,
    ).astype(bf16)
    latent_lin = jnp.dot(normed, latent_full, preferred_element_type=f32)
    latent_raw = latent_lin[:, :RANK]
    inverse_lat = lax.rsqrt(jnp.mean(latent_raw * latent_raw, axis=-1, keepdims=True) + EPSILON)
    latent_unit = latent_raw * inverse_lat
    latent_scale = latent_gains.astype(f32)
    latent = (latent_unit * latent_scale).astype(bf16)
    key_rope = rotate(latent_lin[:, RANK:], cosine, sine_part).astype(bf16)
    keys_values = (
        jnp.dot(latent, expand_full, preferred_element_type=f32)
        .astype(bf16)
        .reshape(seq_len, local_heads, NOPE + VDIM)
    )
    key_nope = keys_values[..., :NOPE]
    values = keys_values[..., NOPE:]
    query_nope = queries[..., :NOPE]
    query_rope = queries[..., NOPE:]
    score_scale = 1.0 / math.sqrt(NOPE + ROPE)
    position = jnp.arange(seq_len, dtype=jnp.int32)
    visible = (position[None, :] <= position[:, None]) | (position[None, :] < prefix[0])

    def scores_of():
        raw_scores = jnp.einsum("ihd,jhd->hij", query_nope, key_nope, preferred_element_type=f32)
        raw_scores = raw_scores + jnp.einsum(
            "ihd,jd->hij", query_rope, key_rope, preferred_element_type=f32
        )
        return jnp.where(visible[None], raw_scores * score_scale, MASKED)

    scores = scores_of()
    row_max = jnp.max(scores, axis=-1, keepdims=True)
    shifted = jnp.exp(scores - row_max)
    row_total = jnp.sum(shifted, axis=-1, keepdims=True)
    log_total = row_max + jnp.log(row_total)
    probs_low = (shifted / row_total).astype(bf16)
    heads_out = (
        jnp.einsum("hij,jhd->ihd", probs_low, values, preferred_element_type=f32)
        .astype(bf16)
        .reshape(seq_len, local_heads * VDIM)
    )
    attended = lax.psum(jnp.dot(heads_out, output_full, preferred_element_type=f32), "tp")
    middle = hidden + attended
    inverse_mid = lax.rsqrt(jnp.mean(middle * middle, axis=-1, keepdims=True) + EPSILON)
    normal_mid = middle * inverse_mid
    moe_scale = moe_gains.astype(f32)
    moe_in = (normal_mid * moe_scale).astype(bf16)
    logits = jnp.dot(moe_in, router_full, preferred_element_type=f32)
    logit_max = jnp.max(logits, axis=-1, keepdims=True)
    logit_exp = jnp.exp(logits - logit_max)
    router_probs = logit_exp / jnp.sum(logit_exp, axis=-1, keepdims=True)
    experts = router_full.shape[1]
    top_count = routes.shape[1]
    choose = routes[:, :, None] == jnp.arange(experts, dtype=jnp.int32)[None, None, :]
    gate_values = jnp.sum(jnp.where(choose, router_probs[:, None, :], 0.0), axis=-1)
    capacity = top_count * seq_len * 4 // (3 * experts)
    flat_routes = routes.reshape(seq_len * top_count)
    onehot = (flat_routes[:, None] == jnp.arange(experts, dtype=jnp.int32)[None, :]).astype(
        jnp.int32
    )
    earlier = jnp.cumsum(onehot, axis=0) - onehot
    slot_index = flat_routes * capacity + jnp.sum(earlier * onehot, axis=1)
    placed = jnp.arange(experts * capacity, dtype=jnp.int32)[:, None] == slot_index[None, :]
    dispatch = jnp.sum(
        placed.reshape(experts * capacity, seq_len, top_count).astype(f32), axis=2
    ).astype(bf16)
    gate_slot = jnp.sum(jnp.where(placed, gate_values.reshape(1, seq_len * top_count), 0.0), axis=1)

    def send_slots(slot_rows):
        return lax.all_to_all(slot_rows, "fsdp", split_axis=0, concat_axis=1, tiled=True)

    def return_slots(partials):
        return (
            lax.all_to_all(
                partials.astype(jnp.bfloat16), "fsdp", split_axis=1, concat_axis=0, tiled=True
            )
            .astype(partials.dtype)
            .reshape(experts * capacity, width)
        )

    expert_in = (
        jnp.dot(dispatch, moe_in, preferred_element_type=f32)
        .astype(bf16)
        .reshape(experts, capacity, width)
    )
    received = send_slots(expert_in)
    gate_act = jnp.einsum("ecd,edf->ecf", received, expert_gate, preferred_element_type=f32)
    up_act = jnp.einsum("ecd,edf->ecf", received, expert_up, preferred_element_type=f32)
    silu_gate, silu_slope = silu_parts(gate_act)
    expert_hidden = (silu_gate * up_act).astype(bf16)
    expert_out = jnp.einsum("ecf,efd->ecd", expert_hidden, expert_down, preferred_element_type=f32)
    returned = return_slots(expert_out)
    picked = jnp.take(returned, slot_index, axis=0).reshape(seq_len, top_count, width)
    routed = jnp.sum(gate_values[:, :, None] * picked, axis=1)
    gate_sh = jnp.dot(moe_in, gate_full, preferred_element_type=f32)
    up_sh = jnp.dot(moe_in, up_full, preferred_element_type=f32)
    silu_sh, slope_sh = silu_parts(gate_sh)
    shared_hidden = (silu_sh * up_sh).astype(bf16)
    moe_part = routed + jnp.dot(shared_hidden, down_full, preferred_element_type=f32)
    moe_out = lax.psum(moe_part.astype(jnp.bfloat16), "tp").astype(jnp.float32)
    activations = middle + moe_out
    mask_float = valid_mask.astype(f32)
    offset = activations - teacher.astype(f32)
    square_sum, valid_sum = lax.psum(
        (jnp.sum(mask_float[:, None] * offset * offset), jnp.sum(mask_float)), "fsdp"
    )
    valid_total = jnp.maximum(valid_sum, 1.0)
    loss_value = square_sum / (width * valid_total)
    grad_out = seq_len * fsdp_size / valid_total * mask_float[:, None] * offset
    grad_moe = grad_out.astype(bf16)
    down_shared_grad = jnp.einsum("tf,td->fd", shared_hidden, grad_moe, preferred_element_type=f32)
    grad_sh_hidden = jnp.einsum("td,fd->tf", grad_moe, down_full, preferred_element_type=f32)
    grad_gate_sh = (grad_sh_hidden * up_sh * slope_sh).astype(bf16)
    grad_up_sh = (grad_sh_hidden * silu_sh).astype(bf16)
    gate_shared_grad = jnp.einsum("td,tf->df", moe_in, grad_gate_sh, preferred_element_type=f32)
    up_shared_grad = jnp.einsum("td,tf->df", moe_in, grad_up_sh, preferred_element_type=f32)
    grad_moe_in = jnp.einsum("tf,df->td", grad_gate_sh, gate_full, preferred_element_type=f32)
    grad_moe_in = grad_moe_in + jnp.einsum(
        "tf,df->td", grad_up_sh, up_full, preferred_element_type=f32
    )
    grad_gates = jnp.sum(picked * grad_moe.astype(f32)[:, None, :], axis=-1)
    grad_slots = (
        (jnp.dot(dispatch, grad_moe, preferred_element_type=f32) * gate_slot[:, None])
        .astype(bf16)
        .reshape(experts, capacity, width)
    )
    grad_received = send_slots(grad_slots)
    expert_down_grad = jnp.einsum(
        "ecf,ecd->efd", expert_hidden, grad_received, preferred_element_type=f32
    )
    grad_expert_hidden = jnp.einsum(
        "ecd,efd->ecf", grad_received, expert_down, preferred_element_type=f32
    )
    grad_gate_act = (grad_expert_hidden * up_act * silu_slope).astype(bf16)
    grad_up_act = (grad_expert_hidden * silu_gate).astype(bf16)
    expert_gate_grad = jnp.einsum(
        "ecd,ecf->edf", received, grad_gate_act, preferred_element_type=f32
    )
    expert_up_grad = jnp.einsum("ecd,ecf->edf", received, grad_up_act, preferred_element_type=f32)
    grad_expert_in = jnp.einsum(
        "ecf,edf->ecd", grad_gate_act, expert_gate, preferred_element_type=f32
    )
    grad_expert_in = grad_expert_in + jnp.einsum(
        "ecf,edf->ecd", grad_up_act, expert_up, preferred_element_type=f32
    )
    grad_returned = return_slots(grad_expert_in)
    grad_moe_in = grad_moe_in + jnp.sum(
        jnp.take(grad_returned, slot_index, axis=0).reshape(seq_len, top_count, width), axis=1
    )
    grad_moe_in, grad_gates = (
        lax.psum(grad_moe_in.astype(jnp.bfloat16), "tp").astype(jnp.float32),
        lax.psum(grad_gates.astype(jnp.bfloat16), "tp").astype(jnp.float32),
    )
    grad_router_probs = jnp.sum(jnp.where(choose, grad_gates[:, :, None], 0.0), axis=1)
    grad_logits = router_probs * (
        grad_router_probs - jnp.sum(router_probs * grad_router_probs, axis=-1, keepdims=True)
    )
    router_grad = jnp.einsum(
        "td,te->de", moe_in.astype(f32), grad_logits, precision=HIGHEST, preferred_element_type=f32
    )
    grad_moe_in = grad_moe_in + jnp.einsum(
        "te,de->td",
        grad_logits,
        router_full.astype(f32),
        precision=HIGHEST,
        preferred_element_type=f32,
    )
    moe_gain_grad = jnp.sum(grad_moe_in * normal_mid, axis=0)
    grad_middle = grad_out + norm_back(grad_moe_in * moe_scale, normal_mid, inverse_mid)
    grad_attended = grad_middle.astype(bf16)
    output_grad = jnp.einsum("tf,td->fd", heads_out, grad_attended, preferred_element_type=f32)
    grad_heads = (
        jnp.einsum("td,fd->tf", grad_attended, output_full, preferred_element_type=f32)
        .astype(bf16)
        .reshape(seq_len, local_heads, VDIM)
    )
    attn_probs = jnp.exp(scores_of() - log_total)
    probs_again = attn_probs.astype(bf16)
    grad_probs = jnp.einsum("ihd,jhd->hij", grad_heads, values, preferred_element_type=f32)
    grad_values = jnp.einsum("hij,ihd->jhd", probs_again, grad_heads, preferred_element_type=f32)
    grad_scores = (
        attn_probs * (grad_probs - jnp.sum(attn_probs * grad_probs, axis=-1, keepdims=True))
    ).astype(bf16)
    grad_q_nope = (
        jnp.einsum("hij,jhd->ihd", grad_scores, key_nope, preferred_element_type=f32) * score_scale
    )
    grad_q_rope = (
        jnp.einsum("hij,jd->ihd", grad_scores, key_rope, preferred_element_type=f32) * score_scale
    )
    grad_keys = (
        jnp.einsum("hij,ihd->jhd", grad_scores, query_nope, preferred_element_type=f32)
        * score_scale
    )
    grad_key_rope = (
        jnp.einsum("hij,ihd->jd", grad_scores, query_rope, preferred_element_type=f32) * score_scale
    )
    grad_query = (
        jnp.concatenate(
            [grad_q_nope, unrotate(grad_q_rope, cosine[:, None, :], sine_part[:, None, :])], axis=-1
        )
        .astype(bf16)
        .reshape(seq_len, local_heads * (NOPE + ROPE))
    )
    query_grad = jnp.einsum("td,tq->dq", normed, grad_query, preferred_element_type=f32)
    grad_normed = jnp.einsum("tq,dq->td", grad_query, query_full, preferred_element_type=f32)
    grad_kv = (
        jnp.concatenate([grad_keys, grad_values], axis=-1)
        .astype(bf16)
        .reshape(seq_len, local_heads * (NOPE + VDIM))
    )
    expand_grad = jnp.einsum("tr,tq->rq", latent, grad_kv, preferred_element_type=f32)
    grad_latent = jnp.einsum("tq,rq->tr", grad_kv, expand_full, preferred_element_type=f32)
    grad_normed, grad_latent, grad_key_rope = (
        lax.psum(grad_normed.astype(jnp.bfloat16), "tp").astype(jnp.float32),
        lax.psum(grad_latent.astype(jnp.bfloat16), "tp").astype(jnp.float32),
        lax.psum(grad_key_rope.astype(jnp.bfloat16), "tp").astype(jnp.float32),
    )
    latent_gain_grad = jnp.sum(grad_latent * latent_unit, axis=0)
    grad_latent_raw = norm_back(grad_latent * latent_scale, latent_unit, inverse_lat)
    grad_latent_lin = jnp.concatenate(
        [grad_latent_raw, unrotate(grad_key_rope, cosine, sine_part)], axis=-1
    ).astype(bf16)
    latent_grad = jnp.einsum("td,tr->dr", normed, grad_latent_lin, preferred_element_type=f32)
    grad_normed = grad_normed + jnp.einsum(
        "tr,dr->td", grad_latent_lin, latent_full, preferred_element_type=f32
    )
    norm_gain_grad = jnp.sum(grad_normed * normal_in, axis=0)
    input_grad = grad_middle + norm_back(grad_normed * norm_scale, normal_in, inverse_in)
    (
        norm_out,
        query_out,
        latent_out,
        lgain_out,
        expand_out,
        output_out,
        mgain_out,
        router_out,
        gate_out,
        up_out,
        down_out,
    ) = (
        lax.psum_scatter(norm_gain_grad, "fsdp", scatter_dimension=0, tiled=True),
        lax.psum_scatter(query_grad, "fsdp", scatter_dimension=0, tiled=True),
        lax.psum_scatter(latent_grad, "fsdp", scatter_dimension=0, tiled=True),
        lax.psum_scatter(latent_gain_grad, "fsdp", scatter_dimension=0, tiled=True),
        lax.psum_scatter(expand_grad, "fsdp", scatter_dimension=0, tiled=True),
        lax.psum_scatter(output_grad, "fsdp", scatter_dimension=1, tiled=True),
        lax.psum_scatter(moe_gain_grad, "fsdp", scatter_dimension=0, tiled=True),
        lax.psum_scatter(router_grad, "fsdp", scatter_dimension=0, tiled=True),
        lax.psum_scatter(gate_shared_grad, "fsdp", scatter_dimension=0, tiled=True),
        lax.psum_scatter(up_shared_grad, "fsdp", scatter_dimension=0, tiled=True),
        lax.psum_scatter(down_shared_grad, "fsdp", scatter_dimension=1, tiled=True),
    )
    own_start = lax.axis_index("tp") * inputs.shape[0]
    own_activations = lax.dynamic_slice_in_dim(activations, own_start, inputs.shape[0], 0)
    own_input_grad = lax.dynamic_slice_in_dim(input_grad, own_start, inputs.shape[0], 0)
    return (
        loss_value,
        own_activations,
        own_input_grad,
        norm_out,
        query_out,
        latent_out,
        lgain_out,
        expand_out,
        output_out,
        mgain_out,
        router_out,
        gate_out,
        up_out,
        down_out,
        expert_gate_grad,
        expert_up_grad,
        expert_down_grad,
    )


def shards(*arrays):
    fsdp_size = lax.axis_size("fsdp")
    seq_len = arrays[4].shape[0]
    experts = arrays[12].shape[1]
    capacity = arrays[4].shape[1] * seq_len * 4 // (3 * experts)
    fits = fsdp_size * seq_len <= 2 * experts * capacity and fsdp_size == experts
    aligned = arrays[5].shape[0] == BLOCK and arrays[13].shape[1] % BLOCK == 0 and arrays[13].shape[1] <= fsdp_size * BLOCK
    if fits and aligned and fsdp_size % 4 == 0:
        return token_shards(*arrays)
    return slot_shards(*arrays)


def solution(mesh):
    return jax.shard_map(
        shards,
        mesh=mesh,
        in_specs=(
            P(("fsdp", "tp"), None),
            P("fsdp", None),
            P("fsdp"),
            P("fsdp"),
            P("fsdp", None),
            P("fsdp"),
            P("fsdp", "tp"),
            P("fsdp", None),
            P("fsdp"),
            P("fsdp", "tp"),
            P("tp", "fsdp"),
            P("fsdp"),
            P("fsdp", None),
            P("fsdp", "tp"),
            P("fsdp", "tp"),
            P("tp", "fsdp"),
            P("fsdp", None, "tp"),
            P("fsdp", None, "tp"),
            P("fsdp", "tp", None),
        ),
        out_specs=(
            P(),
            P(("fsdp", "tp"), None),
            P(("fsdp", "tp"), None),
            P("fsdp"),
            P("fsdp", "tp"),
            P("fsdp", None),
            P("fsdp"),
            P("fsdp", "tp"),
            P("tp", "fsdp"),
            P("fsdp"),
            P("fsdp", None),
            P("fsdp", "tp"),
            P("fsdp", "tp"),
            P("tp", "fsdp"),
            P("fsdp", None, "tp"),
            P("fsdp", None, "tp"),
            P("fsdp", "tp", None),
        ),
        check_vma=False,
    )
```

```python
import functools
import math

import jax
import jax.numpy as jnp
from jax import lax
from jax.experimental import pallas as pl
from jax.experimental.pallas import tpu as pltpu
from jax.sharding import PartitionSpec as P

HEADS = 16
NOPE = 128
ROPE = 64
RANK = 512
VDIM = 128


EPSILON = 1e-06
HIGHEST = lax.Precision.HIGHEST
MASKED = -1e30


def rope_tables(length, dim_size):
    places = jnp.arange(length).astype(jnp.float32)
    exponent = jnp.arange(dim_size // 2).astype(jnp.float32) * (2.0 / dim_size)
    angles = places[:, None] * jnp.exp(exponent * -math.log(10000.0))[None, :]
    return (jnp.cos(angles), jnp.sin(angles))


def rotate(values, cosine, sine_part):
    half_width = values.shape[-1] // 2
    lower_half = values[..., :half_width]
    upper_half = values[..., half_width:]
    return jnp.concatenate(
        [
            lower_half * cosine - upper_half * sine_part,
            upper_half * cosine + lower_half * sine_part,
        ],
        axis=-1,
    )


def unrotate(gradient, cosine, sine_part):
    half_width = gradient.shape[-1] // 2
    lower_half = gradient[..., :half_width]
    upper_half = gradient[..., half_width:]
    return jnp.concatenate(
        [
            lower_half * cosine + upper_half * sine_part,
            upper_half * cosine - lower_half * sine_part,
        ],
        axis=-1,
    )


def silu_parts(gate_act):
    sigmoid_val = jax.nn.sigmoid(gate_act)
    return (gate_act * sigmoid_val, sigmoid_val * (1.0 + gate_act * (1.0 - sigmoid_val)))


def norm_back(grad_scaled, unit_rows, inverse):
    return inverse * (
        grad_scaled - unit_rows * jnp.mean(grad_scaled * unit_rows, axis=-1, keepdims=True)
    )


def swap_tp(value):
    return lax.ppermute(value, "tp", [(0, 1), (1, 0)])


def half_rows(value, which, rows):
    return lax.dynamic_slice_in_dim(value, which * rows, rows, 0)


def tp_scatter(partial, which, rows):
    other = half_rows(partial, 1 - which, rows).astype(jnp.bfloat16)
    return half_rows(partial, which, rows) + swap_tp(other).astype(jnp.float32)


def tp_sum(partial):
    low_partial = partial.astype(jnp.bfloat16)
    return low_partial.astype(jnp.float32) + swap_tp(low_partial).astype(jnp.float32)


def tp_gather(own, which):
    other = swap_tp(own)
    first = jnp.where(which == 0, own, other)
    second = jnp.where(which == 0, other, own)
    return jnp.concatenate([first, second], axis=0)


MESH = pl.DeviceIdType.MESH
CROSS = ("x", "y", "up", "down")
BLOCK = 128


def both(first, second):
    if first is None:
        return second
    if second is None:
        return first
    return jnp.logical_and(first, second)


def under(condition, body):
    if condition is None:
        body()
    else:
        pl.when(condition)(body)


class Grid:
    def __init__(self, fsdp_size, dims, tie=-1):
        self.tie = tie
        index = lax.axis_index("fsdp")
        self.core = lax.rem(index, 2)
        self.y = lax.rem(lax.div(index, 2), 2)
        self.z = lax.div(index, 4)
        self.x = lax.axis_index("tp")
        self.depth = fsdp_size // 4
        self.dims = dims
        self.crosses = CROSS if "x" in dims else CROSS[1:]
        self.chips = self.depth * 2 * (2 if "x" in dims else 1)

    def device(self, x, y, z, core):
        return {"fsdp": z * 4 + y * 2 + core, "tp": x}

    def chip(self, x, y, z):
        return (z * 2 + y) * 2 + x if "x" in self.dims else z * 2 + y

    def here(self):
        return self.x, self.y, self.z

    def partner(self):
        return self.device(self.x, self.y, self.z, 1 - self.core)

    def neighbour(self, cross):
        if cross == "x":
            return (1 - self.x, self.y, self.z), None
        if cross == "y":
            return (self.x, 1 - self.y, self.z), None
        if cross == "up":
            return (self.x, self.y, self.z + 1), self.z + 1 < self.depth
        return (self.x, self.y, self.z - 1), self.z >= 1

    def level(self, rank):
        inner = jnp.logical_or(self.z == 1, self.z == 2)
        rank = jnp.where(jnp.logical_and(inner, rank >= 2), 5 - rank, rank)
        high, low = lax.div(self.z, 2), lax.rem(self.z, 2)
        far, near = lax.div(rank, 2), lax.rem(rank, 2)
        return 2 * (high + far - 2 * high * far) + (low + near - 2 * low * near)

    def entry(self, number):
        steps = (0, 1) if "x" in self.dims else (0,)
        found = [(r, dy, dx) for r in range(self.depth) for dy in (0, 1) for dx in steps]
        if "x" in self.dims:
            found.sort(key=lambda e: (sum(e), self.tie * e[0]))
        else:
            found.sort(key=lambda e: e[0] + 2.1 * e[1])
        codes = [4 * e[0] + 2 * e[1] + e[2] for e in found]
        code = jnp.int32(0) + (codes[number] if isinstance(number, int) else 0)
        if not isinstance(number, int):
            for at, value in enumerate(codes):
                code = jnp.where(number == at, value, code)
        dx, dy = lax.rem(code, 2), lax.rem(lax.div(code, 2), 2)
        x, y = self.x + dx - 2 * self.x * dx, self.y + dy - 2 * self.y * dy
        return x, y, self.level(lax.div(code, 4))

    def children(self, order, chip):
        zero = dict(x=chip[0] == self.x, y=chip[1] == self.y, z=chip[2] == self.z)
        found, rest = [], None
        for dim in reversed(order):
            if dim == "z":
                found.append(("up", both(rest, (chip[2] <= self.z) & (self.z + 1 < self.depth))))
                found.append(("down", both(rest, (chip[2] >= self.z) & (self.z >= 1))))
            else:
                found.append((dim, both(rest, zero[dim])))
            rest = both(rest, zero[dim])
        return found

    def parent(self, order, chip):
        zero = dict(x=chip[0] == self.x, y=chip[1] == self.y, z=chip[2] == self.z)
        rest, turned = None, {}
        for dim in reversed(order):
            turned[dim] = both(rest, jnp.logical_not(zero[dim]))
            rest = both(rest, zero[dim])
        x = jnp.where(turned["x"], 1 - self.x, self.x) if "x" in order else self.x
        y = jnp.where(turned["y"], 1 - self.y, self.y)
        above = chip[2] > self.z
        z = jnp.where(turned["z"], jnp.where(above, self.z + 1, self.z - 1), self.z)
        side = jnp.where(above, self.crosses.index("down"), self.crosses.index("up"))
        side = jnp.where(turned["y"], self.crosses.index("y"), side)
        if "x" in order:
            side = jnp.where(turned["x"], self.crosses.index("x"), side)
        return (x, y, z), side

    def greet(self):
        barrier = pltpu.get_barrier_semaphore()
        pl.semaphore_signal(barrier, inc=1, device_id=self.partner(), device_id_type=MESH)
        count = 1
        for cross in self.crosses:
            chip, exists = self.neighbour(cross)

            def send(chip=chip):
                there = self.device(*chip, self.core)
                pl.semaphore_signal(barrier, inc=1, device_id=there, device_id_type=MESH)

            under(exists, send)
            count = count + (1 if exists is None else jnp.where(exists, 1, 0))
        pl.semaphore_wait(barrier, count)

    def greet_plane(self):
        barrier = pltpu.get_barrier_semaphore()
        size = self.depth * 4
        me = lax.axis_index("fsdp")

        def send(step, carry):
            there = {"fsdp": lax.rem(me + step, size), "tp": self.x}
            pl.semaphore_signal(barrier, inc=1, device_id=there, device_id_type=MESH)
            return carry

        lax.fori_loop(1, size, send, 0)
        across = {"fsdp": me, "tp": 1 - self.x}
        pl.semaphore_signal(barrier, inc=1, device_id=across, device_id_type=MESH)
        pl.semaphore_wait(barrier, size)


def owner_of(block, chips):
    extra = 2 * lax.rem(3 * (block - chips) + 1 + 3 * chips, chips) + 1
    return jnp.where(block < chips, 2 * block, extra)


def block_of(device, chips):
    back = pow(3, -1, chips)
    chip, core = lax.div(device, 2), lax.rem(device, 2)
    return jnp.where(core == 0, chip, chips + lax.rem(back * (chip - 1 + chips), chips))


class Exchange:
    def __init__(self, fsdp_size, tp, blocks, sources, targets, cut, to_owner, send_sem, recv_sem, own_sem):
        self.size, self.tp, self.blocks = fsdp_size, tp, blocks
        self.sources, self.targets, self.cut, self.to_owner = sources, targets, cut, to_owner
        self.send_sem, self.recv_sem, self.own_sem = send_sem, recv_sem, own_sem
        self.me = lax.axis_index("fsdp")
        self.block = block_of(self.me, fsdp_size // 2)
        self.owns = self.block < blocks

    def remote(self, array, block, other, there, send, recv):
        source, target = self.cut[array](self.sources[array], self.targets[array], block, other)
        return pltpu.make_async_remote_copy(
            src_ref=source,
            dst_ref=target,
            send_sem=self.send_sem.at[array, send],
            recv_sem=self.recv_sem.at[array, recv],
            device_id={"fsdp": there, "tp": self.tp},
            device_id_type=MESH,
        )

    def local(self, array, block):
        source, target = self.cut[array](self.sources[array], self.targets[array], block, self.me)
        return pltpu.make_async_copy(source, target, self.own_sem.at[array])

    def by_block(self, act, act_local, low, high):
        def one(number, carry):
            block = lax.rem(number + lax.div(self.me * self.blocks, self.size), self.blocks)
            owner = owner_of(block, self.size // 2)
            for array in range(len(self.sources)):
                if self.to_owner:
                    copy = self.remote(array, block, self.me, owner, block, self.me)
                else:
                    copy = self.remote(array, block, self.me, owner, 0, block)
                pl.when(self.me != owner)(getattr(copy, act))
                if act_local:
                    pl.when(self.me == owner)(getattr(self.local(array, block), act_local))
            return carry

        lax.fori_loop(low, high, one, 0)

    def by_device(self, act, act_local, low, high):
        def one(number, carry):
            other = lax.rem(self.me + number, self.size)
            for array in range(len(self.sources)):
                if self.to_owner:
                    copy = self.remote(array, self.block, other, other, 0, other)
                else:
                    copy = self.remote(array, self.block, other, other, other, self.block)
                pl.when(self.me != other)(getattr(copy, act))
                if act_local:
                    pl.when(self.me == other)(getattr(self.local(array, self.block), act_local))
            return carry

        def every():
            lax.fori_loop(low, high, one, 0)

        pl.when(self.owns)(every)

    def start(self, step, steps):
        total = self.blocks if self.to_owner else self.size
        low, high = lax.div(step * total, steps), lax.div((step + 1) * total, steps)
        (self.by_block if self.to_owner else self.by_device)("start", "start", low, high)

    def finish(self):
        if self.to_owner:
            self.by_device("wait_recv", None, 0, self.size)
            self.by_block("wait_send", "wait", 0, self.blocks)
        else:
            self.by_block("wait_recv", None, 0, self.blocks)
            self.by_device("wait_send", "wait", 0, self.size)


def exchange_sems(fsdp_size, arrays):
    dma = pltpu.SemaphoreType.DMA
    return [dma((arrays, fsdp_size)), dma((arrays, fsdp_size)), dma((arrays,))] if arrays else []


def gather_kernel(fsdp_size, pieces, places, count, blocks, cut, *refs):
    moved = len(cut)
    shards, sources = refs[:count], refs[count : count + moved]
    refs = refs[count + moved :]
    outs, targets = refs[:count], refs[count : count + moved]
    send_sem, recv_sem, pair_send, pair_recv, own_sem, cross_sem = refs[
        count + moved : count + moved + 6
    ]
    grid = Grid(fsdp_size, "zy")
    halved = [piece[1] for piece in pieces].index(None)
    exchange = Exchange(
        fsdp_size, grid.x, blocks, sources, targets, cut, True, *refs[count + moved + 6 :]
    )

    def first_row(piece, plane):
        first, rows = pieces[piece][1], pieces[piece][2]
        return pl.multiple_of(plane * rows, 16) if first is None else first

    def target(piece, chip, core):
        array, _, rows, _ = pieces[piece]
        return places[array](outs[array], chip, core, first_row(piece, chip[0]), rows)

    def source(piece, chip, own):
        array, _, rows, _ = pieces[piece]
        if own:
            return shards[array].at[pl.ds(first_row(piece, grid.x), rows)]
        return target(piece, chip, grid.core)

    def across(chip, own=False):
        index = grid.chip(*chip)
        return pltpu.make_async_remote_copy(
            src_ref=source(halved, chip, own),
            dst_ref=target(halved, chip, grid.core),
            send_sem=cross_sem.at[0, index],
            recv_sem=cross_sem.at[1, index],
            device_id=grid.device(1 - grid.x, grid.y, grid.z, grid.core),
            device_id_type=MESH,
        )

    def across_pair(chip, core):
        index, far = grid.chip(*chip), (1 - grid.x, chip[1], chip[2])
        return pltpu.make_async_remote_copy(
            src_ref=target(halved, far, grid.core),
            dst_ref=target(halved, far, core),
            send_sem=cross_sem.at[2, index],
            recv_sem=cross_sem.at[3, index],
            device_id=grid.partner(),
            device_id_type=MESH,
        )

    def crossed(chip):
        across((1 - grid.x, chip[1], chip[2])).wait_recv()
        across_pair(chip, grid.core).start()

    def hops(piece, chip, own):
        index, found = grid.chip(*chip), []
        for cross, wanted in grid.children(pieces[piece][3], chip):
            there, _ = grid.neighbour(cross)
            copy = pltpu.make_async_remote_copy(
                src_ref=source(piece, chip, own),
                dst_ref=target(piece, chip, grid.core),
                send_sem=send_sem.at[piece, index, grid.crosses.index(cross)],
                recv_sem=recv_sem.at[piece, index],
                device_id=grid.device(*there, grid.core),
                device_id_type=MESH,
            )
            found.append((wanted, copy))
        return found

    def pair(piece, chip, core, own=False, landing=False):
        index = grid.chip(*chip)
        return pltpu.make_async_remote_copy(
            src_ref=source(piece, chip, own),
            dst_ref=target(piece, chip, core),
            send_sem=pair_send.at[piece, index],
            recv_sem=(recv_sem if landing else pair_recv).at[piece, index],
            device_id=grid.partner(),
            device_id_type=MESH,
        )

    own_copies = [
        pltpu.make_async_copy(
            source(piece, grid.here(), True), target(piece, grid.here(), grid.core), own_sem.at[piece]
        )
        for piece in range(len(pieces))
    ]
    grid.greet_plane()

    def relay(chip, own):
        for piece in range(len(pieces)):
            if not own:
                pair(piece, chip, grid.core, landing=True).wait_recv()
            for wanted, copy in hops(piece, chip, own):
                under(wanted, copy.start)
            pair(piece, chip, grid.core, own).start()
            if piece == halved:
                across(chip, own).start()

    relay(grid.here(), True)
    for copy in own_copies:
        copy.start()

    def step(number, carry):
        relay(grid.entry(number), False)
        crossed(grid.entry(number - 1))
        exchange.start(number - 1, grid.chips - 1)
        return carry

    lax.fori_loop(1, grid.chips, step, 0)
    crossed(grid.entry(grid.chips - 1))

    def finish(number, carry):
        chip = grid.entry(number)
        for piece in range(len(pieces)):
            for wanted, copy in hops(piece, chip, False):
                under(wanted, copy.wait_send)
            pair(piece, chip, grid.core).wait_send()
            pair(piece, chip, 1 - grid.core).wait_recv()
        across(chip).wait_send()
        across_pair(chip, grid.core).wait_send()
        across_pair(chip, 1 - grid.core).wait_recv()
        return carry

    lax.fori_loop(0, grid.chips, finish, 0)
    for copy in own_copies:
        copy.wait()
    exchange.finish()


def gather_call(fsdp_size, pieces, places, shards, shapes, collective_id, blocks, cut, sources, targets):
    count, chips = len(shards), fsdp_size // 2
    dma = pltpu.SemaphoreType.DMA
    moved = sum(s.size * s.dtype.itemsize for s in shapes)
    return pl.pallas_call(
        functools.partial(gather_kernel, fsdp_size, pieces, places, count, blocks, cut),
        out_shape=tuple(shapes) + tuple(targets),
        in_specs=[pl.BlockSpec(memory_space=pltpu.VMEM)] * count
        + [pl.BlockSpec(memory_space=pl.ANY)] * len(sources),
        out_specs=tuple([pl.BlockSpec(memory_space=pl.ANY)] * (count + len(targets))),
        scratch_shapes=[
            dma((len(pieces), chips, 4)),
            dma((len(pieces), chips)),
            dma((len(pieces), chips)),
            dma((len(pieces), chips)),
            dma((len(pieces),)),
            dma((4, chips)),
            *exchange_sems(fsdp_size, len(sources)),
        ],
        compiler_params=pltpu.CompilerParams(collective_id=collective_id, has_side_effects=True),
        cost_estimate=pl.CostEstimate(flops=0, bytes_accessed=8 * moved, transcendentals=0),
    )(*shards, *sources)


class WeightGrads:
    inputs, outputs = 5, 3
    PIECES = (1, 3, 5)

    def __init__(self, slots, hidden, width):
        bf16 = jnp.bfloat16
        dma = pltpu.SemaphoreType.DMA
        self.hidden = hidden
        self.shapes = [jax.ShapeDtypeStruct((hidden, width), bf16)] * self.outputs
        self.scratch = [
            pltpu.VMEM((2, slots, BLOCK), bf16),
            pltpu.VMEM((slots, width), bf16),
            pltpu.VMEM((2, BLOCK, width), bf16),
            dma((2,)),
            dma((1,)),
            dma((2,)),
        ]

    def make(self, *refs):
        return WeightGradsRun(self, refs)


class WeightGradsRun:
    def __init__(self, job, refs):
        self.lefts, self.rights, self.outs = refs[:3], refs[3:5], refs[5:8]
        self.left, self.right, self.result = refs[8:11]
        self.left_sem, self.right_sem, self.out_sem = refs[11:]
        self.blocks = -(-job.hidden // BLOCK)
        self.rest = job.hidden - (self.blocks - 1) * BLOCK
        self.total = 3 * self.blocks

    def left_copy(self, which, number):
        slot, block = lax.rem(number, 2), lax.rem(number, self.blocks)
        span = pl.ds(pl.multiple_of(block * BLOCK, BLOCK), BLOCK)
        return pltpu.make_async_copy(
            self.lefts[which].at[:, span], self.left.at[slot], self.left_sem.at[slot]
        )

    def left_start(self, number):
        for which in range(3):
            pl.when(lax.div(number, self.blocks) == which)(self.left_copy(which, number).start)

    def right_copy(self, which):
        return pltpu.make_async_copy(self.rights[which], self.right, self.right_sem.at[0])

    def out_copies(self, which, number):
        slot, block = lax.rem(number, 2), lax.rem(number, self.blocks)
        full = pl.ds(pl.multiple_of(block * BLOCK, BLOCK), BLOCK)
        part = pl.ds((self.blocks - 1) * BLOCK, self.rest)
        out, sem = self.outs[which], self.out_sem.at[slot]
        return [
            (
                block < self.blocks - 1,
                pltpu.make_async_copy(self.result.at[slot], out.at[full], sem),
            ),
            (
                block == self.blocks - 1,
                pltpu.make_async_copy(self.result.at[slot, pl.ds(0, self.rest)], out.at[part], sem),
            ),
        ]

    def begin(self):
        self.right_copy(0).start()
        self.left_copy(0, jnp.int32(0)).start()

    def out_wait(self, number):
        for wanted, copy in self.out_copies(0, number):
            pl.when(wanted)(copy.wait)

    def run(self, number):
        slot = lax.rem(number, 2)
        self.left_copy(0, number).wait()
        pl.when(number + 1 < self.total)(lambda: self.left_start(number + 1))
        pl.when(lax.rem(number, 2 * self.blocks) == 0)(self.right_copy(0).wait)
        pl.when(number >= 2)(lambda: self.out_wait(number - 2))
        self.result[slot] = lax.dot_general(
            self.left[slot],
            self.right[...],
            (((0,), (0,)), ((), ())),
            preferred_element_type=jnp.float32,
        ).astype(jnp.bfloat16)
        for which in range(3):
            for wanted, copy in self.out_copies(which, number):
                pl.when(wanted & (lax.div(number, self.blocks) == which))(copy.start)
        pl.when(number == 2 * self.blocks - 1)(self.right_copy(1).start)

    def tick(self, step, piece):
        if piece in WeightGrads.PIECES:
            number = (step - 1) * len(WeightGrads.PIECES) + WeightGrads.PIECES.index(piece)
            pl.when((number >= 0) & (number < self.total))(lambda: self.run(number))

    def finish(self, steps):
        for number in range(len(WeightGrads.PIECES) * (steps - 1), self.total):
            self.run(jnp.int32(0) + number)
        for number in (self.total - 2, self.total - 1):
            self.out_wait(jnp.int32(0) + number)


def reduce_kernel(fsdp_size, dims, pieces, places, count, blocks, cut, side, halved, *refs):
    moved, taken = len(cut), side.inputs if side else 0
    partials, sources = refs[:count], refs[count : count + moved]
    side_refs = refs[count + moved : count + moved + taken]
    refs = refs[count + moved + taken :]
    outs, targets = refs[:count], refs[count : count + moved]
    refs = refs[count + moved :]
    if side:
        side_refs, refs = side_refs + refs[: side.outputs], refs[side.outputs :]
    held, other, landed = (refs[i * count : (1 + i) * count] for i in range(3))
    send_sem, recv_sem, load_sem, pair_send, pair_recv = refs[3 * count : 3 * count + 5]
    refs = refs[3 * count + 5 :]
    grid = Grid(fsdp_size, dims)
    ways = len(grid.crosses)
    empty = grid.chips * ways
    exchange, job = None, None
    if moved:
        exchange = Exchange(fsdp_size, grid.x, blocks, sources, targets, cut, False, *refs[:3])
        refs = refs[3:]
    if halved is not None:
        half, half_sem = refs[:2]
        refs = refs[2:]
    if side:
        job = side.make(*side_refs, *refs)

    def load(array, chip):
        index = grid.chip(*chip)
        return pltpu.make_async_copy(
            places[array](partials[array], chip, grid.core),
            held[array].at[index],
            load_sem.at[array, index],
        )

    def pair(array, chip):
        index = grid.chip(*chip)
        return pltpu.make_async_remote_copy(
            src_ref=places[array](partials[array], chip, 1 - grid.core),
            dst_ref=other[array].at[index],
            send_sem=pair_send.at[array, index],
            recv_sem=pair_recv.at[array, index],
            device_id=grid.partner(),
            device_id_type=MESH,
        )

    def hop(piece, chip, there, side_seen):
        array, first, rows, _ = pieces[piece]
        index = grid.chip(*chip)
        slot = index * ways + side_seen
        return pltpu.make_async_remote_copy(
            src_ref=held[array].at[index, pl.ds(first, rows)],
            dst_ref=landed[array].at[slot, pl.ds(first, rows)],
            send_sem=send_sem.at[piece, index],
            recv_sem=recv_sem.at[piece, slot],
            device_id=grid.device(*there, grid.core),
            device_id_type=MESH,
        )

    def add_up(piece, chip, root):
        array, first, rows, order = pieces[piece]
        index, slots, some = grid.chip(*chip), [], grid.z < 0
        for cross, wanted in grid.children(order, chip):
            way = grid.crosses.index(cross)
            under(wanted, hop(piece, chip, grid.here(), way).wait_recv)
            slot = index * ways + way
            slots.append(slot if wanted is None else jnp.where(wanted, slot, empty))
            some = None if wanted is None or some is None else jnp.logical_or(some, wanted)
        tile = 16 if rows % 16 == 0 else rows

        def add_all(used):
            def add(i, carry):
                span = pl.ds(pl.multiple_of(first + i * tile, tile), tile)
                total = held[array][index, span].astype(jnp.float32)
                total += other[array][index, span].astype(jnp.float32)
                for slot in used:
                    total += landed[array][slot, span].astype(jnp.float32)
                if root and array == halved:
                    start = grid.x * half.shape[0] + first + i * tile
                    outs[array][pl.ds(pl.multiple_of(start, tile), tile)] = total
                elif root:
                    outs[array][span] = total
                else:
                    held[array][index, span] = total.astype(held[array].dtype)
                return carry

            lax.fori_loop(0, rows // tile, add, 0)

        if root or some is None:
            add_all(slots)
        else:
            pl.when(some)(lambda: add_all(slots))
            pl.when(jnp.logical_not(some))(lambda: add_all([]))

    def swap_half():
        rows = half.shape[0]
        span = pl.ds(pl.multiple_of(grid.x * rows, 16), rows)
        return pltpu.make_async_remote_copy(
            src_ref=outs[halved].at[span],
            dst_ref=half,
            send_sem=half_sem.at[0],
            recv_sem=half_sem.at[1],
            device_id=grid.device(1 - grid.x, grid.y, grid.z, grid.core),
            device_id_type=MESH,
        )

    def fetched(array, chip):
        load(array, chip).wait()
        pair(array, chip).wait_recv()

    firsts = [min(p for p, piece in enumerate(pieces) if piece[0] == a) for a in range(count)]
    for array in range(count):
        landed[array][empty] = jnp.zeros(landed[array].shape[1:], landed[array].dtype)
    if moved:
        grid.greet_plane()
    else:
        grid.greet()
    last = grid.chips - 1

    def begin(number, carry):
        chip = grid.entry(last - number)
        for array in range(count):
            load(array, chip).start()
            pair(array, chip).start()
        return carry

    lax.fori_loop(0, grid.chips, begin, 0)
    if job:
        job.begin()

    def step(number, carry):
        chip = grid.entry(last - number)
        for piece in range(len(pieces)):
            if piece in firsts:
                fetched(pieces[piece][0], chip)
            add_up(piece, chip, False)
            hop(piece, chip, *grid.parent(pieces[piece][3], chip)).start()
            if job:
                job.tick(number, piece)
        if exchange:
            exchange.start(number, last)
        return carry

    lax.fori_loop(0, last, step, 0)
    if job:
        job.finish(last)
    for piece in range(len(pieces)):
        if piece in firsts:
            fetched(pieces[piece][0], grid.here())
        add_up(piece, grid.here(), True)
        if pieces[piece][0] == halved:
            swap = swap_half()
            swap.start()

    def finish(number, carry):
        chip = grid.entry(last - number)
        for array in range(count):
            pair(array, chip).wait_send()

        def sent():
            for piece in range(len(pieces)):
                hop(piece, chip, *grid.parent(pieces[piece][3], chip)).wait_send()

        pl.when(number < last)(sent)
        return carry

    lax.fori_loop(0, grid.chips, finish, 0)
    if halved is not None:
        swap.wait()
        start = (1 - grid.x) * half.shape[0]
        outs[halved][pl.ds(pl.multiple_of(start, 16), half.shape[0])] = half[...]
    if exchange:
        exchange.finish()


def reduce_call(
    fsdp_size,
    dims,
    pieces,
    places,
    partials,
    shapes,
    collective_id,
    blocks=0,
    cut=(),
    sources=(),
    targets=(),
    side=None,
    extra=(),
    halved=None,
):
    count = len(partials)
    ways = 4 if "x" in dims else 3
    chips = fsdp_size // 2 * (2 if "x" in dims else 1)
    dma = pltpu.SemaphoreType.DMA
    held = [pltpu.VMEM((chips, *s), p.dtype) for s, p in zip(shapes, partials)]
    landed = [pltpu.VMEM((chips * ways + 1, *s), p.dtype) for s, p in zip(shapes, partials)]
    moved = sum(p.size * p.dtype.itemsize for p in partials)
    sums = [(2 * s[0], s[1]) if at == halved else s for at, s in enumerate(shapes)]
    swapped = []
    if halved is not None:
        swapped = [pltpu.VMEM(shapes[halved], jnp.float32), dma((2,))]
    side_outs = tuple(side.shapes) if side else ()
    return pl.pallas_call(
        functools.partial(
            reduce_kernel, fsdp_size, dims, pieces, places, count, blocks, cut, side, halved
        ),
        out_shape=tuple(jax.ShapeDtypeStruct(s, jnp.float32) for s in sums)
        + tuple(targets)
        + side_outs,
        in_specs=[pl.BlockSpec(memory_space=pl.ANY)] * (count + len(sources) + len(extra)),
        out_specs=tuple(
            [pl.BlockSpec(memory_space=pltpu.VMEM)] * count
            + [pl.BlockSpec(memory_space=pl.ANY)] * (len(targets) + len(side_outs))
        ),
        scratch_shapes=[
            *held,
            *held,
            *landed,
            dma((len(pieces), chips)),
            dma((len(pieces), chips * ways)),
            dma((count, chips)),
            dma((count, chips)),
            dma((count, chips)),
            *exchange_sems(fsdp_size, len(sources)),
            *swapped,
            *(side.scratch if side else ()),
        ],
        compiler_params=pltpu.CompilerParams(
            collective_id=collective_id, has_side_effects=True, vmem_limit_bytes=67043328
        ),
        cost_estimate=pl.CostEstimate(flops=0, bytes_accessed=16 * moved, transcendentals=0),
    )(*partials, *sources, *extra)


def token_row(chip, core, rows):
    x, y, z = chip
    return ((z * 4 + y * 2 + core) * 2 + x) * rows


def reduce_tokens(partials, collective_id):
    fsdp_size = lax.axis_size("fsdp")
    rows = partials[0].shape[0] // (2 * fsdp_size)
    unit = rows // 4

    def place(ref, chip, core):
        return ref.at[pl.ds(pl.multiple_of(token_row(chip, core, rows), 16), rows)]

    pieces = [(0, at * unit, unit, order) for at, order in enumerate(("xyz", "zyx", "zxy", "zyx"))]
    pieces += [(array, 0, rows, "zyx") for array in range(1, len(partials))]
    shapes = [(rows, p.shape[1]) for p in partials]
    return reduce_call(
        fsdp_size, "xyz", pieces, [place] * len(partials), partials, shapes, collective_id
    )


def plane_row(chip, core):
    return chip[2] * 4 + chip[1] * 2 + core


def row_place(rows):
    def place(ref, chip, core, first=0, count=rows):
        return ref.at[pl.ds(pl.multiple_of(plane_row(chip, core) * rows + first, 8), count)]

    return place


def column_place(columns, rows):
    def place(ref, chip, core, first=0, count=rows):
        start = pl.multiple_of(plane_row(chip, core) * columns, 128)
        return ref.at[pl.ds(first, count), pl.ds(start, columns)]

    return place


def weight_pieces(query, latent, expand, output, small):
    return [
        (4, 0, small, "zy"),
        (0, 0, query // 2, "zy"),
        (1, 0, latent, "zy"),
        (0, query // 2, query // 2, "zy"),
        (2, 0, expand, "yz"),
        (3, 0, output // 2, "zy"),
        (3, output // 2, output // 2, "zy"),
    ]


def block_span(block):
    return pl.ds(pl.multiple_of(block * BLOCK, BLOCK), BLOCK)


def cut_columns(rows):
    def to_owner(source, target, block, other):
        there = pl.ds(pl.multiple_of(other * rows, rows), rows)
        return source.at[:, block_span(block)], target.at[there]

    def from_owner(source, target, block, other):
        there = pl.ds(pl.multiple_of(other * rows, rows), rows)
        return source.at[there], target.at[:, block_span(block)]

    return to_owner, from_owner


def cut_rows(columns):
    def to_owner(source, target, block, other):
        there = pl.ds(pl.multiple_of(other * columns, columns), columns)
        return source.at[block_span(block)], target.at[:, there]

    def from_owner(source, target, block, other):
        there = pl.ds(pl.multiple_of(other * columns, columns), columns)
        return source.at[:, there], target.at[block_span(block)]

    return to_owner, from_owner


def gather_weights(query, latent, expand, output, small, gate, up, down, collective_id):
    size = lax.axis_size("fsdp")
    shards = [query, latent, expand, output, small]
    places = [row_place(s.shape[0]) for s in shards]
    shapes = [
        jax.ShapeDtypeStruct((s.shape[0] * size, s.shape[1]), s.dtype) for s in shards
    ]
    for at in (1, 3):
        rows, columns = shards[at].shape
        places[at] = column_place(columns, rows)
        shapes[at] = jax.ShapeDtypeStruct((rows, columns * size), shards[at].dtype)
    columns, rows = cut_columns(gate.shape[0]), cut_rows(down.shape[1])
    tall = jax.ShapeDtypeStruct((gate.shape[0] * size, BLOCK), gate.dtype)
    flat = jax.ShapeDtypeStruct((BLOCK, down.shape[1] * size), down.dtype)
    return gather_call(
        size,
        [
            (1, None, latent.shape[0] // 2, "zy") if piece[0] == 1 else piece
            for piece in weight_pieces(*[s.shape[0] for s in shards])
        ],
        places,
        shards,
        shapes,
        collective_id,
        gate.shape[1] // BLOCK,
        (columns[0], columns[0], rows[0]),
        [gate, up, down],
        [tall, tall, flat],
    )


def reduce_weights(
    query, latent, expand, output, small, gate, up, down, blocks, collective_id, side, extra
):
    size = lax.axis_size("fsdp")
    partials = [query, latent, expand, output, small]
    shapes = [(p.shape[0] // size, p.shape[1]) for p in partials]
    places = [row_place(s[0]) for s in shapes]
    for at in (1, 3):
        rows, columns = partials[at].shape
        shapes[at] = (rows, columns // size)
        places[at] = column_place(columns // size, rows)
    half = partials[1].shape[0] // 2
    shapes[1] = (half, shapes[1][1])

    def half_place(ref, chip, core):
        start = pl.multiple_of(plane_row(chip, core) * shapes[1][1], 128)
        first = pl.multiple_of(chip[0] * half, 16)
        return ref.at[pl.ds(first, half), pl.ds(start, shapes[1][1])]

    places[1] = half_place
    columns, rows = cut_columns(gate.shape[0] // size), cut_rows(down.shape[1] // size)
    wide = jax.ShapeDtypeStruct((gate.shape[0] // size, blocks * BLOCK), gate.dtype)
    long = jax.ShapeDtypeStruct((blocks * BLOCK, down.shape[1] // size), down.dtype)
    return reduce_call(
        size,
        "zy",
        weight_pieces(*[s[0] for s in shapes]),
        places,
        partials,
        shapes,
        collective_id,
        blocks,
        (columns[1], columns[1], rows[1]),
        [gate, up, down],
        [wide, wide, long],
        side,
        extra,
        1,
    )


class Spread:
    ORDERS = ("xyz", "zyx", "zxy", "zyx")

    def __init__(self, fsdp_size, own, room, lead, sems):
        self.lead = lead
        self.grid = Grid(fsdp_size, "xyz", 1)
        self.own, self.room = own, room
        self.rows = own.shape[0]
        self.part = self.rows // len(self.ORDERS)
        self.send_sem, self.recv_sem, self.pair_send, self.pair_recv = sems
        self.units = fsdp_size // 2

    def unit(self, step):
        grid = self.grid
        flip = lax.rem(step, 2)
        return grid.y + flip - 2 * grid.y * flip, grid.level(lax.div(step, 2))

    def span(self, chip, piece):
        start = token_row(chip, self.grid.core, self.rows) + piece * self.part
        return self.room.at[pl.ds(pl.multiple_of(start, self.part), self.part)]

    def copies(self, chip, piece, own=False):
        grid, found = self.grid, []
        index, here = grid.chip(*chip), self.span(chip, piece)
        source = self.own.at[pl.ds(piece * self.part, self.part)] if own else here
        for cross, wanted in grid.children(self.ORDERS[piece], chip):
            there, _ = grid.neighbour(cross)
            copy = pltpu.make_async_remote_copy(
                src_ref=source,
                dst_ref=here,
                send_sem=self.send_sem.at[piece, index, grid.crosses.index(cross)],
                recv_sem=self.recv_sem.at[piece, index],
                device_id=grid.device(*there, grid.core),
                device_id_type=MESH,
            )
            found.append((wanted, copy))
        return found

    def pair(self, chip, piece, own=False, landing=False):
        grid = self.grid
        index, here = grid.chip(*chip), self.span(chip, piece)
        return pltpu.make_async_remote_copy(
            src_ref=self.own.at[pl.ds(piece * self.part, self.part)] if own else here,
            dst_ref=here,
            send_sem=self.pair_send.at[piece, index],
            recv_sem=(self.recv_sem if landing else self.pair_recv).at[piece, index],
            device_id=grid.partner(),
            device_id_type=MESH,
        )

    def relay(self, chip, piece, own=False):
        if not own:
            self.pair(chip, piece, landing=True).wait_recv()
        for wanted, copy in self.copies(chip, piece, own):
            under(wanted, copy.start)
        self.pair(chip, piece, own).start()

    def begin(self):
        grid = self.grid
        grid.greet()
        for piece in range(len(self.ORDERS)):
            self.relay(grid.here(), piece, own=True)
        start = token_row(grid.here(), grid.core, self.rows)
        self.room[pl.ds(pl.multiple_of(start, self.rows), self.rows)] = self.own[...]

        def early(number, carry):
            chip = grid.entry(number)
            for piece in range(len(self.ORDERS)):
                self.relay(chip, piece)
            return carry

        lax.fori_loop(1, self.lead, early, 0)

    def ahead(self, step):
        return [self.grid.entry(self.lead + 2 * step + one) for one in (0, 1)]

    def tick(self, step, chips, number):
        pieces = len(self.ORDERS)
        late = self.lead + 2 * step + number // pieces
        chip = chips[number // pieces]
        pl.when(late < 2 * self.units)(lambda: self.relay(chip, number % pieces))

    def arrived(self, step):
        y, z = self.unit(step)
        for x in (0, 1):
            for piece in range(len(self.ORDERS)):
                self.pair((x, y, z), piece).wait_recv()

    def drain(self):
        def finish(number, carry):
            chip = self.grid.entry(number)
            for piece in range(len(self.ORDERS)):
                for wanted, copy in self.copies(chip, piece):
                    under(wanted, copy.wait_send)
                self.pair(chip, piece).wait_send()
            return carry

        lax.fori_loop(0, 2 * self.units, finish, 0)


def spread_sems(fsdp_size):
    dma = pltpu.SemaphoreType.DMA
    return [dma((4, fsdp_size, 4)), dma((4, fsdp_size)), dma((4, fsdp_size)), dma((4, fsdp_size))]


class Stage:
    def __init__(self, buffers, results, sems):
        self.buffers, self.results, self.sems = buffers, results, sems

    def copy(self, number, step, unit):
        buffer = self.buffers[number]
        rows = buffer.shape[1]
        slot = lax.rem(step, 2)
        there = self.results[number].at[pl.ds(pl.multiple_of(unit * rows, rows), rows)]
        return pltpu.make_async_copy(buffer.at[slot], there, self.sems.at[number, slot])

    def reuse(self, step):
        def wait():
            for number in range(len(self.buffers)):
                self.copy(number, step, 0).wait()

        pl.when(step >= 2)(wait)

    def put(self, number, step, unit):
        self.copy(number, step, unit).start()

    def finish(self, steps):
        for step in (steps - 2, steps - 1):
            for number in range(len(self.buffers)):
                self.copy(number, step, 0).wait()


def dot(left, right):
    return jnp.dot(left, right, preferred_element_type=jnp.float32)


def dot_nt(left, right):
    return lax.dot_general(
        left, right, (((1,), (1,)), ((), ())), preferred_element_type=jnp.float32
    )


def dispatch_of(place_ref, sequence, capacity, seq_len):
    row = place_ref[pl.ds(sequence, 1), :]
    slot = lax.broadcasted_iota(jnp.int32, (capacity, seq_len), 0)
    return jnp.where(slot == row, 1.0, 0.0)


def forward_kernel(
    fsdp_size,
    experts,
    capacity,
    own,
    place_ref,
    gate_hbm,
    up_hbm,
    down_hbm,
    wide_hbm,
    block_hbm,
    tokens_out,
    received_out,
    gate_out,
    up_out,
    hidden_out,
    weight_out,
    shared_out,
    sh_out,
    part_out,
    room,
    picks,
    packs,
    chances,
    tall,
    received,
    gate_act,
    up_act,
    hidden,
    weight,
    shared,
    sh_act,
    part,
    gate_ref,
    up_ref,
    down_ref,
    wide_ref,
    block_ref,
    weight_sem,
    stage_sem,
    room_sem,
    *sems,
):
    f32, bf16 = jnp.float32, jnp.bfloat16
    seq_len = place_ref.shape[1]
    spread = Spread(fsdp_size, own, room, 3, sems)
    expert = lax.axis_index("fsdp")
    stage = Stage(
        [received, gate_act, up_act, hidden, weight, shared, sh_act, part],
        [received_out, gate_out, up_out, hidden_out, weight_out, shared_out, sh_out, part_out],
        stage_sem,
    )
    lanes = lax.broadcasted_iota(jnp.int32, (2 * seq_len, BLOCK), 1)

    def tokens_copy(unit):
        span = pl.ds(pl.multiple_of(unit * 2 * seq_len, 2 * seq_len), 2 * seq_len)
        return pltpu.make_async_copy(room.at[span], tokens_out.at[span], room_sem.at[unit])

    weights = [
        pltpu.make_async_copy(source, target, weight_sem.at[number])
        for number, (source, target) in enumerate([(gate_hbm, gate_ref), (up_hbm, up_ref), (down_hbm, down_ref), (wide_hbm, wide_ref), (block_hbm, block_ref)])
    ]
    for copy in weights:
        copy.start()
    spread.begin()
    for copy in weights:
        copy.wait()
    units = down_ref.shape[0]
    if units < hidden.shape[2]:
        hidden[:, :, units:] = jnp.zeros((2, 2 * capacity, hidden.shape[2] - units), bf16)
    for one in (0, 1):
        tall[one, capacity:] = block_ref[...]

    def body(step, carry):
        slot = lax.rem(step, 2)
        y, z = spread.unit(step)
        unit = z * 2 + y
        chips = spread.ahead(step)
        spread.arrived(step)
        tokens_copy(unit).start()
        stage.reuse(step)
        rows = [
            pl.ds(pl.multiple_of((2 * unit + one) * seq_len, seq_len), seq_len) for one in (0, 1)
        ]
        slots = [pl.ds(one * capacity, capacity) for one in (0, 1)]
        own_rows = [pl.ds(one * seq_len, seq_len) for one in (0, 1)]
        spread.tick(step, chips, 0)
        for one in (0, 1):
            pick = dispatch_of(place_ref, 2 * unit + one, capacity, seq_len)
            picks[one] = pick.astype(bf16)
            packs[one, :, :capacity] = jnp.transpose(pick).astype(bf16)
            received[slot, slots[one]] = dot(picks[one], room[rows[one]]).astype(bf16)
        stage.put(0, step, unit)
        spread.tick(step, chips, 1)
        both_rows = pl.ds(pl.multiple_of(unit * 2 * seq_len, 2 * seq_len), 2 * seq_len)
        wide = dot(room[both_rows], wide_ref[...])
        shared[slot] = wide[:, : 2 * BLOCK]
        gate_sh, up_sh = wide[:, :BLOCK], wide[:, BLOCK : 2 * BLOCK]
        act = (silu_parts(gate_sh)[0] * up_sh).astype(bf16)
        sh_act[slot] = act
        for one in (0, 1):
            packs[one, :, capacity:] = act[one * seq_len : (one + 1) * seq_len]
        logits = jnp.where(lanes < experts, wide[:, 2 * BLOCK :], MASKED)
        logit_exp = jnp.exp(logits - jnp.max(logits, axis=1, keepdims=True))
        chance = jnp.sum(jnp.where(lanes == expert, logit_exp, 0.0), axis=1, keepdims=True)
        chance = chance / jnp.sum(logit_exp, axis=1, keepdims=True)
        coarse = chance.astype(bf16).astype(f32)
        chances[...] = jnp.where(
            lanes == 0, coarse, jnp.where(lanes == 1, chance - coarse, 0.0)
        ).astype(bf16)
        stage.put(5, step, unit)
        stage.put(6, step, unit)
        spread.tick(step, chips, 2)
        gate_act[slot] = dot_nt(received[slot], gate_ref[...])
        stage.put(1, step, unit)
        spread.tick(step, chips, 3)
        up_act[slot] = dot_nt(received[slot], up_ref[...])
        stage.put(2, step, unit)
        spread.tick(step, chips, 4)
        for one in (0, 1):
            halves = dot(picks[one], chances[own_rows[one]])
            scale = halves[:, 0:1] + halves[:, 1:2]
            weight[slot, slots[one]] = jnp.broadcast_to(scale, (capacity, BLOCK))
            act = silu_parts(gate_act[slot, slots[one]])[0] * up_act[slot, slots[one]]
            hidden[slot, slots[one], :units] = (scale * act).astype(bf16)
        stage.put(3, step, unit)
        stage.put(4, step, unit)
        spread.tick(step, chips, 5)
        result = dot(hidden[slot, :, :units], down_ref[...]).astype(bf16)
        for one in (0, 1):
            tall[one, :capacity] = result[one * capacity : (one + 1) * capacity]
        spread.tick(step, chips, 6)
        part[slot, own_rows[0]] = dot(packs[0], tall[0]).astype(bf16)
        spread.tick(step, chips, 7)
        part[slot, own_rows[1]] = dot(packs[1], tall[1]).astype(bf16)
        stage.put(7, step, unit)
        return carry

    lax.fori_loop(0, spread.units, body, 0)
    stage.finish(spread.units)
    for unit in range(spread.units):
        tokens_copy(unit).wait()
    spread.drain()


def experts_forward(own, place, gate, up, down, wide, block, capacity, experts, collective_id):
    fsdp_size = lax.axis_size("fsdp")
    f32, bf16 = jnp.float32, jnp.bfloat16
    seq_len, width, hidden = place.shape[1], own.shape[1], gate.shape[0]
    tokens, slots = fsdp_size * seq_len, fsdp_size * capacity
    padded = -(-hidden // BLOCK) * BLOCK
    shape = jax.ShapeDtypeStruct
    outs = [
        shape((tokens, width), bf16),
        shape((slots, width), bf16),
        shape((slots, hidden), f32),
        shape((slots, hidden), f32),
        shape((slots, padded), bf16),
        shape((slots, BLOCK), f32),
        shape((tokens, 2 * BLOCK), f32),
        shape((tokens, BLOCK), bf16),
        shape((tokens, width), bf16),
    ]
    stages = [pltpu.VMEM((2, 2 * o.shape[0] // fsdp_size, o.shape[1]), o.dtype) for o in outs[1:]]
    dma = pltpu.SemaphoreType.DMA
    return pl.pallas_call(
        functools.partial(forward_kernel, fsdp_size, experts, capacity),
        out_shape=tuple(outs),
        in_specs=[pl.BlockSpec(memory_space=pltpu.VMEM)] * 2
        + [pl.BlockSpec(memory_space=pl.ANY)] * 5,
        out_specs=tuple([pl.BlockSpec(memory_space=pl.ANY)] * len(outs)),
        scratch_shapes=[
            pltpu.VMEM((tokens, width), bf16),
            pltpu.VMEM((2, capacity, seq_len), bf16),
            pltpu.VMEM((2, seq_len, capacity + BLOCK), bf16),
            pltpu.VMEM((2 * seq_len, BLOCK), bf16),
            pltpu.VMEM((2, capacity + BLOCK, width), bf16),
            *stages,
            *[pltpu.VMEM(w.shape, w.dtype) for w in (gate, up, down, wide, block)],
            dma((5,)),
            dma((len(stages), 2)),
            dma((fsdp_size // 2,)),
            *spread_sems(fsdp_size),
        ],
        compiler_params=pltpu.CompilerParams(
            collective_id=collective_id, has_side_effects=True, vmem_limit_bytes=67043328
        ),
        cost_estimate=pl.CostEstimate(
            flops=6 * slots * width * hidden, bytes_accessed=100_000_000, transcendentals=0
        ),
    )(own, place, gate, up, down, wide, block)


def backward_kernel(
    fsdp_size,
    capacity,
    own,
    place_ref,
    gate_hbm,
    up_hbm,
    down_hbm,
    pair_hbm,
    block_hbm,
    gate_in,
    up_in,
    weight_in,
    shared_in,
    grads_out,
    slots_out,
    gate_out,
    up_out,
    pair_out,
    chance_out,
    part_out,
    room,
    picks,
    packs,
    tall,
    gate_act,
    up_act,
    weight,
    shared,
    picked,
    gate_grad,
    up_grad,
    pair_grad,
    chance_grad,
    part,
    gate_ref,
    up_ref,
    down_ref,
    pair_ref,
    block_ref,
    weight_sem,
    load_sem,
    stage_sem,
    room_sem,
    *sems,
):
    f32, bf16 = jnp.float32, jnp.bfloat16
    seq_len = place_ref.shape[1]
    spread = Spread(fsdp_size, own, room, 4, sems)
    expert = lax.axis_index("fsdp")
    stage = Stage(
        [picked, gate_grad, up_grad, pair_grad, chance_grad, part],
        [slots_out, gate_out, up_out, pair_out, chance_out, part_out],
        stage_sem,
    )
    saved = [gate_in, up_in, weight_in, shared_in]
    loads = [gate_act, up_act, weight, shared]

    def load(number, step):
        y, z = spread.unit(step)
        slot, rows = lax.rem(step, 2), loads[number].shape[1]
        span = pl.ds(pl.multiple_of((z * 2 + y) * rows, rows), rows)
        return pltpu.make_async_copy(
            saved[number].at[span], loads[number].at[slot], load_sem.at[number, slot]
        )

    def grads_copy(unit):
        span = pl.ds(pl.multiple_of(unit * 2 * seq_len, 2 * seq_len), 2 * seq_len)
        return pltpu.make_async_copy(room.at[span], grads_out.at[span], room_sem.at[unit])

    for number in range(len(saved)):
        load(number, 0).start()
    weights = [
        pltpu.make_async_copy(source, target, weight_sem.at[number])
        for number, (source, target) in enumerate([(gate_hbm, gate_ref), (up_hbm, up_ref), (down_hbm, down_ref), (pair_hbm, pair_ref), (block_hbm, block_ref)])
    ]
    for copy in weights:
        copy.start()
    spread.begin()
    for copy in weights:
        copy.wait()
    units = down_ref.shape[0]
    if units < gate_grad.shape[2]:
        for grad in (gate_grad, up_grad):
            grad[:, :, units:] = jnp.zeros((2, 2 * capacity, grad.shape[2] - units), bf16)
    for one in (0, 1):
        tall[one, capacity:] = pair_ref[...]
    expert_lane = lax.broadcasted_iota(jnp.int32, (capacity, BLOCK), 1) == expert

    def body(step, carry):
        slot = lax.rem(step, 2)
        y, z = spread.unit(step)
        unit = z * 2 + y
        later = step + 1
        chips = spread.ahead(step)
        spread.arrived(step)
        grads_copy(unit).start()
        stage.reuse(step)
        rows = [
            pl.ds(pl.multiple_of((2 * unit + one) * seq_len, seq_len), seq_len) for one in (0, 1)
        ]
        both_rows = pl.ds(pl.multiple_of(unit * 2 * seq_len, 2 * seq_len), 2 * seq_len)
        slots = [pl.ds(one * capacity, capacity) for one in (0, 1)]
        own_rows = [pl.ds(one * seq_len, seq_len) for one in (0, 1)]
        for number in range(len(saved)):
            load(number, step).wait()

        def ahead():
            for number in range(len(saved)):
                load(number, later).start()

        pl.when(later < spread.units)(ahead)
        spread.tick(step, chips, 0)
        for one in (0, 1):
            pick = dispatch_of(place_ref, 2 * unit + one, capacity, seq_len)
            picks[one] = pick.astype(bf16)
            packs[one, :, :capacity] = jnp.transpose(pick).astype(bf16)
            picked[slot, slots[one]] = dot(picks[one], room[rows[one]]).astype(bf16)
        stage.put(0, step, unit)
        spread.tick(step, chips, 1)
        raw = dot_nt(picked[slot], down_ref[...])
        scale = weight[slot, :, 0:1]
        silu_gate, slope = silu_parts(gate_act[slot])
        up_value = up_act[slot]
        gate_sum = jnp.sum(raw * (silu_gate * up_value), axis=1, keepdims=True)
        scaled = scale * raw
        gate_grad[slot, :, :units] = (scaled * up_value * slope).astype(bf16)
        up_grad[slot, :, :units] = (scaled * silu_gate).astype(bf16)
        stage.put(1, step, unit)
        stage.put(2, step, unit)
        spread.tick(step, chips, 2)
        for one in (0, 1):
            column = gate_sum[one * capacity : (one + 1) * capacity]
            column = jnp.where(expert_lane, column, 0.0).astype(bf16)
            chance_grad[slot, own_rows[one]] = dot(packs[one, :, :capacity], column).astype(bf16)
        stage.put(4, step, unit)
        grad_sh = dot_nt(room[both_rows], block_ref[...])
        silu_sh, slope_sh = silu_parts(shared[slot, :, :BLOCK])
        gate_sh = (grad_sh * shared[slot, :, BLOCK:] * slope_sh).astype(bf16)
        up_sh = (grad_sh * silu_sh).astype(bf16)
        pair_grad[slot, :, :BLOCK] = gate_sh
        pair_grad[slot, :, BLOCK:] = up_sh
        for one in (0, 1):
            own_seq = slice(one * seq_len, (one + 1) * seq_len)
            packs[one, :, capacity : capacity + BLOCK] = gate_sh[own_seq]
            packs[one, :, capacity + BLOCK :] = up_sh[own_seq]
        stage.put(3, step, unit)
        spread.tick(step, chips, 3)
        back = dot(gate_grad[slot, :, :units], gate_ref[...])
        spread.tick(step, chips, 4)
        back = (back + dot(up_grad[slot, :, :units], up_ref[...])).astype(bf16)
        for one in (0, 1):
            tall[one, :capacity] = back[one * capacity : (one + 1) * capacity]
        spread.tick(step, chips, 5)
        part[slot, own_rows[0]] = dot(packs[0], tall[0]).astype(bf16)
        spread.tick(step, chips, 6)
        part[slot, own_rows[1]] = dot(packs[1], tall[1]).astype(bf16)
        stage.put(5, step, unit)
        spread.tick(step, chips, 7)
        return carry

    lax.fori_loop(0, spread.units, body, 0)
    stage.finish(spread.units)
    for unit in range(spread.units):
        grads_copy(unit).wait()
    spread.drain()


def experts_backward(
    own, place, gate, up, down, pair, block, gate_act, up_act, weight, shared, capacity, collective_id
):
    fsdp_size = lax.axis_size("fsdp")
    bf16 = jnp.bfloat16
    seq_len, width, hidden = place.shape[1], own.shape[1], gate.shape[0]
    tokens, slots = fsdp_size * seq_len, fsdp_size * capacity
    padded = -(-hidden // BLOCK) * BLOCK
    shape = jax.ShapeDtypeStruct
    outs = [
        shape((tokens, width), bf16),
        shape((slots, width), bf16),
        shape((slots, padded), bf16),
        shape((slots, padded), bf16),
        shape((tokens, 2 * BLOCK), bf16),
        shape((tokens, BLOCK), bf16),
        shape((tokens, width), bf16),
    ]

    def slots_of(arrays):
        return [pltpu.VMEM((2, 2 * a.shape[0] // fsdp_size, a.shape[1]), a.dtype) for a in arrays]

    saved = [gate_act, up_act, weight, shared]
    dma = pltpu.SemaphoreType.DMA
    return pl.pallas_call(
        functools.partial(backward_kernel, fsdp_size, capacity),
        out_shape=tuple(outs),
        in_specs=[pl.BlockSpec(memory_space=pltpu.VMEM)] * 2
        + [pl.BlockSpec(memory_space=pl.ANY)] * 9,
        out_specs=tuple([pl.BlockSpec(memory_space=pl.ANY)] * len(outs)),
        scratch_shapes=[
            pltpu.VMEM((tokens, width), bf16),
            pltpu.VMEM((2, capacity, seq_len), bf16),
            pltpu.VMEM((2, seq_len, capacity + 2 * BLOCK), bf16),
            pltpu.VMEM((2, capacity + 2 * BLOCK, width), bf16),
            *slots_of(saved),
            *slots_of(outs[1:]),
            *[pltpu.VMEM(w.shape, w.dtype) for w in (gate, up, down, pair, block)],
            dma((5,)),
            dma((4, 2)),
            dma((len(outs) - 1, 2)),
            dma((fsdp_size // 2,)),
            *spread_sems(fsdp_size),
        ],
        compiler_params=pltpu.CompilerParams(
            collective_id=collective_id, has_side_effects=True, vmem_limit_bytes=67043328
        ),
        cost_estimate=pl.CostEstimate(
            flops=6 * slots * width * hidden, bytes_accessed=100_000_000, transcendentals=0
        ),
    )(own, place, gate, up, down, pair, block, *saved)


def token_shards(
    inputs,
    teacher,
    valid_mask,
    prefix,
    routes,
    norm_gain,
    query_weight,
    latent_weight,
    latent_gain,
    expand_weight,
    output_weight,
    moe_gain,
    router_weight,
    shared_gate,
    shared_up,
    shared_down,
    expert_gate,
    expert_up,
    expert_down,
):
    f32 = jnp.float32
    bf16 = jnp.bfloat16
    tp_size = lax.axis_size("tp")
    fsdp_size = lax.axis_size("fsdp")
    own_tp = lax.axis_index("tp")
    own_expert = lax.axis_index("fsdp")
    local_heads = HEADS // tp_size
    own_rows = inputs.shape[0]
    width = inputs.shape[1]
    seq_len = own_rows * tp_size

    expert_count = router_weight.shape[1]
    route_rows = routes.shape[1] * seq_len // BLOCK
    valid_rows = seq_len // BLOCK
    parts = [
        routes.T.reshape(route_rows, BLOCK).astype(f32),
        valid_mask.reshape(valid_rows, BLOCK).astype(f32),
        norm_gain.reshape(1, BLOCK).astype(f32),
        moe_gain.reshape(1, BLOCK).astype(f32),
        jnp.pad(latent_gain, (0, BLOCK - latent_gain.shape[0])).reshape(1, BLOCK).astype(f32),
        router_weight.T.astype(f32),
    ]
    small = jnp.concatenate(parts, axis=0)
    small_rows = -(-small.shape[0] // 8) * 8
    small = jnp.pad(small, ((0, small_rows - small.shape[0]), (0, 0)))
    blocks = shared_gate.shape[1] // BLOCK
    (
        query_full,
        latent_full,
        expand_full,
        output_full,
        small_all,
        gate_block,
        up_block,
        down_block,
    ) = gather_weights(
        query_weight,
        latent_weight.T,
        expand_weight,
        output_weight,
        small,
        shared_gate,
        shared_up,
        shared_down,
        1,
    )
    small_all = small_all.reshape(fsdp_size, small_rows, BLOCK)
    gain_row = route_rows + valid_rows
    norm_gains = small_all[:, gain_row].reshape(width)
    latent_gains = small_all[:, gain_row + 2, : latent_gain.shape[0]].reshape(RANK)

    hidden = tp_gather(inputs, own_tp).astype(f32)
    cosine, sine_part = rope_tables(seq_len, ROPE)
    inverse_in = lax.rsqrt(jnp.mean(hidden * hidden, axis=-1, keepdims=True) + EPSILON)
    normal_in = hidden * inverse_in
    norm_scale = norm_gains.astype(f32)
    normed = (normal_in * norm_scale).astype(bf16)
    query_lin = jnp.dot(normed, query_full, preferred_element_type=f32).reshape(
        seq_len, local_heads, NOPE + ROPE
    )
    queries = jnp.concatenate(
        [
            query_lin[..., :NOPE],
            rotate(query_lin[..., NOPE:], cosine[:, None, :], sine_part[:, None, :]),
        ],
        axis=-1,
    ).astype(bf16)
    latent_lin = jnp.einsum("td,rd->tr", normed, latent_full, preferred_element_type=f32)
    latent_raw = latent_lin[:, :RANK]
    inverse_lat = lax.rsqrt(jnp.mean(latent_raw * latent_raw, axis=-1, keepdims=True) + EPSILON)
    latent_unit = latent_raw * inverse_lat
    latent_scale = latent_gains.astype(f32)
    latent = (latent_unit * latent_scale).astype(bf16)
    key_rope = rotate(latent_lin[:, RANK:], cosine, sine_part).astype(bf16)
    keys_values = (
        jnp.dot(latent, expand_full, preferred_element_type=f32)
        .astype(bf16)
        .reshape(seq_len, local_heads, NOPE + VDIM)
    )
    key_nope = keys_values[..., :NOPE]
    values = keys_values[..., NOPE:]
    query_nope = queries[..., :NOPE]
    query_rope = queries[..., NOPE:]
    score_scale = 1.0 / math.sqrt(NOPE + ROPE)
    position = jnp.arange(seq_len, dtype=jnp.int32)
    visible = (position[None, :] <= position[:, None]) | (position[None, :] < prefix[0])
    raw_scores = jnp.einsum("ihd,jhd->hij", query_nope, key_nope, preferred_element_type=f32)
    raw_scores = raw_scores + jnp.einsum(
        "ihd,jd->hij", query_rope, key_rope, preferred_element_type=f32
    )
    scores = jnp.where(visible[None], raw_scores * score_scale, MASKED)
    row_max = jnp.max(scores, axis=-1, keepdims=True)
    shifted = jnp.exp(scores - row_max)
    attn_probs = shifted / jnp.sum(shifted, axis=-1, keepdims=True)
    probs_low = attn_probs.astype(bf16)
    heads_out = (
        jnp.einsum("hij,jhd->ihd", probs_low, values, preferred_element_type=f32)
        .astype(bf16)
        .reshape(seq_len, local_heads * VDIM)
    )
    attended = jnp.dot(heads_out, output_full, preferred_element_type=f32)
    small_all, gate_block, up_block, down_block, attended = lax.optimization_barrier(
        (small_all, gate_block, up_block, down_block, attended)
    )
    attended = tp_scatter(attended, own_tp, own_rows)

    routes_all = small_all[:, :route_rows].reshape(fsdp_size, routes.shape[1], seq_len)
    valid_all = small_all[:, route_rows:gain_row]
    moe_gains = small_all[:, gain_row + 1].reshape(width)
    router_rows = small_all[:, gain_row + 3 : gain_row + 3 + expert_count]
    router_full = jnp.transpose(router_rows, (1, 0, 2)).reshape(expert_count, width).astype(bf16)
    holds_block = block_of(own_expert, fsdp_size // 2) < blocks
    gate_block = jnp.where(holds_block, gate_block, 0)
    up_block = jnp.where(holds_block, up_block, 0)
    down_block = jnp.where(holds_block, down_block, 0)

    middle = inputs.astype(f32) + attended
    inverse_mid = lax.rsqrt(jnp.mean(middle * middle, axis=-1, keepdims=True) + EPSILON)
    normal_mid = middle * inverse_mid
    moe_scale = moe_gains.astype(f32)
    moe_in = (normal_mid * moe_scale).astype(bf16)

    def route(logits):
        logit_exp = jnp.exp(logits - jnp.max(logits, axis=-1, keepdims=True))
        return logit_exp / jnp.sum(logit_exp, axis=-1, keepdims=True)

    router_probs = route(jnp.einsum("td,ed->te", moe_in, router_full, preferred_element_type=f32))
    experts = expert_count
    top_count = routes.shape[1]
    capacity = top_count * seq_len * 4 // (3 * experts)

    named = jnp.any(routes_all == own_expert.astype(f32), axis=1)
    ahead = jnp.dot(
        named.astype(bf16),
        (position[:, None] < position[None, :]).astype(bf16),
        preferred_element_type=f32,
    ).astype(jnp.int32)
    place = jnp.where(named, ahead, -1)
    wide_block = jnp.concatenate(
        [gate_block, up_block, jnp.pad(router_full, ((0, BLOCK - experts), (0, 0))).T], axis=1
    )
    (
        tokens,
        received,
        gate_act,
        up_act,
        gated_hidden,
        gate_weight,
        shared_acts,
        shared_hidden,
        moe_part,
    ) = experts_forward(
        moe_in,
        place,
        expert_gate[0].T,
        expert_up[0].T,
        expert_down[0],
        wide_block,
        down_block,
        capacity,
        experts,
        2,
    )
    activations = middle + reduce_tokens([moe_part], 3)[0]

    own_mask = half_rows(valid_mask, own_tp, own_rows).astype(f32)
    offset = activations - half_rows(teacher, own_tp, own_rows).astype(f32)
    valid_total = jnp.maximum(jnp.sum(valid_all), 1.0)
    square_part = jnp.sum(own_mask[:, None] * offset * offset)
    grad_out = seq_len * fsdp_size / valid_total * own_mask[:, None] * offset
    grad_moe = grad_out.astype(bf16)

    (
        grads,
        grad_slots,
        grad_gate_act,
        grad_up_act,
        grad_sh_pair,
        grad_probs_part,
        grad_part,
    ) = experts_backward(
        grad_moe,
        place,
        expert_gate[0].T,
        expert_up[0].T,
        expert_down[0],
        jnp.concatenate([gate_block.T, up_block.T], axis=0),
        down_block,
        gate_act,
        up_act,
        gate_weight,
        shared_acts,
        capacity,
        4,
    )
    grad_moe_in, grad_router_probs = reduce_tokens([grad_part, grad_probs_part], 5)
    down_shared_grad = jnp.einsum("tf,td->fd", shared_hidden, grads, preferred_element_type=f32)
    pair_grad = jnp.einsum("td,tf->df", tokens, grad_sh_pair, preferred_element_type=f32)
    gate_shared_grad = pair_grad[:, :BLOCK].astype(bf16)
    up_shared_grad = pair_grad[:, BLOCK:].astype(bf16)
    grad_router_probs = grad_router_probs[:, :experts]

    grad_logits = router_probs * (
        grad_router_probs - jnp.sum(router_probs * grad_router_probs, axis=-1, keepdims=True)
    )
    router_grad = jnp.einsum(
        "td,te->ed", moe_in.astype(f32), grad_logits, precision=HIGHEST, preferred_element_type=f32
    )
    grad_moe_in = grad_moe_in + jnp.einsum(
        "te,ed->td",
        grad_logits,
        router_full.astype(f32),
        precision=HIGHEST,
        preferred_element_type=f32,
    )
    moe_gain_grad = jnp.sum(grad_moe_in * normal_mid, axis=0)
    grad_middle = grad_out + norm_back(grad_moe_in * moe_scale, normal_mid, inverse_mid)
    grad_attended = tp_gather(grad_middle.astype(bf16), own_tp)

    output_grad = jnp.einsum("tf,td->fd", heads_out, grad_attended, preferred_element_type=f32)
    grad_heads = (
        jnp.einsum("td,fd->tf", grad_attended, output_full, preferred_element_type=f32)
        .astype(bf16)
        .reshape(seq_len, local_heads, VDIM)
    )
    grad_probs = jnp.einsum("ihd,jhd->hij", grad_heads, values, preferred_element_type=f32)
    grad_values = jnp.einsum("hij,ihd->jhd", probs_low, grad_heads, preferred_element_type=f32)
    grad_scores = (
        attn_probs * (grad_probs - jnp.sum(attn_probs * grad_probs, axis=-1, keepdims=True))
    ).astype(bf16)
    grad_q_nope = (
        jnp.einsum("hij,jhd->ihd", grad_scores, key_nope, preferred_element_type=f32) * score_scale
    )
    grad_q_rope = (
        jnp.einsum("hij,jd->ihd", grad_scores, key_rope, preferred_element_type=f32) * score_scale
    )
    grad_keys = (
        jnp.einsum("hij,ihd->jhd", grad_scores, query_nope, preferred_element_type=f32)
        * score_scale
    )
    grad_key_rope = (
        jnp.einsum("hij,ihd->jd", grad_scores, query_rope, preferred_element_type=f32) * score_scale
    )
    grad_query = (
        jnp.concatenate(
            [grad_q_nope, unrotate(grad_q_rope, cosine[:, None, :], sine_part[:, None, :])], axis=-1
        )
        .astype(bf16)
        .reshape(seq_len, local_heads * (NOPE + ROPE))
    )
    query_grad = jnp.einsum("td,tq->dq", normed, grad_query, preferred_element_type=f32)
    grad_normed = jnp.einsum("tq,dq->td", grad_query, query_full, preferred_element_type=f32)
    grad_kv = (
        jnp.concatenate([grad_keys, grad_values], axis=-1)
        .astype(bf16)
        .reshape(seq_len, local_heads * (NOPE + VDIM))
    )
    expand_grad = jnp.einsum("tr,tq->rq", latent, grad_kv, preferred_element_type=f32)
    grad_latent = jnp.einsum("tq,rq->tr", grad_kv, expand_full, preferred_element_type=f32)
    grad_both = tp_sum(jnp.concatenate([grad_latent, grad_key_rope], axis=1))
    grad_latent, grad_key_rope = grad_both[:, :RANK], grad_both[:, RANK:]
    latent_gain_grad = jnp.sum(grad_latent * latent_unit, axis=0)
    grad_latent_raw = norm_back(grad_latent * latent_scale, latent_unit, inverse_lat)
    grad_latent_lin = jnp.concatenate(
        [grad_latent_raw, unrotate(grad_key_rope, cosine, sine_part)], axis=-1
    ).astype(bf16)
    latent_grad = jnp.einsum("tr,td->rd", grad_latent_lin, normed, preferred_element_type=f32)
    grad_normed = tp_scatter(grad_normed, own_tp, own_rows) + jnp.einsum(
        "tr,rd->td",
        half_rows(grad_latent_lin, own_tp, own_rows),
        latent_full,
        preferred_element_type=f32,
    )
    own_normal = half_rows(normal_in, own_tp, own_rows)
    own_inverse = half_rows(inverse_in, own_tp, own_rows)
    norm_gain_grad = jnp.sum(grad_normed * own_normal, axis=0)
    input_grad = grad_middle + norm_back(grad_normed * norm_scale, own_normal, own_inverse)

    small = jnp.concatenate(
        [
            jnp.transpose(router_grad.reshape(experts, fsdp_size, BLOCK), (1, 0, 2)),
            norm_gain_grad.reshape(fsdp_size, 1, BLOCK),
            moe_gain_grad.reshape(fsdp_size, 1, BLOCK),
            jnp.pad(
                0.5 * latent_gain_grad.reshape(fsdp_size, 1, RANK // fsdp_size),
                ((0, 0), (0, 0), (0, BLOCK - RANK // fsdp_size)),
            ),
            jnp.full((fsdp_size, 1, BLOCK), square_part),
        ],
        axis=1,
    )
    small = jnp.pad(small, ((0, 0), (0, -(experts + 4) % 8), (0, 0))).reshape(-1, BLOCK)
    small = small + swap_tp(small)
    query_out, latent_out, expand_out, output_out, small_out, gate_out, up_out, down_out, *expert_grads = (
        reduce_weights(
            query_grad.astype(bf16),
            latent_grad.astype(bf16),
            expand_grad.astype(bf16),
            output_grad.astype(bf16),
            small,
            gate_shared_grad,
            up_shared_grad,
            down_shared_grad.astype(bf16),
            blocks,
            6,
            WeightGrads(received.shape[0], expert_down.shape[1], width),
            [grad_gate_act, grad_up_act, gated_hidden, received, grad_slots],
        )
    )
    return (
        small_out[experts + 3, 0] / (width * valid_total),
        activations,
        input_grad,
        small_out[experts],
        query_out,
        latent_out.T,
        small_out[experts + 2, : RANK // fsdp_size],
        expand_out,
        output_out,
        small_out[experts + 1],
        small_out[:experts].T,
        gate_out.astype(f32),
        up_out.astype(f32),
        down_out.astype(f32),
        expert_grads[0].T.astype(f32)[None],
        expert_grads[1].T.astype(f32)[None],
        expert_grads[2].astype(f32)[None],
    )


def slot_shards(
    inputs,
    teacher,
    valid_mask,
    prefix,
    routes,
    norm_gain,
    query_weight,
    latent_weight,
    latent_gain,
    expand_weight,
    output_weight,
    moe_gain,
    router_weight,
    shared_gate,
    shared_up,
    shared_down,
    expert_gate,
    expert_up,
    expert_down,
):
    f32 = jnp.float32
    bf16 = jnp.bfloat16
    tp_size = lax.axis_size("tp")
    fsdp_size = lax.axis_size("fsdp")
    local_heads = HEADS // tp_size
    (
        norm_gains,
        query_full,
        latent_full,
        latent_gains,
        expand_full,
        output_full,
        moe_gains,
        router_full,
        gate_full,
        up_full,
        down_full,
    ) = (
        lax.all_gather(norm_gain, "fsdp", axis=0, tiled=True),
        lax.all_gather(query_weight, "fsdp", axis=0, tiled=True),
        lax.all_gather(latent_weight, "fsdp", axis=0, tiled=True),
        lax.all_gather(latent_gain, "fsdp", axis=0, tiled=True),
        lax.all_gather(expand_weight, "fsdp", axis=0, tiled=True),
        lax.all_gather(output_weight, "fsdp", axis=1, tiled=True),
        lax.all_gather(moe_gain, "fsdp", axis=0, tiled=True),
        lax.all_gather(router_weight, "fsdp", axis=0, tiled=True),
        lax.all_gather(shared_gate, "fsdp", axis=0, tiled=True),
        lax.all_gather(shared_up, "fsdp", axis=0, tiled=True),
        lax.all_gather(shared_down, "fsdp", axis=1, tiled=True),
    )
    gathered = lax.all_gather(inputs, "tp", axis=0, tiled=True)
    seq_len = gathered.shape[0]
    width = gathered.shape[1]
    hidden = gathered.astype(f32)
    cosine, sine_part = rope_tables(seq_len, ROPE)
    inverse_in = lax.rsqrt(jnp.mean(hidden * hidden, axis=-1, keepdims=True) + EPSILON)
    normal_in = hidden * inverse_in
    norm_scale = norm_gains.astype(f32)
    normed = (normal_in * norm_scale).astype(bf16)
    query_lin = jnp.dot(normed, query_full, preferred_element_type=f32).reshape(
        seq_len, local_heads, NOPE + ROPE
    )
    queries = jnp.concatenate(
        [
            query_lin[..., :NOPE],
            rotate(query_lin[..., NOPE:], cosine[:, None, :], sine_part[:, None, :]),
        ],
        axis=-1,
    ).astype(bf16)
    latent_lin = jnp.dot(normed, latent_full, preferred_element_type=f32)
    latent_raw = latent_lin[:, :RANK]
    inverse_lat = lax.rsqrt(jnp.mean(latent_raw * latent_raw, axis=-1, keepdims=True) + EPSILON)
    latent_unit = latent_raw * inverse_lat
    latent_scale = latent_gains.astype(f32)
    latent = (latent_unit * latent_scale).astype(bf16)
    key_rope = rotate(latent_lin[:, RANK:], cosine, sine_part).astype(bf16)
    keys_values = (
        jnp.dot(latent, expand_full, preferred_element_type=f32)
        .astype(bf16)
        .reshape(seq_len, local_heads, NOPE + VDIM)
    )
    key_nope = keys_values[..., :NOPE]
    values = keys_values[..., NOPE:]
    query_nope = queries[..., :NOPE]
    query_rope = queries[..., NOPE:]
    score_scale = 1.0 / math.sqrt(NOPE + ROPE)
    position = jnp.arange(seq_len, dtype=jnp.int32)
    visible = (position[None, :] <= position[:, None]) | (position[None, :] < prefix[0])

    def scores_of():
        raw_scores = jnp.einsum("ihd,jhd->hij", query_nope, key_nope, preferred_element_type=f32)
        raw_scores = raw_scores + jnp.einsum(
            "ihd,jd->hij", query_rope, key_rope, preferred_element_type=f32
        )
        return jnp.where(visible[None], raw_scores * score_scale, MASKED)

    scores = scores_of()
    row_max = jnp.max(scores, axis=-1, keepdims=True)
    shifted = jnp.exp(scores - row_max)
    row_total = jnp.sum(shifted, axis=-1, keepdims=True)
    log_total = row_max + jnp.log(row_total)
    probs_low = (shifted / row_total).astype(bf16)
    heads_out = (
        jnp.einsum("hij,jhd->ihd", probs_low, values, preferred_element_type=f32)
        .astype(bf16)
        .reshape(seq_len, local_heads * VDIM)
    )
    attended = lax.psum(jnp.dot(heads_out, output_full, preferred_element_type=f32), "tp")
    middle = hidden + attended
    inverse_mid = lax.rsqrt(jnp.mean(middle * middle, axis=-1, keepdims=True) + EPSILON)
    normal_mid = middle * inverse_mid
    moe_scale = moe_gains.astype(f32)
    moe_in = (normal_mid * moe_scale).astype(bf16)
    logits = jnp.dot(moe_in, router_full, preferred_element_type=f32)
    logit_max = jnp.max(logits, axis=-1, keepdims=True)
    logit_exp = jnp.exp(logits - logit_max)
    router_probs = logit_exp / jnp.sum(logit_exp, axis=-1, keepdims=True)
    experts = router_full.shape[1]
    top_count = routes.shape[1]
    choose = routes[:, :, None] == jnp.arange(experts, dtype=jnp.int32)[None, None, :]
    gate_values = jnp.sum(jnp.where(choose, router_probs[:, None, :], 0.0), axis=-1)
    capacity = top_count * seq_len * 4 // (3 * experts)
    flat_routes = routes.reshape(seq_len * top_count)
    onehot = (flat_routes[:, None] == jnp.arange(experts, dtype=jnp.int32)[None, :]).astype(
        jnp.int32
    )
    earlier = jnp.cumsum(onehot, axis=0) - onehot
    slot_index = flat_routes * capacity + jnp.sum(earlier * onehot, axis=1)
    placed = jnp.arange(experts * capacity, dtype=jnp.int32)[:, None] == slot_index[None, :]
    dispatch = jnp.sum(
        placed.reshape(experts * capacity, seq_len, top_count).astype(f32), axis=2
    ).astype(bf16)
    gate_slot = jnp.sum(jnp.where(placed, gate_values.reshape(1, seq_len * top_count), 0.0), axis=1)

    def send_slots(slot_rows):
        return lax.all_to_all(slot_rows, "fsdp", split_axis=0, concat_axis=1, tiled=True)

    def return_slots(partials):
        return (
            lax.all_to_all(
                partials.astype(jnp.bfloat16), "fsdp", split_axis=1, concat_axis=0, tiled=True
            )
            .astype(partials.dtype)
            .reshape(experts * capacity, width)
        )

    expert_in = (
        jnp.dot(dispatch, moe_in, preferred_element_type=f32)
        .astype(bf16)
        .reshape(experts, capacity, width)
    )
    received = send_slots(expert_in)
    gate_act = jnp.einsum("ecd,edf->ecf", received, expert_gate, preferred_element_type=f32)
    up_act = jnp.einsum("ecd,edf->ecf", received, expert_up, preferred_element_type=f32)
    silu_gate, silu_slope = silu_parts(gate_act)
    expert_hidden = (silu_gate * up_act).astype(bf16)
    expert_out = jnp.einsum("ecf,efd->ecd", expert_hidden, expert_down, preferred_element_type=f32)
    returned = return_slots(expert_out)
    picked = jnp.take(returned, slot_index, axis=0).reshape(seq_len, top_count, width)
    routed = jnp.sum(gate_values[:, :, None] * picked, axis=1)
    gate_sh = jnp.dot(moe_in, gate_full, preferred_element_type=f32)
    up_sh = jnp.dot(moe_in, up_full, preferred_element_type=f32)
    silu_sh, slope_sh = silu_parts(gate_sh)
    shared_hidden = (silu_sh * up_sh).astype(bf16)
    moe_part = routed + jnp.dot(shared_hidden, down_full, preferred_element_type=f32)
    moe_out = lax.psum(moe_part.astype(jnp.bfloat16), "tp").astype(jnp.float32)
    activations = middle + moe_out
    mask_float = valid_mask.astype(f32)
    offset = activations - teacher.astype(f32)
    square_sum, valid_sum = lax.psum(
        (jnp.sum(mask_float[:, None] * offset * offset), jnp.sum(mask_float)), "fsdp"
    )
    valid_total = jnp.maximum(valid_sum, 1.0)
    loss_value = square_sum / (width * valid_total)
    grad_out = seq_len * fsdp_size / valid_total * mask_float[:, None] * offset
    grad_moe = grad_out.astype(bf16)
    down_shared_grad = jnp.einsum("tf,td->fd", shared_hidden, grad_moe, preferred_element_type=f32)
    grad_sh_hidden = jnp.einsum("td,fd->tf", grad_moe, down_full, preferred_element_type=f32)
    grad_gate_sh = (grad_sh_hidden * up_sh * slope_sh).astype(bf16)
    grad_up_sh = (grad_sh_hidden * silu_sh).astype(bf16)
    gate_shared_grad = jnp.einsum("td,tf->df", moe_in, grad_gate_sh, preferred_element_type=f32)
    up_shared_grad = jnp.einsum("td,tf->df", moe_in, grad_up_sh, preferred_element_type=f32)
    grad_moe_in = jnp.einsum("tf,df->td", grad_gate_sh, gate_full, preferred_element_type=f32)
    grad_moe_in = grad_moe_in + jnp.einsum(
        "tf,df->td", grad_up_sh, up_full, preferred_element_type=f32
    )
    grad_gates = jnp.sum(picked * grad_moe.astype(f32)[:, None, :], axis=-1)
    grad_slots = (
        (jnp.dot(dispatch, grad_moe, preferred_element_type=f32) * gate_slot[:, None])
        .astype(bf16)
        .reshape(experts, capacity, width)
    )
    grad_received = send_slots(grad_slots)
    expert_down_grad = jnp.einsum(
        "ecf,ecd->efd", expert_hidden, grad_received, preferred_element_type=f32
    )
    grad_expert_hidden = jnp.einsum(
        "ecd,efd->ecf", grad_received, expert_down, preferred_element_type=f32
    )
    grad_gate_act = (grad_expert_hidden * up_act * silu_slope).astype(bf16)
    grad_up_act = (grad_expert_hidden * silu_gate).astype(bf16)
    expert_gate_grad = jnp.einsum(
        "ecd,ecf->edf", received, grad_gate_act, preferred_element_type=f32
    )
    expert_up_grad = jnp.einsum("ecd,ecf->edf", received, grad_up_act, preferred_element_type=f32)
    grad_expert_in = jnp.einsum(
        "ecf,edf->ecd", grad_gate_act, expert_gate, preferred_element_type=f32
    )
    grad_expert_in = grad_expert_in + jnp.einsum(
        "ecf,edf->ecd", grad_up_act, expert_up, preferred_element_type=f32
    )
    grad_returned = return_slots(grad_expert_in)
    grad_moe_in = grad_moe_in + jnp.sum(
        jnp.take(grad_returned, slot_index, axis=0).reshape(seq_len, top_count, width), axis=1
    )
    grad_moe_in, grad_gates = (
        lax.psum(grad_moe_in.astype(jnp.bfloat16), "tp").astype(jnp.float32),
        lax.psum(grad_gates.astype(jnp.bfloat16), "tp").astype(jnp.float32),
    )
    grad_router_probs = jnp.sum(jnp.where(choose, grad_gates[:, :, None], 0.0), axis=1)
    grad_logits = router_probs * (
        grad_router_probs - jnp.sum(router_probs * grad_router_probs, axis=-1, keepdims=True)
    )
    router_grad = jnp.einsum(
        "td,te->de", moe_in.astype(f32), grad_logits, precision=HIGHEST, preferred_element_type=f32
    )
    grad_moe_in = grad_moe_in + jnp.einsum(
        "te,de->td",
        grad_logits,
        router_full.astype(f32),
        precision=HIGHEST,
        preferred_element_type=f32,
    )
    moe_gain_grad = jnp.sum(grad_moe_in * normal_mid, axis=0)
    grad_middle = grad_out + norm_back(grad_moe_in * moe_scale, normal_mid, inverse_mid)
    grad_attended = grad_middle.astype(bf16)
    output_grad = jnp.einsum("tf,td->fd", heads_out, grad_attended, preferred_element_type=f32)
    grad_heads = (
        jnp.einsum("td,fd->tf", grad_attended, output_full, preferred_element_type=f32)
        .astype(bf16)
        .reshape(seq_len, local_heads, VDIM)
    )
    attn_probs = jnp.exp(scores_of() - log_total)
    probs_again = attn_probs.astype(bf16)
    grad_probs = jnp.einsum("ihd,jhd->hij", grad_heads, values, preferred_element_type=f32)
    grad_values = jnp.einsum("hij,ihd->jhd", probs_again, grad_heads, preferred_element_type=f32)
    grad_scores = (
        attn_probs * (grad_probs - jnp.sum(attn_probs * grad_probs, axis=-1, keepdims=True))
    ).astype(bf16)
    grad_q_nope = (
        jnp.einsum("hij,jhd->ihd", grad_scores, key_nope, preferred_element_type=f32) * score_scale
    )
    grad_q_rope = (
        jnp.einsum("hij,jd->ihd", grad_scores, key_rope, preferred_element_type=f32) * score_scale
    )
    grad_keys = (
        jnp.einsum("hij,ihd->jhd", grad_scores, query_nope, preferred_element_type=f32)
        * score_scale
    )
    grad_key_rope = (
        jnp.einsum("hij,ihd->jd", grad_scores, query_rope, preferred_element_type=f32) * score_scale
    )
    grad_query = (
        jnp.concatenate(
            [grad_q_nope, unrotate(grad_q_rope, cosine[:, None, :], sine_part[:, None, :])], axis=-1
        )
        .astype(bf16)
        .reshape(seq_len, local_heads * (NOPE + ROPE))
    )
    query_grad = jnp.einsum("td,tq->dq", normed, grad_query, preferred_element_type=f32)
    grad_normed = jnp.einsum("tq,dq->td", grad_query, query_full, preferred_element_type=f32)
    grad_kv = (
        jnp.concatenate([grad_keys, grad_values], axis=-1)
        .astype(bf16)
        .reshape(seq_len, local_heads * (NOPE + VDIM))
    )
    expand_grad = jnp.einsum("tr,tq->rq", latent, grad_kv, preferred_element_type=f32)
    grad_latent = jnp.einsum("tq,rq->tr", grad_kv, expand_full, preferred_element_type=f32)
    grad_normed, grad_latent, grad_key_rope = (
        lax.psum(grad_normed.astype(jnp.bfloat16), "tp").astype(jnp.float32),
        lax.psum(grad_latent.astype(jnp.bfloat16), "tp").astype(jnp.float32),
        lax.psum(grad_key_rope.astype(jnp.bfloat16), "tp").astype(jnp.float32),
    )
    latent_gain_grad = jnp.sum(grad_latent * latent_unit, axis=0)
    grad_latent_raw = norm_back(grad_latent * latent_scale, latent_unit, inverse_lat)
    grad_latent_lin = jnp.concatenate(
        [grad_latent_raw, unrotate(grad_key_rope, cosine, sine_part)], axis=-1
    ).astype(bf16)
    latent_grad = jnp.einsum("td,tr->dr", normed, grad_latent_lin, preferred_element_type=f32)
    grad_normed = grad_normed + jnp.einsum(
        "tr,dr->td", grad_latent_lin, latent_full, preferred_element_type=f32
    )
    norm_gain_grad = jnp.sum(grad_normed * normal_in, axis=0)
    input_grad = grad_middle + norm_back(grad_normed * norm_scale, normal_in, inverse_in)
    (
        norm_out,
        query_out,
        latent_out,
        lgain_out,
        expand_out,
        output_out,
        mgain_out,
        router_out,
        gate_out,
        up_out,
        down_out,
    ) = (
        lax.psum_scatter(norm_gain_grad, "fsdp", scatter_dimension=0, tiled=True),
        lax.psum_scatter(query_grad, "fsdp", scatter_dimension=0, tiled=True),
        lax.psum_scatter(latent_grad, "fsdp", scatter_dimension=0, tiled=True),
        lax.psum_scatter(latent_gain_grad, "fsdp", scatter_dimension=0, tiled=True),
        lax.psum_scatter(expand_grad, "fsdp", scatter_dimension=0, tiled=True),
        lax.psum_scatter(output_grad, "fsdp", scatter_dimension=1, tiled=True),
        lax.psum_scatter(moe_gain_grad, "fsdp", scatter_dimension=0, tiled=True),
        lax.psum_scatter(router_grad, "fsdp", scatter_dimension=0, tiled=True),
        lax.psum_scatter(gate_shared_grad, "fsdp", scatter_dimension=0, tiled=True),
        lax.psum_scatter(up_shared_grad, "fsdp", scatter_dimension=0, tiled=True),
        lax.psum_scatter(down_shared_grad, "fsdp", scatter_dimension=1, tiled=True),
    )
    own_start = lax.axis_index("tp") * inputs.shape[0]
    own_activations = lax.dynamic_slice_in_dim(activations, own_start, inputs.shape[0], 0)
    own_input_grad = lax.dynamic_slice_in_dim(input_grad, own_start, inputs.shape[0], 0)
    return (
        loss_value,
        own_activations,
        own_input_grad,
        norm_out,
        query_out,
        latent_out,
        lgain_out,
        expand_out,
        output_out,
        mgain_out,
        router_out,
        gate_out,
        up_out,
        down_out,
        expert_gate_grad,
        expert_up_grad,
        expert_down_grad,
    )


def shards(*arrays):
    fsdp_size = lax.axis_size("fsdp")
    seq_len = arrays[4].shape[0]
    experts = arrays[12].shape[1]
    capacity = arrays[4].shape[1] * seq_len * 4 // (3 * experts)
    fits = fsdp_size * seq_len <= 2 * experts * capacity and fsdp_size == experts
    aligned = arrays[5].shape[0] == BLOCK and arrays[13].shape[1] % BLOCK == 0 and arrays[13].shape[1] <= fsdp_size * BLOCK
    if fits and aligned and fsdp_size % 4 == 0:
        return token_shards(*arrays)
    return slot_shards(*arrays)


def solution(mesh):
    return jax.shard_map(
        shards,
        mesh=mesh,
        in_specs=(
            P(("fsdp", "tp"), None),
            P("fsdp", None),
            P("fsdp"),
            P("fsdp"),
            P("fsdp", None),
            P("fsdp"),
            P("fsdp", "tp"),
            P("fsdp", None),
            P("fsdp"),
            P("fsdp", "tp"),
            P("tp", "fsdp"),
            P("fsdp"),
            P("fsdp", None),
            P("fsdp", "tp"),
            P("fsdp", "tp"),
            P("tp", "fsdp"),
            P("fsdp", None, "tp"),
            P("fsdp", None, "tp"),
            P("fsdp", "tp", None),
        ),
        out_specs=(
            P(),
            P(("fsdp", "tp"), None),
            P(("fsdp", "tp"), None),
            P("fsdp"),
            P("fsdp", "tp"),
            P("fsdp", None),
            P("fsdp"),
            P("fsdp", "tp"),
            P("tp", "fsdp"),
            P("fsdp"),
            P("fsdp", None),
            P("fsdp", "tp"),
            P("fsdp", "tp"),
            P("tp", "fsdp"),
            P("fsdp", None, "tp"),
            P("fsdp", None, "tp"),
            P("fsdp", "tp", None),
        ),
        check_vma=False,
    )
```

```python
import functools
import math

import jax
import jax.numpy as jnp
from jax import lax
from jax.experimental import pallas as pl
from jax.experimental.pallas import tpu as pltpu
from jax.sharding import PartitionSpec as P

HEADS = 16
NOPE = 128
ROPE = 64
RANK = 512
VDIM = 128


EPSILON = 1e-06
HIGHEST = lax.Precision.HIGHEST
MASKED = -1e30


def rope_tables(length, dim_size):
    places = jnp.arange(length).astype(jnp.float32)
    exponent = jnp.arange(dim_size // 2).astype(jnp.float32) * (2.0 / dim_size)
    angles = places[:, None] * jnp.exp(exponent * -math.log(10000.0))[None, :]
    return (jnp.cos(angles), jnp.sin(angles))


def rotate(values, cosine, sine_part):
    half_width = values.shape[-1] // 2
    lower_half = values[..., :half_width]
    upper_half = values[..., half_width:]
    return jnp.concatenate(
        [
            lower_half * cosine - upper_half * sine_part,
            upper_half * cosine + lower_half * sine_part,
        ],
        axis=-1,
    )


def unrotate(gradient, cosine, sine_part):
    half_width = gradient.shape[-1] // 2
    lower_half = gradient[..., :half_width]
    upper_half = gradient[..., half_width:]
    return jnp.concatenate(
        [
            lower_half * cosine + upper_half * sine_part,
            upper_half * cosine - lower_half * sine_part,
        ],
        axis=-1,
    )


def silu_parts(gate_act):
    sigmoid_val = jax.nn.sigmoid(gate_act)
    return (gate_act * sigmoid_val, sigmoid_val * (1.0 + gate_act * (1.0 - sigmoid_val)))


def norm_back(grad_scaled, unit_rows, inverse):
    return inverse * (
        grad_scaled - unit_rows * jnp.mean(grad_scaled * unit_rows, axis=-1, keepdims=True)
    )


def swap_tp(value):
    return lax.ppermute(value, "tp", [(0, 1), (1, 0)])


def half_rows(value, which, rows):
    return lax.dynamic_slice_in_dim(value, which * rows, rows, 0)


def tp_scatter(partial, which, rows):
    other = half_rows(partial, 1 - which, rows).astype(jnp.bfloat16)
    return half_rows(partial, which, rows) + swap_tp(other).astype(jnp.float32)


def tp_sum(partial):
    low_partial = partial.astype(jnp.bfloat16)
    return low_partial.astype(jnp.float32) + swap_tp(low_partial).astype(jnp.float32)


def tp_gather(own, which):
    other = swap_tp(own)
    first = jnp.where(which == 0, own, other)
    second = jnp.where(which == 0, other, own)
    return jnp.concatenate([first, second], axis=0)


MESH = pl.DeviceIdType.MESH
CROSS = ("x", "y", "up", "down")
BLOCK = 128


def both(first, second):
    if first is None:
        return second
    if second is None:
        return first
    return jnp.logical_and(first, second)


def under(condition, body):
    if condition is None:
        body()
    else:
        pl.when(condition)(body)


class Grid:
    def __init__(self, fsdp_size, dims, tie=-1):
        self.tie = tie
        index = lax.axis_index("fsdp")
        self.core = lax.rem(index, 2)
        self.y = lax.rem(lax.div(index, 2), 2)
        self.z = lax.div(index, 4)
        self.x = lax.axis_index("tp")
        self.depth = fsdp_size // 4
        self.dims = dims
        self.crosses = CROSS if "x" in dims else CROSS[1:]
        self.chips = self.depth * 2 * (2 if "x" in dims else 1)

    def device(self, x, y, z, core):
        return {"fsdp": z * 4 + y * 2 + core, "tp": x}

    def chip(self, x, y, z):
        return (z * 2 + y) * 2 + x if "x" in self.dims else z * 2 + y

    def here(self):
        return self.x, self.y, self.z

    def partner(self):
        return self.device(self.x, self.y, self.z, 1 - self.core)

    def neighbour(self, cross):
        if cross == "x":
            return (1 - self.x, self.y, self.z), None
        if cross == "y":
            return (self.x, 1 - self.y, self.z), None
        if cross == "up":
            return (self.x, self.y, self.z + 1), self.z + 1 < self.depth
        return (self.x, self.y, self.z - 1), self.z >= 1

    def level(self, rank):
        inner = jnp.logical_or(self.z == 1, self.z == 2)
        rank = jnp.where(jnp.logical_and(inner, rank >= 2), 5 - rank, rank)
        high, low = lax.div(self.z, 2), lax.rem(self.z, 2)
        far, near = lax.div(rank, 2), lax.rem(rank, 2)
        return 2 * (high + far - 2 * high * far) + (low + near - 2 * low * near)

    def entry(self, number):
        steps = (0, 1) if "x" in self.dims else (0,)
        found = [(r, dy, dx) for r in range(self.depth) for dy in (0, 1) for dx in steps]
        if "x" in self.dims:
            found.sort(key=lambda e: (sum(e), self.tie * e[0]))
        else:
            found.sort(key=lambda e: e[0] + 2.1 * e[1])
        codes = [4 * e[0] + 2 * e[1] + e[2] for e in found]
        code = jnp.int32(0) + (codes[number] if isinstance(number, int) else 0)
        if not isinstance(number, int):
            for at, value in enumerate(codes):
                code = jnp.where(number == at, value, code)
        dx, dy = lax.rem(code, 2), lax.rem(lax.div(code, 2), 2)
        x, y = self.x + dx - 2 * self.x * dx, self.y + dy - 2 * self.y * dy
        return x, y, self.level(lax.div(code, 4))

    def children(self, order, chip):
        zero = dict(x=chip[0] == self.x, y=chip[1] == self.y, z=chip[2] == self.z)
        found, rest = [], None
        for dim in reversed(order):
            if dim == "z":
                found.append(("up", both(rest, (chip[2] <= self.z) & (self.z + 1 < self.depth))))
                found.append(("down", both(rest, (chip[2] >= self.z) & (self.z >= 1))))
            else:
                found.append((dim, both(rest, zero[dim])))
            rest = both(rest, zero[dim])
        return found

    def parent(self, order, chip):
        zero = dict(x=chip[0] == self.x, y=chip[1] == self.y, z=chip[2] == self.z)
        rest, turned = None, {}
        for dim in reversed(order):
            turned[dim] = both(rest, jnp.logical_not(zero[dim]))
            rest = both(rest, zero[dim])
        x = jnp.where(turned["x"], 1 - self.x, self.x) if "x" in order else self.x
        y = jnp.where(turned["y"], 1 - self.y, self.y)
        above = chip[2] > self.z
        z = jnp.where(turned["z"], jnp.where(above, self.z + 1, self.z - 1), self.z)
        side = jnp.where(above, self.crosses.index("down"), self.crosses.index("up"))
        side = jnp.where(turned["y"], self.crosses.index("y"), side)
        if "x" in order:
            side = jnp.where(turned["x"], self.crosses.index("x"), side)
        return (x, y, z), side

    def greet(self):
        barrier = pltpu.get_barrier_semaphore()
        pl.semaphore_signal(barrier, inc=1, device_id=self.partner(), device_id_type=MESH)
        count = 1
        for cross in self.crosses:
            chip, exists = self.neighbour(cross)

            def send(chip=chip):
                there = self.device(*chip, self.core)
                pl.semaphore_signal(barrier, inc=1, device_id=there, device_id_type=MESH)

            under(exists, send)
            count = count + (1 if exists is None else jnp.where(exists, 1, 0))
        pl.semaphore_wait(barrier, count)

    def greet_plane(self):
        barrier = pltpu.get_barrier_semaphore()
        size = self.depth * 4
        me = lax.axis_index("fsdp")

        def send(step, carry):
            there = {"fsdp": lax.rem(me + step, size), "tp": self.x}
            pl.semaphore_signal(barrier, inc=1, device_id=there, device_id_type=MESH)
            return carry

        lax.fori_loop(1, size, send, 0)
        across = {"fsdp": me, "tp": 1 - self.x}
        pl.semaphore_signal(barrier, inc=1, device_id=across, device_id_type=MESH)
        pl.semaphore_wait(barrier, size)


def owner_of(block, chips):
    extra = 2 * lax.rem(3 * (block - chips) + 1 + 3 * chips, chips) + 1
    return jnp.where(block < chips, 2 * block, extra)


def block_of(device, chips):
    back = pow(3, -1, chips)
    chip, core = lax.div(device, 2), lax.rem(device, 2)
    return jnp.where(core == 0, chip, chips + lax.rem(back * (chip - 1 + chips), chips))


class Exchange:
    def __init__(self, fsdp_size, tp, blocks, sources, targets, cut, to_owner, send_sem, recv_sem, own_sem):
        self.size, self.tp, self.blocks = fsdp_size, tp, blocks
        self.sources, self.targets, self.cut, self.to_owner = sources, targets, cut, to_owner
        self.send_sem, self.recv_sem, self.own_sem = send_sem, recv_sem, own_sem
        self.me = lax.axis_index("fsdp")
        self.block = block_of(self.me, fsdp_size // 2)
        self.owns = self.block < blocks

    def remote(self, array, block, other, there, send, recv):
        source, target = self.cut[array](self.sources[array], self.targets[array], block, other)
        return pltpu.make_async_remote_copy(
            src_ref=source,
            dst_ref=target,
            send_sem=self.send_sem.at[array, send],
            recv_sem=self.recv_sem.at[array, recv],
            device_id={"fsdp": there, "tp": self.tp},
            device_id_type=MESH,
        )

    def local(self, array, block):
        source, target = self.cut[array](self.sources[array], self.targets[array], block, self.me)
        return pltpu.make_async_copy(source, target, self.own_sem.at[array])

    def by_block(self, act, act_local, low, high):
        def one(number, carry):
            block = lax.rem(number + lax.div(self.me * self.blocks, self.size), self.blocks)
            owner = owner_of(block, self.size // 2)
            for array in range(len(self.sources)):
                if self.to_owner:
                    copy = self.remote(array, block, self.me, owner, block, self.me)
                else:
                    copy = self.remote(array, block, self.me, owner, 0, block)
                pl.when(self.me != owner)(getattr(copy, act))
                if act_local:
                    pl.when(self.me == owner)(getattr(self.local(array, block), act_local))
            return carry

        lax.fori_loop(low, high, one, 0)

    def by_device(self, act, act_local, low, high):
        def one(number, carry):
            other = lax.rem(self.me + number, self.size)
            for array in range(len(self.sources)):
                if self.to_owner:
                    copy = self.remote(array, self.block, other, other, 0, other)
                else:
                    copy = self.remote(array, self.block, other, other, other, self.block)
                pl.when(self.me != other)(getattr(copy, act))
                if act_local:
                    pl.when(self.me == other)(getattr(self.local(array, self.block), act_local))
            return carry

        def every():
            lax.fori_loop(low, high, one, 0)

        pl.when(self.owns)(every)

    def start(self, step, steps):
        total = self.blocks if self.to_owner else self.size
        low, high = lax.div(step * total, steps), lax.div((step + 1) * total, steps)
        (self.by_block if self.to_owner else self.by_device)("start", "start", low, high)

    def finish(self):
        if self.to_owner:
            self.by_device("wait_recv", None, 0, self.size)
            self.by_block("wait_send", "wait", 0, self.blocks)
        else:
            self.by_block("wait_recv", None, 0, self.blocks)
            self.by_device("wait_send", "wait", 0, self.size)


def exchange_sems(fsdp_size, arrays):
    dma = pltpu.SemaphoreType.DMA
    return [dma((arrays, fsdp_size)), dma((arrays, fsdp_size)), dma((arrays,))] if arrays else []


def gather_kernel(fsdp_size, pieces, places, count, blocks, cut, *refs):
    moved = len(cut)
    shards, sources = refs[:count], refs[count : count + moved]
    refs = refs[count + moved :]
    outs, targets = refs[:count], refs[count : count + moved]
    send_sem, recv_sem, pair_send, pair_recv, own_sem, cross_sem = refs[
        count + moved : count + moved + 6
    ]
    grid = Grid(fsdp_size, "zy")
    halved = [piece[1] for piece in pieces].index(None)
    exchange = Exchange(
        fsdp_size, grid.x, blocks, sources, targets, cut, True, *refs[count + moved + 6 :]
    )

    def first_row(piece, plane):
        first, rows = pieces[piece][1], pieces[piece][2]
        return pl.multiple_of(plane * rows, 16) if first is None else first

    def target(piece, chip, core):
        array, _, rows, _ = pieces[piece]
        return places[array](outs[array], chip, core, first_row(piece, chip[0]), rows)

    def source(piece, chip, own):
        array, _, rows, _ = pieces[piece]
        if own:
            return shards[array].at[pl.ds(first_row(piece, grid.x), rows)]
        return target(piece, chip, grid.core)

    def across(chip, own=False):
        index = grid.chip(*chip)
        return pltpu.make_async_remote_copy(
            src_ref=source(halved, chip, own),
            dst_ref=target(halved, chip, grid.core),
            send_sem=cross_sem.at[0, index],
            recv_sem=cross_sem.at[1, index],
            device_id=grid.device(1 - grid.x, grid.y, grid.z, grid.core),
            device_id_type=MESH,
        )

    def across_pair(chip, core):
        index, far = grid.chip(*chip), (1 - grid.x, chip[1], chip[2])
        return pltpu.make_async_remote_copy(
            src_ref=target(halved, far, grid.core),
            dst_ref=target(halved, far, core),
            send_sem=cross_sem.at[2, index],
            recv_sem=cross_sem.at[3, index],
            device_id=grid.partner(),
            device_id_type=MESH,
        )

    def crossed(chip):
        across((1 - grid.x, chip[1], chip[2])).wait_recv()
        across_pair(chip, grid.core).start()

    def hops(piece, chip, own):
        index, found = grid.chip(*chip), []
        for cross, wanted in grid.children(pieces[piece][3], chip):
            there, _ = grid.neighbour(cross)
            copy = pltpu.make_async_remote_copy(
                src_ref=source(piece, chip, own),
                dst_ref=target(piece, chip, grid.core),
                send_sem=send_sem.at[piece, index, grid.crosses.index(cross)],
                recv_sem=recv_sem.at[piece, index],
                device_id=grid.device(*there, grid.core),
                device_id_type=MESH,
            )
            found.append((wanted, copy))
        return found

    def pair(piece, chip, core, own=False, landing=False):
        index = grid.chip(*chip)
        return pltpu.make_async_remote_copy(
            src_ref=source(piece, chip, own),
            dst_ref=target(piece, chip, core),
            send_sem=pair_send.at[piece, index],
            recv_sem=(recv_sem if landing else pair_recv).at[piece, index],
            device_id=grid.partner(),
            device_id_type=MESH,
        )

    own_copies = [
        pltpu.make_async_copy(
            source(piece, grid.here(), True), target(piece, grid.here(), grid.core), own_sem.at[piece]
        )
        for piece in range(len(pieces))
    ]
    grid.greet_plane()

    def relay(chip, own):
        for piece in range(len(pieces)):
            if not own:
                pair(piece, chip, grid.core, landing=True).wait_recv()
            for wanted, copy in hops(piece, chip, own):
                under(wanted, copy.start)
            pair(piece, chip, grid.core, own).start()
            if piece == halved:
                across(chip, own).start()

    relay(grid.here(), True)
    for copy in own_copies:
        copy.start()

    def step(number, carry):
        relay(grid.entry(number), False)
        crossed(grid.entry(number - 1))
        exchange.start(number - 1, grid.chips - 1)
        return carry

    lax.fori_loop(1, grid.chips, step, 0)
    crossed(grid.entry(grid.chips - 1))

    def finish(number, carry):
        chip = grid.entry(number)
        for piece in range(len(pieces)):
            for wanted, copy in hops(piece, chip, False):
                under(wanted, copy.wait_send)
            pair(piece, chip, grid.core).wait_send()
            pair(piece, chip, 1 - grid.core).wait_recv()
        across(chip).wait_send()
        across_pair(chip, grid.core).wait_send()
        across_pair(chip, 1 - grid.core).wait_recv()
        return carry

    lax.fori_loop(0, grid.chips, finish, 0)
    for copy in own_copies:
        copy.wait()
    exchange.finish()


def gather_call(fsdp_size, pieces, places, shards, shapes, collective_id, blocks, cut, sources, targets):
    count, chips = len(shards), fsdp_size // 2
    dma = pltpu.SemaphoreType.DMA
    moved = sum(s.size * s.dtype.itemsize for s in shapes)
    return pl.pallas_call(
        functools.partial(gather_kernel, fsdp_size, pieces, places, count, blocks, cut),
        out_shape=tuple(shapes) + tuple(targets),
        in_specs=[pl.BlockSpec(memory_space=pltpu.VMEM)] * count
        + [pl.BlockSpec(memory_space=pl.ANY)] * len(sources),
        out_specs=tuple([pl.BlockSpec(memory_space=pl.ANY)] * (count + len(targets))),
        scratch_shapes=[
            dma((len(pieces), chips, 4)),
            dma((len(pieces), chips)),
            dma((len(pieces), chips)),
            dma((len(pieces), chips)),
            dma((len(pieces),)),
            dma((4, chips)),
            *exchange_sems(fsdp_size, len(sources)),
        ],
        compiler_params=pltpu.CompilerParams(collective_id=collective_id, has_side_effects=True),
        cost_estimate=pl.CostEstimate(flops=0, bytes_accessed=8 * moved, transcendentals=0),
    )(*shards, *sources)


class WeightGrads:
    inputs, outputs = 5, 3
    PIECES = (1, 3, 5)

    def __init__(self, slots, hidden, width):
        bf16 = jnp.bfloat16
        dma = pltpu.SemaphoreType.DMA
        self.hidden = hidden
        self.shapes = [jax.ShapeDtypeStruct((hidden, width), bf16)] * self.outputs
        self.scratch = [
            pltpu.VMEM((2, slots, BLOCK), bf16),
            pltpu.VMEM((slots, width), bf16),
            pltpu.VMEM((2, BLOCK, width), bf16),
            dma((2,)),
            dma((1,)),
            dma((2,)),
        ]

    def make(self, *refs):
        return WeightGradsRun(self, refs)


class WeightGradsRun:
    def __init__(self, job, refs):
        self.lefts, self.rights, self.outs = refs[:3], refs[3:5], refs[5:8]
        self.left, self.right, self.result = refs[8:11]
        self.left_sem, self.right_sem, self.out_sem = refs[11:]
        self.blocks = -(-job.hidden // BLOCK)
        self.rest = job.hidden - (self.blocks - 1) * BLOCK
        self.total = 3 * self.blocks

    def left_copy(self, which, number):
        slot, block = lax.rem(number, 2), lax.rem(number, self.blocks)
        span = pl.ds(pl.multiple_of(block * BLOCK, BLOCK), BLOCK)
        return pltpu.make_async_copy(
            self.lefts[which].at[:, span], self.left.at[slot], self.left_sem.at[slot]
        )

    def left_start(self, number):
        for which in range(3):
            pl.when(lax.div(number, self.blocks) == which)(self.left_copy(which, number).start)

    def right_copy(self, which):
        return pltpu.make_async_copy(self.rights[which], self.right, self.right_sem.at[0])

    def out_copies(self, which, number):
        slot, block = lax.rem(number, 2), lax.rem(number, self.blocks)
        full = pl.ds(pl.multiple_of(block * BLOCK, BLOCK), BLOCK)
        part = pl.ds((self.blocks - 1) * BLOCK, self.rest)
        out, sem = self.outs[which], self.out_sem.at[slot]
        return [
            (
                block < self.blocks - 1,
                pltpu.make_async_copy(self.result.at[slot], out.at[full], sem),
            ),
            (
                block == self.blocks - 1,
                pltpu.make_async_copy(self.result.at[slot, pl.ds(0, self.rest)], out.at[part], sem),
            ),
        ]

    def begin(self):
        self.right_copy(0).start()
        self.left_copy(0, jnp.int32(0)).start()

    def out_wait(self, number):
        for wanted, copy in self.out_copies(0, number):
            pl.when(wanted)(copy.wait)

    def run(self, number):
        slot = lax.rem(number, 2)
        self.left_copy(0, number).wait()
        pl.when(number + 1 < self.total)(lambda: self.left_start(number + 1))
        pl.when(lax.rem(number, 2 * self.blocks) == 0)(self.right_copy(0).wait)
        pl.when(number >= 2)(lambda: self.out_wait(number - 2))
        self.result[slot] = lax.dot_general(
            self.left[slot],
            self.right[...],
            (((0,), (0,)), ((), ())),
            preferred_element_type=jnp.float32,
        ).astype(jnp.bfloat16)
        for which in range(3):
            for wanted, copy in self.out_copies(which, number):
                pl.when(wanted & (lax.div(number, self.blocks) == which))(copy.start)
        pl.when(number == 2 * self.blocks - 1)(self.right_copy(1).start)

    def tick(self, step, piece):
        if piece in WeightGrads.PIECES:
            number = (step - 1) * len(WeightGrads.PIECES) + WeightGrads.PIECES.index(piece)
            pl.when((number >= 0) & (number < self.total))(lambda: self.run(number))

    def finish(self, steps):
        for number in range(len(WeightGrads.PIECES) * (steps - 1), self.total):
            self.run(jnp.int32(0) + number)
        for number in (self.total - 2, self.total - 1):
            self.out_wait(jnp.int32(0) + number)


def reduce_kernel(fsdp_size, dims, pieces, places, count, blocks, cut, side, halved, *refs):
    moved, taken = len(cut), side.inputs if side else 0
    partials, sources = refs[:count], refs[count : count + moved]
    side_refs = refs[count + moved : count + moved + taken]
    refs = refs[count + moved + taken :]
    outs, targets = refs[:count], refs[count : count + moved]
    refs = refs[count + moved :]
    if side:
        side_refs, refs = side_refs + refs[: side.outputs], refs[side.outputs :]
    held, other, landed = (refs[i * count : (1 + i) * count] for i in range(3))
    send_sem, recv_sem, load_sem, pair_send, pair_recv = refs[3 * count : 3 * count + 5]
    refs = refs[3 * count + 5 :]
    grid = Grid(fsdp_size, dims)
    ways = len(grid.crosses)
    empty = grid.chips * ways
    exchange, job = None, None
    if moved:
        exchange = Exchange(fsdp_size, grid.x, blocks, sources, targets, cut, False, *refs[:3])
        refs = refs[3:]
    if halved is not None:
        half, half_sem = refs[:2]
        refs = refs[2:]
    if side:
        job = side.make(*side_refs, *refs)

    def load(array, chip):
        index = grid.chip(*chip)
        return pltpu.make_async_copy(
            places[array](partials[array], chip, grid.core),
            held[array].at[index],
            load_sem.at[array, index],
        )

    def pair(array, chip):
        index = grid.chip(*chip)
        return pltpu.make_async_remote_copy(
            src_ref=places[array](partials[array], chip, 1 - grid.core),
            dst_ref=other[array].at[index],
            send_sem=pair_send.at[array, index],
            recv_sem=pair_recv.at[array, index],
            device_id=grid.partner(),
            device_id_type=MESH,
        )

    def hop(piece, chip, there, side_seen):
        array, first, rows, _ = pieces[piece]
        index = grid.chip(*chip)
        slot = index * ways + side_seen
        return pltpu.make_async_remote_copy(
            src_ref=held[array].at[index, pl.ds(first, rows)],
            dst_ref=landed[array].at[slot, pl.ds(first, rows)],
            send_sem=send_sem.at[piece, index],
            recv_sem=recv_sem.at[piece, slot],
            device_id=grid.device(*there, grid.core),
            device_id_type=MESH,
        )

    def add_up(piece, chip, root):
        array, first, rows, order = pieces[piece]
        index, slots, some = grid.chip(*chip), [], grid.z < 0
        for cross, wanted in grid.children(order, chip):
            way = grid.crosses.index(cross)
            under(wanted, hop(piece, chip, grid.here(), way).wait_recv)
            slot = index * ways + way
            slots.append(slot if wanted is None else jnp.where(wanted, slot, empty))
            some = None if wanted is None or some is None else jnp.logical_or(some, wanted)
        tile = 16 if rows % 16 == 0 else rows

        def add_all(used):
            def add(i, carry):
                span = pl.ds(pl.multiple_of(first + i * tile, tile), tile)
                total = held[array][index, span].astype(jnp.float32)
                total += other[array][index, span].astype(jnp.float32)
                for slot in used:
                    total += landed[array][slot, span].astype(jnp.float32)
                if root and array == halved:
                    start = grid.x * half.shape[0] + first + i * tile
                    outs[array][pl.ds(pl.multiple_of(start, tile), tile)] = total
                elif root:
                    outs[array][span] = total
                else:
                    held[array][index, span] = total.astype(held[array].dtype)
                return carry

            lax.fori_loop(0, rows // tile, add, 0)

        if root or some is None:
            add_all(slots)
        else:
            pl.when(some)(lambda: add_all(slots))
            pl.when(jnp.logical_not(some))(lambda: add_all([]))

    def swap_half():
        rows = half.shape[0]
        span = pl.ds(pl.multiple_of(grid.x * rows, 16), rows)
        return pltpu.make_async_remote_copy(
            src_ref=outs[halved].at[span],
            dst_ref=half,
            send_sem=half_sem.at[0],
            recv_sem=half_sem.at[1],
            device_id=grid.device(1 - grid.x, grid.y, grid.z, grid.core),
            device_id_type=MESH,
        )

    def fetched(array, chip):
        load(array, chip).wait()
        pair(array, chip).wait_recv()

    firsts = [min(p for p, piece in enumerate(pieces) if piece[0] == a) for a in range(count)]
    for array in range(count):
        landed[array][empty] = jnp.zeros(landed[array].shape[1:], landed[array].dtype)
    if moved:
        grid.greet_plane()
    else:
        grid.greet()
    last = grid.chips - 1

    def begin(number, carry):
        chip = grid.entry(last - number)
        for array in range(count):
            load(array, chip).start()
            pair(array, chip).start()
        return carry

    lax.fori_loop(0, grid.chips, begin, 0)
    if job:
        job.begin()

    def step(number, carry):
        chip = grid.entry(last - number)
        for piece in range(len(pieces)):
            if piece in firsts:
                fetched(pieces[piece][0], chip)
            add_up(piece, chip, False)
            hop(piece, chip, *grid.parent(pieces[piece][3], chip)).start()
            if job:
                job.tick(number, piece)
        if exchange:
            exchange.start(number, last)
        return carry

    lax.fori_loop(0, last, step, 0)
    if job:
        job.finish(last)
    for piece in range(len(pieces)):
        if piece in firsts:
            fetched(pieces[piece][0], grid.here())
        add_up(piece, grid.here(), True)
        if pieces[piece][0] == halved:
            swap = swap_half()
            swap.start()

    def finish(number, carry):
        chip = grid.entry(last - number)
        for array in range(count):
            pair(array, chip).wait_send()

        def sent():
            for piece in range(len(pieces)):
                hop(piece, chip, *grid.parent(pieces[piece][3], chip)).wait_send()

        pl.when(number < last)(sent)
        return carry

    lax.fori_loop(0, grid.chips, finish, 0)
    if halved is not None:
        swap.wait()
        start = (1 - grid.x) * half.shape[0]
        outs[halved][pl.ds(pl.multiple_of(start, 16), half.shape[0])] = half[...]
    if exchange:
        exchange.finish()


def reduce_call(
    fsdp_size,
    dims,
    pieces,
    places,
    partials,
    shapes,
    collective_id,
    blocks=0,
    cut=(),
    sources=(),
    targets=(),
    side=None,
    extra=(),
    halved=None,
):
    count = len(partials)
    ways = 4 if "x" in dims else 3
    chips = fsdp_size // 2 * (2 if "x" in dims else 1)
    dma = pltpu.SemaphoreType.DMA
    held = [pltpu.VMEM((chips, *s), p.dtype) for s, p in zip(shapes, partials)]
    landed = [pltpu.VMEM((chips * ways + 1, *s), p.dtype) for s, p in zip(shapes, partials)]
    moved = sum(p.size * p.dtype.itemsize for p in partials)
    sums = [(2 * s[0], s[1]) if at == halved else s for at, s in enumerate(shapes)]
    swapped = []
    if halved is not None:
        swapped = [pltpu.VMEM(shapes[halved], jnp.float32), dma((2,))]
    side_outs = tuple(side.shapes) if side else ()
    return pl.pallas_call(
        functools.partial(
            reduce_kernel, fsdp_size, dims, pieces, places, count, blocks, cut, side, halved
        ),
        out_shape=tuple(jax.ShapeDtypeStruct(s, jnp.float32) for s in sums)
        + tuple(targets)
        + side_outs,
        in_specs=[pl.BlockSpec(memory_space=pl.ANY)] * (count + len(sources) + len(extra)),
        out_specs=tuple(
            [pl.BlockSpec(memory_space=pltpu.VMEM)] * count
            + [pl.BlockSpec(memory_space=pl.ANY)] * (len(targets) + len(side_outs))
        ),
        scratch_shapes=[
            *held,
            *held,
            *landed,
            dma((len(pieces), chips)),
            dma((len(pieces), chips * ways)),
            dma((count, chips)),
            dma((count, chips)),
            dma((count, chips)),
            *exchange_sems(fsdp_size, len(sources)),
            *swapped,
            *(side.scratch if side else ()),
        ],
        compiler_params=pltpu.CompilerParams(
            collective_id=collective_id, has_side_effects=True, vmem_limit_bytes=67043328
        ),
        cost_estimate=pl.CostEstimate(flops=0, bytes_accessed=16 * moved, transcendentals=0),
    )(*partials, *sources, *extra)


def token_row(chip, core, rows):
    x, y, z = chip
    return ((z * 4 + y * 2 + core) * 2 + x) * rows


def reduce_tokens(partials, collective_id):
    fsdp_size = lax.axis_size("fsdp")
    rows = partials[0].shape[0] // (2 * fsdp_size)
    unit = rows // 4

    def place(ref, chip, core):
        return ref.at[pl.ds(pl.multiple_of(token_row(chip, core, rows), 16), rows)]

    pieces = [(0, at * unit, unit, order) for at, order in enumerate(("xyz", "zyx", "zxy", "zyx"))]
    pieces += [(array, 0, rows, "zyx") for array in range(1, len(partials))]
    shapes = [(rows, p.shape[1]) for p in partials]
    return reduce_call(
        fsdp_size, "xyz", pieces, [place] * len(partials), partials, shapes, collective_id
    )


def plane_row(chip, core):
    return chip[2] * 4 + chip[1] * 2 + core


def row_place(rows):
    def place(ref, chip, core, first=0, count=rows):
        return ref.at[pl.ds(pl.multiple_of(plane_row(chip, core) * rows + first, 8), count)]

    return place


def column_place(columns, rows):
    def place(ref, chip, core, first=0, count=rows):
        start = pl.multiple_of(plane_row(chip, core) * columns, 128)
        return ref.at[pl.ds(first, count), pl.ds(start, columns)]

    return place


def weight_pieces(query, latent, expand, output, small):
    return [
        (4, 0, small, "zy"),
        (0, 0, query // 2, "zy"),
        (1, 0, latent, "zy"),
        (0, query // 2, query // 2, "zy"),
        (2, 0, expand, "yz"),
        (3, 0, output // 2, "zy"),
        (3, output // 2, output // 2, "zy"),
    ]


def block_span(block):
    return pl.ds(pl.multiple_of(block * BLOCK, BLOCK), BLOCK)


def cut_columns(rows):
    def to_owner(source, target, block, other):
        there = pl.ds(pl.multiple_of(other * rows, rows), rows)
        return source.at[:, block_span(block)], target.at[there]

    def from_owner(source, target, block, other):
        there = pl.ds(pl.multiple_of(other * rows, rows), rows)
        return source.at[there], target.at[:, block_span(block)]

    return to_owner, from_owner


def cut_rows(columns):
    def to_owner(source, target, block, other):
        there = pl.ds(pl.multiple_of(other * columns, columns), columns)
        return source.at[block_span(block)], target.at[:, there]

    def from_owner(source, target, block, other):
        there = pl.ds(pl.multiple_of(other * columns, columns), columns)
        return source.at[:, there], target.at[block_span(block)]

    return to_owner, from_owner


def gather_weights(query, latent, expand, output, small, gate, up, down, collective_id):
    size = lax.axis_size("fsdp")
    shards = [query, latent, expand, output, small]
    places = [row_place(s.shape[0]) for s in shards]
    shapes = [
        jax.ShapeDtypeStruct((s.shape[0] * size, s.shape[1]), s.dtype) for s in shards
    ]
    for at in (1, 3):
        rows, columns = shards[at].shape
        places[at] = column_place(columns, rows)
        shapes[at] = jax.ShapeDtypeStruct((rows, columns * size), shards[at].dtype)
    columns, rows = cut_columns(gate.shape[0]), cut_rows(down.shape[1])
    tall = jax.ShapeDtypeStruct((gate.shape[0] * size, BLOCK), gate.dtype)
    flat = jax.ShapeDtypeStruct((BLOCK, down.shape[1] * size), down.dtype)
    return gather_call(
        size,
        [
            (1, None, latent.shape[0] // 2, "zy") if piece[0] == 1 else piece
            for piece in weight_pieces(*[s.shape[0] for s in shards])
        ],
        places,
        shards,
        shapes,
        collective_id,
        gate.shape[1] // BLOCK,
        (columns[0], columns[0], rows[0]),
        [gate, up, down],
        [tall, tall, flat],
    )


def grad_pieces(query, latent, expand, output, small):
    pieces = weight_pieces(query, latent, expand, output, small)
    at = pieces.index((2, 0, expand, "yz"))
    halves = [(2, 0, expand // 2, "yz"), (2, expand // 2, expand // 2, "zy")]
    return pieces[:at] + halves + pieces[at + 1 :]


def reduce_weights(
    query, latent, expand, output, small, gate, up, down, blocks, collective_id, side, extra
):
    size = lax.axis_size("fsdp")
    partials = [query, latent, expand, output, small]
    shapes = [(p.shape[0] // size, p.shape[1]) for p in partials]
    places = [row_place(s[0]) for s in shapes]
    for at in (1, 3):
        rows, columns = partials[at].shape
        shapes[at] = (rows, columns // size)
        places[at] = column_place(columns // size, rows)
    half = partials[1].shape[0] // 2
    shapes[1] = (half, shapes[1][1])

    def half_place(ref, chip, core):
        start = pl.multiple_of(plane_row(chip, core) * shapes[1][1], 128)
        first = pl.multiple_of(chip[0] * half, 16)
        return ref.at[pl.ds(first, half), pl.ds(start, shapes[1][1])]

    places[1] = half_place
    columns, rows = cut_columns(gate.shape[0] // size), cut_rows(down.shape[1] // size)
    wide = jax.ShapeDtypeStruct((gate.shape[0] // size, blocks * BLOCK), gate.dtype)
    long = jax.ShapeDtypeStruct((blocks * BLOCK, down.shape[1] // size), down.dtype)
    return reduce_call(
        size,
        "zy",
        grad_pieces(*[s[0] for s in shapes]),
        places,
        partials,
        shapes,
        collective_id,
        blocks,
        (columns[1], columns[1], rows[1]),
        [gate, up, down],
        [wide, wide, long],
        side,
        extra,
        1,
    )


class Spread:
    ORDERS = ("xyz", "zyx", "zxy", "zyx")

    def __init__(self, fsdp_size, own, room, lead, sems):
        self.lead = lead
        self.grid = Grid(fsdp_size, "xyz", 1)
        self.own, self.room = own, room
        self.rows = own.shape[0]
        self.part = self.rows // len(self.ORDERS)
        self.send_sem, self.recv_sem, self.pair_send, self.pair_recv = sems
        self.units = fsdp_size // 2

    def unit(self, step):
        grid = self.grid
        flip = lax.rem(step, 2)
        return grid.y + flip - 2 * grid.y * flip, grid.level(lax.div(step, 2))

    def span(self, chip, piece):
        start = token_row(chip, self.grid.core, self.rows) + piece * self.part
        return self.room.at[pl.ds(pl.multiple_of(start, self.part), self.part)]

    def copies(self, chip, piece, own=False):
        grid, found = self.grid, []
        index, here = grid.chip(*chip), self.span(chip, piece)
        source = self.own.at[pl.ds(piece * self.part, self.part)] if own else here
        for cross, wanted in grid.children(self.ORDERS[piece], chip):
            there, _ = grid.neighbour(cross)
            copy = pltpu.make_async_remote_copy(
                src_ref=source,
                dst_ref=here,
                send_sem=self.send_sem.at[piece, index, grid.crosses.index(cross)],
                recv_sem=self.recv_sem.at[piece, index],
                device_id=grid.device(*there, grid.core),
                device_id_type=MESH,
            )
            found.append((wanted, copy))
        return found

    def pair(self, chip, piece, own=False, landing=False):
        grid = self.grid
        index, here = grid.chip(*chip), self.span(chip, piece)
        return pltpu.make_async_remote_copy(
            src_ref=self.own.at[pl.ds(piece * self.part, self.part)] if own else here,
            dst_ref=here,
            send_sem=self.pair_send.at[piece, index],
            recv_sem=(self.recv_sem if landing else self.pair_recv).at[piece, index],
            device_id=grid.partner(),
            device_id_type=MESH,
        )

    def relay(self, chip, piece, own=False):
        if not own:
            self.pair(chip, piece, landing=True).wait_recv()
        for wanted, copy in self.copies(chip, piece, own):
            under(wanted, copy.start)
        self.pair(chip, piece, own).start()

    def begin(self):
        grid = self.grid
        grid.greet()
        for piece in range(len(self.ORDERS)):
            self.relay(grid.here(), piece, own=True)
        start = token_row(grid.here(), grid.core, self.rows)
        self.room[pl.ds(pl.multiple_of(start, self.rows), self.rows)] = self.own[...]

        def early(number, carry):
            chip = grid.entry(number)
            for piece in range(len(self.ORDERS)):
                self.relay(chip, piece)
            return carry

        lax.fori_loop(1, self.lead, early, 0)

    def ahead(self, step):
        return [self.grid.entry(self.lead + 2 * step + one) for one in (0, 1)]

    def tick(self, step, chips, number):
        pieces = len(self.ORDERS)
        late = self.lead + 2 * step + number // pieces
        chip = chips[number // pieces]
        pl.when(late < 2 * self.units)(lambda: self.relay(chip, number % pieces))

    def arrived(self, step):
        y, z = self.unit(step)
        for x in (0, 1):
            for piece in range(len(self.ORDERS)):
                self.pair((x, y, z), piece).wait_recv()

    def drain(self):
        def finish(number, carry):
            chip = self.grid.entry(number)
            for piece in range(len(self.ORDERS)):
                for wanted, copy in self.copies(chip, piece):
                    under(wanted, copy.wait_send)
                self.pair(chip, piece).wait_send()
            return carry

        lax.fori_loop(0, 2 * self.units, finish, 0)


def spread_sems(fsdp_size):
    dma = pltpu.SemaphoreType.DMA
    return [dma((4, fsdp_size, 4)), dma((4, fsdp_size)), dma((4, fsdp_size)), dma((4, fsdp_size))]


class Stage:
    def __init__(self, buffers, results, sems):
        self.buffers, self.results, self.sems = buffers, results, sems

    def copy(self, number, step, unit):
        buffer = self.buffers[number]
        rows = buffer.shape[1]
        slot = lax.rem(step, 2)
        there = self.results[number].at[pl.ds(pl.multiple_of(unit * rows, rows), rows)]
        return pltpu.make_async_copy(buffer.at[slot], there, self.sems.at[number, slot])

    def reuse(self, step):
        def wait():
            for number in range(len(self.buffers)):
                self.copy(number, step, 0).wait()

        pl.when(step >= 2)(wait)

    def put(self, number, step, unit):
        self.copy(number, step, unit).start()

    def finish(self, steps):
        for step in (steps - 2, steps - 1):
            for number in range(len(self.buffers)):
                self.copy(number, step, 0).wait()


def dot(left, right):
    return jnp.dot(left, right, preferred_element_type=jnp.float32)


def dot_nt(left, right):
    return lax.dot_general(
        left, right, (((1,), (1,)), ((), ())), preferred_element_type=jnp.float32
    )


def dispatch_of(place_ref, sequence, capacity, seq_len):
    row = place_ref[pl.ds(sequence, 1), :]
    slot = lax.broadcasted_iota(jnp.int32, (capacity, seq_len), 0)
    return jnp.where(slot == row, 1.0, 0.0)


def forward_kernel(
    fsdp_size,
    experts,
    capacity,
    own,
    place_ref,
    gate_hbm,
    up_hbm,
    down_hbm,
    wide_hbm,
    block_hbm,
    tokens_out,
    received_out,
    gate_out,
    up_out,
    hidden_out,
    weight_out,
    shared_out,
    sh_out,
    part_out,
    room,
    picks,
    packs,
    chances,
    tall,
    received,
    gate_act,
    up_act,
    hidden,
    weight,
    shared,
    sh_act,
    part,
    gate_ref,
    up_ref,
    down_ref,
    wide_ref,
    block_ref,
    weight_sem,
    stage_sem,
    room_sem,
    *sems,
):
    f32, bf16 = jnp.float32, jnp.bfloat16
    seq_len = place_ref.shape[1]
    spread = Spread(fsdp_size, own, room, 3, sems)
    expert = lax.axis_index("fsdp")
    stage = Stage(
        [received, gate_act, up_act, hidden, weight, shared, sh_act, part],
        [received_out, gate_out, up_out, hidden_out, weight_out, shared_out, sh_out, part_out],
        stage_sem,
    )
    lanes = lax.broadcasted_iota(jnp.int32, (2 * seq_len, BLOCK), 1)

    def tokens_copy(unit):
        span = pl.ds(pl.multiple_of(unit * 2 * seq_len, 2 * seq_len), 2 * seq_len)
        return pltpu.make_async_copy(room.at[span], tokens_out.at[span], room_sem.at[unit])

    weights = [
        pltpu.make_async_copy(source, target, weight_sem.at[number])
        for number, (source, target) in enumerate([(gate_hbm, gate_ref), (up_hbm, up_ref), (down_hbm, down_ref), (wide_hbm, wide_ref), (block_hbm, block_ref)])
    ]
    for copy in weights:
        copy.start()
    spread.begin()
    for copy in weights:
        copy.wait()
    units = down_ref.shape[0]
    if units < hidden.shape[2]:
        hidden[:, :, units:] = jnp.zeros((2, 2 * capacity, hidden.shape[2] - units), bf16)
    for one in (0, 1):
        tall[one, capacity:] = block_ref[...]

    def body(step, carry):
        slot = lax.rem(step, 2)
        y, z = spread.unit(step)
        unit = z * 2 + y
        chips = spread.ahead(step)
        spread.arrived(step)
        tokens_copy(unit).start()
        stage.reuse(step)
        rows = [
            pl.ds(pl.multiple_of((2 * unit + one) * seq_len, seq_len), seq_len) for one in (0, 1)
        ]
        slots = [pl.ds(one * capacity, capacity) for one in (0, 1)]
        own_rows = [pl.ds(one * seq_len, seq_len) for one in (0, 1)]
        spread.tick(step, chips, 0)
        for one in (0, 1):
            pick = dispatch_of(place_ref, 2 * unit + one, capacity, seq_len)
            picks[one] = pick.astype(bf16)
            packs[one, :, :capacity] = jnp.transpose(pick).astype(bf16)
            received[slot, slots[one]] = dot(picks[one], room[rows[one]]).astype(bf16)
        stage.put(0, step, unit)
        spread.tick(step, chips, 1)
        both_rows = pl.ds(pl.multiple_of(unit * 2 * seq_len, 2 * seq_len), 2 * seq_len)
        wide = dot(room[both_rows], wide_ref[...])
        shared[slot] = wide[:, : 2 * BLOCK]
        gate_sh, up_sh = wide[:, :BLOCK], wide[:, BLOCK : 2 * BLOCK]
        act = (silu_parts(gate_sh)[0] * up_sh).astype(bf16)
        sh_act[slot] = act
        for one in (0, 1):
            packs[one, :, capacity:] = act[one * seq_len : (one + 1) * seq_len]
        logits = jnp.where(lanes < experts, wide[:, 2 * BLOCK :], MASKED)
        logit_exp = jnp.exp(logits - jnp.max(logits, axis=1, keepdims=True))
        chance = jnp.sum(jnp.where(lanes == expert, logit_exp, 0.0), axis=1, keepdims=True)
        chance = chance / jnp.sum(logit_exp, axis=1, keepdims=True)
        coarse = chance.astype(bf16).astype(f32)
        chances[...] = jnp.where(
            lanes == 0, coarse, jnp.where(lanes == 1, chance - coarse, 0.0)
        ).astype(bf16)
        stage.put(5, step, unit)
        stage.put(6, step, unit)
        spread.tick(step, chips, 2)
        gate_act[slot] = dot_nt(received[slot], gate_ref[...])
        stage.put(1, step, unit)
        spread.tick(step, chips, 3)
        up_act[slot] = dot_nt(received[slot], up_ref[...])
        stage.put(2, step, unit)
        spread.tick(step, chips, 4)
        for one in (0, 1):
            halves = dot(picks[one], chances[own_rows[one]])
            scale = halves[:, 0:1] + halves[:, 1:2]
            weight[slot, slots[one]] = jnp.broadcast_to(scale, (capacity, BLOCK))
            act = silu_parts(gate_act[slot, slots[one]])[0] * up_act[slot, slots[one]]
            hidden[slot, slots[one], :units] = (scale * act).astype(bf16)
        stage.put(3, step, unit)
        stage.put(4, step, unit)
        spread.tick(step, chips, 5)
        result = dot(hidden[slot, :, :units], down_ref[...]).astype(bf16)
        for one in (0, 1):
            tall[one, :capacity] = result[one * capacity : (one + 1) * capacity]
        spread.tick(step, chips, 6)
        part[slot, own_rows[0]] = dot(packs[0], tall[0]).astype(bf16)
        spread.tick(step, chips, 7)
        part[slot, own_rows[1]] = dot(packs[1], tall[1]).astype(bf16)
        stage.put(7, step, unit)
        return carry

    lax.fori_loop(0, spread.units, body, 0)
    stage.finish(spread.units)
    for unit in range(spread.units):
        tokens_copy(unit).wait()
    spread.drain()


def experts_forward(own, place, gate, up, down, wide, block, capacity, experts, collective_id):
    fsdp_size = lax.axis_size("fsdp")
    f32, bf16 = jnp.float32, jnp.bfloat16
    seq_len, width, hidden = place.shape[1], own.shape[1], gate.shape[0]
    tokens, slots = fsdp_size * seq_len, fsdp_size * capacity
    padded = -(-hidden // BLOCK) * BLOCK
    shape = jax.ShapeDtypeStruct
    outs = [
        shape((tokens, width), bf16),
        shape((slots, width), bf16),
        shape((slots, hidden), f32),
        shape((slots, hidden), f32),
        shape((slots, padded), bf16),
        shape((slots, BLOCK), f32),
        shape((tokens, 2 * BLOCK), f32),
        shape((tokens, BLOCK), bf16),
        shape((tokens, width), bf16),
    ]
    stages = [pltpu.VMEM((2, 2 * o.shape[0] // fsdp_size, o.shape[1]), o.dtype) for o in outs[1:]]
    dma = pltpu.SemaphoreType.DMA
    return pl.pallas_call(
        functools.partial(forward_kernel, fsdp_size, experts, capacity),
        out_shape=tuple(outs),
        in_specs=[pl.BlockSpec(memory_space=pltpu.VMEM)] * 2
        + [pl.BlockSpec(memory_space=pl.ANY)] * 5,
        out_specs=tuple([pl.BlockSpec(memory_space=pl.ANY)] * len(outs)),
        scratch_shapes=[
            pltpu.VMEM((tokens, width), bf16),
            pltpu.VMEM((2, capacity, seq_len), bf16),
            pltpu.VMEM((2, seq_len, capacity + BLOCK), bf16),
            pltpu.VMEM((2 * seq_len, BLOCK), bf16),
            pltpu.VMEM((2, capacity + BLOCK, width), bf16),
            *stages,
            *[pltpu.VMEM(w.shape, w.dtype) for w in (gate, up, down, wide, block)],
            dma((5,)),
            dma((len(stages), 2)),
            dma((fsdp_size // 2,)),
            *spread_sems(fsdp_size),
        ],
        compiler_params=pltpu.CompilerParams(
            collective_id=collective_id, has_side_effects=True, vmem_limit_bytes=67043328
        ),
        cost_estimate=pl.CostEstimate(
            flops=6 * slots * width * hidden, bytes_accessed=100_000_000, transcendentals=0
        ),
    )(own, place, gate, up, down, wide, block)


def backward_kernel(
    fsdp_size,
    capacity,
    own,
    place_ref,
    gate_hbm,
    up_hbm,
    down_hbm,
    pair_hbm,
    block_hbm,
    gate_in,
    up_in,
    weight_in,
    shared_in,
    grads_out,
    slots_out,
    gate_out,
    up_out,
    pair_out,
    chance_out,
    part_out,
    room,
    picks,
    packs,
    tall,
    gate_act,
    up_act,
    weight,
    shared,
    picked,
    gate_grad,
    up_grad,
    pair_grad,
    chance_grad,
    part,
    gate_ref,
    up_ref,
    down_ref,
    pair_ref,
    block_ref,
    weight_sem,
    load_sem,
    stage_sem,
    room_sem,
    *sems,
):
    f32, bf16 = jnp.float32, jnp.bfloat16
    seq_len = place_ref.shape[1]
    spread = Spread(fsdp_size, own, room, 4, sems)
    expert = lax.axis_index("fsdp")
    stage = Stage(
        [picked, gate_grad, up_grad, pair_grad, chance_grad, part],
        [slots_out, gate_out, up_out, pair_out, chance_out, part_out],
        stage_sem,
    )
    saved = [gate_in, up_in, weight_in, shared_in]
    loads = [gate_act, up_act, weight, shared]

    def load(number, step):
        y, z = spread.unit(step)
        slot, rows = lax.rem(step, 2), loads[number].shape[1]
        span = pl.ds(pl.multiple_of((z * 2 + y) * rows, rows), rows)
        return pltpu.make_async_copy(
            saved[number].at[span], loads[number].at[slot], load_sem.at[number, slot]
        )

    def grads_copy(unit):
        span = pl.ds(pl.multiple_of(unit * 2 * seq_len, 2 * seq_len), 2 * seq_len)
        return pltpu.make_async_copy(room.at[span], grads_out.at[span], room_sem.at[unit])

    for number in range(len(saved)):
        load(number, 0).start()
    weights = [
        pltpu.make_async_copy(source, target, weight_sem.at[number])
        for number, (source, target) in enumerate([(gate_hbm, gate_ref), (up_hbm, up_ref), (down_hbm, down_ref), (pair_hbm, pair_ref), (block_hbm, block_ref)])
    ]
    for copy in weights:
        copy.start()
    spread.begin()
    for copy in weights:
        copy.wait()
    units = down_ref.shape[0]
    if units < gate_grad.shape[2]:
        for grad in (gate_grad, up_grad):
            grad[:, :, units:] = jnp.zeros((2, 2 * capacity, grad.shape[2] - units), bf16)
    for one in (0, 1):
        tall[one, capacity:] = pair_ref[...]
    expert_lane = lax.broadcasted_iota(jnp.int32, (capacity, BLOCK), 1) == expert

    def body(step, carry):
        slot = lax.rem(step, 2)
        y, z = spread.unit(step)
        unit = z * 2 + y
        later = step + 1
        chips = spread.ahead(step)
        spread.arrived(step)
        grads_copy(unit).start()
        stage.reuse(step)
        rows = [
            pl.ds(pl.multiple_of((2 * unit + one) * seq_len, seq_len), seq_len) for one in (0, 1)
        ]
        both_rows = pl.ds(pl.multiple_of(unit * 2 * seq_len, 2 * seq_len), 2 * seq_len)
        slots = [pl.ds(one * capacity, capacity) for one in (0, 1)]
        own_rows = [pl.ds(one * seq_len, seq_len) for one in (0, 1)]
        for number in range(len(saved)):
            load(number, step).wait()

        def ahead():
            for number in range(len(saved)):
                load(number, later).start()

        pl.when(later < spread.units)(ahead)
        spread.tick(step, chips, 0)
        for one in (0, 1):
            pick = dispatch_of(place_ref, 2 * unit + one, capacity, seq_len)
            picks[one] = pick.astype(bf16)
            packs[one, :, :capacity] = jnp.transpose(pick).astype(bf16)
            picked[slot, slots[one]] = dot(picks[one], room[rows[one]]).astype(bf16)
        stage.put(0, step, unit)
        spread.tick(step, chips, 1)
        raw = dot_nt(picked[slot], down_ref[...])
        scale = weight[slot, :, 0:1]
        silu_gate, slope = silu_parts(gate_act[slot])
        up_value = up_act[slot]
        gate_sum = jnp.sum(raw * (silu_gate * up_value), axis=1, keepdims=True)
        scaled = scale * raw
        gate_grad[slot, :, :units] = (scaled * up_value * slope).astype(bf16)
        up_grad[slot, :, :units] = (scaled * silu_gate).astype(bf16)
        stage.put(1, step, unit)
        stage.put(2, step, unit)
        spread.tick(step, chips, 2)
        for one in (0, 1):
            column = gate_sum[one * capacity : (one + 1) * capacity]
            column = jnp.where(expert_lane, column, 0.0).astype(bf16)
            chance_grad[slot, own_rows[one]] = dot(packs[one, :, :capacity], column).astype(bf16)
        stage.put(4, step, unit)
        grad_sh = dot_nt(room[both_rows], block_ref[...])
        silu_sh, slope_sh = silu_parts(shared[slot, :, :BLOCK])
        gate_sh = (grad_sh * shared[slot, :, BLOCK:] * slope_sh).astype(bf16)
        up_sh = (grad_sh * silu_sh).astype(bf16)
        pair_grad[slot, :, :BLOCK] = gate_sh
        pair_grad[slot, :, BLOCK:] = up_sh
        for one in (0, 1):
            own_seq = slice(one * seq_len, (one + 1) * seq_len)
            packs[one, :, capacity : capacity + BLOCK] = gate_sh[own_seq]
            packs[one, :, capacity + BLOCK :] = up_sh[own_seq]
        stage.put(3, step, unit)
        spread.tick(step, chips, 3)
        back = dot(gate_grad[slot, :, :units], gate_ref[...])
        spread.tick(step, chips, 4)
        back = (back + dot(up_grad[slot, :, :units], up_ref[...])).astype(bf16)
        for one in (0, 1):
            tall[one, :capacity] = back[one * capacity : (one + 1) * capacity]
        spread.tick(step, chips, 5)
        part[slot, own_rows[0]] = dot(packs[0], tall[0]).astype(bf16)
        spread.tick(step, chips, 6)
        part[slot, own_rows[1]] = dot(packs[1], tall[1]).astype(bf16)
        stage.put(5, step, unit)
        spread.tick(step, chips, 7)
        return carry

    lax.fori_loop(0, spread.units, body, 0)
    stage.finish(spread.units)
    for unit in range(spread.units):
        grads_copy(unit).wait()
    spread.drain()


def experts_backward(
    own, place, gate, up, down, pair, block, gate_act, up_act, weight, shared, capacity, collective_id
):
    fsdp_size = lax.axis_size("fsdp")
    bf16 = jnp.bfloat16
    seq_len, width, hidden = place.shape[1], own.shape[1], gate.shape[0]
    tokens, slots = fsdp_size * seq_len, fsdp_size * capacity
    padded = -(-hidden // BLOCK) * BLOCK
    shape = jax.ShapeDtypeStruct
    outs = [
        shape((tokens, width), bf16),
        shape((slots, width), bf16),
        shape((slots, padded), bf16),
        shape((slots, padded), bf16),
        shape((tokens, 2 * BLOCK), bf16),
        shape((tokens, BLOCK), bf16),
        shape((tokens, width), bf16),
    ]

    def slots_of(arrays):
        return [pltpu.VMEM((2, 2 * a.shape[0] // fsdp_size, a.shape[1]), a.dtype) for a in arrays]

    saved = [gate_act, up_act, weight, shared]
    dma = pltpu.SemaphoreType.DMA
    return pl.pallas_call(
        functools.partial(backward_kernel, fsdp_size, capacity),
        out_shape=tuple(outs),
        in_specs=[pl.BlockSpec(memory_space=pltpu.VMEM)] * 2
        + [pl.BlockSpec(memory_space=pl.ANY)] * 9,
        out_specs=tuple([pl.BlockSpec(memory_space=pl.ANY)] * len(outs)),
        scratch_shapes=[
            pltpu.VMEM((tokens, width), bf16),
            pltpu.VMEM((2, capacity, seq_len), bf16),
            pltpu.VMEM((2, seq_len, capacity + 2 * BLOCK), bf16),
            pltpu.VMEM((2, capacity + 2 * BLOCK, width), bf16),
            *slots_of(saved),
            *slots_of(outs[1:]),
            *[pltpu.VMEM(w.shape, w.dtype) for w in (gate, up, down, pair, block)],
            dma((5,)),
            dma((4, 2)),
            dma((len(outs) - 1, 2)),
            dma((fsdp_size // 2,)),
            *spread_sems(fsdp_size),
        ],
        compiler_params=pltpu.CompilerParams(
            collective_id=collective_id, has_side_effects=True, vmem_limit_bytes=67043328
        ),
        cost_estimate=pl.CostEstimate(
            flops=6 * slots * width * hidden, bytes_accessed=100_000_000, transcendentals=0
        ),
    )(own, place, gate, up, down, pair, block, *saved)


def closing_kernel(experts, small, total, *refs):
    count = (len(refs) - 5) // 2
    loss, norm, moe, latent, router = refs[count : count + 5]
    norm[...] = small[experts : experts + 1]
    moe[...] = small[experts + 1 : experts + 2]
    latent[...] = small[experts + 2 : experts + 3, : latent.shape[1]]
    loss[...] = small[experts + 3 : experts + 4, 0:1] / total[...]
    router[...] = small[:experts]
    for source, target in zip(refs[:count], refs[count + 5 :]):
        target[...] = source[...].astype(jnp.float32)


def closing(small, total, grads, experts, latent_rows):
    def shape(*dims):
        return jax.ShapeDtypeStruct(dims, jnp.float32)

    outs = [shape(1, 1), shape(1, BLOCK), shape(1, BLOCK), shape(1, latent_rows)]
    outs += [shape(experts, BLOCK)] + [shape(*g.shape) for g in grads]
    return pl.pallas_call(
        functools.partial(closing_kernel, experts),
        out_shape=tuple(outs),
        in_specs=[pl.BlockSpec(memory_space=pltpu.VMEM)] * (2 + len(grads)),
        out_specs=tuple([pl.BlockSpec(memory_space=pltpu.VMEM)] * len(outs)),
    )(small, total, *grads)


def token_shards(
    inputs,
    teacher,
    valid_mask,
    prefix,
    routes,
    norm_gain,
    query_weight,
    latent_weight,
    latent_gain,
    expand_weight,
    output_weight,
    moe_gain,
    router_weight,
    shared_gate,
    shared_up,
    shared_down,
    expert_gate,
    expert_up,
    expert_down,
):
    f32 = jnp.float32
    bf16 = jnp.bfloat16
    tp_size = lax.axis_size("tp")
    fsdp_size = lax.axis_size("fsdp")
    own_tp = lax.axis_index("tp")
    own_expert = lax.axis_index("fsdp")
    local_heads = HEADS // tp_size
    own_rows = inputs.shape[0]
    width = inputs.shape[1]
    seq_len = own_rows * tp_size

    expert_count = router_weight.shape[1]
    route_rows = routes.shape[1] * seq_len // BLOCK
    valid_rows = seq_len // BLOCK
    parts = [
        routes.T.reshape(route_rows, BLOCK).astype(f32),
        valid_mask.reshape(valid_rows, BLOCK).astype(f32),
        norm_gain.reshape(1, BLOCK).astype(f32),
        moe_gain.reshape(1, BLOCK).astype(f32),
        jnp.pad(latent_gain, (0, BLOCK - latent_gain.shape[0])).reshape(1, BLOCK).astype(f32),
        router_weight.T.astype(f32),
    ]
    small = jnp.concatenate(parts, axis=0)
    small_rows = -(-small.shape[0] // 8) * 8
    small = jnp.pad(small, ((0, small_rows - small.shape[0]), (0, 0)))
    blocks = shared_gate.shape[1] // BLOCK
    (
        query_full,
        latent_full,
        expand_full,
        output_full,
        small_all,
        gate_block,
        up_block,
        down_block,
    ) = gather_weights(
        query_weight,
        latent_weight.T,
        expand_weight,
        output_weight,
        small,
        shared_gate,
        shared_up,
        shared_down,
        1,
    )
    small_all = small_all.reshape(fsdp_size, small_rows, BLOCK)
    gain_row = route_rows + valid_rows
    norm_gains = small_all[:, gain_row].reshape(width)
    latent_gains = small_all[:, gain_row + 2, : latent_gain.shape[0]].reshape(RANK)

    hidden = tp_gather(inputs, own_tp).astype(f32)
    cosine, sine_part = rope_tables(seq_len, ROPE)
    inverse_in = lax.rsqrt(jnp.mean(hidden * hidden, axis=-1, keepdims=True) + EPSILON)
    normal_in = hidden * inverse_in
    norm_scale = norm_gains.astype(f32)
    normed = (normal_in * norm_scale).astype(bf16)
    query_lin = jnp.dot(normed, query_full, preferred_element_type=f32).reshape(
        seq_len, local_heads, NOPE + ROPE
    )
    queries = jnp.concatenate(
        [
            query_lin[..., :NOPE],
            rotate(query_lin[..., NOPE:], cosine[:, None, :], sine_part[:, None, :]),
        ],
        axis=-1,
    ).astype(bf16)
    latent_lin = jnp.einsum("td,rd->tr", normed, latent_full, preferred_element_type=f32)
    latent_raw = latent_lin[:, :RANK]
    inverse_lat = lax.rsqrt(jnp.mean(latent_raw * latent_raw, axis=-1, keepdims=True) + EPSILON)
    latent_unit = latent_raw * inverse_lat
    latent_scale = latent_gains.astype(f32)
    latent = (latent_unit * latent_scale).astype(bf16)
    key_rope = rotate(latent_lin[:, RANK:], cosine, sine_part).astype(bf16)
    keys_values = (
        jnp.dot(latent, expand_full, preferred_element_type=f32)
        .astype(bf16)
        .reshape(seq_len, local_heads, NOPE + VDIM)
    )
    key_nope = keys_values[..., :NOPE]
    values = keys_values[..., NOPE:]
    query_nope = queries[..., :NOPE]
    query_rope = queries[..., NOPE:]
    score_scale = 1.0 / math.sqrt(NOPE + ROPE)
    position = jnp.arange(seq_len, dtype=jnp.int32)
    visible = (position[None, :] <= position[:, None]) | (position[None, :] < prefix[0])
    raw_scores = jnp.einsum("ihd,jhd->hij", query_nope, key_nope, preferred_element_type=f32)
    raw_scores = raw_scores + jnp.einsum(
        "ihd,jd->hij", query_rope, key_rope, preferred_element_type=f32
    )
    scores = jnp.where(visible[None], raw_scores * score_scale, MASKED)
    row_max = jnp.max(scores, axis=-1, keepdims=True)
    shifted = jnp.exp(scores - row_max)
    attn_probs = shifted / jnp.sum(shifted, axis=-1, keepdims=True)
    probs_low = attn_probs.astype(bf16)
    heads_out = (
        jnp.einsum("hij,jhd->ihd", probs_low, values, preferred_element_type=f32)
        .astype(bf16)
        .reshape(seq_len, local_heads * VDIM)
    )
    attended = jnp.dot(heads_out, output_full, preferred_element_type=f32)
    small_all, gate_block, up_block, down_block, attended = lax.optimization_barrier(
        (small_all, gate_block, up_block, down_block, attended)
    )
    attended = tp_scatter(attended, own_tp, own_rows)

    routes_all = small_all[:, :route_rows].reshape(fsdp_size, routes.shape[1], seq_len)
    valid_all = small_all[:, route_rows:gain_row]
    moe_gains = small_all[:, gain_row + 1].reshape(width)
    router_rows = small_all[:, gain_row + 3 : gain_row + 3 + expert_count]
    router_full = jnp.transpose(router_rows, (1, 0, 2)).reshape(expert_count, width).astype(bf16)
    holds_block = block_of(own_expert, fsdp_size // 2) < blocks
    gate_block = jnp.where(holds_block, gate_block, 0)
    up_block = jnp.where(holds_block, up_block, 0)
    down_block = jnp.where(holds_block, down_block, 0)

    middle = inputs.astype(f32) + attended
    inverse_mid = lax.rsqrt(jnp.mean(middle * middle, axis=-1, keepdims=True) + EPSILON)
    normal_mid = middle * inverse_mid
    moe_scale = moe_gains.astype(f32)
    moe_in = (normal_mid * moe_scale).astype(bf16)

    def route(logits):
        logit_exp = jnp.exp(logits - jnp.max(logits, axis=-1, keepdims=True))
        return logit_exp / jnp.sum(logit_exp, axis=-1, keepdims=True)

    router_probs = route(jnp.einsum("td,ed->te", moe_in, router_full, preferred_element_type=f32))
    experts = expert_count
    top_count = routes.shape[1]
    capacity = top_count * seq_len * 4 // (3 * experts)

    named = jnp.any(routes_all == own_expert.astype(f32), axis=1)
    ahead = jnp.dot(
        named.astype(bf16),
        (position[:, None] < position[None, :]).astype(bf16),
        preferred_element_type=f32,
    ).astype(jnp.int32)
    place = jnp.where(named, ahead, -1)
    wide_block = jnp.concatenate(
        [gate_block, up_block, jnp.pad(router_full, ((0, BLOCK - experts), (0, 0))).T], axis=1
    )
    (
        tokens,
        received,
        gate_act,
        up_act,
        gated_hidden,
        gate_weight,
        shared_acts,
        shared_hidden,
        moe_part,
    ) = experts_forward(
        moe_in,
        place,
        expert_gate[0].T,
        expert_up[0].T,
        expert_down[0],
        wide_block,
        down_block,
        capacity,
        experts,
        2,
    )
    activations = middle + reduce_tokens([moe_part], 3)[0]

    own_mask = half_rows(valid_mask, own_tp, own_rows).astype(f32)
    offset = activations - half_rows(teacher, own_tp, own_rows).astype(f32)
    valid_total = jnp.maximum(jnp.sum(valid_all), 1.0)
    square_part = jnp.sum(own_mask[:, None] * offset * offset)
    grad_out = seq_len * fsdp_size / valid_total * own_mask[:, None] * offset
    grad_moe = grad_out.astype(bf16)

    (
        grads,
        grad_slots,
        grad_gate_act,
        grad_up_act,
        grad_sh_pair,
        grad_probs_part,
        grad_part,
    ) = experts_backward(
        grad_moe,
        place,
        expert_gate[0].T,
        expert_up[0].T,
        expert_down[0],
        jnp.concatenate([gate_block.T, up_block.T], axis=0),
        down_block,
        gate_act,
        up_act,
        gate_weight,
        shared_acts,
        capacity,
        4,
    )
    grad_moe_in, grad_router_probs = reduce_tokens([grad_part, grad_probs_part], 5)
    down_shared_grad = jnp.einsum("tf,td->fd", shared_hidden, grads, preferred_element_type=f32)
    pair_grad = jnp.einsum("td,tf->df", tokens, grad_sh_pair, preferred_element_type=f32)
    gate_shared_grad = pair_grad[:, :BLOCK].astype(bf16)
    up_shared_grad = pair_grad[:, BLOCK:].astype(bf16)
    grad_router_probs = grad_router_probs[:, :experts]

    grad_logits = router_probs * (
        grad_router_probs - jnp.sum(router_probs * grad_router_probs, axis=-1, keepdims=True)
    )
    router_grad = jnp.einsum(
        "td,te->ed", moe_in.astype(f32), grad_logits, precision=HIGHEST, preferred_element_type=f32
    )
    grad_moe_in = grad_moe_in + jnp.einsum(
        "te,ed->td",
        grad_logits,
        router_full.astype(f32),
        precision=HIGHEST,
        preferred_element_type=f32,
    )
    moe_gain_grad = jnp.sum(grad_moe_in * normal_mid, axis=0)
    grad_middle = grad_out + norm_back(grad_moe_in * moe_scale, normal_mid, inverse_mid)
    grad_attended = tp_gather(grad_middle.astype(bf16), own_tp)

    output_grad = jnp.einsum("tf,td->fd", heads_out, grad_attended, preferred_element_type=f32)
    grad_heads = (
        jnp.einsum("td,fd->tf", grad_attended, output_full, preferred_element_type=f32)
        .astype(bf16)
        .reshape(seq_len, local_heads, VDIM)
    )
    grad_probs = jnp.einsum("ihd,jhd->hij", grad_heads, values, preferred_element_type=f32)
    grad_values = jnp.einsum("hij,ihd->jhd", probs_low, grad_heads, preferred_element_type=f32)
    grad_scores = (
        attn_probs * (grad_probs - jnp.sum(attn_probs * grad_probs, axis=-1, keepdims=True))
    ).astype(bf16)
    grad_q_nope = (
        jnp.einsum("hij,jhd->ihd", grad_scores, key_nope, preferred_element_type=f32) * score_scale
    )
    grad_q_rope = (
        jnp.einsum("hij,jd->ihd", grad_scores, key_rope, preferred_element_type=f32) * score_scale
    )
    grad_keys = (
        jnp.einsum("hij,ihd->jhd", grad_scores, query_nope, preferred_element_type=f32)
        * score_scale
    )
    grad_key_rope = (
        jnp.einsum("hij,ihd->jd", grad_scores, query_rope, preferred_element_type=f32) * score_scale
    )
    grad_query = (
        jnp.concatenate(
            [grad_q_nope, unrotate(grad_q_rope, cosine[:, None, :], sine_part[:, None, :])], axis=-1
        )
        .astype(bf16)
        .reshape(seq_len, local_heads * (NOPE + ROPE))
    )
    query_grad = jnp.einsum("td,tq->dq", normed, grad_query, preferred_element_type=f32)
    grad_normed = jnp.einsum("tq,dq->td", grad_query, query_full, preferred_element_type=f32)
    grad_kv = (
        jnp.concatenate([grad_keys, grad_values], axis=-1)
        .astype(bf16)
        .reshape(seq_len, local_heads * (NOPE + VDIM))
    )
    expand_grad = jnp.einsum("tr,tq->rq", latent, grad_kv, preferred_element_type=f32)
    grad_latent = jnp.einsum("tq,rq->tr", grad_kv, expand_full, preferred_element_type=f32)
    grad_both = tp_sum(jnp.concatenate([grad_latent, grad_key_rope], axis=1))
    grad_latent, grad_key_rope = grad_both[:, :RANK], grad_both[:, RANK:]
    latent_gain_grad = jnp.sum(grad_latent * latent_unit, axis=0)
    grad_latent_raw = norm_back(grad_latent * latent_scale, latent_unit, inverse_lat)
    grad_latent_lin = jnp.concatenate(
        [grad_latent_raw, unrotate(grad_key_rope, cosine, sine_part)], axis=-1
    ).astype(bf16)
    latent_grad = jnp.einsum("tr,td->rd", grad_latent_lin, normed, preferred_element_type=f32)
    grad_normed = tp_scatter(grad_normed, own_tp, own_rows) + jnp.einsum(
        "tr,rd->td",
        half_rows(grad_latent_lin, own_tp, own_rows),
        latent_full,
        preferred_element_type=f32,
    )
    own_normal = half_rows(normal_in, own_tp, own_rows)
    own_inverse = half_rows(inverse_in, own_tp, own_rows)
    norm_gain_grad = jnp.sum(grad_normed * own_normal, axis=0)
    input_grad = grad_middle + norm_back(grad_normed * norm_scale, own_normal, own_inverse)

    small = jnp.concatenate(
        [
            jnp.transpose(router_grad.reshape(experts, fsdp_size, BLOCK), (1, 0, 2)),
            norm_gain_grad.reshape(fsdp_size, 1, BLOCK),
            moe_gain_grad.reshape(fsdp_size, 1, BLOCK),
            jnp.pad(
                0.5 * latent_gain_grad.reshape(fsdp_size, 1, RANK // fsdp_size),
                ((0, 0), (0, 0), (0, BLOCK - RANK // fsdp_size)),
            ),
            jnp.full((fsdp_size, 1, BLOCK), square_part),
        ],
        axis=1,
    )
    small = jnp.pad(small, ((0, 0), (0, -(experts + 4) % 8), (0, 0))).reshape(-1, BLOCK)
    small = small + swap_tp(small)
    query_out, latent_out, expand_out, output_out, small_out, gate_out, up_out, down_out, *expert_grads = (
        reduce_weights(
            query_grad.astype(bf16),
            latent_grad.astype(bf16),
            expand_grad.astype(bf16),
            output_grad.astype(bf16),
            small,
            gate_shared_grad,
            up_shared_grad,
            down_shared_grad.astype(bf16),
            blocks,
            6,
            WeightGrads(received.shape[0], expert_down.shape[1], width),
            [grad_gate_act, grad_up_act, gated_hidden, received, grad_slots],
        )
    )
    dense_grads = [query_out, latent_out, expand_out, output_out, gate_out, up_out, down_out]
    loss, norm_out, mgain_out, lgain_out, router_out, *dense_grads = closing(
        small_out,
        (width * valid_total).reshape(1, 1),
        dense_grads,
        experts,
        RANK // fsdp_size,
    )
    return (
        loss.reshape(()),
        activations,
        input_grad,
        norm_out.reshape(-1),
        dense_grads[0],
        dense_grads[1].T,
        lgain_out.reshape(-1),
        dense_grads[2],
        dense_grads[3],
        mgain_out.reshape(-1),
        router_out.T,
        dense_grads[4],
        dense_grads[5],
        dense_grads[6],
        expert_grads[0].T.astype(f32)[None],
        expert_grads[1].T.astype(f32)[None],
        expert_grads[2].astype(f32)[None],
    )


def slot_shards(
    inputs,
    teacher,
    valid_mask,
    prefix,
    routes,
    norm_gain,
    query_weight,
    latent_weight,
    latent_gain,
    expand_weight,
    output_weight,
    moe_gain,
    router_weight,
    shared_gate,
    shared_up,
    shared_down,
    expert_gate,
    expert_up,
    expert_down,
):
    f32 = jnp.float32
    bf16 = jnp.bfloat16
    tp_size = lax.axis_size("tp")
    fsdp_size = lax.axis_size("fsdp")
    local_heads = HEADS // tp_size
    (
        norm_gains,
        query_full,
        latent_full,
        latent_gains,
        expand_full,
        output_full,
        moe_gains,
        router_full,
        gate_full,
        up_full,
        down_full,
    ) = (
        lax.all_gather(norm_gain, "fsdp", axis=0, tiled=True),
        lax.all_gather(query_weight, "fsdp", axis=0, tiled=True),
        lax.all_gather(latent_weight, "fsdp", axis=0, tiled=True),
        lax.all_gather(latent_gain, "fsdp", axis=0, tiled=True),
        lax.all_gather(expand_weight, "fsdp", axis=0, tiled=True),
        lax.all_gather(output_weight, "fsdp", axis=1, tiled=True),
        lax.all_gather(moe_gain, "fsdp", axis=0, tiled=True),
        lax.all_gather(router_weight, "fsdp", axis=0, tiled=True),
        lax.all_gather(shared_gate, "fsdp", axis=0, tiled=True),
        lax.all_gather(shared_up, "fsdp", axis=0, tiled=True),
        lax.all_gather(shared_down, "fsdp", axis=1, tiled=True),
    )
    gathered = lax.all_gather(inputs, "tp", axis=0, tiled=True)
    seq_len = gathered.shape[0]
    width = gathered.shape[1]
    hidden = gathered.astype(f32)
    cosine, sine_part = rope_tables(seq_len, ROPE)
    inverse_in = lax.rsqrt(jnp.mean(hidden * hidden, axis=-1, keepdims=True) + EPSILON)
    normal_in = hidden * inverse_in
    norm_scale = norm_gains.astype(f32)
    normed = (normal_in * norm_scale).astype(bf16)
    query_lin = jnp.dot(normed, query_full, preferred_element_type=f32).reshape(
        seq_len, local_heads, NOPE + ROPE
    )
    queries = jnp.concatenate(
        [
            query_lin[..., :NOPE],
            rotate(query_lin[..., NOPE:], cosine[:, None, :], sine_part[:, None, :]),
        ],
        axis=-1,
    ).astype(bf16)
    latent_lin = jnp.dot(normed, latent_full, preferred_element_type=f32)
    latent_raw = latent_lin[:, :RANK]
    inverse_lat = lax.rsqrt(jnp.mean(latent_raw * latent_raw, axis=-1, keepdims=True) + EPSILON)
    latent_unit = latent_raw * inverse_lat
    latent_scale = latent_gains.astype(f32)
    latent = (latent_unit * latent_scale).astype(bf16)
    key_rope = rotate(latent_lin[:, RANK:], cosine, sine_part).astype(bf16)
    keys_values = (
        jnp.dot(latent, expand_full, preferred_element_type=f32)
        .astype(bf16)
        .reshape(seq_len, local_heads, NOPE + VDIM)
    )
    key_nope = keys_values[..., :NOPE]
    values = keys_values[..., NOPE:]
    query_nope = queries[..., :NOPE]
    query_rope = queries[..., NOPE:]
    score_scale = 1.0 / math.sqrt(NOPE + ROPE)
    position = jnp.arange(seq_len, dtype=jnp.int32)
    visible = (position[None, :] <= position[:, None]) | (position[None, :] < prefix[0])

    def scores_of():
        raw_scores = jnp.einsum("ihd,jhd->hij", query_nope, key_nope, preferred_element_type=f32)
        raw_scores = raw_scores + jnp.einsum(
            "ihd,jd->hij", query_rope, key_rope, preferred_element_type=f32
        )
        return jnp.where(visible[None], raw_scores * score_scale, MASKED)

    scores = scores_of()
    row_max = jnp.max(scores, axis=-1, keepdims=True)
    shifted = jnp.exp(scores - row_max)
    row_total = jnp.sum(shifted, axis=-1, keepdims=True)
    log_total = row_max + jnp.log(row_total)
    probs_low = (shifted / row_total).astype(bf16)
    heads_out = (
        jnp.einsum("hij,jhd->ihd", probs_low, values, preferred_element_type=f32)
        .astype(bf16)
        .reshape(seq_len, local_heads * VDIM)
    )
    attended = lax.psum(jnp.dot(heads_out, output_full, preferred_element_type=f32), "tp")
    middle = hidden + attended
    inverse_mid = lax.rsqrt(jnp.mean(middle * middle, axis=-1, keepdims=True) + EPSILON)
    normal_mid = middle * inverse_mid
    moe_scale = moe_gains.astype(f32)
    moe_in = (normal_mid * moe_scale).astype(bf16)
    logits = jnp.dot(moe_in, router_full, preferred_element_type=f32)
    logit_max = jnp.max(logits, axis=-1, keepdims=True)
    logit_exp = jnp.exp(logits - logit_max)
    router_probs = logit_exp / jnp.sum(logit_exp, axis=-1, keepdims=True)
    experts = router_full.shape[1]
    top_count = routes.shape[1]
    choose = routes[:, :, None] == jnp.arange(experts, dtype=jnp.int32)[None, None, :]
    gate_values = jnp.sum(jnp.where(choose, router_probs[:, None, :], 0.0), axis=-1)
    capacity = top_count * seq_len * 4 // (3 * experts)
    flat_routes = routes.reshape(seq_len * top_count)
    onehot = (flat_routes[:, None] == jnp.arange(experts, dtype=jnp.int32)[None, :]).astype(
        jnp.int32
    )
    earlier = jnp.cumsum(onehot, axis=0) - onehot
    slot_index = flat_routes * capacity + jnp.sum(earlier * onehot, axis=1)
    placed = jnp.arange(experts * capacity, dtype=jnp.int32)[:, None] == slot_index[None, :]
    dispatch = jnp.sum(
        placed.reshape(experts * capacity, seq_len, top_count).astype(f32), axis=2
    ).astype(bf16)
    gate_slot = jnp.sum(jnp.where(placed, gate_values.reshape(1, seq_len * top_count), 0.0), axis=1)

    def send_slots(slot_rows):
        return lax.all_to_all(slot_rows, "fsdp", split_axis=0, concat_axis=1, tiled=True)

    def return_slots(partials):
        return (
            lax.all_to_all(
                partials.astype(jnp.bfloat16), "fsdp", split_axis=1, concat_axis=0, tiled=True
            )
            .astype(partials.dtype)
            .reshape(experts * capacity, width)
        )

    expert_in = (
        jnp.dot(dispatch, moe_in, preferred_element_type=f32)
        .astype(bf16)
        .reshape(experts, capacity, width)
    )
    received = send_slots(expert_in)
    gate_act = jnp.einsum("ecd,edf->ecf", received, expert_gate, preferred_element_type=f32)
    up_act = jnp.einsum("ecd,edf->ecf", received, expert_up, preferred_element_type=f32)
    silu_gate, silu_slope = silu_parts(gate_act)
    expert_hidden = (silu_gate * up_act).astype(bf16)
    expert_out = jnp.einsum("ecf,efd->ecd", expert_hidden, expert_down, preferred_element_type=f32)
    returned = return_slots(expert_out)
    picked = jnp.take(returned, slot_index, axis=0).reshape(seq_len, top_count, width)
    routed = jnp.sum(gate_values[:, :, None] * picked, axis=1)
    gate_sh = jnp.dot(moe_in, gate_full, preferred_element_type=f32)
    up_sh = jnp.dot(moe_in, up_full, preferred_element_type=f32)
    silu_sh, slope_sh = silu_parts(gate_sh)
    shared_hidden = (silu_sh * up_sh).astype(bf16)
    moe_part = routed + jnp.dot(shared_hidden, down_full, preferred_element_type=f32)
    moe_out = lax.psum(moe_part.astype(jnp.bfloat16), "tp").astype(jnp.float32)
    activations = middle + moe_out
    mask_float = valid_mask.astype(f32)
    offset = activations - teacher.astype(f32)
    square_sum, valid_sum = lax.psum(
        (jnp.sum(mask_float[:, None] * offset * offset), jnp.sum(mask_float)), "fsdp"
    )
    valid_total = jnp.maximum(valid_sum, 1.0)
    loss_value = square_sum / (width * valid_total)
    grad_out = seq_len * fsdp_size / valid_total * mask_float[:, None] * offset
    grad_moe = grad_out.astype(bf16)
    down_shared_grad = jnp.einsum("tf,td->fd", shared_hidden, grad_moe, preferred_element_type=f32)
    grad_sh_hidden = jnp.einsum("td,fd->tf", grad_moe, down_full, preferred_element_type=f32)
    grad_gate_sh = (grad_sh_hidden * up_sh * slope_sh).astype(bf16)
    grad_up_sh = (grad_sh_hidden * silu_sh).astype(bf16)
    gate_shared_grad = jnp.einsum("td,tf->df", moe_in, grad_gate_sh, preferred_element_type=f32)
    up_shared_grad = jnp.einsum("td,tf->df", moe_in, grad_up_sh, preferred_element_type=f32)
    grad_moe_in = jnp.einsum("tf,df->td", grad_gate_sh, gate_full, preferred_element_type=f32)
    grad_moe_in = grad_moe_in + jnp.einsum(
        "tf,df->td", grad_up_sh, up_full, preferred_element_type=f32
    )
    grad_gates = jnp.sum(picked * grad_moe.astype(f32)[:, None, :], axis=-1)
    grad_slots = (
        (jnp.dot(dispatch, grad_moe, preferred_element_type=f32) * gate_slot[:, None])
        .astype(bf16)
        .reshape(experts, capacity, width)
    )
    grad_received = send_slots(grad_slots)
    expert_down_grad = jnp.einsum(
        "ecf,ecd->efd", expert_hidden, grad_received, preferred_element_type=f32
    )
    grad_expert_hidden = jnp.einsum(
        "ecd,efd->ecf", grad_received, expert_down, preferred_element_type=f32
    )
    grad_gate_act = (grad_expert_hidden * up_act * silu_slope).astype(bf16)
    grad_up_act = (grad_expert_hidden * silu_gate).astype(bf16)
    expert_gate_grad = jnp.einsum(
        "ecd,ecf->edf", received, grad_gate_act, preferred_element_type=f32
    )
    expert_up_grad = jnp.einsum("ecd,ecf->edf", received, grad_up_act, preferred_element_type=f32)
    grad_expert_in = jnp.einsum(
        "ecf,edf->ecd", grad_gate_act, expert_gate, preferred_element_type=f32
    )
    grad_expert_in = grad_expert_in + jnp.einsum(
        "ecf,edf->ecd", grad_up_act, expert_up, preferred_element_type=f32
    )
    grad_returned = return_slots(grad_expert_in)
    grad_moe_in = grad_moe_in + jnp.sum(
        jnp.take(grad_returned, slot_index, axis=0).reshape(seq_len, top_count, width), axis=1
    )
    grad_moe_in, grad_gates = (
        lax.psum(grad_moe_in.astype(jnp.bfloat16), "tp").astype(jnp.float32),
        lax.psum(grad_gates.astype(jnp.bfloat16), "tp").astype(jnp.float32),
    )
    grad_router_probs = jnp.sum(jnp.where(choose, grad_gates[:, :, None], 0.0), axis=1)
    grad_logits = router_probs * (
        grad_router_probs - jnp.sum(router_probs * grad_router_probs, axis=-1, keepdims=True)
    )
    router_grad = jnp.einsum(
        "td,te->de", moe_in.astype(f32), grad_logits, precision=HIGHEST, preferred_element_type=f32
    )
    grad_moe_in = grad_moe_in + jnp.einsum(
        "te,de->td",
        grad_logits,
        router_full.astype(f32),
        precision=HIGHEST,
        preferred_element_type=f32,
    )
    moe_gain_grad = jnp.sum(grad_moe_in * normal_mid, axis=0)
    grad_middle = grad_out + norm_back(grad_moe_in * moe_scale, normal_mid, inverse_mid)
    grad_attended = grad_middle.astype(bf16)
    output_grad = jnp.einsum("tf,td->fd", heads_out, grad_attended, preferred_element_type=f32)
    grad_heads = (
        jnp.einsum("td,fd->tf", grad_attended, output_full, preferred_element_type=f32)
        .astype(bf16)
        .reshape(seq_len, local_heads, VDIM)
    )
    attn_probs = jnp.exp(scores_of() - log_total)
    probs_again = attn_probs.astype(bf16)
    grad_probs = jnp.einsum("ihd,jhd->hij", grad_heads, values, preferred_element_type=f32)
    grad_values = jnp.einsum("hij,ihd->jhd", probs_again, grad_heads, preferred_element_type=f32)
    grad_scores = (
        attn_probs * (grad_probs - jnp.sum(attn_probs * grad_probs, axis=-1, keepdims=True))
    ).astype(bf16)
    grad_q_nope = (
        jnp.einsum("hij,jhd->ihd", grad_scores, key_nope, preferred_element_type=f32) * score_scale
    )
    grad_q_rope = (
        jnp.einsum("hij,jd->ihd", grad_scores, key_rope, preferred_element_type=f32) * score_scale
    )
    grad_keys = (
        jnp.einsum("hij,ihd->jhd", grad_scores, query_nope, preferred_element_type=f32)
        * score_scale
    )
    grad_key_rope = (
        jnp.einsum("hij,ihd->jd", grad_scores, query_rope, preferred_element_type=f32) * score_scale
    )
    grad_query = (
        jnp.concatenate(
            [grad_q_nope, unrotate(grad_q_rope, cosine[:, None, :], sine_part[:, None, :])], axis=-1
        )
        .astype(bf16)
        .reshape(seq_len, local_heads * (NOPE + ROPE))
    )
    query_grad = jnp.einsum("td,tq->dq", normed, grad_query, preferred_element_type=f32)
    grad_normed = jnp.einsum("tq,dq->td", grad_query, query_full, preferred_element_type=f32)
    grad_kv = (
        jnp.concatenate([grad_keys, grad_values], axis=-1)
        .astype(bf16)
        .reshape(seq_len, local_heads * (NOPE + VDIM))
    )
    expand_grad = jnp.einsum("tr,tq->rq", latent, grad_kv, preferred_element_type=f32)
    grad_latent = jnp.einsum("tq,rq->tr", grad_kv, expand_full, preferred_element_type=f32)
    grad_normed, grad_latent, grad_key_rope = (
        lax.psum(grad_normed.astype(jnp.bfloat16), "tp").astype(jnp.float32),
        lax.psum(grad_latent.astype(jnp.bfloat16), "tp").astype(jnp.float32),
        lax.psum(grad_key_rope.astype(jnp.bfloat16), "tp").astype(jnp.float32),
    )
    latent_gain_grad = jnp.sum(grad_latent * latent_unit, axis=0)
    grad_latent_raw = norm_back(grad_latent * latent_scale, latent_unit, inverse_lat)
    grad_latent_lin = jnp.concatenate(
        [grad_latent_raw, unrotate(grad_key_rope, cosine, sine_part)], axis=-1
    ).astype(bf16)
    latent_grad = jnp.einsum("td,tr->dr", normed, grad_latent_lin, preferred_element_type=f32)
    grad_normed = grad_normed + jnp.einsum(
        "tr,dr->td", grad_latent_lin, latent_full, preferred_element_type=f32
    )
    norm_gain_grad = jnp.sum(grad_normed * normal_in, axis=0)
    input_grad = grad_middle + norm_back(grad_normed * norm_scale, normal_in, inverse_in)
    (
        norm_out,
        query_out,
        latent_out,
        lgain_out,
        expand_out,
        output_out,
        mgain_out,
        router_out,
        gate_out,
        up_out,
        down_out,
    ) = (
        lax.psum_scatter(norm_gain_grad, "fsdp", scatter_dimension=0, tiled=True),
        lax.psum_scatter(query_grad, "fsdp", scatter_dimension=0, tiled=True),
        lax.psum_scatter(latent_grad, "fsdp", scatter_dimension=0, tiled=True),
        lax.psum_scatter(latent_gain_grad, "fsdp", scatter_dimension=0, tiled=True),
        lax.psum_scatter(expand_grad, "fsdp", scatter_dimension=0, tiled=True),
        lax.psum_scatter(output_grad, "fsdp", scatter_dimension=1, tiled=True),
        lax.psum_scatter(moe_gain_grad, "fsdp", scatter_dimension=0, tiled=True),
        lax.psum_scatter(router_grad, "fsdp", scatter_dimension=0, tiled=True),
        lax.psum_scatter(gate_shared_grad, "fsdp", scatter_dimension=0, tiled=True),
        lax.psum_scatter(up_shared_grad, "fsdp", scatter_dimension=0, tiled=True),
        lax.psum_scatter(down_shared_grad, "fsdp", scatter_dimension=1, tiled=True),
    )
    own_start = lax.axis_index("tp") * inputs.shape[0]
    own_activations = lax.dynamic_slice_in_dim(activations, own_start, inputs.shape[0], 0)
    own_input_grad = lax.dynamic_slice_in_dim(input_grad, own_start, inputs.shape[0], 0)
    return (
        loss_value,
        own_activations,
        own_input_grad,
        norm_out,
        query_out,
        latent_out,
        lgain_out,
        expand_out,
        output_out,
        mgain_out,
        router_out,
        gate_out,
        up_out,
        down_out,
        expert_gate_grad,
        expert_up_grad,
        expert_down_grad,
    )


def shards(*arrays):
    fsdp_size = lax.axis_size("fsdp")
    seq_len = arrays[4].shape[0]
    experts = arrays[12].shape[1]
    capacity = arrays[4].shape[1] * seq_len * 4 // (3 * experts)
    fits = fsdp_size * seq_len <= 2 * experts * capacity and fsdp_size == experts
    aligned = arrays[5].shape[0] == BLOCK and arrays[13].shape[1] % BLOCK == 0 and arrays[13].shape[1] <= fsdp_size * BLOCK
    if fits and aligned and fsdp_size % 4 == 0:
        return token_shards(*arrays)
    return slot_shards(*arrays)


def solution(mesh):
    return jax.shard_map(
        shards,
        mesh=mesh,
        in_specs=(
            P(("fsdp", "tp"), None),
            P("fsdp", None),
            P("fsdp"),
            P("fsdp"),
            P("fsdp", None),
            P("fsdp"),
            P("fsdp", "tp"),
            P("fsdp", None),
            P("fsdp"),
            P("fsdp", "tp"),
            P("tp", "fsdp"),
            P("fsdp"),
            P("fsdp", None),
            P("fsdp", "tp"),
            P("fsdp", "tp"),
            P("tp", "fsdp"),
            P("fsdp", None, "tp"),
            P("fsdp", None, "tp"),
            P("fsdp", "tp", None),
        ),
        out_specs=(
            P(),
            P(("fsdp", "tp"), None),
            P(("fsdp", "tp"), None),
            P("fsdp"),
            P("fsdp", "tp"),
            P("fsdp", None),
            P("fsdp"),
            P("fsdp", "tp"),
            P("tp", "fsdp"),
            P("fsdp"),
            P("fsdp", None),
            P("fsdp", "tp"),
            P("fsdp", "tp"),
            P("tp", "fsdp"),
            P("fsdp", None, "tp"),
            P("fsdp", None, "tp"),
            P("fsdp", "tp", None),
        ),
        check_vma=False,
    )
```

```python
import functools
import math

import jax
import jax.numpy as jnp
from jax import lax
from jax.experimental import pallas as pl
from jax.experimental.pallas import tpu as pltpu
from jax.sharding import PartitionSpec as P

HEADS = 16
NOPE = 128
ROPE = 64
RANK = 512
VDIM = 128


EPSILON = 1e-06
HIGHEST = lax.Precision.HIGHEST
MASKED = -1e30


def rope_tables(length, dim_size):
    places = jnp.arange(length).astype(jnp.float32)
    exponent = jnp.arange(dim_size // 2).astype(jnp.float32) * (2.0 / dim_size)
    angles = places[:, None] * jnp.exp(exponent * -math.log(10000.0))[None, :]
    return (jnp.cos(angles), jnp.sin(angles))


def rotate(values, cosine, sine_part):
    half_width = values.shape[-1] // 2
    lower_half = values[..., :half_width]
    upper_half = values[..., half_width:]
    return jnp.concatenate(
        [
            lower_half * cosine - upper_half * sine_part,
            upper_half * cosine + lower_half * sine_part,
        ],
        axis=-1,
    )


def unrotate(gradient, cosine, sine_part):
    half_width = gradient.shape[-1] // 2
    lower_half = gradient[..., :half_width]
    upper_half = gradient[..., half_width:]
    return jnp.concatenate(
        [
            lower_half * cosine + upper_half * sine_part,
            upper_half * cosine - lower_half * sine_part,
        ],
        axis=-1,
    )


def silu_parts(gate_act):
    sigmoid_val = jax.nn.sigmoid(gate_act)
    return (gate_act * sigmoid_val, sigmoid_val * (1.0 + gate_act * (1.0 - sigmoid_val)))


def norm_back(grad_scaled, unit_rows, inverse):
    return inverse * (
        grad_scaled - unit_rows * jnp.mean(grad_scaled * unit_rows, axis=-1, keepdims=True)
    )


def swap_tp(value):
    return lax.ppermute(value, "tp", [(0, 1), (1, 0)])


def half_rows(value, which, rows):
    return lax.dynamic_slice_in_dim(value, which * rows, rows, 0)


def tp_scatter(partial, which, rows):
    other = half_rows(partial, 1 - which, rows).astype(jnp.bfloat16)
    return half_rows(partial, which, rows) + swap_tp(other).astype(jnp.float32)


def tp_sum(partial):
    low_partial = partial.astype(jnp.bfloat16)
    return low_partial.astype(jnp.float32) + swap_tp(low_partial).astype(jnp.float32)


def tp_gather(own, which):
    other = swap_tp(own)
    first = jnp.where(which == 0, own, other)
    second = jnp.where(which == 0, other, own)
    return jnp.concatenate([first, second], axis=0)


MESH = pl.DeviceIdType.MESH
CROSS = ("x", "y", "up", "down")
BLOCK = 128


def both(first, second):
    if first is None:
        return second
    if second is None:
        return first
    return jnp.logical_and(first, second)


def under(condition, body):
    if condition is None:
        body()
    else:
        pl.when(condition)(body)


class Grid:
    def __init__(self, fsdp_size, dims, tie=-1):
        self.tie = tie
        index = lax.axis_index("fsdp")
        self.core = lax.rem(index, 2)
        self.y = lax.rem(lax.div(index, 2), 2)
        self.z = lax.div(index, 4)
        self.x = lax.axis_index("tp")
        self.depth = fsdp_size // 4
        self.dims = dims
        self.crosses = CROSS if "x" in dims else CROSS[1:]
        self.chips = self.depth * 2 * (2 if "x" in dims else 1)

    def device(self, x, y, z, core):
        return {"fsdp": z * 4 + y * 2 + core, "tp": x}

    def chip(self, x, y, z):
        return (z * 2 + y) * 2 + x if "x" in self.dims else z * 2 + y

    def here(self):
        return self.x, self.y, self.z

    def partner(self):
        return self.device(self.x, self.y, self.z, 1 - self.core)

    def neighbour(self, cross):
        if cross == "x":
            return (1 - self.x, self.y, self.z), None
        if cross == "y":
            return (self.x, 1 - self.y, self.z), None
        if cross == "up":
            return (self.x, self.y, self.z + 1), self.z + 1 < self.depth
        return (self.x, self.y, self.z - 1), self.z >= 1

    def level(self, rank):
        inner = jnp.logical_or(self.z == 1, self.z == 2)
        rank = jnp.where(jnp.logical_and(inner, rank >= 2), 5 - rank, rank)
        high, low = lax.div(self.z, 2), lax.rem(self.z, 2)
        far, near = lax.div(rank, 2), lax.rem(rank, 2)
        return 2 * (high + far - 2 * high * far) + (low + near - 2 * low * near)

    def entry(self, number):
        steps = (0, 1) if "x" in self.dims else (0,)
        found = [(r, dy, dx) for r in range(self.depth) for dy in (0, 1) for dx in steps]
        if "x" in self.dims:
            found.sort(key=lambda e: (sum(e), self.tie * e[0]))
        else:
            found.sort(key=lambda e: e[0] + 2.1 * e[1])
        codes = [4 * e[0] + 2 * e[1] + e[2] for e in found]
        code = jnp.int32(0) + (codes[number] if isinstance(number, int) else 0)
        if not isinstance(number, int):
            for at, value in enumerate(codes):
                code = jnp.where(number == at, value, code)
        dx, dy = lax.rem(code, 2), lax.rem(lax.div(code, 2), 2)
        x, y = self.x + dx - 2 * self.x * dx, self.y + dy - 2 * self.y * dy
        return x, y, self.level(lax.div(code, 4))

    def children(self, order, chip):
        zero = dict(x=chip[0] == self.x, y=chip[1] == self.y, z=chip[2] == self.z)
        found, rest = [], None
        for dim in reversed(order):
            if dim == "z":
                found.append(("up", both(rest, (chip[2] <= self.z) & (self.z + 1 < self.depth))))
                found.append(("down", both(rest, (chip[2] >= self.z) & (self.z >= 1))))
            else:
                found.append((dim, both(rest, zero[dim])))
            rest = both(rest, zero[dim])
        return found

    def parent(self, order, chip):
        zero = dict(x=chip[0] == self.x, y=chip[1] == self.y, z=chip[2] == self.z)
        rest, turned = None, {}
        for dim in reversed(order):
            turned[dim] = both(rest, jnp.logical_not(zero[dim]))
            rest = both(rest, zero[dim])
        x = jnp.where(turned["x"], 1 - self.x, self.x) if "x" in order else self.x
        y = jnp.where(turned["y"], 1 - self.y, self.y)
        above = chip[2] > self.z
        z = jnp.where(turned["z"], jnp.where(above, self.z + 1, self.z - 1), self.z)
        side = jnp.where(above, self.crosses.index("down"), self.crosses.index("up"))
        side = jnp.where(turned["y"], self.crosses.index("y"), side)
        if "x" in order:
            side = jnp.where(turned["x"], self.crosses.index("x"), side)
        return (x, y, z), side

    def greet(self):
        barrier = pltpu.get_barrier_semaphore()
        pl.semaphore_signal(barrier, inc=1, device_id=self.partner(), device_id_type=MESH)
        count = 1
        for cross in self.crosses:
            chip, exists = self.neighbour(cross)

            def send(chip=chip):
                there = self.device(*chip, self.core)
                pl.semaphore_signal(barrier, inc=1, device_id=there, device_id_type=MESH)

            under(exists, send)
            count = count + (1 if exists is None else jnp.where(exists, 1, 0))
        pl.semaphore_wait(barrier, count)

    def greet_plane(self):
        barrier = pltpu.get_barrier_semaphore()
        size = self.depth * 4
        me = lax.axis_index("fsdp")

        def send(step, carry):
            there = {"fsdp": lax.rem(me + step, size), "tp": self.x}
            pl.semaphore_signal(barrier, inc=1, device_id=there, device_id_type=MESH)
            return carry

        lax.fori_loop(1, size, send, 0)
        across = {"fsdp": me, "tp": 1 - self.x}
        pl.semaphore_signal(barrier, inc=1, device_id=across, device_id_type=MESH)
        pl.semaphore_wait(barrier, size)


def owner_of(block, chips):
    extra = 2 * lax.rem(3 * (block - chips) + 1 + 3 * chips, chips) + 1
    return jnp.where(block < chips, 2 * block, extra)


def block_of(device, chips):
    back = pow(3, -1, chips)
    chip, core = lax.div(device, 2), lax.rem(device, 2)
    return jnp.where(core == 0, chip, chips + lax.rem(back * (chip - 1 + chips), chips))


class Exchange:
    def __init__(self, fsdp_size, tp, blocks, sources, targets, cut, to_owner, send_sem, recv_sem, own_sem):
        self.size, self.tp, self.blocks = fsdp_size, tp, blocks
        self.sources, self.targets, self.cut, self.to_owner = sources, targets, cut, to_owner
        self.send_sem, self.recv_sem, self.own_sem = send_sem, recv_sem, own_sem
        self.me = lax.axis_index("fsdp")
        self.block = block_of(self.me, fsdp_size // 2)
        self.owns = self.block < blocks

    def remote(self, array, block, other, there, send, recv):
        source, target = self.cut[array](self.sources[array], self.targets[array], block, other)
        return pltpu.make_async_remote_copy(
            src_ref=source,
            dst_ref=target,
            send_sem=self.send_sem.at[array, send],
            recv_sem=self.recv_sem.at[array, recv],
            device_id={"fsdp": there, "tp": self.tp},
            device_id_type=MESH,
        )

    def local(self, array, block):
        source, target = self.cut[array](self.sources[array], self.targets[array], block, self.me)
        return pltpu.make_async_copy(source, target, self.own_sem.at[array])

    def by_block(self, act, act_local, low, high):
        def one(number, carry):
            block = lax.rem(number + lax.div(self.me * self.blocks, self.size), self.blocks)
            owner = owner_of(block, self.size // 2)
            for array in range(len(self.sources)):
                if self.to_owner:
                    copy = self.remote(array, block, self.me, owner, block, self.me)
                else:
                    copy = self.remote(array, block, self.me, owner, 0, block)
                pl.when(self.me != owner)(getattr(copy, act))
                if act_local:
                    pl.when(self.me == owner)(getattr(self.local(array, block), act_local))
            return carry

        lax.fori_loop(low, high, one, 0)

    def by_device(self, act, act_local, low, high):
        def one(number, carry):
            other = lax.rem(self.me + number, self.size)
            for array in range(len(self.sources)):
                if self.to_owner:
                    copy = self.remote(array, self.block, other, other, 0, other)
                else:
                    copy = self.remote(array, self.block, other, other, other, self.block)
                pl.when(self.me != other)(getattr(copy, act))
                if act_local:
                    pl.when(self.me == other)(getattr(self.local(array, self.block), act_local))
            return carry

        def every():
            lax.fori_loop(low, high, one, 0)

        pl.when(self.owns)(every)

    def start(self, step, steps):
        total = self.blocks if self.to_owner else self.size
        low, high = lax.div(step * total, steps), lax.div((step + 1) * total, steps)
        (self.by_block if self.to_owner else self.by_device)("start", "start", low, high)

    def finish(self):
        if self.to_owner:
            self.by_device("wait_recv", None, 0, self.size)
            self.by_block("wait_send", "wait", 0, self.blocks)
        else:
            self.by_block("wait_recv", None, 0, self.blocks)
            self.by_device("wait_send", "wait", 0, self.size)


def exchange_sems(fsdp_size, arrays):
    dma = pltpu.SemaphoreType.DMA
    return [dma((arrays, fsdp_size)), dma((arrays, fsdp_size)), dma((arrays,))] if arrays else []


def gather_kernel(fsdp_size, pieces, places, count, blocks, cut, *refs):
    moved = len(cut)
    shards, sources = refs[:count], refs[count : count + moved]
    refs = refs[count + moved :]
    outs, targets = refs[:count], refs[count : count + moved]
    send_sem, recv_sem, pair_send, pair_recv, own_sem, cross_sem = refs[
        count + moved : count + moved + 6
    ]
    grid = Grid(fsdp_size, "zy")
    halved = [piece[1] for piece in pieces].index(None)
    exchange = Exchange(
        fsdp_size, grid.x, blocks, sources, targets, cut, True, *refs[count + moved + 6 :]
    )

    def first_row(piece, plane):
        first, rows = pieces[piece][1], pieces[piece][2]
        return pl.multiple_of(plane * rows, 16) if first is None else first

    def target(piece, chip, core):
        array, _, rows, _ = pieces[piece]
        return places[array](outs[array], chip, core, first_row(piece, chip[0]), rows)

    def source(piece, chip, own):
        array, _, rows, _ = pieces[piece]
        if own:
            return shards[array].at[pl.ds(first_row(piece, grid.x), rows)]
        return target(piece, chip, grid.core)

    def across(chip, own=False):
        index = grid.chip(*chip)
        return pltpu.make_async_remote_copy(
            src_ref=source(halved, chip, own),
            dst_ref=target(halved, chip, grid.core),
            send_sem=cross_sem.at[0, index],
            recv_sem=cross_sem.at[1, index],
            device_id=grid.device(1 - grid.x, grid.y, grid.z, grid.core),
            device_id_type=MESH,
        )

    def across_pair(chip, core):
        index, far = grid.chip(*chip), (1 - grid.x, chip[1], chip[2])
        return pltpu.make_async_remote_copy(
            src_ref=target(halved, far, grid.core),
            dst_ref=target(halved, far, core),
            send_sem=cross_sem.at[2, index],
            recv_sem=cross_sem.at[3, index],
            device_id=grid.partner(),
            device_id_type=MESH,
        )

    def crossed(chip):
        across((1 - grid.x, chip[1], chip[2])).wait_recv()
        across_pair(chip, grid.core).start()

    def hops(piece, chip, own):
        index, found = grid.chip(*chip), []
        for cross, wanted in grid.children(pieces[piece][3], chip):
            there, _ = grid.neighbour(cross)
            copy = pltpu.make_async_remote_copy(
                src_ref=source(piece, chip, own),
                dst_ref=target(piece, chip, grid.core),
                send_sem=send_sem.at[piece, index, grid.crosses.index(cross)],
                recv_sem=recv_sem.at[piece, index],
                device_id=grid.device(*there, grid.core),
                device_id_type=MESH,
            )
            found.append((wanted, copy))
        return found

    def pair(piece, chip, core, own=False, landing=False):
        index = grid.chip(*chip)
        return pltpu.make_async_remote_copy(
            src_ref=source(piece, chip, own),
            dst_ref=target(piece, chip, core),
            send_sem=pair_send.at[piece, index],
            recv_sem=(recv_sem if landing else pair_recv).at[piece, index],
            device_id=grid.partner(),
            device_id_type=MESH,
        )

    own_copies = [
        pltpu.make_async_copy(
            source(piece, grid.here(), True), target(piece, grid.here(), grid.core), own_sem.at[piece]
        )
        for piece in range(len(pieces))
    ]
    grid.greet_plane()

    def relay(chip, own):
        for piece in range(len(pieces)):
            if not own:
                pair(piece, chip, grid.core, landing=True).wait_recv()
            for wanted, copy in hops(piece, chip, own):
                under(wanted, copy.start)
            pair(piece, chip, grid.core, own).start()
            if piece == halved:
                across(chip, own).start()

    relay(grid.here(), True)
    for copy in own_copies:
        copy.start()

    def step(number, carry):
        relay(grid.entry(number), False)
        crossed(grid.entry(number - 1))
        exchange.start(number - 1, grid.chips - 1)
        return carry

    lax.fori_loop(1, grid.chips, step, 0)
    crossed(grid.entry(grid.chips - 1))

    def finish(number, carry):
        chip = grid.entry(number)
        for piece in range(len(pieces)):
            for wanted, copy in hops(piece, chip, False):
                under(wanted, copy.wait_send)
            pair(piece, chip, grid.core).wait_send()
            pair(piece, chip, 1 - grid.core).wait_recv()
        across(chip).wait_send()
        across_pair(chip, grid.core).wait_send()
        across_pair(chip, 1 - grid.core).wait_recv()
        return carry

    lax.fori_loop(0, grid.chips, finish, 0)
    for copy in own_copies:
        copy.wait()
    exchange.finish()


def gather_call(fsdp_size, pieces, places, shards, shapes, collective_id, blocks, cut, sources, targets):
    count, chips = len(shards), fsdp_size // 2
    dma = pltpu.SemaphoreType.DMA
    moved = sum(s.size * s.dtype.itemsize for s in shapes)
    return pl.pallas_call(
        functools.partial(gather_kernel, fsdp_size, pieces, places, count, blocks, cut),
        out_shape=tuple(shapes) + tuple(targets),
        in_specs=[pl.BlockSpec(memory_space=pltpu.VMEM)] * count
        + [pl.BlockSpec(memory_space=pl.ANY)] * len(sources),
        out_specs=tuple([pl.BlockSpec(memory_space=pl.ANY)] * (count + len(targets))),
        scratch_shapes=[
            dma((len(pieces), chips, 4)),
            dma((len(pieces), chips)),
            dma((len(pieces), chips)),
            dma((len(pieces), chips)),
            dma((len(pieces),)),
            dma((4, chips)),
            *exchange_sems(fsdp_size, len(sources)),
        ],
        compiler_params=pltpu.CompilerParams(collective_id=collective_id, has_side_effects=True),
        cost_estimate=pl.CostEstimate(flops=0, bytes_accessed=8 * moved, transcendentals=0),
    )(*shards, *sources)


class WeightGrads:
    inputs, outputs = 5, 3
    PIECES = (1, 3, 5)

    def __init__(self, slots, hidden, width):
        bf16 = jnp.bfloat16
        dma = pltpu.SemaphoreType.DMA
        self.hidden = hidden
        self.shapes = [jax.ShapeDtypeStruct((hidden, width), bf16)] * self.outputs
        self.scratch = [
            pltpu.VMEM((2, slots, BLOCK), bf16),
            pltpu.VMEM((slots, width), bf16),
            pltpu.VMEM((2, BLOCK, width), bf16),
            dma((2,)),
            dma((1,)),
            dma((2,)),
        ]

    def make(self, *refs):
        return WeightGradsRun(self, refs)


class WeightGradsRun:
    def __init__(self, job, refs):
        self.lefts, self.rights, self.outs = refs[:3], refs[3:5], refs[5:8]
        self.left, self.right, self.result = refs[8:11]
        self.left_sem, self.right_sem, self.out_sem = refs[11:]
        self.blocks = -(-job.hidden // BLOCK)
        self.rest = job.hidden - (self.blocks - 1) * BLOCK
        self.total = 3 * self.blocks

    def left_copy(self, which, number):
        slot, block = lax.rem(number, 2), lax.rem(number, self.blocks)
        span = pl.ds(pl.multiple_of(block * BLOCK, BLOCK), BLOCK)
        return pltpu.make_async_copy(
            self.lefts[which].at[:, span], self.left.at[slot], self.left_sem.at[slot]
        )

    def left_start(self, number):
        for which in range(3):
            pl.when(lax.div(number, self.blocks) == which)(self.left_copy(which, number).start)

    def right_copy(self, which):
        return pltpu.make_async_copy(self.rights[which], self.right, self.right_sem.at[0])

    def out_copies(self, which, number):
        slot, block = lax.rem(number, 2), lax.rem(number, self.blocks)
        full = pl.ds(pl.multiple_of(block * BLOCK, BLOCK), BLOCK)
        part = pl.ds((self.blocks - 1) * BLOCK, self.rest)
        out, sem = self.outs[which], self.out_sem.at[slot]
        return [
            (
                block < self.blocks - 1,
                pltpu.make_async_copy(self.result.at[slot], out.at[full], sem),
            ),
            (
                block == self.blocks - 1,
                pltpu.make_async_copy(self.result.at[slot, pl.ds(0, self.rest)], out.at[part], sem),
            ),
        ]

    def begin(self):
        self.right_copy(0).start()
        self.left_copy(0, jnp.int32(0)).start()

    def out_wait(self, number):
        for wanted, copy in self.out_copies(0, number):
            pl.when(wanted)(copy.wait)

    def run(self, number):
        slot = lax.rem(number, 2)
        self.left_copy(0, number).wait()
        pl.when(number + 1 < self.total)(lambda: self.left_start(number + 1))
        pl.when(lax.rem(number, 2 * self.blocks) == 0)(self.right_copy(0).wait)
        pl.when(number >= 2)(lambda: self.out_wait(number - 2))
        self.result[slot] = lax.dot_general(
            self.left[slot],
            self.right[...],
            (((0,), (0,)), ((), ())),
            preferred_element_type=jnp.float32,
        ).astype(jnp.bfloat16)
        for which in range(3):
            for wanted, copy in self.out_copies(which, number):
                pl.when(wanted & (lax.div(number, self.blocks) == which))(copy.start)
        pl.when(number == 2 * self.blocks - 1)(self.right_copy(1).start)

    def tick(self, step, piece):
        if piece in WeightGrads.PIECES:
            number = (step - 1) * len(WeightGrads.PIECES) + WeightGrads.PIECES.index(piece)
            pl.when((number >= 0) & (number < self.total))(lambda: self.run(number))

    def finish(self, steps):
        for number in range(len(WeightGrads.PIECES) * (steps - 1), self.total):
            self.run(jnp.int32(0) + number)
        for number in (self.total - 2, self.total - 1):
            self.out_wait(jnp.int32(0) + number)


def reduce_kernel(fsdp_size, dims, pieces, places, count, blocks, cut, side, halved, *refs):
    moved, taken = len(cut), side.inputs if side else 0
    partials, sources = refs[:count], refs[count : count + moved]
    side_refs = refs[count + moved : count + moved + taken]
    refs = refs[count + moved + taken :]
    outs, targets = refs[:count], refs[count : count + moved]
    refs = refs[count + moved :]
    if side:
        side_refs, refs = side_refs + refs[: side.outputs], refs[side.outputs :]
    held, other, landed = (refs[i * count : (1 + i) * count] for i in range(3))
    send_sem, recv_sem, load_sem, pair_send, pair_recv = refs[3 * count : 3 * count + 5]
    refs = refs[3 * count + 5 :]
    grid = Grid(fsdp_size, dims)
    ways = len(grid.crosses)
    empty = grid.chips * ways
    exchange, job = None, None
    if moved:
        exchange = Exchange(fsdp_size, grid.x, blocks, sources, targets, cut, False, *refs[:3])
        refs = refs[3:]
    if halved is not None:
        half, half_sem = refs[:2]
        refs = refs[2:]
    if side:
        job = side.make(*side_refs, *refs)

    def load(array, chip):
        index = grid.chip(*chip)
        return pltpu.make_async_copy(
            places[array](partials[array], chip, grid.core),
            held[array].at[index],
            load_sem.at[array, index],
        )

    def pair(array, chip):
        index = grid.chip(*chip)
        return pltpu.make_async_remote_copy(
            src_ref=places[array](partials[array], chip, 1 - grid.core),
            dst_ref=other[array].at[index],
            send_sem=pair_send.at[array, index],
            recv_sem=pair_recv.at[array, index],
            device_id=grid.partner(),
            device_id_type=MESH,
        )

    def hop(piece, chip, there, side_seen):
        array, first, rows, _ = pieces[piece]
        index = grid.chip(*chip)
        slot = index * ways + side_seen
        return pltpu.make_async_remote_copy(
            src_ref=held[array].at[index, pl.ds(first, rows)],
            dst_ref=landed[array].at[slot, pl.ds(first, rows)],
            send_sem=send_sem.at[piece, index],
            recv_sem=recv_sem.at[piece, slot],
            device_id=grid.device(*there, grid.core),
            device_id_type=MESH,
        )

    def add_up(piece, chip, root):
        array, first, rows, order = pieces[piece]
        index, slots, some = grid.chip(*chip), [], grid.z < 0
        for cross, wanted in grid.children(order, chip):
            way = grid.crosses.index(cross)
            under(wanted, hop(piece, chip, grid.here(), way).wait_recv)
            slot = index * ways + way
            slots.append(slot if wanted is None else jnp.where(wanted, slot, empty))
            some = None if wanted is None or some is None else jnp.logical_or(some, wanted)
        tile = 16 if rows % 16 == 0 else rows

        def add_all(used):
            def add(i, carry):
                span = pl.ds(pl.multiple_of(first + i * tile, tile), tile)
                total = held[array][index, span].astype(jnp.float32)
                total += other[array][index, span].astype(jnp.float32)
                for slot in used:
                    total += landed[array][slot, span].astype(jnp.float32)
                if root and array == halved:
                    start = grid.x * half.shape[0] + first + i * tile
                    outs[array][pl.ds(pl.multiple_of(start, tile), tile)] = total
                elif root:
                    outs[array][span] = total
                else:
                    held[array][index, span] = total.astype(held[array].dtype)
                return carry

            lax.fori_loop(0, rows // tile, add, 0)

        if root or some is None:
            add_all(slots)
        else:
            pl.when(some)(lambda: add_all(slots))
            pl.when(jnp.logical_not(some))(lambda: add_all([]))

    def swap_half():
        rows = half.shape[0]
        span = pl.ds(pl.multiple_of(grid.x * rows, 16), rows)
        return pltpu.make_async_remote_copy(
            src_ref=outs[halved].at[span],
            dst_ref=half,
            send_sem=half_sem.at[0],
            recv_sem=half_sem.at[1],
            device_id=grid.device(1 - grid.x, grid.y, grid.z, grid.core),
            device_id_type=MESH,
        )

    def fetched(array, chip):
        load(array, chip).wait()
        pair(array, chip).wait_recv()

    firsts = [min(p for p, piece in enumerate(pieces) if piece[0] == a) for a in range(count)]
    for array in range(count):
        landed[array][empty] = jnp.zeros(landed[array].shape[1:], landed[array].dtype)
    if moved:
        grid.greet_plane()
    else:
        grid.greet()
    last = grid.chips - 1

    def begin(number, carry):
        chip = grid.entry(last - number)
        for array in range(count):
            load(array, chip).start()
            pair(array, chip).start()
        return carry

    lax.fori_loop(0, grid.chips, begin, 0)
    if job:
        job.begin()

    def step(number, carry):
        chip = grid.entry(last - number)
        for piece in range(len(pieces)):
            if piece in firsts:
                fetched(pieces[piece][0], chip)
            add_up(piece, chip, False)
            hop(piece, chip, *grid.parent(pieces[piece][3], chip)).start()
            if job:
                job.tick(number, piece)
        if exchange:
            exchange.start(number, last)
        return carry

    lax.fori_loop(0, last, step, 0)
    if job:
        job.finish(last)
    for piece in range(len(pieces)):
        if piece in firsts:
            fetched(pieces[piece][0], grid.here())
        add_up(piece, grid.here(), True)
        if pieces[piece][0] == halved:
            swap = swap_half()
            swap.start()

    def finish(number, carry):
        chip = grid.entry(last - number)
        for array in range(count):
            pair(array, chip).wait_send()

        def sent():
            for piece in range(len(pieces)):
                hop(piece, chip, *grid.parent(pieces[piece][3], chip)).wait_send()

        pl.when(number < last)(sent)
        return carry

    lax.fori_loop(0, grid.chips, finish, 0)
    if halved is not None:
        swap.wait()
        start = (1 - grid.x) * half.shape[0]
        outs[halved][pl.ds(pl.multiple_of(start, 16), half.shape[0])] = half[...]
    if exchange:
        exchange.finish()


def reduce_call(
    fsdp_size,
    dims,
    pieces,
    places,
    partials,
    shapes,
    collective_id,
    blocks=0,
    cut=(),
    sources=(),
    targets=(),
    side=None,
    extra=(),
    halved=None,
):
    count = len(partials)
    ways = 4 if "x" in dims else 3
    chips = fsdp_size // 2 * (2 if "x" in dims else 1)
    dma = pltpu.SemaphoreType.DMA
    held = [pltpu.VMEM((chips, *s), p.dtype) for s, p in zip(shapes, partials)]
    landed = [pltpu.VMEM((chips * ways + 1, *s), p.dtype) for s, p in zip(shapes, partials)]
    moved = sum(p.size * p.dtype.itemsize for p in partials)
    sums = [(2 * s[0], s[1]) if at == halved else s for at, s in enumerate(shapes)]
    swapped = []
    if halved is not None:
        swapped = [pltpu.VMEM(shapes[halved], jnp.float32), dma((2,))]
    side_outs = tuple(side.shapes) if side else ()
    return pl.pallas_call(
        functools.partial(
            reduce_kernel, fsdp_size, dims, pieces, places, count, blocks, cut, side, halved
        ),
        out_shape=tuple(jax.ShapeDtypeStruct(s, jnp.float32) for s in sums)
        + tuple(targets)
        + side_outs,
        in_specs=[pl.BlockSpec(memory_space=pl.ANY)] * (count + len(sources) + len(extra)),
        out_specs=tuple(
            [pl.BlockSpec(memory_space=pltpu.VMEM)] * count
            + [pl.BlockSpec(memory_space=pl.ANY)] * (len(targets) + len(side_outs))
        ),
        scratch_shapes=[
            *held,
            *held,
            *landed,
            dma((len(pieces), chips)),
            dma((len(pieces), chips * ways)),
            dma((count, chips)),
            dma((count, chips)),
            dma((count, chips)),
            *exchange_sems(fsdp_size, len(sources)),
            *swapped,
            *(side.scratch if side else ()),
        ],
        compiler_params=pltpu.CompilerParams(
            collective_id=collective_id, has_side_effects=True, vmem_limit_bytes=67043328
        ),
        cost_estimate=pl.CostEstimate(flops=0, bytes_accessed=16 * moved, transcendentals=0),
    )(*partials, *sources, *extra)


def token_row(chip, core, rows):
    x, y, z = chip
    return ((z * 4 + y * 2 + core) * 2 + x) * rows


def reduce_tokens(partials, collective_id):
    fsdp_size = lax.axis_size("fsdp")
    rows = partials[0].shape[0] // (2 * fsdp_size)
    unit = rows // 4

    def place(ref, chip, core):
        return ref.at[pl.ds(pl.multiple_of(token_row(chip, core, rows), 16), rows)]

    pieces = [(0, at * unit, unit, order) for at, order in enumerate(("xyz", "zyx", "zxy", "zyx"))]
    pieces += [(array, 0, rows, "zyx") for array in range(1, len(partials))]
    shapes = [(rows, p.shape[1]) for p in partials]
    return reduce_call(
        fsdp_size, "xyz", pieces, [place] * len(partials), partials, shapes, collective_id
    )


def plane_row(chip, core):
    return chip[2] * 4 + chip[1] * 2 + core


def row_place(rows):
    def place(ref, chip, core, first=0, count=rows):
        return ref.at[pl.ds(pl.multiple_of(plane_row(chip, core) * rows + first, 8), count)]

    return place


def column_place(columns, rows):
    def place(ref, chip, core, first=0, count=rows):
        start = pl.multiple_of(plane_row(chip, core) * columns, 128)
        return ref.at[pl.ds(first, count), pl.ds(start, columns)]

    return place


def weight_pieces(query, latent, expand, output, small):
    return [
        (4, 0, small, "zy"),
        (0, 0, query // 2, "zy"),
        (1, 0, latent, "zy"),
        (0, query // 2, query // 2, "zy"),
        (2, 0, expand, "yz"),
        (3, 0, output // 2, "zy"),
        (3, output // 2, output // 2, "zy"),
    ]


def block_span(block):
    return pl.ds(pl.multiple_of(block * BLOCK, BLOCK), BLOCK)


def cut_columns(rows):
    def to_owner(source, target, block, other):
        there = pl.ds(pl.multiple_of(other * rows, rows), rows)
        return source.at[:, block_span(block)], target.at[there]

    def from_owner(source, target, block, other):
        there = pl.ds(pl.multiple_of(other * rows, rows), rows)
        return source.at[there], target.at[:, block_span(block)]

    return to_owner, from_owner


def cut_rows(columns):
    def to_owner(source, target, block, other):
        there = pl.ds(pl.multiple_of(other * columns, columns), columns)
        return source.at[block_span(block)], target.at[:, there]

    def from_owner(source, target, block, other):
        there = pl.ds(pl.multiple_of(other * columns, columns), columns)
        return source.at[:, there], target.at[block_span(block)]

    return to_owner, from_owner


def gather_weights(query, latent, expand, output, small, gate, up, down, collective_id):
    size = lax.axis_size("fsdp")
    shards = [query, latent, expand, output, small]
    places = [row_place(s.shape[0]) for s in shards]
    shapes = [
        jax.ShapeDtypeStruct((s.shape[0] * size, s.shape[1]), s.dtype) for s in shards
    ]
    for at in (1, 3):
        rows, columns = shards[at].shape
        places[at] = column_place(columns, rows)
        shapes[at] = jax.ShapeDtypeStruct((rows, columns * size), shards[at].dtype)
    columns, rows = cut_columns(gate.shape[0]), cut_rows(down.shape[1])
    tall = jax.ShapeDtypeStruct((gate.shape[0] * size, BLOCK), gate.dtype)
    flat = jax.ShapeDtypeStruct((BLOCK, down.shape[1] * size), down.dtype)
    return gather_call(
        size,
        [
            (1, None, latent.shape[0] // 2, "zy") if piece[0] == 1 else piece
            for piece in weight_pieces(*[s.shape[0] for s in shards])
        ],
        places,
        shards,
        shapes,
        collective_id,
        gate.shape[1] // BLOCK,
        (columns[0], columns[0], rows[0]),
        [gate, up, down],
        [tall, tall, flat],
    )


def grad_pieces(query, latent, expand, output, small):
    pieces = weight_pieces(query, latent, expand, output, small)
    at = pieces.index((2, 0, expand, "yz"))
    halves = [(2, 0, expand // 2, "yz"), (2, expand // 2, expand // 2, "zy")]
    return pieces[:at] + halves + pieces[at + 1 :]


def reduce_weights(
    query, latent, expand, output, small, gate, up, down, blocks, collective_id, side, extra
):
    size = lax.axis_size("fsdp")
    partials = [query, latent, expand, output, small]
    shapes = [(p.shape[0] // size, p.shape[1]) for p in partials]
    places = [row_place(s[0]) for s in shapes]
    for at in (1, 3):
        rows, columns = partials[at].shape
        shapes[at] = (rows, columns // size)
        places[at] = column_place(columns // size, rows)
    half = partials[1].shape[0] // 2
    shapes[1] = (half, shapes[1][1])

    def half_place(ref, chip, core):
        start = pl.multiple_of(plane_row(chip, core) * shapes[1][1], 128)
        first = pl.multiple_of(chip[0] * half, 16)
        return ref.at[pl.ds(first, half), pl.ds(start, shapes[1][1])]

    places[1] = half_place
    columns, rows = cut_columns(gate.shape[0] // size), cut_rows(down.shape[1] // size)
    wide = jax.ShapeDtypeStruct((gate.shape[0] // size, blocks * BLOCK), gate.dtype)
    long = jax.ShapeDtypeStruct((blocks * BLOCK, down.shape[1] // size), down.dtype)
    return reduce_call(
        size,
        "zy",
        grad_pieces(*[s[0] for s in shapes]),
        places,
        partials,
        shapes,
        collective_id,
        blocks,
        (columns[1], columns[1], rows[1]),
        [gate, up, down],
        [wide, wide, long],
        side,
        extra,
        1,
    )


class Spread:
    ORDERS = ("xyz", "zyx", "zxy", "zyx")

    def __init__(self, fsdp_size, own, room, lead, sems):
        self.lead = lead
        self.grid = Grid(fsdp_size, "xyz", 1)
        self.own, self.room = own, room
        self.rows = own.shape[0]
        self.part = self.rows // len(self.ORDERS)
        self.send_sem, self.recv_sem, self.pair_send, self.pair_recv = sems
        self.units = fsdp_size // 2

    def unit(self, step):
        grid = self.grid
        flip = lax.rem(step, 2)
        return grid.y + flip - 2 * grid.y * flip, grid.level(lax.div(step, 2))

    def span(self, chip, piece):
        start = token_row(chip, self.grid.core, self.rows) + piece * self.part
        return self.room.at[pl.ds(pl.multiple_of(start, self.part), self.part)]

    def copies(self, chip, piece, own=False):
        grid, found = self.grid, []
        index, here = grid.chip(*chip), self.span(chip, piece)
        source = self.own.at[pl.ds(piece * self.part, self.part)] if own else here
        for cross, wanted in grid.children(self.ORDERS[piece], chip):
            there, _ = grid.neighbour(cross)
            copy = pltpu.make_async_remote_copy(
                src_ref=source,
                dst_ref=here,
                send_sem=self.send_sem.at[piece, index, grid.crosses.index(cross)],
                recv_sem=self.recv_sem.at[piece, index],
                device_id=grid.device(*there, grid.core),
                device_id_type=MESH,
            )
            found.append((wanted, copy))
        return found

    def pair(self, chip, piece, own=False, landing=False):
        grid = self.grid
        index, here = grid.chip(*chip), self.span(chip, piece)
        return pltpu.make_async_remote_copy(
            src_ref=self.own.at[pl.ds(piece * self.part, self.part)] if own else here,
            dst_ref=here,
            send_sem=self.pair_send.at[piece, index],
            recv_sem=(self.recv_sem if landing else self.pair_recv).at[piece, index],
            device_id=grid.partner(),
            device_id_type=MESH,
        )

    def relay(self, chip, piece, own=False):
        if not own:
            self.pair(chip, piece, landing=True).wait_recv()
        for wanted, copy in self.copies(chip, piece, own):
            under(wanted, copy.start)
        self.pair(chip, piece, own).start()

    def begin(self):
        grid = self.grid
        grid.greet()
        for piece in range(len(self.ORDERS)):
            self.relay(grid.here(), piece, own=True)
        start = token_row(grid.here(), grid.core, self.rows)
        self.room[pl.ds(pl.multiple_of(start, self.rows), self.rows)] = self.own[...]

        def early(number, carry):
            chip = grid.entry(number)
            for piece in range(len(self.ORDERS)):
                self.relay(chip, piece)
            return carry

        lax.fori_loop(1, self.lead, early, 0)

    def ahead(self, step):
        return [self.grid.entry(self.lead + 2 * step + one) for one in (0, 1)]

    def tick(self, step, chips, number):
        pieces = len(self.ORDERS)
        late = self.lead + 2 * step + number // pieces
        chip = chips[number // pieces]
        pl.when(late < 2 * self.units)(lambda: self.relay(chip, number % pieces))

    def arrived(self, step):
        y, z = self.unit(step)
        for x in (0, 1):
            for piece in range(len(self.ORDERS)):
                self.pair((x, y, z), piece).wait_recv()

    def drain(self):
        def finish(number, carry):
            chip = self.grid.entry(number)
            for piece in range(len(self.ORDERS)):
                for wanted, copy in self.copies(chip, piece):
                    under(wanted, copy.wait_send)
                self.pair(chip, piece).wait_send()
            return carry

        lax.fori_loop(0, 2 * self.units, finish, 0)


def spread_sems(fsdp_size):
    dma = pltpu.SemaphoreType.DMA
    return [dma((4, fsdp_size, 4)), dma((4, fsdp_size)), dma((4, fsdp_size)), dma((4, fsdp_size))]


class Stage:
    def __init__(self, buffers, results, sems):
        self.buffers, self.results, self.sems = buffers, results, sems

    def copy(self, number, step, unit):
        buffer = self.buffers[number]
        rows = buffer.shape[1]
        slot = lax.rem(step, 2)
        there = self.results[number].at[pl.ds(pl.multiple_of(unit * rows, rows), rows)]
        return pltpu.make_async_copy(buffer.at[slot], there, self.sems.at[number, slot])

    def reuse(self, step):
        def wait():
            for number in range(len(self.buffers)):
                self.copy(number, step, 0).wait()

        pl.when(step >= 2)(wait)

    def put(self, number, step, unit):
        self.copy(number, step, unit).start()

    def finish(self, steps):
        for step in (steps - 2, steps - 1):
            for number in range(len(self.buffers)):
                self.copy(number, step, 0).wait()


def dot(left, right):
    return jnp.dot(left, right, preferred_element_type=jnp.float32)


def dot_nt(left, right):
    return lax.dot_general(
        left, right, (((1,), (1,)), ((), ())), preferred_element_type=jnp.float32
    )


def dispatch_of(place_ref, sequence, capacity, seq_len):
    row = place_ref[pl.ds(sequence, 1), :]
    slot = lax.broadcasted_iota(jnp.int32, (capacity, seq_len), 0)
    return jnp.where(slot == row, 1.0, 0.0)


def forward_kernel(
    fsdp_size,
    experts,
    capacity,
    own,
    place_ref,
    gate_hbm,
    up_hbm,
    down_hbm,
    wide_hbm,
    block_hbm,
    tokens_out,
    received_out,
    gate_out,
    up_out,
    hidden_out,
    weight_out,
    shared_out,
    sh_out,
    part_out,
    room,
    picks,
    packs,
    chances,
    tall,
    received,
    gate_act,
    up_act,
    hidden,
    weight,
    shared,
    sh_act,
    part,
    gate_ref,
    up_ref,
    down_ref,
    wide_ref,
    block_ref,
    weight_sem,
    stage_sem,
    room_sem,
    *sems,
):
    f32, bf16 = jnp.float32, jnp.bfloat16
    seq_len = place_ref.shape[1]
    spread = Spread(fsdp_size, own, room, 3, sems)
    expert = lax.axis_index("fsdp")
    stage = Stage(
        [received, gate_act, up_act, hidden, weight, shared, sh_act, part],
        [received_out, gate_out, up_out, hidden_out, weight_out, shared_out, sh_out, part_out],
        stage_sem,
    )
    lanes = lax.broadcasted_iota(jnp.int32, (2 * seq_len, BLOCK), 1)

    def tokens_copy(unit):
        span = pl.ds(pl.multiple_of(unit * 2 * seq_len, 2 * seq_len), 2 * seq_len)
        return pltpu.make_async_copy(room.at[span], tokens_out.at[span], room_sem.at[unit])

    weights = [
        pltpu.make_async_copy(source, target, weight_sem.at[number])
        for number, (source, target) in enumerate([(gate_hbm, gate_ref), (up_hbm, up_ref), (down_hbm, down_ref), (wide_hbm, wide_ref), (block_hbm, block_ref)])
    ]
    for copy in weights:
        copy.start()
    spread.begin()
    for copy in weights:
        copy.wait()
    units = down_ref.shape[0]
    if units < hidden.shape[2]:
        hidden[:, :, units:] = jnp.zeros((2, 2 * capacity, hidden.shape[2] - units), bf16)
    for one in (0, 1):
        tall[one, capacity:] = block_ref[...]

    def body(step, carry):
        slot = lax.rem(step, 2)
        y, z = spread.unit(step)
        unit = z * 2 + y
        chips = spread.ahead(step)
        spread.arrived(step)
        tokens_copy(unit).start()
        stage.reuse(step)
        rows = [
            pl.ds(pl.multiple_of((2 * unit + one) * seq_len, seq_len), seq_len) for one in (0, 1)
        ]
        slots = [pl.ds(one * capacity, capacity) for one in (0, 1)]
        own_rows = [pl.ds(one * seq_len, seq_len) for one in (0, 1)]
        spread.tick(step, chips, 0)
        for one in (0, 1):
            pick = dispatch_of(place_ref, 2 * unit + one, capacity, seq_len)
            picks[one] = pick.astype(bf16)
            packs[one, :, :capacity] = jnp.transpose(pick).astype(bf16)
            received[slot, slots[one]] = dot(picks[one], room[rows[one]]).astype(bf16)
        stage.put(0, step, unit)
        spread.tick(step, chips, 1)
        both_rows = pl.ds(pl.multiple_of(unit * 2 * seq_len, 2 * seq_len), 2 * seq_len)
        wide = dot(room[both_rows], wide_ref[...])
        shared[slot] = wide[:, : 2 * BLOCK]
        gate_sh, up_sh = wide[:, :BLOCK], wide[:, BLOCK : 2 * BLOCK]
        act = (silu_parts(gate_sh)[0] * up_sh).astype(bf16)
        sh_act[slot] = act
        for one in (0, 1):
            packs[one, :, capacity:] = act[one * seq_len : (one + 1) * seq_len]
        logits = jnp.where(lanes < experts, wide[:, 2 * BLOCK :], MASKED)
        logit_exp = jnp.exp(logits - jnp.max(logits, axis=1, keepdims=True))
        chance = jnp.sum(jnp.where(lanes == expert, logit_exp, 0.0), axis=1, keepdims=True)
        chance = chance / jnp.sum(logit_exp, axis=1, keepdims=True)
        coarse = chance.astype(bf16).astype(f32)
        chances[...] = jnp.where(
            lanes == 0, coarse, jnp.where(lanes == 1, chance - coarse, 0.0)
        ).astype(bf16)
        stage.put(5, step, unit)
        stage.put(6, step, unit)
        spread.tick(step, chips, 2)
        gate_act[slot] = dot_nt(received[slot], gate_ref[...])
        stage.put(1, step, unit)
        spread.tick(step, chips, 3)
        up_act[slot] = dot_nt(received[slot], up_ref[...])
        stage.put(2, step, unit)
        spread.tick(step, chips, 4)
        for one in (0, 1):
            halves = dot(picks[one], chances[own_rows[one]])
            scale = halves[:, 0:1] + halves[:, 1:2]
            weight[slot, slots[one]] = jnp.broadcast_to(scale, (capacity, BLOCK))
            act = silu_parts(gate_act[slot, slots[one]])[0] * up_act[slot, slots[one]]
            hidden[slot, slots[one], :units] = (scale * act).astype(bf16)
        stage.put(3, step, unit)
        stage.put(4, step, unit)
        spread.tick(step, chips, 5)
        result = dot(hidden[slot, :, :units], down_ref[...]).astype(bf16)
        for one in (0, 1):
            tall[one, :capacity] = result[one * capacity : (one + 1) * capacity]
        spread.tick(step, chips, 6)
        part[slot, own_rows[0]] = dot(packs[0], tall[0]).astype(bf16)
        spread.tick(step, chips, 7)
        part[slot, own_rows[1]] = dot(packs[1], tall[1]).astype(bf16)
        stage.put(7, step, unit)
        return carry

    lax.fori_loop(0, spread.units, body, 0)
    stage.finish(spread.units)
    for unit in range(spread.units):
        tokens_copy(unit).wait()
    spread.drain()


def experts_forward(own, place, gate, up, down, wide, block, capacity, experts, collective_id):
    fsdp_size = lax.axis_size("fsdp")
    f32, bf16 = jnp.float32, jnp.bfloat16
    seq_len, width, hidden = place.shape[1], own.shape[1], gate.shape[0]
    tokens, slots = fsdp_size * seq_len, fsdp_size * capacity
    padded = -(-hidden // BLOCK) * BLOCK
    shape = jax.ShapeDtypeStruct
    outs = [
        shape((tokens, width), bf16),
        shape((slots, width), bf16),
        shape((slots, hidden), f32),
        shape((slots, hidden), f32),
        shape((slots, padded), bf16),
        shape((slots, BLOCK), f32),
        shape((tokens, 2 * BLOCK), f32),
        shape((tokens, BLOCK), bf16),
        shape((tokens, width), bf16),
    ]
    stages = [pltpu.VMEM((2, 2 * o.shape[0] // fsdp_size, o.shape[1]), o.dtype) for o in outs[1:]]
    dma = pltpu.SemaphoreType.DMA
    return pl.pallas_call(
        functools.partial(forward_kernel, fsdp_size, experts, capacity),
        out_shape=tuple(outs),
        in_specs=[pl.BlockSpec(memory_space=pltpu.VMEM)] * 2
        + [pl.BlockSpec(memory_space=pl.ANY)] * 5,
        out_specs=tuple([pl.BlockSpec(memory_space=pl.ANY)] * len(outs)),
        scratch_shapes=[
            pltpu.VMEM((tokens, width), bf16),
            pltpu.VMEM((2, capacity, seq_len), bf16),
            pltpu.VMEM((2, seq_len, capacity + BLOCK), bf16),
            pltpu.VMEM((2 * seq_len, BLOCK), bf16),
            pltpu.VMEM((2, capacity + BLOCK, width), bf16),
            *stages,
            *[pltpu.VMEM(w.shape, w.dtype) for w in (gate, up, down, wide, block)],
            dma((5,)),
            dma((len(stages), 2)),
            dma((fsdp_size // 2,)),
            *spread_sems(fsdp_size),
        ],
        compiler_params=pltpu.CompilerParams(
            collective_id=collective_id, has_side_effects=True, vmem_limit_bytes=67043328
        ),
        cost_estimate=pl.CostEstimate(
            flops=6 * slots * width * hidden, bytes_accessed=100_000_000, transcendentals=0
        ),
    )(own, place, gate, up, down, wide, block)


def backward_kernel(
    fsdp_size,
    capacity,
    own,
    place_ref,
    gate_hbm,
    up_hbm,
    down_hbm,
    pair_hbm,
    block_hbm,
    gate_in,
    up_in,
    weight_in,
    shared_in,
    grads_out,
    slots_out,
    gate_out,
    up_out,
    pair_out,
    chance_out,
    part_out,
    room,
    picks,
    packs,
    tall,
    gate_act,
    up_act,
    weight,
    shared,
    picked,
    gate_grad,
    up_grad,
    pair_grad,
    chance_grad,
    part,
    gate_ref,
    up_ref,
    down_ref,
    pair_ref,
    block_ref,
    weight_sem,
    load_sem,
    stage_sem,
    room_sem,
    *sems,
):
    f32, bf16 = jnp.float32, jnp.bfloat16
    seq_len = place_ref.shape[1]
    spread = Spread(fsdp_size, own, room, 4, sems)
    expert = lax.axis_index("fsdp")
    stage = Stage(
        [picked, gate_grad, up_grad, pair_grad, chance_grad, part],
        [slots_out, gate_out, up_out, pair_out, chance_out, part_out],
        stage_sem,
    )
    saved = [gate_in, up_in, weight_in, shared_in]
    loads = [gate_act, up_act, weight, shared]

    def load(number, step):
        y, z = spread.unit(step)
        slot, rows = lax.rem(step, 2), loads[number].shape[1]
        span = pl.ds(pl.multiple_of((z * 2 + y) * rows, rows), rows)
        return pltpu.make_async_copy(
            saved[number].at[span], loads[number].at[slot], load_sem.at[number, slot]
        )

    def grads_copy(unit):
        span = pl.ds(pl.multiple_of(unit * 2 * seq_len, 2 * seq_len), 2 * seq_len)
        return pltpu.make_async_copy(room.at[span], grads_out.at[span], room_sem.at[unit])

    for number in range(len(saved)):
        load(number, 0).start()
    weights = [
        pltpu.make_async_copy(source, target, weight_sem.at[number])
        for number, (source, target) in enumerate([(gate_hbm, gate_ref), (up_hbm, up_ref), (down_hbm, down_ref), (pair_hbm, pair_ref), (block_hbm, block_ref)])
    ]
    for copy in weights:
        copy.start()
    spread.begin()
    for copy in weights:
        copy.wait()
    units = down_ref.shape[0]
    if units < gate_grad.shape[2]:
        for grad in (gate_grad, up_grad):
            grad[:, :, units:] = jnp.zeros((2, 2 * capacity, grad.shape[2] - units), bf16)
    for one in (0, 1):
        tall[one, capacity:] = pair_ref[...]
    expert_lane = lax.broadcasted_iota(jnp.int32, (capacity, BLOCK), 1) == expert

    def body(step, carry):
        slot = lax.rem(step, 2)
        y, z = spread.unit(step)
        unit = z * 2 + y
        later = step + 1
        chips = spread.ahead(step)
        spread.arrived(step)
        grads_copy(unit).start()
        stage.reuse(step)
        rows = [
            pl.ds(pl.multiple_of((2 * unit + one) * seq_len, seq_len), seq_len) for one in (0, 1)
        ]
        both_rows = pl.ds(pl.multiple_of(unit * 2 * seq_len, 2 * seq_len), 2 * seq_len)
        slots = [pl.ds(one * capacity, capacity) for one in (0, 1)]
        own_rows = [pl.ds(one * seq_len, seq_len) for one in (0, 1)]
        for number in range(len(saved)):
            load(number, step).wait()

        def ahead():
            for number in range(len(saved)):
                load(number, later).start()

        pl.when(later < spread.units)(ahead)
        spread.tick(step, chips, 0)
        for one in (0, 1):
            pick = dispatch_of(place_ref, 2 * unit + one, capacity, seq_len)
            picks[one] = pick.astype(bf16)
            packs[one, :, :capacity] = jnp.transpose(pick).astype(bf16)
            picked[slot, slots[one]] = dot(picks[one], room[rows[one]]).astype(bf16)
        stage.put(0, step, unit)
        spread.tick(step, chips, 1)
        raw = dot_nt(picked[slot], down_ref[...])
        scale = weight[slot, :, 0:1]
        silu_gate, slope = silu_parts(gate_act[slot])
        up_value = up_act[slot]
        gate_sum = jnp.sum(raw * (silu_gate * up_value), axis=1, keepdims=True)
        scaled = scale * raw
        gate_grad[slot, :, :units] = (scaled * up_value * slope).astype(bf16)
        up_grad[slot, :, :units] = (scaled * silu_gate).astype(bf16)
        stage.put(1, step, unit)
        stage.put(2, step, unit)
        spread.tick(step, chips, 2)
        for one in (0, 1):
            column = gate_sum[one * capacity : (one + 1) * capacity]
            column = jnp.where(expert_lane, column, 0.0).astype(bf16)
            chance_grad[slot, own_rows[one]] = dot(packs[one, :, :capacity], column).astype(bf16)
        stage.put(4, step, unit)
        grad_sh = dot_nt(room[both_rows], block_ref[...])
        silu_sh, slope_sh = silu_parts(shared[slot, :, :BLOCK])
        gate_sh = (grad_sh * shared[slot, :, BLOCK:] * slope_sh).astype(bf16)
        up_sh = (grad_sh * silu_sh).astype(bf16)
        pair_grad[slot, :, :BLOCK] = gate_sh
        pair_grad[slot, :, BLOCK:] = up_sh
        for one in (0, 1):
            own_seq = slice(one * seq_len, (one + 1) * seq_len)
            packs[one, :, capacity : capacity + BLOCK] = gate_sh[own_seq]
            packs[one, :, capacity + BLOCK :] = up_sh[own_seq]
        stage.put(3, step, unit)
        spread.tick(step, chips, 3)
        back = dot(gate_grad[slot, :, :units], gate_ref[...])
        spread.tick(step, chips, 4)
        back = (back + dot(up_grad[slot, :, :units], up_ref[...])).astype(bf16)
        for one in (0, 1):
            tall[one, :capacity] = back[one * capacity : (one + 1) * capacity]
        spread.tick(step, chips, 5)
        part[slot, own_rows[0]] = dot(packs[0], tall[0]).astype(bf16)
        spread.tick(step, chips, 6)
        part[slot, own_rows[1]] = dot(packs[1], tall[1]).astype(bf16)
        stage.put(5, step, unit)
        spread.tick(step, chips, 7)
        return carry

    lax.fori_loop(0, spread.units, body, 0)
    stage.finish(spread.units)
    for unit in range(spread.units):
        grads_copy(unit).wait()
    spread.drain()


def experts_backward(
    own, place, gate, up, down, pair, block, gate_act, up_act, weight, shared, capacity, collective_id
):
    fsdp_size = lax.axis_size("fsdp")
    bf16 = jnp.bfloat16
    seq_len, width, hidden = place.shape[1], own.shape[1], gate.shape[0]
    tokens, slots = fsdp_size * seq_len, fsdp_size * capacity
    padded = -(-hidden // BLOCK) * BLOCK
    shape = jax.ShapeDtypeStruct
    outs = [
        shape((tokens, width), bf16),
        shape((slots, width), bf16),
        shape((slots, padded), bf16),
        shape((slots, padded), bf16),
        shape((tokens, 2 * BLOCK), bf16),
        shape((tokens, BLOCK), bf16),
        shape((tokens, width), bf16),
    ]

    def slots_of(arrays):
        return [pltpu.VMEM((2, 2 * a.shape[0] // fsdp_size, a.shape[1]), a.dtype) for a in arrays]

    saved = [gate_act, up_act, weight, shared]
    dma = pltpu.SemaphoreType.DMA
    return pl.pallas_call(
        functools.partial(backward_kernel, fsdp_size, capacity),
        out_shape=tuple(outs),
        in_specs=[pl.BlockSpec(memory_space=pltpu.VMEM)] * 2
        + [pl.BlockSpec(memory_space=pl.ANY)] * 9,
        out_specs=tuple([pl.BlockSpec(memory_space=pl.ANY)] * len(outs)),
        scratch_shapes=[
            pltpu.VMEM((tokens, width), bf16),
            pltpu.VMEM((2, capacity, seq_len), bf16),
            pltpu.VMEM((2, seq_len, capacity + 2 * BLOCK), bf16),
            pltpu.VMEM((2, capacity + 2 * BLOCK, width), bf16),
            *slots_of(saved),
            *slots_of(outs[1:]),
            *[pltpu.VMEM(w.shape, w.dtype) for w in (gate, up, down, pair, block)],
            dma((5,)),
            dma((4, 2)),
            dma((len(outs) - 1, 2)),
            dma((fsdp_size // 2,)),
            *spread_sems(fsdp_size),
        ],
        compiler_params=pltpu.CompilerParams(
            collective_id=collective_id, has_side_effects=True, vmem_limit_bytes=67043328
        ),
        cost_estimate=pl.CostEstimate(
            flops=6 * slots * width * hidden, bytes_accessed=100_000_000, transcendentals=0
        ),
    )(own, place, gate, up, down, pair, block, *saved)


def packing_kernel(routes, valid, norm, moe, latent, router, out):
    out[...] = jnp.zeros_like(out)
    row = 0
    for source in (routes, valid):
        for line in range(source.shape[0]):
            for start in range(0, source.shape[1], BLOCK):
                piece = source[line : line + 1, start : start + BLOCK]
                out[row : row + 1] = piece.astype(jnp.float32)
                row += 1
    for source in (norm, moe, latent, router):
        lines, lanes = source.shape
        out[row : row + lines, :lanes] = source[...].astype(jnp.float32)
        row += lines


def packing(arrays, rows):
    return pl.pallas_call(
        packing_kernel,
        out_shape=jax.ShapeDtypeStruct((rows, BLOCK), jnp.float32),
        in_specs=[pl.BlockSpec(memory_space=pltpu.VMEM)] * len(arrays),
        out_specs=pl.BlockSpec(memory_space=pltpu.VMEM),
    )(*arrays)


def closing_kernel(experts, small, total, *refs):
    count = (len(refs) - 5) // 2
    loss, norm, moe, latent, router = refs[count : count + 5]
    norm[...] = small[experts : experts + 1]
    moe[...] = small[experts + 1 : experts + 2]
    latent[...] = small[experts + 2 : experts + 3, : latent.shape[1]]
    loss[...] = small[experts + 3 : experts + 4, 0:1] / total[...]
    router[...] = small[:experts]
    for source, target in zip(refs[:count], refs[count + 5 :]):
        target[...] = source[...].astype(jnp.float32)


def closing(small, total, grads, experts, latent_rows):
    def shape(*dims):
        return jax.ShapeDtypeStruct(dims, jnp.float32)

    outs = [shape(1, 1), shape(1, BLOCK), shape(1, BLOCK), shape(1, latent_rows)]
    outs += [shape(experts, BLOCK)] + [shape(*g.shape) for g in grads]
    return pl.pallas_call(
        functools.partial(closing_kernel, experts),
        out_shape=tuple(outs),
        in_specs=[pl.BlockSpec(memory_space=pltpu.VMEM)] * (2 + len(grads)),
        out_specs=tuple([pl.BlockSpec(memory_space=pltpu.VMEM)] * len(outs)),
    )(small, total, *grads)


def token_shards(
    inputs,
    teacher,
    valid_mask,
    prefix,
    routes,
    norm_gain,
    query_weight,
    latent_weight,
    latent_gain,
    expand_weight,
    output_weight,
    moe_gain,
    router_weight,
    shared_gate,
    shared_up,
    shared_down,
    expert_gate,
    expert_up,
    expert_down,
):
    f32 = jnp.float32
    bf16 = jnp.bfloat16
    tp_size = lax.axis_size("tp")
    fsdp_size = lax.axis_size("fsdp")
    own_tp = lax.axis_index("tp")
    own_expert = lax.axis_index("fsdp")
    local_heads = HEADS // tp_size
    own_rows = inputs.shape[0]
    width = inputs.shape[1]
    seq_len = own_rows * tp_size

    expert_count = router_weight.shape[1]
    route_rows = routes.shape[1] * seq_len // BLOCK
    valid_rows = seq_len // BLOCK
    small_rows = -(-(route_rows + valid_rows + 3 + expert_count) // 8) * 8
    small = packing(
        [
            routes.T,
            valid_mask.reshape(1, seq_len),
            norm_gain.reshape(1, BLOCK),
            moe_gain.reshape(1, BLOCK),
            latent_gain.reshape(1, -1),
            router_weight.T,
        ],
        small_rows,
    )
    blocks = shared_gate.shape[1] // BLOCK
    (
        query_full,
        latent_full,
        expand_full,
        output_full,
        small_all,
        gate_block,
        up_block,
        down_block,
    ) = gather_weights(
        query_weight,
        latent_weight.T,
        expand_weight,
        output_weight,
        small,
        shared_gate,
        shared_up,
        shared_down,
        1,
    )
    small_all = small_all.reshape(fsdp_size, small_rows, BLOCK)
    gain_row = route_rows + valid_rows
    norm_gains = small_all[:, gain_row].reshape(width)
    latent_gains = small_all[:, gain_row + 2, : latent_gain.shape[0]].reshape(RANK)

    hidden = tp_gather(inputs, own_tp).astype(f32)
    cosine, sine_part = rope_tables(seq_len, ROPE)
    inverse_in = lax.rsqrt(jnp.mean(hidden * hidden, axis=-1, keepdims=True) + EPSILON)
    normal_in = hidden * inverse_in
    norm_scale = norm_gains.astype(f32)
    normed = (normal_in * norm_scale).astype(bf16)
    query_lin = jnp.dot(normed, query_full, preferred_element_type=f32).reshape(
        seq_len, local_heads, NOPE + ROPE
    )
    queries = jnp.concatenate(
        [
            query_lin[..., :NOPE],
            rotate(query_lin[..., NOPE:], cosine[:, None, :], sine_part[:, None, :]),
        ],
        axis=-1,
    ).astype(bf16)
    latent_lin = jnp.einsum("td,rd->tr", normed, latent_full, preferred_element_type=f32)
    latent_raw = latent_lin[:, :RANK]
    inverse_lat = lax.rsqrt(jnp.mean(latent_raw * latent_raw, axis=-1, keepdims=True) + EPSILON)
    latent_unit = latent_raw * inverse_lat
    latent_scale = latent_gains.astype(f32)
    latent = (latent_unit * latent_scale).astype(bf16)
    key_rope = rotate(latent_lin[:, RANK:], cosine, sine_part).astype(bf16)
    keys_values = (
        jnp.dot(latent, expand_full, preferred_element_type=f32)
        .astype(bf16)
        .reshape(seq_len, local_heads, NOPE + VDIM)
    )
    key_nope = keys_values[..., :NOPE]
    values = keys_values[..., NOPE:]
    query_nope = queries[..., :NOPE]
    query_rope = queries[..., NOPE:]
    score_scale = 1.0 / math.sqrt(NOPE + ROPE)
    position = jnp.arange(seq_len, dtype=jnp.int32)
    visible = (position[None, :] <= position[:, None]) | (position[None, :] < prefix[0])
    raw_scores = jnp.einsum("ihd,jhd->hij", query_nope, key_nope, preferred_element_type=f32)
    raw_scores = raw_scores + jnp.einsum(
        "ihd,jd->hij", query_rope, key_rope, preferred_element_type=f32
    )
    scores = jnp.where(visible[None], raw_scores * score_scale, MASKED)
    row_max = jnp.max(scores, axis=-1, keepdims=True)
    shifted = jnp.exp(scores - row_max)
    attn_probs = shifted / jnp.sum(shifted, axis=-1, keepdims=True)
    probs_low = attn_probs.astype(bf16)
    heads_out = (
        jnp.einsum("hij,jhd->ihd", probs_low, values, preferred_element_type=f32)
        .astype(bf16)
        .reshape(seq_len, local_heads * VDIM)
    )
    attended = jnp.dot(heads_out, output_full, preferred_element_type=f32)
    small_all, gate_block, up_block, down_block, attended = lax.optimization_barrier(
        (small_all, gate_block, up_block, down_block, attended)
    )
    attended = tp_scatter(attended, own_tp, own_rows)

    routes_all = small_all[:, :route_rows].reshape(fsdp_size, routes.shape[1], seq_len)
    valid_all = small_all[:, route_rows:gain_row]
    moe_gains = small_all[:, gain_row + 1].reshape(width)
    router_rows = small_all[:, gain_row + 3 : gain_row + 3 + expert_count]
    router_full = jnp.transpose(router_rows, (1, 0, 2)).reshape(expert_count, width).astype(bf16)
    holds_block = block_of(own_expert, fsdp_size // 2) < blocks
    gate_block = jnp.where(holds_block, gate_block, 0)
    up_block = jnp.where(holds_block, up_block, 0)
    down_block = jnp.where(holds_block, down_block, 0)

    middle = inputs.astype(f32) + attended
    inverse_mid = lax.rsqrt(jnp.mean(middle * middle, axis=-1, keepdims=True) + EPSILON)
    normal_mid = middle * inverse_mid
    moe_scale = moe_gains.astype(f32)
    moe_in = (normal_mid * moe_scale).astype(bf16)

    def route(logits):
        logit_exp = jnp.exp(logits - jnp.max(logits, axis=-1, keepdims=True))
        return logit_exp / jnp.sum(logit_exp, axis=-1, keepdims=True)

    router_probs = route(jnp.einsum("td,ed->te", moe_in, router_full, preferred_element_type=f32))
    experts = expert_count
    top_count = routes.shape[1]
    capacity = top_count * seq_len * 4 // (3 * experts)

    named = jnp.any(routes_all == own_expert.astype(f32), axis=1)
    ahead = jnp.dot(
        named.astype(bf16),
        (position[:, None] < position[None, :]).astype(bf16),
        preferred_element_type=f32,
    ).astype(jnp.int32)
    place = jnp.where(named, ahead, -1)
    wide_block = jnp.concatenate(
        [gate_block, up_block, jnp.pad(router_full, ((0, BLOCK - experts), (0, 0))).T], axis=1
    )
    (
        tokens,
        received,
        gate_act,
        up_act,
        gated_hidden,
        gate_weight,
        shared_acts,
        shared_hidden,
        moe_part,
    ) = experts_forward(
        moe_in,
        place,
        expert_gate[0].T,
        expert_up[0].T,
        expert_down[0],
        wide_block,
        down_block,
        capacity,
        experts,
        2,
    )
    activations = middle + reduce_tokens([moe_part], 3)[0]

    own_mask = half_rows(valid_mask, own_tp, own_rows).astype(f32)
    offset = activations - half_rows(teacher, own_tp, own_rows).astype(f32)
    valid_total = jnp.maximum(jnp.sum(valid_all), 1.0)
    square_part = jnp.sum(own_mask[:, None] * offset * offset)
    grad_out = seq_len * fsdp_size / valid_total * own_mask[:, None] * offset
    grad_moe = grad_out.astype(bf16)

    (
        grads,
        grad_slots,
        grad_gate_act,
        grad_up_act,
        grad_sh_pair,
        grad_probs_part,
        grad_part,
    ) = experts_backward(
        grad_moe,
        place,
        expert_gate[0].T,
        expert_up[0].T,
        expert_down[0],
        jnp.concatenate([gate_block.T, up_block.T], axis=0),
        down_block,
        gate_act,
        up_act,
        gate_weight,
        shared_acts,
        capacity,
        4,
    )
    grad_moe_in, grad_router_probs = reduce_tokens([grad_part, grad_probs_part], 5)
    down_shared_grad = jnp.einsum("tf,td->fd", shared_hidden, grads, preferred_element_type=f32)
    pair_grad = jnp.einsum("td,tf->df", tokens, grad_sh_pair, preferred_element_type=f32)
    gate_shared_grad = pair_grad[:, :BLOCK].astype(bf16)
    up_shared_grad = pair_grad[:, BLOCK:].astype(bf16)
    grad_router_probs = grad_router_probs[:, :experts]

    grad_logits = router_probs * (
        grad_router_probs - jnp.sum(router_probs * grad_router_probs, axis=-1, keepdims=True)
    )
    router_grad = jnp.einsum(
        "td,te->ed", moe_in.astype(f32), grad_logits, precision=HIGHEST, preferred_element_type=f32
    )
    grad_moe_in = grad_moe_in + jnp.einsum(
        "te,ed->td",
        grad_logits,
        router_full.astype(f32),
        precision=HIGHEST,
        preferred_element_type=f32,
    )
    moe_gain_grad = jnp.sum(grad_moe_in * normal_mid, axis=0)
    grad_middle = grad_out + norm_back(grad_moe_in * moe_scale, normal_mid, inverse_mid)
    grad_attended = tp_gather(grad_middle.astype(bf16), own_tp)

    output_grad = jnp.einsum("tf,td->fd", heads_out, grad_attended, preferred_element_type=f32)
    grad_heads = (
        jnp.einsum("td,fd->tf", grad_attended, output_full, preferred_element_type=f32)
        .astype(bf16)
        .reshape(seq_len, local_heads, VDIM)
    )
    grad_probs = jnp.einsum("ihd,jhd->hij", grad_heads, values, preferred_element_type=f32)
    grad_values = jnp.einsum("hij,ihd->jhd", probs_low, grad_heads, preferred_element_type=f32)
    grad_scores = (
        attn_probs * (grad_probs - jnp.sum(attn_probs * grad_probs, axis=-1, keepdims=True))
    ).astype(bf16)
    grad_q_nope = (
        jnp.einsum("hij,jhd->ihd", grad_scores, key_nope, preferred_element_type=f32) * score_scale
    )
    grad_q_rope = (
        jnp.einsum("hij,jd->ihd", grad_scores, key_rope, preferred_element_type=f32) * score_scale
    )
    grad_keys = (
        jnp.einsum("hij,ihd->jhd", grad_scores, query_nope, preferred_element_type=f32)
        * score_scale
    )
    grad_key_rope = (
        jnp.einsum("hij,ihd->jd", grad_scores, query_rope, preferred_element_type=f32) * score_scale
    )
    grad_query = (
        jnp.concatenate(
            [grad_q_nope, unrotate(grad_q_rope, cosine[:, None, :], sine_part[:, None, :])], axis=-1
        )
        .astype(bf16)
        .reshape(seq_len, local_heads * (NOPE + ROPE))
    )
    query_grad = jnp.einsum("td,tq->dq", normed, grad_query, preferred_element_type=f32)
    grad_normed = jnp.einsum("tq,dq->td", grad_query, query_full, preferred_element_type=f32)
    grad_kv = (
        jnp.concatenate([grad_keys, grad_values], axis=-1)
        .astype(bf16)
        .reshape(seq_len, local_heads * (NOPE + VDIM))
    )
    expand_grad = jnp.einsum("tr,tq->rq", latent, grad_kv, preferred_element_type=f32)
    grad_latent = jnp.einsum("tq,rq->tr", grad_kv, expand_full, preferred_element_type=f32)
    grad_both = tp_sum(jnp.concatenate([grad_latent, grad_key_rope], axis=1))
    grad_latent, grad_key_rope = grad_both[:, :RANK], grad_both[:, RANK:]
    latent_gain_grad = jnp.sum(grad_latent * latent_unit, axis=0)
    grad_latent_raw = norm_back(grad_latent * latent_scale, latent_unit, inverse_lat)
    grad_latent_lin = jnp.concatenate(
        [grad_latent_raw, unrotate(grad_key_rope, cosine, sine_part)], axis=-1
    ).astype(bf16)
    latent_grad = jnp.einsum("tr,td->rd", grad_latent_lin, normed, preferred_element_type=f32)
    grad_normed = tp_scatter(grad_normed, own_tp, own_rows) + jnp.einsum(
        "tr,rd->td",
        half_rows(grad_latent_lin, own_tp, own_rows),
        latent_full,
        preferred_element_type=f32,
    )
    own_normal = half_rows(normal_in, own_tp, own_rows)
    own_inverse = half_rows(inverse_in, own_tp, own_rows)
    norm_gain_grad = jnp.sum(grad_normed * own_normal, axis=0)
    input_grad = grad_middle + norm_back(grad_normed * norm_scale, own_normal, own_inverse)

    small = jnp.concatenate(
        [
            jnp.transpose(router_grad.reshape(experts, fsdp_size, BLOCK), (1, 0, 2)),
            norm_gain_grad.reshape(fsdp_size, 1, BLOCK),
            moe_gain_grad.reshape(fsdp_size, 1, BLOCK),
            jnp.pad(
                0.5 * latent_gain_grad.reshape(fsdp_size, 1, RANK // fsdp_size),
                ((0, 0), (0, 0), (0, BLOCK - RANK // fsdp_size)),
            ),
            jnp.full((fsdp_size, 1, BLOCK), square_part),
        ],
        axis=1,
    )
    small = jnp.pad(small, ((0, 0), (0, -(experts + 4) % 8), (0, 0))).reshape(-1, BLOCK)
    small = small + swap_tp(small)
    query_out, latent_out, expand_out, output_out, small_out, gate_out, up_out, down_out, *expert_grads = (
        reduce_weights(
            query_grad.astype(bf16),
            latent_grad.astype(bf16),
            expand_grad.astype(bf16),
            output_grad.astype(bf16),
            small,
            gate_shared_grad,
            up_shared_grad,
            down_shared_grad.astype(bf16),
            blocks,
            6,
            WeightGrads(received.shape[0], expert_down.shape[1], width),
            [grad_gate_act, grad_up_act, gated_hidden, received, grad_slots],
        )
    )
    dense_grads = [query_out, latent_out, expand_out, output_out, gate_out, up_out, down_out]
    loss, norm_out, mgain_out, lgain_out, router_out, *dense_grads = closing(
        small_out,
        (width * valid_total).reshape(1, 1),
        dense_grads,
        experts,
        RANK // fsdp_size,
    )
    return (
        loss.reshape(()),
        activations,
        input_grad,
        norm_out.reshape(-1),
        dense_grads[0],
        dense_grads[1].T,
        lgain_out.reshape(-1),
        dense_grads[2],
        dense_grads[3],
        mgain_out.reshape(-1),
        router_out.T,
        dense_grads[4],
        dense_grads[5],
        dense_grads[6],
        expert_grads[0].T.astype(f32)[None],
        expert_grads[1].T.astype(f32)[None],
        expert_grads[2].astype(f32)[None],
    )


def slot_shards(
    inputs,
    teacher,
    valid_mask,
    prefix,
    routes,
    norm_gain,
    query_weight,
    latent_weight,
    latent_gain,
    expand_weight,
    output_weight,
    moe_gain,
    router_weight,
    shared_gate,
    shared_up,
    shared_down,
    expert_gate,
    expert_up,
    expert_down,
):
    f32 = jnp.float32
    bf16 = jnp.bfloat16
    tp_size = lax.axis_size("tp")
    fsdp_size = lax.axis_size("fsdp")
    local_heads = HEADS // tp_size
    (
        norm_gains,
        query_full,
        latent_full,
        latent_gains,
        expand_full,
        output_full,
        moe_gains,
        router_full,
        gate_full,
        up_full,
        down_full,
    ) = (
        lax.all_gather(norm_gain, "fsdp", axis=0, tiled=True),
        lax.all_gather(query_weight, "fsdp", axis=0, tiled=True),
        lax.all_gather(latent_weight, "fsdp", axis=0, tiled=True),
        lax.all_gather(latent_gain, "fsdp", axis=0, tiled=True),
        lax.all_gather(expand_weight, "fsdp", axis=0, tiled=True),
        lax.all_gather(output_weight, "fsdp", axis=1, tiled=True),
        lax.all_gather(moe_gain, "fsdp", axis=0, tiled=True),
        lax.all_gather(router_weight, "fsdp", axis=0, tiled=True),
        lax.all_gather(shared_gate, "fsdp", axis=0, tiled=True),
        lax.all_gather(shared_up, "fsdp", axis=0, tiled=True),
        lax.all_gather(shared_down, "fsdp", axis=1, tiled=True),
    )
    gathered = lax.all_gather(inputs, "tp", axis=0, tiled=True)
    seq_len = gathered.shape[0]
    width = gathered.shape[1]
    hidden = gathered.astype(f32)
    cosine, sine_part = rope_tables(seq_len, ROPE)
    inverse_in = lax.rsqrt(jnp.mean(hidden * hidden, axis=-1, keepdims=True) + EPSILON)
    normal_in = hidden * inverse_in
    norm_scale = norm_gains.astype(f32)
    normed = (normal_in * norm_scale).astype(bf16)
    query_lin = jnp.dot(normed, query_full, preferred_element_type=f32).reshape(
        seq_len, local_heads, NOPE + ROPE
    )
    queries = jnp.concatenate(
        [
            query_lin[..., :NOPE],
            rotate(query_lin[..., NOPE:], cosine[:, None, :], sine_part[:, None, :]),
        ],
        axis=-1,
    ).astype(bf16)
    latent_lin = jnp.dot(normed, latent_full, preferred_element_type=f32)
    latent_raw = latent_lin[:, :RANK]
    inverse_lat = lax.rsqrt(jnp.mean(latent_raw * latent_raw, axis=-1, keepdims=True) + EPSILON)
    latent_unit = latent_raw * inverse_lat
    latent_scale = latent_gains.astype(f32)
    latent = (latent_unit * latent_scale).astype(bf16)
    key_rope = rotate(latent_lin[:, RANK:], cosine, sine_part).astype(bf16)
    keys_values = (
        jnp.dot(latent, expand_full, preferred_element_type=f32)
        .astype(bf16)
        .reshape(seq_len, local_heads, NOPE + VDIM)
    )
    key_nope = keys_values[..., :NOPE]
    values = keys_values[..., NOPE:]
    query_nope = queries[..., :NOPE]
    query_rope = queries[..., NOPE:]
    score_scale = 1.0 / math.sqrt(NOPE + ROPE)
    position = jnp.arange(seq_len, dtype=jnp.int32)
    visible = (position[None, :] <= position[:, None]) | (position[None, :] < prefix[0])

    def scores_of():
        raw_scores = jnp.einsum("ihd,jhd->hij", query_nope, key_nope, preferred_element_type=f32)
        raw_scores = raw_scores + jnp.einsum(
            "ihd,jd->hij", query_rope, key_rope, preferred_element_type=f32
        )
        return jnp.where(visible[None], raw_scores * score_scale, MASKED)

    scores = scores_of()
    row_max = jnp.max(scores, axis=-1, keepdims=True)
    shifted = jnp.exp(scores - row_max)
    row_total = jnp.sum(shifted, axis=-1, keepdims=True)
    log_total = row_max + jnp.log(row_total)
    probs_low = (shifted / row_total).astype(bf16)
    heads_out = (
        jnp.einsum("hij,jhd->ihd", probs_low, values, preferred_element_type=f32)
        .astype(bf16)
        .reshape(seq_len, local_heads * VDIM)
    )
    attended = lax.psum(jnp.dot(heads_out, output_full, preferred_element_type=f32), "tp")
    middle = hidden + attended
    inverse_mid = lax.rsqrt(jnp.mean(middle * middle, axis=-1, keepdims=True) + EPSILON)
    normal_mid = middle * inverse_mid
    moe_scale = moe_gains.astype(f32)
    moe_in = (normal_mid * moe_scale).astype(bf16)
    logits = jnp.dot(moe_in, router_full, preferred_element_type=f32)
    logit_max = jnp.max(logits, axis=-1, keepdims=True)
    logit_exp = jnp.exp(logits - logit_max)
    router_probs = logit_exp / jnp.sum(logit_exp, axis=-1, keepdims=True)
    experts = router_full.shape[1]
    top_count = routes.shape[1]
    choose = routes[:, :, None] == jnp.arange(experts, dtype=jnp.int32)[None, None, :]
    gate_values = jnp.sum(jnp.where(choose, router_probs[:, None, :], 0.0), axis=-1)
    capacity = top_count * seq_len * 4 // (3 * experts)
    flat_routes = routes.reshape(seq_len * top_count)
    onehot = (flat_routes[:, None] == jnp.arange(experts, dtype=jnp.int32)[None, :]).astype(
        jnp.int32
    )
    earlier = jnp.cumsum(onehot, axis=0) - onehot
    slot_index = flat_routes * capacity + jnp.sum(earlier * onehot, axis=1)
    placed = jnp.arange(experts * capacity, dtype=jnp.int32)[:, None] == slot_index[None, :]
    dispatch = jnp.sum(
        placed.reshape(experts * capacity, seq_len, top_count).astype(f32), axis=2
    ).astype(bf16)
    gate_slot = jnp.sum(jnp.where(placed, gate_values.reshape(1, seq_len * top_count), 0.0), axis=1)

    def send_slots(slot_rows):
        return lax.all_to_all(slot_rows, "fsdp", split_axis=0, concat_axis=1, tiled=True)

    def return_slots(partials):
        return (
            lax.all_to_all(
                partials.astype(jnp.bfloat16), "fsdp", split_axis=1, concat_axis=0, tiled=True
            )
            .astype(partials.dtype)
            .reshape(experts * capacity, width)
        )

    expert_in = (
        jnp.dot(dispatch, moe_in, preferred_element_type=f32)
        .astype(bf16)
        .reshape(experts, capacity, width)
    )
    received = send_slots(expert_in)
    gate_act = jnp.einsum("ecd,edf->ecf", received, expert_gate, preferred_element_type=f32)
    up_act = jnp.einsum("ecd,edf->ecf", received, expert_up, preferred_element_type=f32)
    silu_gate, silu_slope = silu_parts(gate_act)
    expert_hidden = (silu_gate * up_act).astype(bf16)
    expert_out = jnp.einsum("ecf,efd->ecd", expert_hidden, expert_down, preferred_element_type=f32)
    returned = return_slots(expert_out)
    picked = jnp.take(returned, slot_index, axis=0).reshape(seq_len, top_count, width)
    routed = jnp.sum(gate_values[:, :, None] * picked, axis=1)
    gate_sh = jnp.dot(moe_in, gate_full, preferred_element_type=f32)
    up_sh = jnp.dot(moe_in, up_full, preferred_element_type=f32)
    silu_sh, slope_sh = silu_parts(gate_sh)
    shared_hidden = (silu_sh * up_sh).astype(bf16)
    moe_part = routed + jnp.dot(shared_hidden, down_full, preferred_element_type=f32)
    moe_out = lax.psum(moe_part.astype(jnp.bfloat16), "tp").astype(jnp.float32)
    activations = middle + moe_out
    mask_float = valid_mask.astype(f32)
    offset = activations - teacher.astype(f32)
    square_sum, valid_sum = lax.psum(
        (jnp.sum(mask_float[:, None] * offset * offset), jnp.sum(mask_float)), "fsdp"
    )
    valid_total = jnp.maximum(valid_sum, 1.0)
    loss_value = square_sum / (width * valid_total)
    grad_out = seq_len * fsdp_size / valid_total * mask_float[:, None] * offset
    grad_moe = grad_out.astype(bf16)
    down_shared_grad = jnp.einsum("tf,td->fd", shared_hidden, grad_moe, preferred_element_type=f32)
    grad_sh_hidden = jnp.einsum("td,fd->tf", grad_moe, down_full, preferred_element_type=f32)
    grad_gate_sh = (grad_sh_hidden * up_sh * slope_sh).astype(bf16)
    grad_up_sh = (grad_sh_hidden * silu_sh).astype(bf16)
    gate_shared_grad = jnp.einsum("td,tf->df", moe_in, grad_gate_sh, preferred_element_type=f32)
    up_shared_grad = jnp.einsum("td,tf->df", moe_in, grad_up_sh, preferred_element_type=f32)
    grad_moe_in = jnp.einsum("tf,df->td", grad_gate_sh, gate_full, preferred_element_type=f32)
    grad_moe_in = grad_moe_in + jnp.einsum(
        "tf,df->td", grad_up_sh, up_full, preferred_element_type=f32
    )
    grad_gates = jnp.sum(picked * grad_moe.astype(f32)[:, None, :], axis=-1)
    grad_slots = (
        (jnp.dot(dispatch, grad_moe, preferred_element_type=f32) * gate_slot[:, None])
        .astype(bf16)
        .reshape(experts, capacity, width)
    )
    grad_received = send_slots(grad_slots)
    expert_down_grad = jnp.einsum(
        "ecf,ecd->efd", expert_hidden, grad_received, preferred_element_type=f32
    )
    grad_expert_hidden = jnp.einsum(
        "ecd,efd->ecf", grad_received, expert_down, preferred_element_type=f32
    )
    grad_gate_act = (grad_expert_hidden * up_act * silu_slope).astype(bf16)
    grad_up_act = (grad_expert_hidden * silu_gate).astype(bf16)
    expert_gate_grad = jnp.einsum(
        "ecd,ecf->edf", received, grad_gate_act, preferred_element_type=f32
    )
    expert_up_grad = jnp.einsum("ecd,ecf->edf", received, grad_up_act, preferred_element_type=f32)
    grad_expert_in = jnp.einsum(
        "ecf,edf->ecd", grad_gate_act, expert_gate, preferred_element_type=f32
    )
    grad_expert_in = grad_expert_in + jnp.einsum(
        "ecf,edf->ecd", grad_up_act, expert_up, preferred_element_type=f32
    )
    grad_returned = return_slots(grad_expert_in)
    grad_moe_in = grad_moe_in + jnp.sum(
        jnp.take(grad_returned, slot_index, axis=0).reshape(seq_len, top_count, width), axis=1
    )
    grad_moe_in, grad_gates = (
        lax.psum(grad_moe_in.astype(jnp.bfloat16), "tp").astype(jnp.float32),
        lax.psum(grad_gates.astype(jnp.bfloat16), "tp").astype(jnp.float32),
    )
    grad_router_probs = jnp.sum(jnp.where(choose, grad_gates[:, :, None], 0.0), axis=1)
    grad_logits = router_probs * (
        grad_router_probs - jnp.sum(router_probs * grad_router_probs, axis=-1, keepdims=True)
    )
    router_grad = jnp.einsum(
        "td,te->de", moe_in.astype(f32), grad_logits, precision=HIGHEST, preferred_element_type=f32
    )
    grad_moe_in = grad_moe_in + jnp.einsum(
        "te,de->td",
        grad_logits,
        router_full.astype(f32),
        precision=HIGHEST,
        preferred_element_type=f32,
    )
    moe_gain_grad = jnp.sum(grad_moe_in * normal_mid, axis=0)
    grad_middle = grad_out + norm_back(grad_moe_in * moe_scale, normal_mid, inverse_mid)
    grad_attended = grad_middle.astype(bf16)
    output_grad = jnp.einsum("tf,td->fd", heads_out, grad_attended, preferred_element_type=f32)
    grad_heads = (
        jnp.einsum("td,fd->tf", grad_attended, output_full, preferred_element_type=f32)
        .astype(bf16)
        .reshape(seq_len, local_heads, VDIM)
    )
    attn_probs = jnp.exp(scores_of() - log_total)
    probs_again = attn_probs.astype(bf16)
    grad_probs = jnp.einsum("ihd,jhd->hij", grad_heads, values, preferred_element_type=f32)
    grad_values = jnp.einsum("hij,ihd->jhd", probs_again, grad_heads, preferred_element_type=f32)
    grad_scores = (
        attn_probs * (grad_probs - jnp.sum(attn_probs * grad_probs, axis=-1, keepdims=True))
    ).astype(bf16)
    grad_q_nope = (
        jnp.einsum("hij,jhd->ihd", grad_scores, key_nope, preferred_element_type=f32) * score_scale
    )
    grad_q_rope = (
        jnp.einsum("hij,jd->ihd", grad_scores, key_rope, preferred_element_type=f32) * score_scale
    )
    grad_keys = (
        jnp.einsum("hij,ihd->jhd", grad_scores, query_nope, preferred_element_type=f32)
        * score_scale
    )
    grad_key_rope = (
        jnp.einsum("hij,ihd->jd", grad_scores, query_rope, preferred_element_type=f32) * score_scale
    )
    grad_query = (
        jnp.concatenate(
            [grad_q_nope, unrotate(grad_q_rope, cosine[:, None, :], sine_part[:, None, :])], axis=-1
        )
        .astype(bf16)
        .reshape(seq_len, local_heads * (NOPE + ROPE))
    )
    query_grad = jnp.einsum("td,tq->dq", normed, grad_query, preferred_element_type=f32)
    grad_normed = jnp.einsum("tq,dq->td", grad_query, query_full, preferred_element_type=f32)
    grad_kv = (
        jnp.concatenate([grad_keys, grad_values], axis=-1)
        .astype(bf16)
        .reshape(seq_len, local_heads * (NOPE + VDIM))
    )
    expand_grad = jnp.einsum("tr,tq->rq", latent, grad_kv, preferred_element_type=f32)
    grad_latent = jnp.einsum("tq,rq->tr", grad_kv, expand_full, preferred_element_type=f32)
    grad_normed, grad_latent, grad_key_rope = (
        lax.psum(grad_normed.astype(jnp.bfloat16), "tp").astype(jnp.float32),
        lax.psum(grad_latent.astype(jnp.bfloat16), "tp").astype(jnp.float32),
        lax.psum(grad_key_rope.astype(jnp.bfloat16), "tp").astype(jnp.float32),
    )
    latent_gain_grad = jnp.sum(grad_latent * latent_unit, axis=0)
    grad_latent_raw = norm_back(grad_latent * latent_scale, latent_unit, inverse_lat)
    grad_latent_lin = jnp.concatenate(
        [grad_latent_raw, unrotate(grad_key_rope, cosine, sine_part)], axis=-1
    ).astype(bf16)
    latent_grad = jnp.einsum("td,tr->dr", normed, grad_latent_lin, preferred_element_type=f32)
    grad_normed = grad_normed + jnp.einsum(
        "tr,dr->td", grad_latent_lin, latent_full, preferred_element_type=f32
    )
    norm_gain_grad = jnp.sum(grad_normed * normal_in, axis=0)
    input_grad = grad_middle + norm_back(grad_normed * norm_scale, normal_in, inverse_in)
    (
        norm_out,
        query_out,
        latent_out,
        lgain_out,
        expand_out,
        output_out,
        mgain_out,
        router_out,
        gate_out,
        up_out,
        down_out,
    ) = (
        lax.psum_scatter(norm_gain_grad, "fsdp", scatter_dimension=0, tiled=True),
        lax.psum_scatter(query_grad, "fsdp", scatter_dimension=0, tiled=True),
        lax.psum_scatter(latent_grad, "fsdp", scatter_dimension=0, tiled=True),
        lax.psum_scatter(latent_gain_grad, "fsdp", scatter_dimension=0, tiled=True),
        lax.psum_scatter(expand_grad, "fsdp", scatter_dimension=0, tiled=True),
        lax.psum_scatter(output_grad, "fsdp", scatter_dimension=1, tiled=True),
        lax.psum_scatter(moe_gain_grad, "fsdp", scatter_dimension=0, tiled=True),
        lax.psum_scatter(router_grad, "fsdp", scatter_dimension=0, tiled=True),
        lax.psum_scatter(gate_shared_grad, "fsdp", scatter_dimension=0, tiled=True),
        lax.psum_scatter(up_shared_grad, "fsdp", scatter_dimension=0, tiled=True),
        lax.psum_scatter(down_shared_grad, "fsdp", scatter_dimension=1, tiled=True),
    )
    own_start = lax.axis_index("tp") * inputs.shape[0]
    own_activations = lax.dynamic_slice_in_dim(activations, own_start, inputs.shape[0], 0)
    own_input_grad = lax.dynamic_slice_in_dim(input_grad, own_start, inputs.shape[0], 0)
    return (
        loss_value,
        own_activations,
        own_input_grad,
        norm_out,
        query_out,
        latent_out,
        lgain_out,
        expand_out,
        output_out,
        mgain_out,
        router_out,
        gate_out,
        up_out,
        down_out,
        expert_gate_grad,
        expert_up_grad,
        expert_down_grad,
    )


def shards(*arrays):
    fsdp_size = lax.axis_size("fsdp")
    seq_len = arrays[4].shape[0]
    experts = arrays[12].shape[1]
    capacity = arrays[4].shape[1] * seq_len * 4 // (3 * experts)
    fits = fsdp_size * seq_len <= 2 * experts * capacity and fsdp_size == experts
    aligned = arrays[5].shape[0] == BLOCK and arrays[13].shape[1] % BLOCK == 0 and arrays[13].shape[1] <= fsdp_size * BLOCK
    if fits and aligned and fsdp_size % 4 == 0:
        return token_shards(*arrays)
    return slot_shards(*arrays)


def solution(mesh):
    return jax.shard_map(
        shards,
        mesh=mesh,
        in_specs=(
            P(("fsdp", "tp"), None),
            P("fsdp", None),
            P("fsdp"),
            P("fsdp"),
            P("fsdp", None),
            P("fsdp"),
            P("fsdp", "tp"),
            P("fsdp", None),
            P("fsdp"),
            P("fsdp", "tp"),
            P("tp", "fsdp"),
            P("fsdp"),
            P("fsdp", None),
            P("fsdp", "tp"),
            P("fsdp", "tp"),
            P("tp", "fsdp"),
            P("fsdp", None, "tp"),
            P("fsdp", None, "tp"),
            P("fsdp", "tp", None),
        ),
        out_specs=(
            P(),
            P(("fsdp", "tp"), None),
            P(("fsdp", "tp"), None),
            P("fsdp"),
            P("fsdp", "tp"),
            P("fsdp", None),
            P("fsdp"),
            P("fsdp", "tp"),
            P("tp", "fsdp"),
            P("fsdp"),
            P("fsdp", None),
            P("fsdp", "tp"),
            P("fsdp", "tp"),
            P("tp", "fsdp"),
            P("fsdp", None, "tp"),
            P("fsdp", None, "tp"),
            P("fsdp", "tp", None),
        ),
        check_vma=False,
    )
```
